32 devices in a mesh: enc: 2 (over core), dp: 4 (over z), mp: 4 (over y, x).
Axes of the slice: x: 2, y: 2, z: 4, core: 2. Of those that a mesh axis runs over, the one named last changes fastest.
Arguments:
- token_ids: int32 [2, 16, 256], P('enc', 'dp'), may hold values from 0 to 30719
- query_lengths: int32 [32], P('dp'), may hold values from 1 to 128, 2048 in all
- negative_mask: int32 [32, 16], replicated, may hold values 0 or 1
- positive_index: int32 [32], replicated, may hold values from 0 to 15
- used_rows: int32 [32], replicated, may hold values 0 or 1
- step_count: int32 [1], replicated, may hold values from 2 to 20
- table: float32 [2, 30720, 768], P('enc', ('dp', 'mp')), may hold values from -0.18 to 0.18
- w_mixed: float32 [2, 768, 3, 768], P('enc', 'dp', None, 'mp'), may hold values from -0.21875 to 0.21875
- w_out: float32 [2, 768, 768], P('enc', 'mp', 'dp'), may hold values from -0.875 to 0.875
- w_inner: float32 [2, 768, 3072], P('enc', 'dp', 'mp'), may hold values from -0.21875 to 0.21875
- w_outer: float32 [2, 3072, 768], P('enc', 'mp', 'dp'), may hold values from -0.109375 to 0.109375
- norm_params: float32 [2, 6, 768], P('enc'), as said below
- table_m: float32 [2, 30720, 768], P('enc', ('dp', 'mp')), may hold values from -1.1234977e-06 to 1.1234977e-06
- table_v: float32 [2, 30720, 768], P('enc', ('dp', 'mp')), may hold values from 6.5198705e-15 to 2.6079482e-14
- mixed_m: float32 [2, 768, 3, 768], P('enc', 'dp', None, 'mp'), may hold values from -1.1234977e-06 to 1.1234977e-06
- mixed_v: float32 [2, 768, 3, 768], P('enc', 'dp', None, 'mp'), may hold values from 6.5198705e-15 to 2.6079482e-14
- out_m: float32 [2, 768, 768], P('enc', 'mp', 'dp'), may hold values from -1.1234977e-06 to 1.1234977e-06
- out_v: float32 [2, 768, 768], P('enc', 'mp', 'dp'), may hold values from 6.5198705e-15 to 2.6079482e-14
- inner_m: float32 [2, 768, 3072], P('enc', 'dp', 'mp'), may hold values from -1.1234977e-06 to 1.1234977e-06
- inner_v: float32 [2, 768, 3072], P('enc', 'dp', 'mp'), may hold values from 6.5198705e-15 to 2.6079482e-14
- outer_m: float32 [2, 3072, 768], P('enc', 'mp', 'dp'), may hold values from -1.1234977e-06 to 1.1234977e-06
- outer_v: float32 [2, 3072, 768], P('enc', 'mp', 'dp'), may hold values from 6.5198705e-15 to 2.6079482e-14
- norms_m: float32 [2, 6, 768], P('enc'), may hold values from -4.4684566e-06 to 4.4684566e-06
- norms_v: float32 [2, 6, 768], P('enc'), may hold values from 1.0431793e-13 to 4.172717e-13
Outputs:
- loss: float32 [], replicated
- grad_norm: float32 [], replicated
- table_new: float32 [2, 30720, 768], P('enc', ('dp', 'mp'))
- table_m_new: float32 [2, 30720, 768], P('enc', ('dp', 'mp'))
- table_v_new: float32 [2, 30720, 768], P('enc', ('dp', 'mp'))
- mixed_new: float32 [2, 768, 3, 768], P('enc', 'dp', None, 'mp')
- mixed_m_new: float32 [2, 768, 3, 768], P('enc', 'dp', None, 'mp')
- mixed_v_new: float32 [2, 768, 3, 768], P('enc', 'dp', None, 'mp')
- out_new: float32 [2, 768, 768], P('enc', 'mp', 'dp')
- out_m_new: float32 [2, 768, 768], P('enc', 'mp', 'dp')
- output_second_moment_next: float32 [2, 768, 768], P('enc', 'mp', 'dp')
- inner_new: float32 [2, 768, 3072], P('enc', 'dp', 'mp')
- inner_m_new: float32 [2, 768, 3072], P('enc', 'dp', 'mp')
- inner_v_new: float32 [2, 768, 3072], P('enc', 'dp', 'mp')
- outer_new: float32 [2, 3072, 768], P('enc', 'mp', 'dp')
- outer_m_new: float32 [2, 3072, 768], P('enc', 'mp', 'dp')
- outer_v_new: float32 [2, 3072, 768], P('enc', 'mp', 'dp')
- norms_new: float32 [2, 6, 768], P('enc')
- norms_m_new: float32 [2, 6, 768], P('enc')
- norms_v_new: float32 [2, 6, 768], P('enc')
The draws below stay inside these ranges and needn't reach their ends.
Inputs may be any that keep to these rules, and one draw needn't show every extreme that they name: `norm_params`: gains (rows 0, 2, 4) lie in 0.7 to 1.3, shifts (rows 1, 3, 5) are small.
All inputs are finite; a program needn't handle non-finite values. No bound on the sum of `query_lengths` on one device may be relied on, other than what follows from the above.
Results may differ from the reference program's by a relative error of at most 0.015.
Values may be sent and summed in bfloat16 or wider, within the bound.
A program may use at most 192 MiB of HBM per device.

```python
import math
import jax
import jax.numpy as jnp
import numpy as np
from jax import lax

D = 768
HEADS = 12
HEAD = 64
FF = 3072
VOCAB = 30720
QSLOT = 128
PLEN = 256
NB = 16
NQ = 32
NP = 16
NPARAM = 61350912


def draw_norm_params(key, part):
    key_gain = jax.random.fold_in(key, 11)
    key_shift = jax.random.fold_in(key, 12)
    gains = jax.random.uniform(key_gain, (2, 6, D), jnp.float32, 0.7, 1.3)
    shifts = 0.1 * jax.random.normal(key_shift, (2, 6, D), jnp.float32)
    rows = jnp.arange(6)[None, :, None]
    return jnp.where(rows % 2 == 0, gains, shifts)


def with_ends(entries, key, least, largest):
    shape = entries.shape
    place = [jax.random.randint(jax.random.fold_in(key, axis), (), 0, shape[axis]) for axis in range(len(shape))]
    entries = entries.at[tuple(place)].set(least)
    longest = shape.index(max(shape))
    place[longest] = (place[longest] + 1) % shape[longest]
    return entries.at[tuple(place)].set(largest)


def block_scale(own_key, dims, pieces, smallest, top_value):
    def one(dim, blocks):
        heights = jax.random.uniform(jax.random.fold_in(jax.random.fold_in(own_key, 6), dim), (blocks,), jnp.float32, smallest / len(pieces), top_value / len(pieces))
        return jnp.repeat(jnp.exp(heights), dims[dim] // blocks).reshape((-1,) + (1,) * (len(dims) - dim - 1))

    factor_of = one(*pieces[0])
    for cut in pieces[1:]:
        factor_of = factor_of * one(*cut)
    return factor_of


def rank_bounds(number_of, skew):
    portions = [(1 << 20) // math.isqrt(grade ** skew) + 1 for grade in range(1, number_of + 1)]
    scale = 1 + sum(portions) // (1 << 30)
    return np.cumsum(np.array([max(1, weight // scale) for weight in portions]))


def ranked(own_key, shape, amount, skew):
    grid = rank_bounds(amount, skew)
    pick = jax.random.randint(jax.random.fold_in(own_key, 1), shape, 0, int(grid[amount - 1]))
    standing = jnp.searchsorted(jnp.asarray(grid, jnp.int32), pick, side="right")
    return jax.random.permutation(jax.random.fold_in(own_key, 2), amount)[standing].astype(jnp.int32)


def profile(count, total, most, slope):
    weights = [(1 << 20) // math.isqrt(rank ** slope) + 1 for rank in range(2, count + 1)]
    spare, holding = total - most - (count - 1), [1] * (count - 1)
    while spare > 0:
        free = [i for i in range(count - 1) if holding[i] < most]
        pool, budget = sum([weights[i] for i in free]), spare
        for i in free:
            extra = min(most - holding[i], max(1, budget * weights[i] // pool), spare)
            holding[i] = holding[i] + extra
            spare = spare - extra
    return np.array([most] + holding)


def uneven(own_key, count, total, most, lean):
    if count == 2:
        one = jax.random.randint(own_key, (), max(1, total - most), min(most, total - 1) + 1)
        return jnp.stack([one, total - one])
    tallies = jnp.asarray(profile(count, total, most, lean), jnp.int32)
    pairs = (count - 1) // 2
    giver, receiver = tallies[1:1 + 2 * pairs:2], tallies[2:2 + 2 * pairs:2]
    room = jnp.minimum(giver - 1, most - receiver)
    passed = jax.random.randint(jax.random.fold_in(own_key, 1), (pairs,), 0, 1 << 20) % (room + 1)
    tallies = tallies.at[1:1 + 2 * pairs:2].set(giver - passed).at[2:2 + 2 * pairs:2].set(receiver + passed)
    return tallies[jax.random.permutation(jax.random.fold_in(own_key, 2), count)]


def gaussian(key, extent, scale, most, shards=(), dtype=jnp.bfloat16):
    level = block_scale(key, extent, shards, -0.22, 0.18) if shards else 1.0
    entries = jax.random.normal(key, extent, jnp.float32) * scale * level
    return jnp.minimum(jnp.maximum(entries, -most), most).astype(dtype)


def setup_inputs(seed: int = 0) -> dict:
    seeds = jax.random.split(jax.random.key(seed), 25)
    return {
        "token_ids": with_ends(ranked(seeds[0], (2, NB, PLEN), VOCAB, 2), jax.random.fold_in(seeds[0], 3), 0, VOCAB - 1).astype(jnp.int32),
        "query_lengths": uneven(seeds[1], NQ, NQ * QSLOT // 2, QSLOT, 2).astype(jnp.int32),
        "negative_mask": with_ends((jax.random.randint(seeds[2], (NQ, NP), 0, 8) < 1).astype(jnp.int32), jax.random.fold_in(seeds[2], 1), 0, 1),
        "positive_index": with_ends(jax.random.randint(seeds[3], (NQ,), 0, NP), jax.random.fold_in(seeds[3], 1), 0, NP - 1).astype(jnp.int32),
        "used_rows": with_ends((jax.random.randint(seeds[4], (NQ,), 0, 8) < 7).astype(jnp.int32), jax.random.fold_in(seeds[4], 1), 0, 1),
        "step_count": jax.random.randint(seeds[5], (1,), 2, 21).astype(jnp.int32),
        "table": gaussian(seeds[6], (2, VOCAB, D), 0.03, 0.18, ((0, 2), (1, 16)), jnp.float32),
        "w_mixed": gaussian(seeds[7], (2, D, 3, D), D ** -0.5, 0.21875, ((0, 2), (1, 4), (3, 4)), jnp.float32),
        "w_out": gaussian(seeds[8], (2, D, D), (D // 16) ** -0.5, 0.875, ((0, 2), (1, 4), (2, 4)), jnp.float32),
        "w_inner": gaussian(seeds[9], (2, D, FF), D ** -0.5, 0.21875, ((0, 2), (1, 4), (2, 4)), jnp.float32),
        "w_outer": gaussian(seeds[10], (2, FF, D), FF ** -0.5, 0.109375, ((0, 2), (1, 4), (2, 4)), jnp.float32),
        "norm_params": draw_norm_params(jax.random.fold_in(seeds[24], 71), 0),
        "table_m": gaussian(seeds[12], (2, VOCAB, D), (0.0022 / NPARAM ** 0.5), 1.123497668231721e-06, ((0, 2), (1, 16)), jnp.float32),
        "table_v": jnp.clip(jnp.exp(math.log(2.6079482066195155e-14) - 1.3862944 * jax.random.uniform(seeds[13], (2, VOCAB, D), jnp.float32) ** block_scale(seeds[13], (2, VOCAB, D), ((0, 2), (1, 16)), -0.2, 0.2)), 6.519870516548789e-15, 2.6079482066195155e-14),
        "mixed_m": gaussian(seeds[14], (2, D, 3, D), (0.0022 / NPARAM ** 0.5), 1.123497668231721e-06, ((0, 2), (1, 4), (3, 4)), jnp.float32),
        "mixed_v": jnp.clip(jnp.exp(math.log(2.6079482066195155e-14) - 1.3862944 * jax.random.uniform(seeds[15], (2, D, 3, D), jnp.float32) ** block_scale(seeds[15], (2, D, 3, D), ((0, 2), (1, 4), (3, 4)), -0.2, 0.2)), 6.519870516548789e-15, 2.6079482066195155e-14),
        "out_m": gaussian(seeds[16], (2, D, D), (0.0022 / NPARAM ** 0.5), 1.123497668231721e-06, ((0, 2), (1, 4), (2, 4)), jnp.float32),
        "out_v": jnp.clip(jnp.exp(math.log(2.6079482066195155e-14) - 1.3862944 * jax.random.uniform(seeds[17], (2, D, D), jnp.float32) ** block_scale(seeds[17], (2, D, D), ((0, 2), (1, 4), (2, 4)), -0.2, 0.2)), 6.519870516548789e-15, 2.6079482066195155e-14),
        "inner_m": gaussian(seeds[18], (2, D, FF), (0.0022 / NPARAM ** 0.5), 1.123497668231721e-06, ((0, 2), (1, 4), (2, 4)), jnp.float32),
        "inner_v": jnp.clip(jnp.exp(math.log(2.6079482066195155e-14) - 1.3862944 * jax.random.uniform(seeds[19], (2, D, FF), jnp.float32) ** block_scale(seeds[19], (2, D, FF), ((0, 2), (1, 4), (2, 4)), -0.2, 0.2)), 6.519870516548789e-15, 2.6079482066195155e-14),
        "outer_m": gaussian(seeds[20], (2, FF, D), (0.0022 / NPARAM ** 0.5), 1.123497668231721e-06, ((0, 2), (1, 4), (2, 4)), jnp.float32),
        "outer_v": jnp.clip(jnp.exp(math.log(2.6079482066195155e-14) - 1.3862944 * jax.random.uniform(seeds[21], (2, FF, D), jnp.float32) ** block_scale(seeds[21], (2, FF, D), ((0, 2), (1, 4), (2, 4)), -0.2, 0.2)), 6.519870516548789e-15, 2.6079482066195155e-14),
        "norms_m": gaussian(seeds[22], (2, 6, D), (0.0088 / NPARAM ** 0.5), 4.468456609174609e-06, ((0, 2),), jnp.float32),
        "norms_v": jnp.clip(jnp.exp(math.log(4.1727171305912247e-13) - 1.3862944 * jax.random.uniform(seeds[23], (2, 6, D), jnp.float32) ** block_scale(seeds[23], (2, 6, D), ((0, 2),), -0.2, 0.2)), 1.0431792826478062e-13, 4.1727171305912247e-13),
    }


@jax.custom_vjp
def low(v):
    return lax.optimization_barrier(v.astype(jnp.bfloat16)).astype(jnp.float32)

@jax.custom_vjp
def low_back(v):
    return v

def low_keep(v):
    return (low(v), None)

def low_pass(kept, grad):
    return (grad,)

def back_keep(v):
    return (v, None)

def back_low(kept, grad):
    return (low(grad),)
low.defvjp(low_keep, low_pass)
low_back.defvjp(back_keep, back_low)
exact_arithmetic_level = lax.Precision.HIGHEST
eps_norm = 1e-06
logit_divisor = 0.05
clip_limit = 0.02
beta_one = 0.9
beta_two = 0.999
adam_eps = 1e-08

def layer_norm(x, gain, shift):
    centred = x - lax.optimization_barrier(jnp.mean(x, -1, keepdims=True))
    spread = lax.optimization_barrier(jnp.mean(centred * centred, -1, keepdims=True))
    return centred * lax.rsqrt(spread + eps_norm) * gain + shift

def encode_group(params, ids, lens_block, is_query):
    table, w_mixed, w_out, w_inner, w_outer, norms = params
    group = ids.shape[0]
    diagonal_indices = jnp.arange(PLEN)
    if is_query:
        segment = diagonal_indices // QSLOT
        limit = jnp.where(segment[None, :] == 0, lens_block[:, 0:1], lens_block[:, 1:2])
        key_ok = (diagonal_indices % QSLOT)[None, :] < limit
        allowed = (segment[:, None] == segment[None, :])[None] & key_ok[:, None, :]
    else:
        allowed = jnp.ones((group, PLEN, PLEN), bool)
    embedded = table[ids]
    hidden0 = layer_norm(embedded, norms[0], norms[1])
    mixed = jnp.einsum('gld,dcf->glcf', low(hidden0), w_mixed, precision=exact_arithmetic_level)
    mixed = low_back(low(mixed)).reshape(group, PLEN, 3, HEADS, HEAD)
    queries, keys, values = (mixed[:, :, 0], mixed[:, :, 1], mixed[:, :, 2])
    scores = jnp.einsum('gqhd,gkhd->ghqk', queries, keys, precision=exact_arithmetic_level) * HEAD ** (-0.5)
    scores = jnp.where(allowed[:, None], low_back(scores), -1e+30)
    probs = jax.nn.softmax(scores, -1)
    attended = jnp.einsum('ghqk,gkhd->gqhd', low(probs), values, precision=exact_arithmetic_level)
    attended = low_back(low(attended)).reshape(group, PLEN, D)
    attn_out = low_back(jnp.einsum('gld,de->gle', attended, w_out, precision=exact_arithmetic_level))
    normed = layer_norm(hidden0 + attn_out, norms[2], norms[3])
    inner = low_back(jnp.einsum('gld,df->glf', low(normed), w_inner, precision=exact_arithmetic_level))
    activated = low(jax.nn.gelu(inner, approximate=False))
    outer = low_back(jnp.einsum('glf,fd->gld', activated, w_outer, precision=exact_arithmetic_level))
    final = layer_norm(normed + outer, norms[4], norms[5])
    return jnp.stack([final[:, 0], final[:, QSLOT]], 1)

def encode(params, ids, lens, is_query):
    group = math.gcd(NB, 16)

    def one(item):
        return encode_group(params, item[0], item[1], is_query)
    result = lax.map(jax.checkpoint(one), (ids.reshape(-1, group, PLEN), lens.reshape(-1, group, 2)))
    return result.reshape(NB, 2, D)

def contrast(queries, passages, negative_mask, positive_index, used_rows):
    question_direction_rows = queries * lax.rsqrt(lax.optimization_barrier(jnp.sum(queries * queries, -1, keepdims=True)) + eps_norm)
    document_direction_rows = passages * lax.rsqrt(lax.optimization_barrier(jnp.sum(passages * passages, -1, keepdims=True)) + eps_norm)
    pairwise_cosine_table = jnp.dot(question_direction_rows, document_direction_rows.T, precision=exact_arithmetic_level) / logit_divisor
    excluded = (negative_mask == 1) & (jnp.arange(passages.shape[0])[None, :] != positive_index[:, None])
    pairwise_cosine_table = jnp.where(excluded, -1e+30, pairwise_cosine_table)
    top = lax.optimization_barrier(jnp.max(pairwise_cosine_table, -1, keepdims=True))
    log_total = top[:, 0] + jnp.log(lax.optimization_barrier(jnp.sum(jnp.exp(pairwise_cosine_table - top), -1)))
    target = jnp.take_along_axis(pairwise_cosine_table, positive_index[:, None], 1)[:, 0]
    weight = used_rows.astype(jnp.float32)
    return jnp.sum(weight * (log_total - target)) / jnp.maximum(jnp.sum(weight), 1.0)

def adam_step(weight, grad, first, second, rate, decay, count):
    first_new = beta_one * first + (1.0 - beta_one) * grad
    second_new = beta_two * second + (1.0 - beta_two) * grad * grad
    fix_one = 1.0 - jnp.power(beta_one, count)
    correction_second = 1.0 - jnp.power(beta_two, count)
    update = first_new / fix_one / (jnp.sqrt(second_new / correction_second) + adam_eps) + decay * weight
    return (weight - rate * update, first_new, second_new)

def reference(token_ids, query_lengths, negative_mask, positive_index, used_rows, step_count, table, w_mixed, w_out, w_inner, w_outer, norm_params, table_m, table_v, mixed_m, mixed_v, out_m, out_v, inner_m, inner_v, outer_m, outer_v, norms_m, norms_v):
    lens = query_lengths.reshape(NB, 2)
    empty_lens = jnp.zeros((NB, 2), jnp.int32)

    def loss_fn(weights):
        outputs = []
        for enc in range(2):
            params = (low(weights[0][enc]), low(weights[1][enc]), low(weights[2][enc]), low(weights[3][enc]), low(weights[4][enc]), weights[5][enc])
            outputs.append(encode(params, token_ids[enc], lens if enc == 0 else empty_lens, enc == 0))
        queries = outputs[0].reshape(NQ, D)
        passages = outputs[1][:, 0]
        return contrast(queries, passages, negative_mask, positive_index, used_rows)
    weights = (table, w_mixed, w_out, w_inner, w_outer, norm_params)
    loss, loss_back = jax.vjp(loss_fn, weights)
    grads = loss_back(jnp.ones((), jnp.float32))[0]
    squares = jnp.zeros((), jnp.float32)
    for grad in grads:
        squares = squares + jnp.sum(grad * grad)
    grad_norm = jnp.sqrt(squares)
    clip = jnp.minimum(1.0, clip_limit / (grad_norm + 1e-06))
    count = step_count[0].astype(jnp.float32)
    firsts = (table_m, mixed_m, out_m, inner_m, outer_m, norms_m)
    seconds = (table_v, mixed_v, out_v, inner_v, outer_v, norms_v)
    results = []
    for index in range(6):
        rate = 0.5 if index == 5 else 0.06
        decay = 0.0 if index == 5 else 0.01
        results.append(adam_step(weights[index], grads[index] * clip, firsts[index], seconds[index], rate, decay, count))
    return (loss, grad_norm, results[0][0], results[0][1], results[0][2], results[1][0], results[1][1], results[1][2], results[2][0], results[2][1], results[2][2], results[3][0], results[3][1], results[3][2], results[4][0], results[4][1], results[4][2], results[5][0], results[5][1], results[5][2])
```

```python
from functools import partial

import jax
import jax.numpy as jnp
from jax import lax
from jax.sharding import PartitionSpec as P

HEAD = 64
QSLOT = 128
F32 = jnp.float32
BF16 = jnp.bfloat16

exact_arithmetic_level = lax.Precision.HIGHEST
eps_norm = 1e-06
logit_divisor = 0.05
clip_limit = 0.02
beta_one = 0.9
beta_two = 0.999
adam_eps = 1e-08


def layer_norm(x, gain, shift):
    centred = x - jnp.mean(x, -1, keepdims=True)
    spread = jnp.mean(centred * centred, -1, keepdims=True)
    return centred * lax.rsqrt(spread + eps_norm) * gain + shift


def mul(spec, a, b):
    return jnp.einsum(spec, a, b, preferred_element_type=F32)


def token_counts(ids, lens, is_query, base, rows):
    pos = jnp.arange(ids.shape[1])
    slot = pos // QSLOT
    limit = jnp.where(slot[None, :] == 0, lens[:, 0:1], lens[:, 1:2])
    within = (pos % QSLOT)[None, :] < limit
    same = slot[None, :] == jnp.arange(2)[:, None]
    allowed = jnp.where(is_query, same[:, None, :] & within[None], True)
    local = ids - base
    n_hi = -(-rows // 128)
    high = (local[..., None] >> 7) == jnp.arange(n_hi)
    low = (local[..., None] & 127) == jnp.arange(128)
    left = (allowed[..., None] & high[None]).astype(BF16)
    counts = mul("sbth,btl->sbhl", left, low.astype(BF16))
    return counts.reshape(2 * ids.shape[0], n_hi * 128)[:, :rows]


def contrast(queries, passages, negative_mask, positive_index, used_rows):
    question_direction_rows = queries * lax.rsqrt(
        jnp.sum(queries * queries, -1, keepdims=True) + eps_norm
    )
    document_direction_rows = passages * lax.rsqrt(
        jnp.sum(passages * passages, -1, keepdims=True) + eps_norm
    )
    pairwise_cosine_table = (
        jnp.dot(
            question_direction_rows, document_direction_rows.T, precision=exact_arithmetic_level
        )
        / logit_divisor
    )
    is_positive = jnp.arange(passages.shape[0])[None, :] == positive_index[:, None]
    excluded = (negative_mask == 1) & ~is_positive
    pairwise_cosine_table = jnp.where(excluded, -1e30, pairwise_cosine_table)
    top = jnp.max(pairwise_cosine_table, -1, keepdims=True)
    log_total = top[:, 0] + jnp.log(jnp.sum(jnp.exp(pairwise_cosine_table - top), -1))
    target = jnp.sum(jnp.where(is_positive, pairwise_cosine_table, 0.0), -1)
    weight = used_rows.astype(F32)
    return jnp.sum(weight * (log_total - target)) / jnp.maximum(jnp.sum(weight), 1.0)


def adam_step(weight, grad, first, second, rate, decay, count):
    first_new = beta_one * first + (1.0 - beta_one) * grad
    second_new = beta_two * second + (1.0 - beta_two) * grad * grad
    fix_one = 1.0 - jnp.power(beta_one, count)
    correction_second = 1.0 - jnp.power(beta_two, count)
    update = (
        first_new / fix_one / (jnp.sqrt(second_new / correction_second) + adam_eps) + decay * weight
    )
    return (weight - rate * update, first_new, second_new)


def slot_major(x):
    return x.reshape((x.shape[0] // 2, 2) + x.shape[1:]).swapaxes(0, 1).reshape(x.shape)


def gradients(
    token_ids, query_lengths, negative_mask, positive_index, used_rows, table, w_mixed, w_out, w_inner, w_outer, norm_params
):
    is_query = lax.axis_index("enc") == 0
    d, m = lax.axis_index("dp"), lax.axis_index("mp")
    n_mp = lax.axis_size("mp")
    rows, width = table.shape[1], w_mixed.shape[1]
    hm = w_out.shape[1] // HEAD
    scale = HEAD ** (-0.5)
    norms = norm_params[0]
    base = (d * n_mp + m) * rows

    ids = lax.all_gather(token_ids[0], "dp", axis=0, tiled=True)
    lens = lax.all_gather(query_lengths, "dp", axis=0, tiled=True).reshape(-1, 2)
    blocks = ids.shape[0]
    counts = token_counts(ids, lens, is_query, base, rows)
    cls_ids = jnp.concatenate([ids[:, 0], ids[:, QSLOT]]) - base
    cls_hot = cls_ids[:, None] == jnp.arange(rows)[None, :]

    def mine(x):
        return lax.dynamic_slice_in_dim(x, d * width, width, 1)

    wq, wk, wv = (w_mixed[0, :, i].astype(BF16).reshape(width, hm, HEAD) for i in range(3))
    wo = w_out[0].astype(BF16).reshape(hm, HEAD, width)
    wi, wt = w_inner[0].astype(BF16), w_outer[0].astype(BF16)

    embedded = lax.reduce_precision(table[0], 8, 7)
    hidden, hidden_back = jax.vjp(layer_norm, embedded, norms[0], norms[1])
    hid = hidden.astype(BF16)
    first_rows = lax.psum(
        jnp.dot(cls_hot.astype(F32), hidden, precision=exact_arithmetic_level), ("dp", "mp")
    )
    first_mine = mine(first_rows).astype(BF16)
    q = lax.psum(mul("ci,ihk->hck", first_mine, wq), "dp").astype(BF16)
    u = mul("hck,ihk->hci", q, wk).astype(BF16)
    u = lax.all_gather(lax.all_gather(u, "dp", axis=2, tiled=True), "mp", axis=0, tiled=True)
    scores = jnp.where(counts[None] > 0, mul("hci,vi->hcv", u, hid) * scale, -1e30)
    top = lax.pmax(jnp.max(scores, -1, keepdims=True), ("dp", "mp"))
    weight = counts[None] * jnp.exp(scores - top)
    probs = weight / lax.psum(jnp.sum(weight, -1, keepdims=True), ("dp", "mp"))
    probs_low = probs.astype(BF16)
    z = mul("hcv,vi->hci", probs_low, hid)
    z = lax.psum_scatter(z, "mp", scatter_dimension=0, tiled=True)
    z = lax.psum_scatter(z, "dp", scatter_dimension=2, tiled=True).astype(BF16)
    att = lax.psum(mul("hci,ihk->hck", z, wv), "dp")
    att_low = att.astype(BF16)
    out = lax.psum(mul("hck,hke->ce", att_low, wo), "mp")
    first_sum = first_rows + lax.all_gather(out, "dp", axis=1, tiled=True)
    normed, normed_back = jax.vjp(layer_norm, first_sum, norms[2], norms[3])
    normed_mine = mine(normed).astype(BF16)
    inner = lax.psum(mul("ci,if->cf", normed_mine, wi), "dp")
    act, act_back = jax.vjp(partial(jax.nn.gelu, approximate=False), inner)
    act = act.astype(BF16)
    outer = lax.psum(mul("cf,fe->ce", act, wt), "mp")
    second_sum = normed + lax.all_gather(outer, "dp", axis=1, tiled=True)
    final, final_back = jax.vjp(layer_norm, second_sum, norms[4], norms[5])
    both = lax.all_gather(final, "enc", axis=0)
    loss, loss_back = jax.vjp(
        partial(
            contrast,
            negative_mask=slot_major(negative_mask),
            positive_index=slot_major(positive_index),
            used_rows=slot_major(used_rows),
        ),
        both[0],
        both[1, :blocks],
    )
    d_queries, d_passages = loss_back(jnp.ones((), F32))
    d_passages = jnp.concatenate([d_passages, jnp.zeros_like(d_passages)])
    d_final = jnp.where(is_query, d_queries, d_passages)

    d_second, d_gain2, d_shift2 = final_back(d_final)
    d_outer = mine(d_second).astype(BF16)
    g_outer = mul("cf,ce->fe", act, d_outer)
    d_act = lax.psum(mul("ce,fe->cf", d_outer, wt), "dp")
    d_inner = act_back(d_act)[0].astype(BF16)
    g_inner = mul("ci,cf->if", normed_mine, d_inner)
    d_in = lax.psum(mul("cf,if->ci", d_inner, wi), "mp")
    d_normed = d_second + lax.all_gather(d_in, "dp", axis=1, tiled=True)
    d_first, d_gain1, d_shift1 = normed_back(d_normed)
    d_attn = mine(d_first).astype(BF16)
    g_out = mul("hck,ce->hke", att_low, d_attn).reshape(w_out.shape[1:])
    d_att = lax.psum(mul("ce,hke->hck", d_attn, wo), "dp").astype(BF16)
    w = mul("hck,ihk->hci", d_att, wv).astype(BF16)
    mean_d = jnp.sum(att * d_att.astype(F32), -1, keepdims=True)
    w = lax.all_gather(lax.all_gather(w, "dp", axis=2, tiled=True), "mp", axis=0, tiled=True)
    mean_d = lax.all_gather(mean_d, "mp", axis=0, tiled=True)
    d_probs = mul("hci,vi->hcv", w, hid)
    d_scores = (probs * (d_probs - mean_d)).astype(BF16)
    y = mul("hcv,vi->hci", d_scores, hid)
    y = lax.psum_scatter(y, "mp", scatter_dimension=0, tiled=True)
    y = lax.psum_scatter(y, "dp", scatter_dimension=2, tiled=True).astype(BF16)
    dq = (lax.psum(mul("hci,ihk->hck", y, wk), "dp") * scale).astype(BF16)
    g_q = mul("ci,hck->ihk", first_mine, dq)
    g_k = mul("hci,hck->ihk", y, q) * scale
    g_v = mul("hci,hck->ihk", z, d_att)
    g_mixed = jnp.stack([g_q, g_k, g_v], 1).reshape(w_mixed.shape[1:])
    d_rows = lax.psum(mul("hck,ihk->ci", dq, wq), "mp")
    d_rows = (d_first + lax.all_gather(d_rows, "dp", axis=1, tiled=True)).astype(BF16)
    d_hidden = (
        mul("hcv,hci->vi", d_scores, u) * scale
        + mul("hcv,hci->vi", probs_low, w)
        + mul("cv,ci->vi", cls_hot.astype(BF16), d_rows)
    )
    g_table, d_gain0, d_shift0 = hidden_back(d_hidden)
    sums = lax.psum(jnp.stack([d_gain0, d_shift0]), ("dp", "mp"))
    g_norms = jnp.concatenate([sums, jnp.stack([d_gain1, d_shift1, d_gain2, d_shift2])])
    return loss, (g_table, g_mixed, g_out, g_inner, g_outer, g_norms)


def on_device(
    token_ids,
    query_lengths,
    negative_mask,
    positive_index,
    used_rows,
    step_count,
    table,
    w_mixed,
    w_out,
    w_inner,
    w_outer,
    norm_params,
    table_m,
    table_v,
    mixed_m,
    mixed_v,
    out_m,
    out_v,
    inner_m,
    inner_v,
    outer_m,
    outer_v,
    norms_m,
    norms_v,
):
    loss, grads = gradients(
        token_ids, query_lengths, negative_mask, positive_index, used_rows, table, w_mixed, w_out, w_inner, w_outer, norm_params
    )
    owner = (lax.axis_index("dp") == 0) & (lax.axis_index("mp") == 0)
    squares = jnp.where(owner, jnp.sum(grads[5] * grads[5]), 0.0)
    for grad in grads[:5]:
        squares = squares + jnp.sum(grad * grad)
    grad_norm = jnp.sqrt(lax.psum(squares, ("enc", "dp", "mp")))
    clip = jnp.minimum(1.0, clip_limit / (grad_norm + 1e-06))
    count = step_count[0].astype(F32)
    masters = (table, w_mixed, w_out, w_inner, w_outer, norm_params)
    firsts = (table_m, mixed_m, out_m, inner_m, outer_m, norms_m)
    seconds = (table_v, mixed_v, out_v, inner_v, outer_v, norms_v)
    results = [loss, grad_norm]
    for index in range(6):
        rate, decay = (0.5, 0.0) if index == 5 else (0.06, 0.01)
        results.extend(
            adam_step(
                masters[index], grads[index][None] * clip, firsts[index], seconds[index], rate, decay, count
            )
        )
    return tuple(results)


def solution(mesh):
    table = P("enc", ("dp", "mp"), None)
    mixed = P("enc", "dp", None, "mp")
    columns = P("enc", "mp", "dp")
    units = P("enc", "dp", "mp")
    norms = P("enc", None, None)
    matrices = (table, mixed, columns, units, columns, norms)
    moments = tuple(spec for spec in matrices for _ in range(2))
    updated = tuple(spec for spec in matrices for _ in range(3))
    return jax.shard_map(
        on_device,
        mesh=mesh,
        in_specs=(P("enc", "dp", None), P("dp"), P(), P(), P(), P()) + matrices + moments,
        out_specs=(P(), P()) + updated,
        check_vma=False,
    )
```

```python
import math
from functools import partial

import jax
import jax.numpy as jnp
from jax import lax
from jax.experimental import pallas as pl
from jax.experimental.pallas import tpu as pltpu
from jax.sharding import PartitionSpec as P

HEAD = 64
QSLOT = 128
F32 = jnp.float32
BF16 = jnp.bfloat16

exact_arithmetic_level = lax.Precision.HIGHEST
eps_norm = 1e-06
logit_divisor = 0.05
clip_limit = 0.02
beta_one = 0.9
beta_two = 0.999
adam_eps = 1e-08


def layer_norm(x, gain, shift):
    centred = x - jnp.mean(x, -1, keepdims=True)
    spread = jnp.mean(centred * centred, -1, keepdims=True)
    return centred * lax.rsqrt(spread + eps_norm) * gain + shift


def mul(spec, a, b):
    return jnp.einsum(spec, a, b, preferred_element_type=F32)


def token_counts(ids, lens, is_query, base, rows):
    pos = jnp.arange(ids.shape[1])
    slot = pos // QSLOT
    limit = jnp.where(slot[None, :] == 0, lens[:, 0:1], lens[:, 1:2])
    within = (pos % QSLOT)[None, :] < limit
    same = slot[None, :] == jnp.arange(2)[:, None]
    allowed = jnp.where(is_query, same[:, None, :] & within[None], True)
    local = ids - base
    n_hi = -(-rows // 128)
    high = (local[..., None] >> 7) == jnp.arange(n_hi)
    low = (local[..., None] & 127) == jnp.arange(128)
    left = (allowed[..., None] & high[None]).astype(BF16)
    counts = mul("sbth,btl->sbhl", left, low.astype(BF16))
    return counts.reshape(2 * ids.shape[0], n_hi * 128)[:, :rows]


def contrast(queries, passages, negative_mask, positive_index, used_rows):
    question_direction_rows = queries * lax.rsqrt(
        jnp.sum(queries * queries, -1, keepdims=True) + eps_norm
    )
    document_direction_rows = passages * lax.rsqrt(
        jnp.sum(passages * passages, -1, keepdims=True) + eps_norm
    )
    pairwise_cosine_table = (
        jnp.dot(
            question_direction_rows, document_direction_rows.T, precision=exact_arithmetic_level
        )
        / logit_divisor
    )
    is_positive = jnp.arange(passages.shape[0])[None, :] == positive_index[:, None]
    excluded = (negative_mask == 1) & ~is_positive
    pairwise_cosine_table = jnp.where(excluded, -1e30, pairwise_cosine_table)
    top = jnp.max(pairwise_cosine_table, -1, keepdims=True)
    log_total = top[:, 0] + jnp.log(jnp.sum(jnp.exp(pairwise_cosine_table - top), -1))
    target = jnp.sum(jnp.where(is_positive, pairwise_cosine_table, 0.0), -1)
    weight = used_rows.astype(F32)
    return jnp.sum(weight * (log_total - target)) / jnp.maximum(jnp.sum(weight), 1.0)


def adam_step(weight, grad, first, second, rate, decay, count):
    first_new = beta_one * first + (1.0 - beta_one) * grad
    second_new = beta_two * second + (1.0 - beta_two) * grad * grad
    fix_one = 1.0 - jnp.power(beta_one, count)
    correction_second = 1.0 - jnp.power(beta_two, count)
    update = (
        first_new / fix_one / (jnp.sqrt(second_new / correction_second) + adam_eps) + decay * weight
    )
    return (weight - rate * update, first_new, second_new)


def slot_major(x):
    return x.reshape((x.shape[0] // 2, 2) + x.shape[1:]).swapaxes(0, 1).reshape(x.shape)


def gradients(
    token_ids, query_lengths, negative_mask, positive_index, used_rows, table, w_mixed, w_out, w_inner, w_outer, norm_params
):
    is_query = lax.axis_index("enc") == 0
    d, m = lax.axis_index("dp"), lax.axis_index("mp")
    n_mp = lax.axis_size("mp")
    rows, width = table.shape[1], w_mixed.shape[1]
    hm = w_out.shape[1] // HEAD
    scale = HEAD ** (-0.5)
    norms = norm_params[0]
    base = (d * n_mp + m) * rows

    ids = lax.all_gather(token_ids[0], "dp", axis=0, tiled=True)
    lens = lax.all_gather(query_lengths, "dp", axis=0, tiled=True).reshape(-1, 2)
    blocks = ids.shape[0]
    counts = token_counts(ids, lens, is_query, base, rows)
    cls_ids = jnp.concatenate([ids[:, 0], ids[:, QSLOT]]) - base
    cls_hot = cls_ids[:, None] == jnp.arange(rows)[None, :]

    def mine(x):
        return lax.dynamic_slice_in_dim(x, d * width, width, 1)

    wq, wk, wv = (w_mixed[0, :, i].astype(BF16).reshape(width, hm, HEAD) for i in range(3))
    wo = w_out[0].astype(BF16).reshape(hm, HEAD, width)
    wi, wt = w_inner[0].astype(BF16), w_outer[0].astype(BF16)

    embedded = lax.reduce_precision(table[0], 8, 7)
    hidden, hidden_back = jax.vjp(layer_norm, embedded, norms[0], norms[1])
    hid = hidden.astype(BF16)
    first_rows = lax.psum(
        jnp.dot(cls_hot.astype(F32), hidden, precision=exact_arithmetic_level), ("dp", "mp")
    )
    first_mine = mine(first_rows).astype(BF16)
    q = lax.psum(mul("ci,ihk->hck", first_mine, wq), "dp").astype(BF16)
    u = mul("hck,ihk->hci", q, wk).astype(BF16)
    u = lax.all_gather(lax.all_gather(u, "dp", axis=2, tiled=True), "mp", axis=0, tiled=True)
    scores = jnp.where(counts[None] > 0, mul("hci,vi->hcv", u, hid) * scale, -1e30)
    top = lax.pmax(jnp.max(scores, -1, keepdims=True), ("dp", "mp"))
    weight = counts[None] * jnp.exp(scores - top)
    probs = weight / lax.psum(jnp.sum(weight, -1, keepdims=True), ("dp", "mp"))
    probs_low = probs.astype(BF16)
    z = mul("hcv,vi->hci", probs_low, hid)
    z = lax.psum_scatter(z, "mp", scatter_dimension=0, tiled=True)
    z = lax.psum_scatter(z, "dp", scatter_dimension=2, tiled=True).astype(BF16)
    att = lax.psum(mul("hci,ihk->hck", z, wv), "dp")
    att_low = att.astype(BF16)
    out = lax.psum(mul("hck,hke->ce", att_low, wo), "mp")
    first_sum = first_rows + lax.all_gather(out, "dp", axis=1, tiled=True)
    normed, normed_back = jax.vjp(layer_norm, first_sum, norms[2], norms[3])
    normed_mine = mine(normed).astype(BF16)
    inner = lax.psum(mul("ci,if->cf", normed_mine, wi), "dp")
    act, act_back = jax.vjp(partial(jax.nn.gelu, approximate=False), inner)
    act = act.astype(BF16)
    outer = lax.psum(mul("cf,fe->ce", act, wt), "mp")
    second_sum = normed + lax.all_gather(outer, "dp", axis=1, tiled=True)
    final, final_back = jax.vjp(layer_norm, second_sum, norms[4], norms[5])
    both = lax.all_gather(final, "enc", axis=0)
    loss, loss_back = jax.vjp(
        partial(
            contrast,
            negative_mask=slot_major(negative_mask),
            positive_index=slot_major(positive_index),
            used_rows=slot_major(used_rows),
        ),
        both[0],
        both[1, :blocks],
    )
    d_queries, d_passages = loss_back(jnp.ones((), F32))
    d_passages = jnp.concatenate([d_passages, jnp.zeros_like(d_passages)])
    d_final = jnp.where(is_query, d_queries, d_passages)

    d_second, d_gain2, d_shift2 = final_back(d_final)
    d_outer = mine(d_second).astype(BF16)
    g_outer = mul("cf,ce->fe", act, d_outer)
    d_act = lax.psum(mul("ce,fe->cf", d_outer, wt), "dp")
    d_inner = act_back(d_act)[0].astype(BF16)
    g_inner = mul("ci,cf->if", normed_mine, d_inner)
    d_in = lax.psum(mul("cf,if->ci", d_inner, wi), "mp")
    d_normed = d_second + lax.all_gather(d_in, "dp", axis=1, tiled=True)
    d_first, d_gain1, d_shift1 = normed_back(d_normed)
    d_attn = mine(d_first).astype(BF16)
    g_out = mul("hck,ce->hke", att_low, d_attn).reshape(w_out.shape[1:])
    d_att = lax.psum(mul("ce,hke->hck", d_attn, wo), "dp").astype(BF16)
    w = mul("hck,ihk->hci", d_att, wv).astype(BF16)
    mean_d = jnp.sum(att * d_att.astype(F32), -1, keepdims=True)
    w = lax.all_gather(lax.all_gather(w, "dp", axis=2, tiled=True), "mp", axis=0, tiled=True)
    mean_d = lax.all_gather(mean_d, "mp", axis=0, tiled=True)
    d_probs = mul("hci,vi->hcv", w, hid)
    d_scores = (probs * (d_probs - mean_d)).astype(BF16)
    y = mul("hcv,vi->hci", d_scores, hid)
    y = lax.psum_scatter(y, "mp", scatter_dimension=0, tiled=True)
    y = lax.psum_scatter(y, "dp", scatter_dimension=2, tiled=True).astype(BF16)
    dq = (lax.psum(mul("hci,ihk->hck", y, wk), "dp") * scale).astype(BF16)
    g_q = mul("ci,hck->ihk", first_mine, dq)
    g_k = mul("hci,hck->ihk", y, q) * scale
    g_v = mul("hci,hck->ihk", z, d_att)
    g_mixed = jnp.stack([g_q, g_k, g_v], 1).reshape(w_mixed.shape[1:])
    d_rows = lax.psum(mul("hck,ihk->ci", dq, wq), "mp")
    d_rows = (d_first + lax.all_gather(d_rows, "dp", axis=1, tiled=True)).astype(BF16)
    d_hidden = (
        mul("hcv,hci->vi", d_scores, u) * scale
        + mul("hcv,hci->vi", probs_low, w)
        + mul("cv,ci->vi", cls_hot.astype(BF16), d_rows)
    )
    g_table, d_gain0, d_shift0 = hidden_back(d_hidden)
    sums = lax.psum(jnp.stack([d_gain0, d_shift0]), ("dp", "mp"))
    g_norms = jnp.concatenate([sums, jnp.stack([d_gain1, d_shift1, d_gain2, d_shift2])])
    return loss, (g_table, g_mixed, g_out, g_inner, g_outer, g_norms)


MESH = pl.DeviceIdType.MESH
ENTRY_ID = 3
PHASES = (
    "ids", "rows", "q", "att", "z", "out", "inner", "outer", "final",
    "d_act", "d_in", "d_att", "dq", "y", "d_rows", "sums", "norm",
)
BLOCK = 64


def nt(a, b):
    return lax.dot_general(a, b, (((1,), (1,)), ((), ())), preferred_element_type=F32)


def tn(a, b):
    return lax.dot_general(a, b, (((0,), (0,)), ((), ())), preferred_element_type=F32)


def nn(a, b):
    return jnp.dot(a, b, preferred_element_type=F32)


def exact_nt(a, b):
    return lax.dot_general(
        a, b, (((1,), (1,)), ((), ())), precision=exact_arithmetic_level, preferred_element_type=F32
    )


def exact_nn(a, b):
    return jnp.dot(a, b, precision=exact_arithmetic_level, preferred_element_type=F32)


def slab_norm(slabs, size):
    mean = sum(jnp.sum(s, -1, keepdims=True) for s in slabs) * (1.0 / size)
    slabs = [s - mean for s in slabs]
    spread = sum(jnp.sum(s * s, -1, keepdims=True) for s in slabs) * (1.0 / size)
    r = lax.rsqrt(spread + eps_norm)
    return [s * r for s in slabs], r


def slab_norm_back(hats, r, grads, gains, size):
    scaled = [dy * g for dy, g in zip(grads, gains)]
    mean = sum(jnp.sum(s, -1, keepdims=True) for s in scaled) * (1.0 / size)
    along = sum(jnp.sum(s * h, -1, keepdims=True) for s, h in zip(scaled, hats)) * (1.0 / size)
    d_in = [r * (s - mean - h * along) for s, h in zip(scaled, hats)]
    d_gain = [jnp.sum(dy * h, 0, keepdims=True) for dy, h in zip(grads, hats)]
    d_shift = [jnp.sum(dy, 0, keepdims=True) for dy in grads]
    return d_in, d_gain, d_shift


def split_low(x, parts):
    out = []
    for _ in range(parts):
        piece = x.astype(BF16)
        out.append(piece)
        x = x - piece.astype(F32)
    return out


def grad_kernel(cfg, *refs):
    nd, nm, blk, rows, width, size, hm, ff = cfg
    n = nd * nm
    nb = nd * blk
    c = 2 * nb
    hw = hm * HEAD
    group = hm * c
    half = hm * nb
    heads = nm * group
    vt = 384
    tiles = rows // vt
    scale = HEAD ** (-0.5)
    (
        ids_ref, lens_ref, meta_ref, meta_t_ref, norms_ref,
        table_hbm, mixed_hbm, out_hbm, inner_hbm, outer_hbm,
        small_ref, g_table_hbm, g_q_ref, g_k_ref, g_v_ref, g_out_ref, g_inner_ref, g_outer_ref, g_norms_ref,
        stage, emb, hid, weights, lows, basis, counts, xs, acc, col,
        mixed_f, out_f, inner_f, outer_f, wq, wo, wi, wt, kv,
        ids_buf, rows_src, rows_buf, q_buf, att_src, att_buf, z_src, z_buf, out_buf, inner_buf, outer_buf,
        final_buf, d_act_buf, d_in_buf, d_att_buf, dq_src, dq_buf, y_src, y_buf, d_rows_buf, sums_buf, norm_buf,
        send_sem, recv_sem, kv_send, kv_recv, kv_spread, load_sem, table_sem, store_sem,
    ) = refs
    e, d, m = lax.axis_index("enc"), lax.axis_index("dp"), lax.axis_index("mp")
    me = d * nm + m
    is_query = e == 0
    base = me * rows

    def halves(go, full):
        pl.when(is_query)(lambda: go(full))
        pl.when(jnp.logical_not(is_query))(lambda: go(full // 2))

    def peer(i):
        p = lax.rem(me + i, n)
        return p // nm, lax.rem(p, nm)

    def remote(name, src, dst, where):
        k = PHASES.index(name)
        pltpu.make_async_remote_copy(
            src_ref=src, dst_ref=dst, send_sem=send_sem.at[k], recv_sem=recv_sem.at[k],
            device_id=where, device_id_type=MESH,
        ).start()

    def send_all(name, src_of, dst):
        def go(r):
            def one(i, carry):
                pd, pm = peer(i)
                remote(name, src_of(pd, pm).at[pl.ds(0, r)], dst.at[pl.ds(0, r)], (e, pd, pm))
                return carry
            lax.fori_loop(1, n, one, 0)
        halves(go, dst.shape[0])

    def send_group(name, group_of, src, dst):
        def go(r):
            for pd in range(nd):
                @pl.when(jnp.logical_or(pd != d, group_of != m))
                def _():
                    remote(name, src.at[pl.ds(0, r)], dst.at[pl.ds(0, r)], (e, pd, group_of))
        halves(go, dst.shape[0])

    def send_dp(name, src, dst, both=False):
        def go(r):
            for i in range(1, nd):
                remote(name, src.at[pl.ds(0, r)], dst.at[pl.ds(0, r)], (e, lax.rem(d + i, nd), m))
        if both:
            go(dst.shape[0])
        else:
            halves(go, dst.shape[0])

    def drain(name, buf, sem, count, both=False):
        k = PHASES.index(name)

        def go(r):
            view = buf.at[pl.ds(0, count), pl.ds(0, r)]
            pltpu.make_async_copy(view, view, sem.at[k]).wait()
        if both:
            go(buf.shape[1])
        else:
            halves(go, buf.shape[1])

    loads = []
    for i, (src, dst) in enumerate(((mixed_hbm, mixed_f), (out_hbm, out_f), (inner_hbm, inner_f), (outer_hbm, outer_f))):
        loads.append(pltpu.make_async_copy(src, dst, load_sem.at[i]))
    table_loads = [
        pltpu.make_async_copy(table_hbm.at[pl.ds(i * vt, vt)], stage.at[pl.ds(i * vt, vt)], table_sem.at[i])
        for i in range(tiles)
    ]
    loads[0].start()
    for item in table_loads:
        item.start()
    for item in loads[1:]:
        item.start()

    @pl.when(jnp.logical_not(is_query))
    def _():
        for buf in (
            rows_buf, q_buf, att_buf, z_buf, out_buf, inner_buf, outer_buf, d_act_buf, d_in_buf, d_att_buf, dq_buf, y_buf,
            d_rows_buf,
        ):
            r = buf.shape[1] // 2
            for k in range(buf.shape[0]):
                buf[k, r:, :] = jnp.zeros((r, buf.shape[2]), buf.dtype)

    barrier = pltpu.get_barrier_semaphore()

    def greet(i, carry):
        pd, pm = peer(i)
        pl.semaphore_signal(barrier, inc=1, device_id=(e, pd, pm), device_id_type=MESH)
        return carry
    lax.fori_loop(1, n, greet, 0)
    pl.semaphore_signal(barrier, inc=1, device_id=(1 - e, d, m), device_id_type=MESH)
    pl.semaphore_wait(barrier, n)

    row_i = lax.broadcasted_iota(jnp.int32, (blk, 2 * QSLOT), 0)
    lane_i = lax.broadcasted_iota(jnp.int32, (blk, 2 * QSLOT), 1)
    limit = jnp.zeros((blk, 2 * QSLOT), jnp.int32)
    for b in range(blk):
        here = jnp.where(lane_i < QSLOT, lens_ref[2 * b], lens_ref[2 * b + 1])
        limit = jnp.where(row_i == b, here, limit)
    limit = jnp.where(is_query, limit, QSLOT)
    ids_buf[d] = jnp.where((lane_i & (QSLOT - 1)) >= limit, -1, ids_ref[...])
    send_dp("ids", ids_buf.at[d], ids_buf.at[d], both=True)

    loads[0].wait()
    kv[m, d, :, 0:hw] = mixed_f[1].astype(BF16)
    kv[m, d, :, hw:] = mixed_f[2].astype(BF16)

    def kv_copy(src, sem, where):
        piece = kv.at[m, src]
        return pltpu.make_async_remote_copy(
            src_ref=piece, dst_ref=piece, send_sem=kv_send, recv_sem=sem, device_id=where, device_id_type=MESH
        )

    for i in range(1, nd):
        kv_copy(d, kv_recv.at[d], (e, lax.rem(d + i, nd), m)).start()
    for i in range(1, nm):
        kv_copy(d, kv_spread, (e, d, lax.rem(m + i, nm))).start()
    wq[...] = mixed_f[0].astype(BF16)

    gain0, shift0 = norms_ref[0:1, :], norms_ref[1:2, :]
    for t in range(tiles):
        table_loads[t].wait()

        def normalize(i, carry):
            at = pl.ds(pl.multiple_of(t * vt + i * BLOCK, BLOCK), BLOCK)
            low = stage[at, :].astype(BF16)
            emb[at, :] = low
            x = low.astype(F32)
            x = x - jnp.mean(x, -1, keepdims=True)
            r = lax.rsqrt(jnp.mean(x * x, -1, keepdims=True) + eps_norm)
            hid[at, :] = (x * r * gain0 + shift0).astype(BF16)
            return carry
        lax.fori_loop(0, vt // BLOCK, normalize, 0)

    drain("ids", ids_buf, recv_sem, nd - 1, both=True)
    ids_all = jnp.concatenate([ids_buf[k] for k in range(nd)], axis=0) - base
    cls = jnp.concatenate([ids_all[:, 0:1], ids_all[:, QSLOT : QSLOT + 1]], axis=0)
    hot_at = 2 * heads
    lows[pl.ds(hot_at, c), :] = (cls == lax.broadcasted_iota(jnp.int32, (c, rows), 1)).astype(BF16)

    def pick(t, total):
        at = pl.ds(pl.multiple_of(t * vt, vt), vt)
        return total + nn(lows[pl.ds(hot_at, c), at], emb[at, :])
    found = lax.fori_loop(0, tiles, pick, jnp.zeros((c, size), F32))
    found_hat, _ = slab_norm([found], size)
    owned = jnp.logical_and(cls >= 0, cls < rows)
    found = jnp.where(owned, found_hat[0] * gain0 + shift0, 0.0).astype(BF16)
    for k in range(nd):
        rows_src[k] = found[:, k * width : (k + 1) * width]
    rows_buf[me] = rows_src[d]
    send_all("rows", lambda pd, pm: rows_src.at[pd], rows_buf.at[me])

    flag = jnp.where(is_query, 1, 0)
    for b in range(nb):
        row = ids_all[b : b + 1, :]
        high, low = row >> 7, row & 127
        lane_b = lax.broadcasted_iota(jnp.int32, (16, 2 * QSLOT), 1)
        is_high = lax.broadcasted_iota(jnp.int32, (16, 2 * QSLOT), 0) == high
        left = [jnp.logical_and(is_high, (lane_b >> 7) * flag == s * flag) for s in range(2)]
        left = jnp.concatenate([item.astype(BF16) for item in left], axis=0)
        right = (lax.broadcasted_iota(jnp.int32, (128, 2 * QSLOT), 0) == low).astype(BF16)
        xs[b] = nt(left, right)
    for t in range(rows // 128):
        for s in range(2):
            counts[s * nb : (s + 1) * nb, t * 128 : (t + 1) * 128] = xs[:, s * 16 + t, :]

    for i in range(1, nd):
        src = lax.rem(d + i, nd)
        pltpu.make_async_copy(kv.at[m, src], kv.at[m, src], kv_recv.at[src]).wait()
        for k in range(1, nm):
            kv_copy(src, kv_spread, (e, d, lax.rem(m + k, nm))).start()
    for item in loads[1:]:
        item.wait()
    wo[...] = out_f[...].astype(BF16)
    wi[...] = inner_f[...].astype(BF16)
    wt[...] = outer_f[...].astype(BF16)

    drain("rows", rows_buf, recv_sem, n - 1)
    mine = sum(rows_buf[k].astype(F32) for k in range(n))
    mine_low = mine.astype(BF16)
    q_buf[me] = nn(mine_low, wq[...]).astype(BF16)
    send_all("q", lambda pd, pm: q_buf.at[me], q_buf.at[me])

    lane_h = lax.broadcasted_iota(jnp.int32, (nb, hw), 1) // HEAD

    def expand(x):
        return jnp.concatenate(
            [
                jnp.where(lane_h == j, x[s * nb : (s + 1) * nb], jnp.zeros((), x.dtype))
                for s in range(2)
                for j in range(hm)
            ],
            axis=0,
        )

    def collapse(x):
        out = []
        for s in range(2):
            parts = [x[s * half + j * nb : s * half + (j + 1) * nb] for j in range(hm)]
            total = parts[0]
            for j in range(1, hm):
                total = jnp.where(lane_h == j, parts[j], total)
            out.append(total)
        return jnp.concatenate(out, axis=0)

    def to_rows(cols):
        return jnp.concatenate([cols[j][s * nb : (s + 1) * nb] for s in range(2) for j in range(hm)], axis=0)

    def to_cols(x):
        return [
            jnp.concatenate([x[s * half + j * nb : s * half + (j + 1) * nb] for s in range(2)], axis=0)
            for j in range(hm)
        ]

    def over_heads(cols):
        lane = lax.broadcasted_iota(jnp.int32, (c, hw), 1) // HEAD
        out = jnp.broadcast_to(cols[0], (c, hw))
        for j in range(1, hm):
            out = jnp.where(lane == j, cols[j], out)
        return out

    def with_cols(x, cols):
        tail = lax.broadcasted_iota(jnp.int32, (c, HEAD), 1)
        extra = jnp.zeros((c, HEAD), F32)
        for k, item in enumerate(cols):
            extra = jnp.where(tail == k, item.astype(F32), extra)
        return jnp.concatenate([x, extra.astype(x.dtype)], axis=1)

    blank = jnp.zeros((c, hw), BF16)
    drain("q", q_buf, recv_sem, n - 1)
    spread_view = kv.at[pl.ds(0, nm - 1)]
    pltpu.make_async_copy(spread_view, spread_view, kv_spread).wait()
    queries = []
    for g in range(nm):
        q = sum(q_buf[k * nm + g].astype(F32) for k in range(nd)).astype(BF16)
        queries.append(q)
        wide = expand(q)
        wide = jnp.concatenate([wide, jnp.zeros_like(wide)], axis=1)
        for k in range(nd):
            basis[pl.ds(g * group, group), k * width : (k + 1) * width] = nt(wide, kv[g, k]).astype(BF16)
    q_mine = queries[0]
    for g in range(1, nm):
        q_mine = jnp.where(m == g, queries[g], q_mine)

    def score(t, top):
        at = pl.ds(pl.multiple_of(t * vt, vt), vt)
        s = nt(basis[pl.ds(0, heads), :], hid[at, :]) * scale
        out = []
        for g in range(nm):
            for sl in range(2):
                for j in range(hm):
                    lo = g * group + sl * half + j * nb
                    here = jnp.where(counts[sl * nb : (sl + 1) * nb, at] > 0, s[lo : lo + nb], -1e30)
                    weights[lo : lo + nb, at] = here
                    out.append(jnp.max(here, -1, keepdims=True))
        return jnp.maximum(top, jnp.concatenate(out, axis=0))
    top = lax.fori_loop(0, tiles, score, jnp.full((heads, 1), -1e30, F32))
    col[:, 0:1] = top
    acc[...] = jnp.zeros_like(acc)

    def weigh(t, total):
        at = pl.ds(pl.multiple_of(t * vt, vt), vt)
        out = []
        for g in range(nm):
            for sl in range(2):
                for j in range(hm):
                    lo = g * group + sl * half + j * nb
                    here = counts[sl * nb : (sl + 1) * nb, at] * jnp.exp(weights[lo : lo + nb, at] - col[lo : lo + nb, 0:1])
                    weights[lo : lo + nb, at] = here
                    lows[lo : lo + nb, at] = here.astype(BF16)
                    out.append(jnp.sum(here, -1, keepdims=True))
        acc[...] += nn(lows[pl.ds(0, heads), at], hid[at, :])
        return total + jnp.concatenate(out, axis=0)
    total = lax.fori_loop(0, tiles, weigh, jnp.zeros((heads, 1), F32))

    for g in range(nm):
        z = acc[pl.ds(g * group, group), :].astype(BF16)
        att = jnp.zeros((group, 2 * hw), F32)
        for k in range(nd):
            att = att + nn(z[:, k * width : (k + 1) * width], kv[g, k])
        att = collapse(att[:, hw:]).astype(BF16)
        cols = []
        for item in to_cols(top[g * group : (g + 1) * group]):
            cols += split_low(item, 3)
        for item in to_cols(total[g * group : (g + 1) * group]):
            cols += split_low(item, 2)
        att_src[g] = with_cols(att, cols)
        send_group("att", g, att_src.at[g], att_buf.at[me])
        for k in range(nd):
            z_src[g, k] = z[:, k * width : (k + 1) * width]
    att_buf[me] = att_src[m]
    z_buf[me] = z_src[m, d]
    send_all("z", lambda pd, pm: z_src.at[pm, pd], z_buf.at[me])

    drain("att", att_buf, recv_sem, n - 1)
    tops, sums = [], []
    for k in range(n):
        slab = att_buf[k, :, hw:].astype(F32)
        tops.append([slab[:, 3 * j : 3 * j + 1] + slab[:, 3 * j + 1 : 3 * j + 2] + slab[:, 3 * j + 2 : 3 * j + 3] for j in range(hm)])
        at = 3 * hm
        sums.append([slab[:, at + 2 * j : at + 2 * j + 1] + slab[:, at + 2 * j + 1 : at + 2 * j + 2] for j in range(hm)])
    top_all, inv_all, parts = [], [], []
    for j in range(hm):
        best = tops[0][j]
        for k in range(1, n):
            best = jnp.maximum(best, tops[k][j])
        factor = [jnp.exp(tops[k][j] - best) for k in range(n)]
        whole = sum(factor[k] * sums[k][j] for k in range(n))
        inv = jnp.where(whole > 0, 1.0 / jnp.where(whole > 0, whole, 1.0), 0.0)
        top_all.append(best)
        inv_all.append(inv)
        parts.append([f * inv for f in factor])
    att = sum(att_buf[k, :, 0:hw].astype(F32) * over_heads([parts[j][k] for j in range(hm)]) for k in range(n))
    att_low = att.astype(BF16)
    part = nn(att_low, wo[...]) + jnp.where(m == 0, mine, 0.0)
    out_buf[me] = with_cols(part, top_all + inv_all)
    send_all("out", lambda pd, pm: out_buf.at[me], out_buf.at[me])

    def slabs_of(buf):
        return [sum(buf[k * nm + g, :, 0:width].astype(F32) for g in range(nm)) for k in range(nd)]

    def own(slabs):
        out = slabs[0]
        for k in range(1, nd):
            out = jnp.where(d == k, slabs[k], out)
        return out

    def norm_rows(i):
        return [norms_ref[i : i + 1, k * width : (k + 1) * width] for k in range(nd)]

    drain("z", z_buf, recv_sem, n - 1)
    z_mine = sum(z_buf[k].astype(F32) * to_rows([parts[j][k] for j in range(hm)]) for k in range(n)).astype(BF16)

    drain("out", out_buf, recv_sem, n - 1)
    hats1, r1 = slab_norm(slabs_of(out_buf), size)
    gains1, shifts1 = norm_rows(2), norm_rows(3)
    normed = [h * g + s for h, g, s in zip(hats1, gains1, shifts1)]
    normed_mine = own(normed)
    normed_low = normed_mine.astype(BF16)

    inner_buf[d] = nn(normed_low, wi[...]).astype(BF16)
    send_dp("inner", inner_buf.at[d], inner_buf.at[d])
    for g in range(nm):
        stat = out_buf[g, :, hw:]
        best = to_rows([stat[:, j : j + 1] for j in range(hm)])
        inv = to_rows([stat[:, hm + j : hm + j + 1] for j in range(hm)])
        at = slice(g * group, (g + 1) * group)
        col[at, 1:2] = jnp.exp(col[at, 0:1] - best) * inv
    drain("inner", inner_buf, recv_sem, nd - 1)
    inner = sum(inner_buf[k].astype(F32) for k in range(nd))
    cdf = 0.5 * (1.0 + lax.erf(inner * (0.5 ** 0.5)))
    act = (inner * cdf).astype(BF16)
    slope = cdf + inner * jnp.exp(-0.5 * inner * inner) * ((0.5 / math.pi) ** 0.5)
    outer_buf[me] = nt(act, wt[...]) + jnp.where(m == 0, normed_mine, 0.0)
    send_all("outer", lambda pd, pm: outer_buf.at[me], outer_buf.at[me])
    drain("outer", outer_buf, recv_sem, n - 1)
    hats2, r2 = slab_norm(slabs_of(outer_buf), size)
    gains2, shifts2 = norm_rows(4), norm_rows(5)
    for k in range(nd):
        final_buf[e, k] = hats2[k] * gains2[k] + shifts2[k]
    final_at = PHASES.index("final")
    final_copy = pltpu.make_async_remote_copy(
        src_ref=final_buf.at[e], dst_ref=final_buf.at[e], send_sem=send_sem.at[final_at], recv_sem=recv_sem.at[final_at],
        device_id=(1 - e, d, m), device_id_type=MESH,
    )
    final_copy.start()
    final_copy.wait_recv()

    qs = [final_buf[0, k] for k in range(nd)]
    ps = [final_buf[1, k][0:nb] for k in range(nd)]
    q_r = lax.rsqrt(sum(jnp.sum(x * x, -1, keepdims=True) for x in qs) + eps_norm)
    p_r = lax.rsqrt(sum(jnp.sum(x * x, -1, keepdims=True) for x in ps) + eps_norm)
    q_hat, p_hat = [x * q_r for x in qs], [x * p_r for x in ps]

    def d_sims(left, right, axis, negative, positive, used):
        sims = sum(exact_nt(a, b) for a, b in zip(left, right)) / logit_divisor
        is_positive = lax.broadcasted_iota(jnp.int32, sims.shape, axis) == positive
        sims = jnp.where(jnp.logical_and(negative == 1, jnp.logical_not(is_positive)), -1e30, sims)
        best = jnp.max(sims, axis, keepdims=True)
        log_total = best + jnp.log(jnp.sum(jnp.exp(sims - best), axis, keepdims=True))
        target = jnp.sum(jnp.where(is_positive, sims, 0.0), axis, keepdims=True)
        weight = used.astype(F32)
        count = jnp.maximum(jnp.sum(weight, 1 - axis, keepdims=True), 1.0)
        loss = jnp.sum(weight * (log_total - target), 1 - axis, keepdims=True) / count
        grad = (jnp.exp(sims - log_total) - is_positive.astype(F32)) * (weight / count / logit_divisor)
        return loss, grad

    loss, grad_q = d_sims(q_hat, p_hat, 1, meta_ref[:, 0:nb], meta_ref[:, nb : nb + 1], meta_ref[:, nb + 1 : nb + 2])
    _, grad_p = d_sims(p_hat, q_hat, 0, meta_t_ref[0:nb, :], meta_t_ref[nb : nb + 1, :], meta_t_ref[nb + 1 : nb + 2, :])

    def unit_back(hats, r, grads):
        along = sum(jnp.sum(g * h, -1, keepdims=True) for g, h in zip(grads, hats))
        return [r * (g - h * along) for g, h in zip(grads, hats)]

    d_q = unit_back(q_hat, q_r, [exact_nn(grad_q, x) for x in p_hat])
    d_p = unit_back(p_hat, p_r, [exact_nn(grad_p, x) for x in q_hat])
    d_final = [
        jnp.where(is_query, a, jnp.concatenate([b, jnp.zeros_like(b)], axis=0)) for a, b in zip(d_q, d_p)
    ]

    d_second, d_gain2, d_shift2 = slab_norm_back(hats2, r2, d_final, gains2, size)
    d_outer = own(d_second).astype(BF16)
    d_act_buf[d] = nn(d_outer, wt[...]).astype(BF16)
    send_dp("d_act", d_act_buf.at[d], d_act_buf.at[d])
    g_outer = tn(d_outer, act)
    g_outer_ref[...] = g_outer
    drain("d_act", d_act_buf, recv_sem, nd - 1)
    d_inner = (sum(d_act_buf[k].astype(F32) for k in range(nd)) * slope).astype(BF16)
    d_in_buf[me] = nt(d_inner, wi[...])
    send_all("d_in", lambda pd, pm: d_in_buf.at[me], d_in_buf.at[me])
    g_inner = tn(normed_low, d_inner)
    g_inner_ref[...] = g_inner
    drain("d_in", d_in_buf, recv_sem, n - 1)
    d_normed = [a + b for a, b in zip(d_second, slabs_of(d_in_buf))]
    d_first, d_gain1, d_shift1 = slab_norm_back(hats1, r1, d_normed, gains1, size)
    d_first_mine = own(d_first)
    d_attn = d_first_mine.astype(BF16)

    part = nt(d_attn, wo[...])
    along = att * part
    lane = lax.broadcasted_iota(jnp.int32, (c, hw), 1) // HEAD
    cols = []
    for j in range(hm):
        cols += split_low(jnp.sum(jnp.where(lane == j, along, 0.0), -1, keepdims=True), 2)
    d_att_buf[me] = with_cols(part.astype(BF16), cols)
    send_all("d_att", lambda pd, pm: d_att_buf.at[me], d_att_buf.at[me])
    g_out = tn(att_low, d_attn)
    g_out_ref[...] = g_out
    squares = sum(jnp.sum(g * g, 0, keepdims=True) for g in (g_outer, g_inner))
    squares = jnp.sum(squares, -1, keepdims=True) + jnp.sum(jnp.sum(g_out * g_out, 0, keepdims=True), -1, keepdims=True)

    drain("d_att", d_att_buf, recv_sem, n - 1)
    d_atts = []
    for g in range(nm):
        slab = sum(d_att_buf[k * nm + g].astype(F32) for k in range(nd))
        d_att = slab[:, 0:hw].astype(BF16)
        d_atts.append(d_att)
        col[pl.ds(g * group, group), 2:3] = to_rows(
            [slab[:, hw + 2 * j : hw + 2 * j + 1] + slab[:, hw + 2 * j + 1 : hw + 2 * j + 2] for j in range(hm)]
        )
        wide = expand(d_att)
        wide = jnp.concatenate([jnp.zeros_like(wide), wide], axis=1)
        for k in range(nd):
            basis[pl.ds(heads + g * group, group), k * width : (k + 1) * width] = nt(wide, kv[g, k]).astype(BF16)
    d_att_mine = d_atts[0]
    for g in range(1, nm):
        d_att_mine = jnp.where(m == g, d_atts[g], d_att_mine)
    acc[...] = jnp.zeros_like(acc)

    def backward(t, carry):
        at = pl.ds(pl.multiple_of(t * vt, vt), vt)
        d_probs = nt(basis[pl.ds(heads, heads), :], hid[at, :])
        probs = weights[:, at] * col[:, 1:2]
        d_scores = (probs * (d_probs - col[:, 2:3]) * scale).astype(BF16)
        lows[pl.ds(0, heads), at] = d_scores
        lows[pl.ds(heads, heads), at] = probs.astype(BF16)
        acc[...] += nn(d_scores, hid[at, :])
        return carry
    lax.fori_loop(0, tiles, backward, 0)

    for g in range(nm):
        y = acc[pl.ds(g * group, group), :].astype(BF16)
        dq = jnp.zeros((group, 2 * hw), F32)
        for k in range(nd):
            dq = dq + nn(y[:, k * width : (k + 1) * width], kv[g, k])
            y_src[g, k] = y[:, k * width : (k + 1) * width]
        dq_src[g] = collapse(dq[:, 0:hw]).astype(BF16)
        send_group("dq", g, dq_src.at[g], dq_buf.at[me])
    dq_buf[me] = dq_src[m]
    y_buf[me] = y_src[m, d]
    send_all("y", lambda pd, pm: y_src.at[pm, pd], y_buf.at[me])

    lane_t = 128

    def spread(t, carry):
        at = pl.ds(pl.multiple_of(t * lane_t, lane_t), lane_t)
        stage[at, :] = tn(lows[pl.ds(0, 2 * heads), at], basis[pl.ds(0, 2 * heads), :])
        return carry
    lax.fori_loop(0, rows // lane_t, spread, 0)

    drain("dq", dq_buf, recv_sem, n - 1)
    dq_mine = sum(dq_buf[k].astype(F32) for k in range(n)).astype(BF16)
    d_rows_buf[me] = nt(dq_mine, wq[...]) + jnp.where(m == 0, d_first_mine, 0.0)
    send_all("d_rows", lambda pd, pm: d_rows_buf.at[me], d_rows_buf.at[me])
    g_q = tn(mine_low, dq_mine)
    g_v = tn(z_mine, expand(d_att_mine))
    drain("y", y_buf, recv_sem, n - 1)
    y_mine = sum(y_buf[k].astype(F32) for k in range(n)).astype(BF16)
    g_k = tn(y_mine, expand(q_mine))
    g_q_ref[...] = g_q
    g_k_ref[...] = g_k
    g_v_ref[...] = g_v
    parts3 = sum(jnp.sum(g * g, 0, keepdims=True) for g in (g_q, g_k, g_v))
    squares = squares + jnp.sum(parts3, -1, keepdims=True)

    drain("d_rows", d_rows_buf, recv_sem, n - 1)
    d_rows = jnp.concatenate([s.astype(BF16) for s in slabs_of(d_rows_buf)], axis=1)
    basis[pl.ds(2 * heads, c), :] = d_rows

    def table_back(t, carry):
        d_gain, d_shift, square = carry
        at = pl.ds(pl.multiple_of(t * lane_t, lane_t), lane_t)
        dy = stage[at, :] + tn(lows[pl.ds(hot_at, c), at], basis[pl.ds(2 * heads, c), :])
        x = emb[at, :].astype(F32)
        x = x - jnp.mean(x, -1, keepdims=True)
        r = lax.rsqrt(jnp.mean(x * x, -1, keepdims=True) + eps_norm)
        hat = x * r
        scaled = dy * gain0
        mean = jnp.mean(scaled, -1, keepdims=True)
        along = jnp.mean(scaled * hat, -1, keepdims=True)
        dx = r * (scaled - mean - hat * along)
        stage[at, :] = dx
        fold = lambda v: jnp.sum(v.reshape(lane_t // 8, 8, size), 0)
        return d_gain + fold(dy * hat), d_shift + fold(dy), square + fold(dx * dx)
    zero = jnp.zeros((8, size), F32)
    d_gain, d_shift, square = lax.fori_loop(0, rows // lane_t, table_back, (zero, zero, zero))
    store = pltpu.make_async_copy(stage, g_table_hbm, store_sem)
    store.start()
    d_gain, d_shift = jnp.sum(d_gain, 0, keepdims=True), jnp.sum(d_shift, 0, keepdims=True)
    squares = squares + jnp.sum(jnp.sum(square, 0, keepdims=True), -1, keepdims=True)
    chunks = size // 128
    lines = [v[:, k * 128 : (k + 1) * 128] for v in (d_gain, d_shift) for k in range(chunks)]
    lines.append(jnp.broadcast_to(squares, (1, 128)))
    lines.append(jnp.zeros((16 - len(lines), 128), F32))
    sums_buf[me] = jnp.concatenate(lines, axis=0)

    def send_sums(i, carry):
        pd, pm = peer(i)
        remote("sums", sums_buf.at[me], sums_buf.at[me], (e, pd, pm))
        return carry
    lax.fori_loop(1, n, send_sums, 0)
    drain("sums", sums_buf, recv_sem, n - 1, both=True)
    totals = sum(sums_buf[k] for k in range(n))
    firsts = [jnp.concatenate([totals[v * chunks + k : v * chunks + k + 1] for k in range(chunks)], axis=1) for v in range(2)]
    squares = totals[2 * chunks : 2 * chunks + 1, 0:1]
    for i in range(2):
        g_norms_ref[i : i + 1, :] = firsts[i]
        squares = squares + jnp.sum(firsts[i] * firsts[i], -1, keepdims=True)
    for i, slabs in enumerate((d_gain1, d_shift1, d_gain2, d_shift2)):
        for k in range(nd):
            g_norms_ref[2 + i : 3 + i, k * width : (k + 1) * width] = slabs[k]
            squares = squares + jnp.sum(slabs[k] * slabs[k], -1, keepdims=True)
    norm_buf[e] = jnp.broadcast_to(squares, (8, 128))
    norm_at = PHASES.index("norm")
    norm_copy = pltpu.make_async_remote_copy(
        src_ref=norm_buf.at[e], dst_ref=norm_buf.at[e], send_sem=send_sem.at[norm_at], recv_sem=recv_sem.at[norm_at],
        device_id=(1 - e, d, m), device_id_type=MESH,
    )
    norm_copy.start()
    norm_copy.wait_recv()
    grad_norm = jnp.sqrt(norm_buf[0] + norm_buf[1])
    small_ref[...] = jnp.where(
        lax.broadcasted_iota(jnp.int32, (8, 128), 0) == 0, jnp.broadcast_to(loss, (8, 128)), grad_norm
    )

    final_copy.wait_send()
    norm_copy.wait_send()
    drain("ids", ids_buf, send_sem, nd - 1, both=True)
    for name, buf in (("inner", inner_buf), ("d_act", d_act_buf)):
        drain(name, buf, send_sem, nd - 1)
    for name, buf in (
        ("rows", rows_buf), ("q", q_buf), ("att", att_buf), ("z", z_buf), ("out", out_buf), ("outer", outer_buf),
        ("d_in", d_in_buf), ("d_att", d_att_buf), ("dq", dq_buf), ("y", y_buf), ("d_rows", d_rows_buf),
    ):
        drain(name, buf, send_sem, n - 1)
    drain("sums", sums_buf, send_sem, n - 1, both=True)
    view = kv.at[pl.ds(0, nm - 1)]
    pltpu.make_async_copy(view, view, kv_send).wait()
    view = kv.at[0, pl.ds(0, nd - 1)]
    pltpu.make_async_copy(view, view, kv_send).wait()
    store.wait()


def kernel_gradients(
    token_ids, query_lengths, negative_mask, positive_index, used_rows, table, w_mixed, w_out, w_inner, w_outer, norm_params
):
    nd, nm = lax.axis_size("dp"), lax.axis_size("mp")
    n = nd * nm
    blk = token_ids.shape[1]
    _, rows, size = table.shape
    width, hw, ff = w_mixed.shape[1], w_mixed.shape[3], w_inner.shape[2]
    hm = hw // HEAD
    nb = nd * blk
    c = 2 * nb
    group, heads = hm * c, nm * hm * c
    meta = slot_major(jnp.concatenate([negative_mask, positive_index[:, None], used_rows[:, None]], axis=1))
    S = jax.ShapeDtypeStruct
    outs = (
        S((8, 128), F32), S((rows, size), F32), S((width, hw), F32), S((width, hw), F32), S((width, hw), F32),
        S((hw, width), F32), S((width, ff), F32), S((width, ff), F32), S((8, size), F32),
    )
    vm, hb = pl.BlockSpec(memory_space=pltpu.VMEM), pl.BlockSpec(memory_space=pl.ANY)
    V = pltpu.VMEM
    wide = hw + HEAD
    scratch = [
        V((rows, size), F32), V((rows, size), BF16), V((rows, size), BF16), V((heads, rows), F32),
        V((2 * heads + c, rows), BF16), V((2 * heads + c, size), BF16), V((c, rows), F32), V((nb, 32, 128), F32),
        V((heads, size), F32), V((heads, 128), F32),
        V((3, width, hw), F32), V((hw, width), F32), V((width, ff), F32), V((width, ff), F32),
        V((width, hw), BF16), V((hw, width), BF16), V((width, ff), BF16), V((width, ff), BF16), V((nm, nd, width, 2 * hw), BF16),
        V((nd, blk, 2 * QSLOT), jnp.int32),
        V((nd, c, width), BF16), V((n, c, width), BF16), V((n, c, hw), BF16),
        V((nm, c, wide), BF16), V((n, c, wide), BF16),
        V((nm, nd, group, width), BF16), V((n, group, width), BF16),
        V((n, c, wide), F32), V((nd, c, ff), BF16), V((n, c, width), F32), V((2, nd, c, width), F32),
        V((nd, c, ff), BF16), V((n, c, width), F32), V((n, c, wide), BF16), V((nm, c, hw), BF16), V((n, c, hw), BF16),
        V((nm, nd, group, width), BF16), V((n, group, width), BF16), V((n, c, width), F32),
        V((n, 16, 128), F32), V((2, 8, 128), F32),
        pltpu.SemaphoreType.DMA((len(PHASES),)), pltpu.SemaphoreType.DMA((len(PHASES),)),
        pltpu.SemaphoreType.DMA, pltpu.SemaphoreType.DMA((nd,)), pltpu.SemaphoreType.DMA,
        pltpu.SemaphoreType.DMA((4,)), pltpu.SemaphoreType.DMA((rows // 384,)), pltpu.SemaphoreType.DMA,
    ]
    small, g_table, g_q, g_k, g_v, g_out, g_inner, g_outer, g_norms = pl.pallas_call(
        partial(grad_kernel, (nd, nm, blk, rows, width, size, hm, ff)),
        out_shape=outs,
        in_specs=[vm, pl.BlockSpec(memory_space=pltpu.SMEM), vm, vm, vm, hb, hb, hb, hb, hb],
        out_specs=(vm, hb, vm, vm, vm, vm, vm, vm, vm),
        scratch_shapes=scratch,
        compiler_params=pltpu.CompilerParams(collective_id=ENTRY_ID, has_side_effects=True, vmem_limit_bytes=56 << 20),
        name="gradients",
    )(
        token_ids[0], query_lengths, meta, meta.T, norm_params[0], table[0], w_mixed[0].swapaxes(0, 1), w_out[0], w_inner[0],
        w_outer[0].T,
    )
    g_mixed = jnp.stack([g_q, g_k, g_v], 1)
    return small[0, 0], small[1, 0], (g_table, g_mixed, g_out, g_inner, g_outer.T, g_norms[0:6])


def on_device(
    token_ids,
    query_lengths,
    negative_mask,
    positive_index,
    used_rows,
    step_count,
    table,
    w_mixed,
    w_out,
    w_inner,
    w_outer,
    norm_params,
    table_m,
    table_v,
    mixed_m,
    mixed_v,
    out_m,
    out_v,
    inner_m,
    inner_v,
    outer_m,
    outer_v,
    norms_m,
    norms_v,
):
    operands = (
        token_ids, query_lengths, negative_mask, positive_index, used_rows, table, w_mixed, w_out, w_inner, w_outer, norm_params
    )
    if table.shape[1] % 384 == 0 and w_mixed.shape[1] % 64 == 0 and table.shape[1] <= 2048:
        loss, grad_norm, grads = kernel_gradients(*operands)
    else:
        loss, grads = gradients(*operands)
        owner = (lax.axis_index("dp") == 0) & (lax.axis_index("mp") == 0)
        squares = jnp.where(owner, jnp.sum(grads[5] * grads[5]), 0.0)
        for grad in grads[:5]:
            squares = squares + jnp.sum(grad * grad)
        grad_norm = jnp.sqrt(lax.psum(squares, ("enc", "dp", "mp")))
    clip = jnp.minimum(1.0, clip_limit / (grad_norm + 1e-06))
    count = step_count[0].astype(F32)
    masters = (table, w_mixed, w_out, w_inner, w_outer, norm_params)
    firsts = (table_m, mixed_m, out_m, inner_m, outer_m, norms_m)
    seconds = (table_v, mixed_v, out_v, inner_v, outer_v, norms_v)
    results = [loss, grad_norm]
    for index in range(6):
        rate, decay = (0.5, 0.0) if index == 5 else (0.06, 0.01)
        results.extend(
            adam_step(
                masters[index], grads[index][None] * clip, firsts[index], seconds[index], rate, decay, count
            )
        )
    return tuple(results)


def solution(mesh):
    table = P("enc", ("dp", "mp"), None)
    mixed = P("enc", "dp", None, "mp")
    columns = P("enc", "mp", "dp")
    units = P("enc", "dp", "mp")
    norms = P("enc", None, None)
    matrices = (table, mixed, columns, units, columns, norms)
    moments = tuple(spec for spec in matrices for _ in range(2))
    updated = tuple(spec for spec in matrices for _ in range(3))
    return jax.shard_map(
        on_device,
        mesh=mesh,
        in_specs=(P("enc", "dp", None), P("dp"), P(), P(), P(), P()) + matrices + moments,
        out_specs=(P(), P()) + updated,
        check_vma=False,
    )
```

```python
import math
from functools import partial

import jax
import jax.numpy as jnp
from jax import lax
from jax.experimental import pallas as pl
from jax.experimental.pallas import tpu as pltpu
from jax.sharding import PartitionSpec as P

HEAD = 64
QSLOT = 128
F32 = jnp.float32
BF16 = jnp.bfloat16

exact_arithmetic_level = lax.Precision.HIGHEST
eps_norm = 1e-06
logit_divisor = 0.05
clip_limit = 0.02
beta_one = 0.9
beta_two = 0.999
adam_eps = 1e-08


def layer_norm(x, gain, shift):
    centred = x - jnp.mean(x, -1, keepdims=True)
    spread = jnp.mean(centred * centred, -1, keepdims=True)
    return centred * lax.rsqrt(spread + eps_norm) * gain + shift


def mul(spec, a, b):
    return jnp.einsum(spec, a, b, preferred_element_type=F32)


def token_counts(ids, lens, is_query, base, rows):
    pos = jnp.arange(ids.shape[1])
    slot = pos // QSLOT
    limit = jnp.where(slot[None, :] == 0, lens[:, 0:1], lens[:, 1:2])
    within = (pos % QSLOT)[None, :] < limit
    same = slot[None, :] == jnp.arange(2)[:, None]
    allowed = jnp.where(is_query, same[:, None, :] & within[None], True)
    local = ids - base
    n_hi = -(-rows // 128)
    high = (local[..., None] >> 7) == jnp.arange(n_hi)
    low = (local[..., None] & 127) == jnp.arange(128)
    left = (allowed[..., None] & high[None]).astype(BF16)
    counts = mul("sbth,btl->sbhl", left, low.astype(BF16))
    return counts.reshape(2 * ids.shape[0], n_hi * 128)[:, :rows]


def contrast(queries, passages, negative_mask, positive_index, used_rows):
    question_direction_rows = queries * lax.rsqrt(
        jnp.sum(queries * queries, -1, keepdims=True) + eps_norm
    )
    document_direction_rows = passages * lax.rsqrt(
        jnp.sum(passages * passages, -1, keepdims=True) + eps_norm
    )
    pairwise_cosine_table = (
        jnp.dot(
            question_direction_rows, document_direction_rows.T, precision=exact_arithmetic_level
        )
        / logit_divisor
    )
    is_positive = jnp.arange(passages.shape[0])[None, :] == positive_index[:, None]
    excluded = (negative_mask == 1) & ~is_positive
    pairwise_cosine_table = jnp.where(excluded, -1e30, pairwise_cosine_table)
    top = jnp.max(pairwise_cosine_table, -1, keepdims=True)
    log_total = top[:, 0] + jnp.log(jnp.sum(jnp.exp(pairwise_cosine_table - top), -1))
    target = jnp.sum(jnp.where(is_positive, pairwise_cosine_table, 0.0), -1)
    weight = used_rows.astype(F32)
    return jnp.sum(weight * (log_total - target)) / jnp.maximum(jnp.sum(weight), 1.0)


def adam_step(weight, grad, first, second, rate, decay, count):
    first_new = beta_one * first + (1.0 - beta_one) * grad
    second_new = beta_two * second + (1.0 - beta_two) * grad * grad
    fix_one = 1.0 - jnp.power(beta_one, count)
    correction_second = 1.0 - jnp.power(beta_two, count)
    update = (
        first_new / fix_one / (jnp.sqrt(second_new / correction_second) + adam_eps) + decay * weight
    )
    return (weight - rate * update, first_new, second_new)


def slot_major(x):
    return x.reshape((x.shape[0] // 2, 2) + x.shape[1:]).swapaxes(0, 1).reshape(x.shape)


def gradients(
    token_ids, query_lengths, negative_mask, positive_index, used_rows, table, w_mixed, w_out, w_inner, w_outer, norm_params
):
    is_query = lax.axis_index("enc") == 0
    d, m = lax.axis_index("dp"), lax.axis_index("mp")
    n_mp = lax.axis_size("mp")
    rows, width = table.shape[1], w_mixed.shape[1]
    hm = w_out.shape[1] // HEAD
    scale = HEAD ** (-0.5)
    norms = norm_params[0]
    base = (d * n_mp + m) * rows

    ids = lax.all_gather(token_ids[0], "dp", axis=0, tiled=True)
    lens = lax.all_gather(query_lengths, "dp", axis=0, tiled=True).reshape(-1, 2)
    blocks = ids.shape[0]
    counts = token_counts(ids, lens, is_query, base, rows)
    cls_ids = jnp.concatenate([ids[:, 0], ids[:, QSLOT]]) - base
    cls_hot = cls_ids[:, None] == jnp.arange(rows)[None, :]

    def mine(x):
        return lax.dynamic_slice_in_dim(x, d * width, width, 1)

    wq, wk, wv = (w_mixed[0, :, i].astype(BF16).reshape(width, hm, HEAD) for i in range(3))
    wo = w_out[0].astype(BF16).reshape(hm, HEAD, width)
    wi, wt = w_inner[0].astype(BF16), w_outer[0].astype(BF16)

    embedded = lax.reduce_precision(table[0], 8, 7)
    hidden, hidden_back = jax.vjp(layer_norm, embedded, norms[0], norms[1])
    hid = hidden.astype(BF16)
    first_rows = lax.psum(
        jnp.dot(cls_hot.astype(F32), hidden, precision=exact_arithmetic_level), ("dp", "mp")
    )
    first_mine = mine(first_rows).astype(BF16)
    q = lax.psum(mul("ci,ihk->hck", first_mine, wq), "dp").astype(BF16)
    u = mul("hck,ihk->hci", q, wk).astype(BF16)
    u = lax.all_gather(lax.all_gather(u, "dp", axis=2, tiled=True), "mp", axis=0, tiled=True)
    scores = jnp.where(counts[None] > 0, mul("hci,vi->hcv", u, hid) * scale, -1e30)
    top = lax.pmax(jnp.max(scores, -1, keepdims=True), ("dp", "mp"))
    weight = counts[None] * jnp.exp(scores - top)
    probs = weight / lax.psum(jnp.sum(weight, -1, keepdims=True), ("dp", "mp"))
    probs_low = probs.astype(BF16)
    z = mul("hcv,vi->hci", probs_low, hid)
    z = lax.psum_scatter(z, "mp", scatter_dimension=0, tiled=True)
    z = lax.psum_scatter(z, "dp", scatter_dimension=2, tiled=True).astype(BF16)
    att = lax.psum(mul("hci,ihk->hck", z, wv), "dp")
    att_low = att.astype(BF16)
    out = lax.psum(mul("hck,hke->ce", att_low, wo), "mp")
    first_sum = first_rows + lax.all_gather(out, "dp", axis=1, tiled=True)
    normed, normed_back = jax.vjp(layer_norm, first_sum, norms[2], norms[3])
    normed_mine = mine(normed).astype(BF16)
    inner = lax.psum(mul("ci,if->cf", normed_mine, wi), "dp")
    act, act_back = jax.vjp(partial(jax.nn.gelu, approximate=False), inner)
    act = act.astype(BF16)
    outer = lax.psum(mul("cf,fe->ce", act, wt), "mp")
    second_sum = normed + lax.all_gather(outer, "dp", axis=1, tiled=True)
    final, final_back = jax.vjp(layer_norm, second_sum, norms[4], norms[5])
    both = lax.all_gather(final, "enc", axis=0)
    loss, loss_back = jax.vjp(
        partial(
            contrast,
            negative_mask=slot_major(negative_mask),
            positive_index=slot_major(positive_index),
            used_rows=slot_major(used_rows),
        ),
        both[0],
        both[1, :blocks],
    )
    d_queries, d_passages = loss_back(jnp.ones((), F32))
    d_passages = jnp.concatenate([d_passages, jnp.zeros_like(d_passages)])
    d_final = jnp.where(is_query, d_queries, d_passages)

    d_second, d_gain2, d_shift2 = final_back(d_final)
    d_outer = mine(d_second).astype(BF16)
    g_outer = mul("cf,ce->fe", act, d_outer)
    d_act = lax.psum(mul("ce,fe->cf", d_outer, wt), "dp")
    d_inner = act_back(d_act)[0].astype(BF16)
    g_inner = mul("ci,cf->if", normed_mine, d_inner)
    d_in = lax.psum(mul("cf,if->ci", d_inner, wi), "mp")
    d_normed = d_second + lax.all_gather(d_in, "dp", axis=1, tiled=True)
    d_first, d_gain1, d_shift1 = normed_back(d_normed)
    d_attn = mine(d_first).astype(BF16)
    g_out = mul("hck,ce->hke", att_low, d_attn).reshape(w_out.shape[1:])
    d_att = lax.psum(mul("ce,hke->hck", d_attn, wo), "dp").astype(BF16)
    w = mul("hck,ihk->hci", d_att, wv).astype(BF16)
    mean_d = jnp.sum(att * d_att.astype(F32), -1, keepdims=True)
    w = lax.all_gather(lax.all_gather(w, "dp", axis=2, tiled=True), "mp", axis=0, tiled=True)
    mean_d = lax.all_gather(mean_d, "mp", axis=0, tiled=True)
    d_probs = mul("hci,vi->hcv", w, hid)
    d_scores = (probs * (d_probs - mean_d)).astype(BF16)
    y = mul("hcv,vi->hci", d_scores, hid)
    y = lax.psum_scatter(y, "mp", scatter_dimension=0, tiled=True)
    y = lax.psum_scatter(y, "dp", scatter_dimension=2, tiled=True).astype(BF16)
    dq = (lax.psum(mul("hci,ihk->hck", y, wk), "dp") * scale).astype(BF16)
    g_q = mul("ci,hck->ihk", first_mine, dq)
    g_k = mul("hci,hck->ihk", y, q) * scale
    g_v = mul("hci,hck->ihk", z, d_att)
    g_mixed = jnp.stack([g_q, g_k, g_v], 1).reshape(w_mixed.shape[1:])
    d_rows = lax.psum(mul("hck,ihk->ci", dq, wq), "mp")
    d_rows = (d_first + lax.all_gather(d_rows, "dp", axis=1, tiled=True)).astype(BF16)
    d_hidden = (
        mul("hcv,hci->vi", d_scores, u) * scale
        + mul("hcv,hci->vi", probs_low, w)
        + mul("cv,ci->vi", cls_hot.astype(BF16), d_rows)
    )
    g_table, d_gain0, d_shift0 = hidden_back(d_hidden)
    sums = lax.psum(jnp.stack([d_gain0, d_shift0]), ("dp", "mp"))
    g_norms = jnp.concatenate([sums, jnp.stack([d_gain1, d_shift1, d_gain2, d_shift2])])
    return loss, (g_table, g_mixed, g_out, g_inner, g_outer, g_norms)


MESH = pl.DeviceIdType.MESH
ENTRY_ID = 3
PHASES = (
    "ids", "rows", "q", "att", "z", "out", "inner", "outer", "final",
    "d_act", "d_in", "d_att", "dq", "y", "d_rows", "sums", "norm",
)
BLOCK = 64


def nt(a, b):
    return lax.dot_general(a, b, (((1,), (1,)), ((), ())), preferred_element_type=F32)


def tn(a, b):
    return lax.dot_general(a, b, (((0,), (0,)), ((), ())), preferred_element_type=F32)


def nn(a, b):
    return jnp.dot(a, b, preferred_element_type=F32)


def exact_nt(a, b):
    return lax.dot_general(
        a, b, (((1,), (1,)), ((), ())), precision=exact_arithmetic_level, preferred_element_type=F32
    )


def exact_nn(a, b):
    return jnp.dot(a, b, precision=exact_arithmetic_level, preferred_element_type=F32)


def slab_norm(slabs, size):
    mean = sum(jnp.sum(s, -1, keepdims=True) for s in slabs) * (1.0 / size)
    slabs = [s - mean for s in slabs]
    spread = sum(jnp.sum(s * s, -1, keepdims=True) for s in slabs) * (1.0 / size)
    r = lax.rsqrt(spread + eps_norm)
    return [s * r for s in slabs], r


def slab_norm_back(hats, r, grads, gains, size):
    scaled = [dy * g for dy, g in zip(grads, gains)]
    mean = sum(jnp.sum(s, -1, keepdims=True) for s in scaled) * (1.0 / size)
    along = sum(jnp.sum(s * h, -1, keepdims=True) for s, h in zip(scaled, hats)) * (1.0 / size)
    d_in = [r * (s - mean - h * along) for s, h in zip(scaled, hats)]
    d_gain = [jnp.sum(dy * h, 0, keepdims=True) for dy, h in zip(grads, hats)]
    d_shift = [jnp.sum(dy, 0, keepdims=True) for dy in grads]
    return d_in, d_gain, d_shift


def joined(x, at, parts):
    return sum(x[:, at + i : at + i + 1] for i in range(parts))


def split_low(x, parts):
    out = []
    for _ in range(parts):
        piece = x.astype(BF16)
        out.append(piece)
        x = x - piece.astype(F32)
    return out


def grad_kernel(cfg, *refs):
    nd, nm, blk, rows, width, size, hm, ff = cfg
    n = nd * nm
    nb = nd * blk
    c = 2 * nb
    hw = hm * HEAD
    group = hm * c
    half = hm * nb
    heads = nm * group
    vt = 384
    tiles = rows // vt
    scale = HEAD ** (-0.5)
    (
        ids_ref, lens_ref, positive_ref, used_ref, negative_ref, norms_ref,
        table_hbm, mixed_hbm, out_hbm, inner_hbm, outer_hbm,
        small_ref, g_table_hbm, g_mixed_ref, g_out_ref, g_inner_ref, g_outer_ref, g_norms_ref,
        stage, emb, hid, weights, lows, basis, counts, xs, acc, col,
        mixed_f, out_f, inner_f, outer_f, wq, wo, wi, wt, kv,
        ids_buf, rows_src, rows_buf, q_buf, att_src, att_buf, z_src, z_buf, out_buf, inner_buf, outer_buf,
        final_buf, d_act_buf, d_in_buf, d_att_buf, dq_src, dq_buf, y_src, y_buf, d_rows_buf, sums_buf, norm_buf,
        send_sem, recv_sem, kv_send, kv_recv, kv_spread, load_sem, table_sem, store_sem,
    ) = refs
    e, d, m = lax.axis_index("enc"), lax.axis_index("dp"), lax.axis_index("mp")
    me = d * nm + m
    is_query = e == 0
    base = me * rows

    sent, received = [], []

    def halves(go, full):
        pl.when(is_query)(lambda: go(full))
        pl.when(jnp.logical_not(is_query))(lambda: go(full // 2))

    def peer(i):
        p = lax.rem(me + i, n)
        return p // nm, lax.rem(p, nm)

    def remote(name, src, dst, where):
        k = PHASES.index(name)
        pltpu.make_async_remote_copy(
            src_ref=src, dst_ref=dst, send_sem=send_sem.at[k], recv_sem=recv_sem.at[k],
            device_id=where, device_id_type=MESH,
        ).start()

    def send_all(name, src_of, dst, buf):
        sent.append((name, buf, n - 1, False))

        def go(r):
            def one(i, carry):
                pd, pm = peer(i)
                remote(name, src_of(pd, pm).at[pl.ds(0, r)], dst.at[pl.ds(0, r)], (e, pd, pm))
                return carry
            lax.fori_loop(1, n, one, 0)
        halves(go, dst.shape[0])

    def send_group(name, group_of, src, dst, buf):
        if group_of == 0:
            sent.append((name, buf, n - 1, False))

        def go(r):
            for pd in range(nd):
                @pl.when(jnp.logical_or(pd != d, group_of != m))
                def _():
                    remote(name, src.at[pl.ds(0, r)], dst.at[pl.ds(0, r)], (e, pd, group_of))
        halves(go, dst.shape[0])

    def send_dp(name, src, dst, buf, both=False):
        sent.append((name, buf, nd - 1, both))

        def go(r):
            for i in range(1, nd):
                remote(name, src.at[pl.ds(0, r)], dst.at[pl.ds(0, r)], (e, lax.rem(d + i, nd), m))
        if both:
            go(dst.shape[0])
        else:
            halves(go, dst.shape[0])

    def drain(name, buf, sem, count, both=False):
        k = PHASES.index(name)
        if sem is recv_sem:
            received.append(name)

        def go(r):
            view = buf.at[pl.ds(0, count), pl.ds(0, r)]
            pltpu.make_async_copy(view, view, sem.at[k]).wait()
        if both:
            go(buf.shape[1])
        else:
            halves(go, buf.shape[1])

    def finish():
        for name, buf, count, both in sent:
            drain(name, buf, send_sem, count, both)
            if name not in received:
                drain(name, buf, recv_sem, count, both)
        for item in started:
            item()

    started = []

    loads = []
    for i, (src, dst) in enumerate(((mixed_hbm, mixed_f), (out_hbm, out_f), (inner_hbm, inner_f), (outer_hbm, outer_f))):
        loads.append(pltpu.make_async_copy(src, dst, load_sem.at[i]))
    table_loads = [
        pltpu.make_async_copy(table_hbm.at[pl.ds(i * vt, vt)], stage.at[pl.ds(i * vt, vt)], table_sem.at[i])
        for i in range(tiles)
    ]
    loads[0].start()
    for item in table_loads:
        item.start()
    for item in loads[1:]:
        item.start()

    @pl.when(jnp.logical_not(is_query))
    def _():
        for buf in (
            rows_buf, q_buf, att_buf, z_buf, out_buf, inner_buf, outer_buf, d_act_buf, d_in_buf, d_att_buf, dq_buf, y_buf,
            d_rows_buf,
        ):
            r = buf.shape[1] // 2
            for k in range(buf.shape[0]):
                buf[k, r:, :] = jnp.zeros((r, buf.shape[2]), buf.dtype)

    barrier = pltpu.get_barrier_semaphore()

    def greet(i, carry):
        pd, pm = peer(i)
        pl.semaphore_signal(barrier, inc=1, device_id=(e, pd, pm), device_id_type=MESH)
        return carry
    lax.fori_loop(1, n, greet, 0)
    pl.semaphore_signal(barrier, inc=1, device_id=(1 - e, d, m), device_id_type=MESH)
    pl.semaphore_wait(barrier, n)

    row_i = lax.broadcasted_iota(jnp.int32, (blk, 2 * QSLOT), 0)
    lane_i = lax.broadcasted_iota(jnp.int32, (blk, 2 * QSLOT), 1)
    limit = jnp.zeros((blk, 2 * QSLOT), jnp.int32)
    for b in range(blk):
        here = jnp.where(lane_i < QSLOT, lens_ref[2 * b], lens_ref[2 * b + 1])
        limit = jnp.where(row_i == b, here, limit)
    limit = jnp.where(is_query, limit, QSLOT)
    ids_buf[d] = jnp.where((lane_i & (QSLOT - 1)) >= limit, -1, ids_ref[0])
    send_dp("ids", ids_buf.at[d], ids_buf.at[d], ids_buf, both=True)

    loads[0].wait()
    fold = width // 2
    for i in range(2):
        kv[i, m, d, :, 0:hw] = mixed_f[1 + i, 0:fold].astype(BF16)
        kv[i, m, d, :, hw:] = mixed_f[1 + i, fold:].astype(BF16)

    def kv_copy(i, src, sem, where):
        piece = kv.at[i, m, src]
        return pltpu.make_async_remote_copy(
            src_ref=piece, dst_ref=piece, send_sem=kv_send.at[i], recv_sem=sem, device_id=where, device_id_type=MESH
        )

    def kv_start(i):
        for k in range(1, nd):
            kv_copy(i, d, kv_recv.at[i, d], (e, lax.rem(d + k, nd), m)).start()
        for k in range(1, nm):
            kv_copy(i, d, kv_spread.at[i], (e, d, lax.rem(m + k, nm))).start()

    def kv_forward(i):
        for k in range(1, nd):
            src = lax.rem(d + k, nd)
            pltpu.make_async_copy(kv.at[i, m, src], kv.at[i, m, src], kv_recv.at[i, src]).wait()
            for j in range(1, nm):
                kv_copy(i, src, kv_spread.at[i], (e, d, lax.rem(m + j, nm))).start()

    def kv_wait(i):
        view = kv.at[i, pl.ds(0, nm - 1)]
        pltpu.make_async_copy(view, view, kv_spread.at[i]).wait()

    def kv_left():
        for i in range(2):
            view = kv.at[i, pl.ds(0, nm - 1)]
            pltpu.make_async_copy(view, view, kv_send.at[i]).wait()
            view = kv.at[i, 0, pl.ds(0, nd - 1)]
            pltpu.make_async_copy(view, view, kv_send.at[i]).wait()
    started.append(kv_left)

    def projection(i, g, k):
        both = kv[i, g, k]
        return jnp.concatenate([both[:, 0:hw], both[:, hw:]], axis=0)

    kv_start(0)
    wq[...] = mixed_f[0].astype(BF16)

    gain0, shift0 = norms_ref[0], norms_ref[1]
    for t in range(tiles):
        table_loads[t].wait()

        def to_low(i, carry):
            at = pl.ds(pl.multiple_of(t * vt + i * BLOCK, BLOCK), BLOCK)
            emb[at, :] = stage[at, :].astype(BF16)
            return carry
        lax.fori_loop(0, vt // BLOCK, to_low, 0)

    drain("ids", ids_buf, recv_sem, nd - 1, both=True)
    ids_all = jnp.concatenate([ids_buf[k] for k in range(nd)], axis=0) - base
    cls = jnp.concatenate([ids_all[:, 0:1], ids_all[:, QSLOT : QSLOT + 1]], axis=0)
    hot_at = 2 * heads
    lows[pl.ds(hot_at, c), :] = (cls == lax.broadcasted_iota(jnp.int32, (c, rows), 1)).astype(BF16)

    def pick(t, total):
        at = pl.ds(pl.multiple_of(t * vt, vt), vt)
        return total + nn(lows[pl.ds(hot_at, c), at], emb[at, :])
    found = lax.fori_loop(0, tiles, pick, jnp.zeros((c, size), F32))
    found_hat, _ = slab_norm([found], size)
    owned = jnp.logical_and(cls >= 0, cls < rows)
    found = jnp.where(owned, found_hat[0] * gain0 + shift0, 0.0).astype(BF16)
    for k in range(nd):
        rows_src[k] = found[:, k * width : (k + 1) * width]
    rows_buf[me] = rows_src[d]
    send_all("rows", lambda pd, pm: rows_src.at[pd], rows_buf.at[me], rows_buf)

    flag = jnp.where(is_query, 1, 0)
    for b in range(nb):
        row = ids_all[b : b + 1, :]
        high, low = row >> 7, row & 127
        lane_b = lax.broadcasted_iota(jnp.int32, (16, 2 * QSLOT), 1)
        is_high = lax.broadcasted_iota(jnp.int32, (16, 2 * QSLOT), 0) == high
        left = [jnp.logical_and(is_high, (lane_b >> 7) * flag == s * flag) for s in range(2)]
        left = jnp.concatenate([item.astype(BF16) for item in left], axis=0)
        right = (lax.broadcasted_iota(jnp.int32, (128, 2 * QSLOT), 0) == low).astype(BF16)
        xs[b] = nt(left, right)
    for t in range(rows // 128):
        for s in range(2):
            counts[s * nb : (s + 1) * nb, t * 128 : (t + 1) * 128] = xs[:, s * 16 + t, :]

    kv_forward(0)
    kv_start(1)

    def normalize(i, carry):
        at = pl.ds(pl.multiple_of(i * BLOCK, BLOCK), BLOCK)
        x = emb[at, :].astype(F32)
        x = x - jnp.mean(x, -1, keepdims=True)
        r = lax.rsqrt(jnp.mean(x * x, -1, keepdims=True) + eps_norm)
        hid[at, :] = (x * r * gain0 + shift0).astype(BF16)
        return carry
    lax.fori_loop(0, rows // BLOCK, normalize, 0)
    for item in loads[1:]:
        item.wait()
    wo[...] = out_f[...].astype(BF16)
    wi[...] = inner_f[...].astype(BF16)
    wt[...] = outer_f[...].astype(BF16)

    kv_forward(1)
    drain("rows", rows_buf, recv_sem, n - 1)
    mine = sum(rows_buf[k].astype(F32) for k in range(n))
    mine_low = mine.astype(BF16)
    q_buf[me] = nn(mine_low, wq[...]).astype(BF16)
    send_all("q", lambda pd, pm: q_buf.at[me], q_buf.at[me], q_buf)

    lane_h = lax.broadcasted_iota(jnp.int32, (nb, hw), 1) // HEAD

    def expand(x):
        return jnp.concatenate(
            [
                jnp.where(lane_h == j, x[s * nb : (s + 1) * nb], jnp.zeros((), x.dtype))
                for s in range(2)
                for j in range(hm)
            ],
            axis=0,
        )

    def collapse(x):
        out = []
        for s in range(2):
            parts = [x[s * half + j * nb : s * half + (j + 1) * nb] for j in range(hm)]
            total = parts[0]
            for j in range(1, hm):
                total = jnp.where(lane_h == j, parts[j], total)
            out.append(total)
        return jnp.concatenate(out, axis=0)

    def to_rows(cols):
        return jnp.concatenate([cols[j][s * nb : (s + 1) * nb] for s in range(2) for j in range(hm)], axis=0)

    def to_cols(x):
        return [
            jnp.concatenate([x[s * half + j * nb : s * half + (j + 1) * nb] for s in range(2)], axis=0)
            for j in range(hm)
        ]

    def over_heads(cols):
        lane = lax.broadcasted_iota(jnp.int32, (c, hw), 1) // HEAD
        out = jnp.broadcast_to(cols[0], (c, hw))
        for j in range(1, hm):
            out = jnp.where(lane == j, cols[j], out)
        return out

    def with_cols(x, cols):
        tail = lax.broadcasted_iota(jnp.int32, (c, HEAD), 1)
        extra = jnp.zeros((c, HEAD), F32)
        for k, item in enumerate(cols):
            extra = jnp.where(tail == k, item.astype(F32), extra)
        return jnp.concatenate([x, extra.astype(x.dtype)], axis=1)

    blank = jnp.zeros((c, hw), BF16)
    drain("q", q_buf, recv_sem, n - 1)
    kv_wait(0)
    queries = []
    for g in range(nm):
        q = sum(q_buf[k * nm + g].astype(F32) for k in range(nd)).astype(BF16)
        queries.append(q)
        wide = expand(q)
        for k in range(nd):
            basis[pl.ds(g * group, group), k * width : (k + 1) * width] = nt(wide, projection(0, g, k)).astype(BF16)
    q_mine = queries[0]
    for g in range(1, nm):
        q_mine = jnp.where(m == g, queries[g], q_mine)

    def score(t, top):
        at = pl.ds(pl.multiple_of(t * vt, vt), vt)
        s = nt(basis[pl.ds(0, heads), :], hid[at, :]) * scale
        out = []
        for g in range(nm):
            for sl in range(2):
                for j in range(hm):
                    lo = g * group + sl * half + j * nb
                    here = jnp.where(counts[sl * nb : (sl + 1) * nb, at] > 0, s[lo : lo + nb], -1e30)
                    weights[lo : lo + nb, at] = here
                    out.append(jnp.max(here, -1, keepdims=True))
        return jnp.maximum(top, jnp.concatenate(out, axis=0))
    top = lax.fori_loop(0, tiles, score, jnp.full((heads, 1), -1e30, F32))
    col[:, 0:1] = top
    acc[...] = jnp.zeros_like(acc)

    def weigh(t, total):
        at = pl.ds(pl.multiple_of(t * vt, vt), vt)
        out = []
        for g in range(nm):
            for sl in range(2):
                for j in range(hm):
                    lo = g * group + sl * half + j * nb
                    here = counts[sl * nb : (sl + 1) * nb, at] * jnp.exp(weights[lo : lo + nb, at] - col[lo : lo + nb, 0:1])
                    weights[lo : lo + nb, at] = here
                    lows[lo : lo + nb, at] = here.astype(BF16)
                    out.append(jnp.sum(here, -1, keepdims=True))
        acc[...] += nn(lows[pl.ds(0, heads), at], hid[at, :])
        return total + jnp.concatenate(out, axis=0)
    total = lax.fori_loop(0, tiles, weigh, jnp.zeros((heads, 1), F32))

    kv_wait(1)
    for g in range(nm):
        z = acc[pl.ds(g * group, group), :].astype(BF16)
        att = jnp.zeros((group, hw), F32)
        for k in range(nd):
            att = att + nn(z[:, k * width : (k + 1) * width], projection(1, g, k))
        att = collapse(att).astype(BF16)
        cols = []
        for item in to_cols(top[g * group : (g + 1) * group]):
            cols += split_low(item, 3)
        for item in to_cols(total[g * group : (g + 1) * group]):
            cols += split_low(item, 2)
        att_src[g] = with_cols(att, cols)
        send_group("att", g, att_src.at[g], att_buf.at[me], att_buf)
        for k in range(nd):
            z_src[g, k] = z[:, k * width : (k + 1) * width]
    att_buf[me] = att_src[m]
    z_buf[me] = z_src[m, d]
    send_all("z", lambda pd, pm: z_src.at[pm, pd], z_buf.at[me], z_buf)

    drain("att", att_buf, recv_sem, n - 1)
    tops, sums = [], []
    for k in range(n):
        slab = att_buf[k, :, hw:].astype(F32)
        tops.append([joined(slab, 3 * j, 3) for j in range(hm)])
        sums.append([joined(slab, 3 * hm + 2 * j, 2) for j in range(hm)])
    top_all, inv_all, parts = [], [], []
    for j in range(hm):
        best = tops[0][j]
        for k in range(1, n):
            best = jnp.maximum(best, tops[k][j])
        factor = [jnp.exp(tops[k][j] - best) for k in range(n)]
        whole = sum(factor[k] * sums[k][j] for k in range(n))
        inv = jnp.where(whole > 0, 1.0 / jnp.where(whole > 0, whole, 1.0), 0.0)
        top_all.append(best)
        inv_all.append(inv)
        parts.append([f * inv for f in factor])
    att = sum(att_buf[k, :, 0:hw].astype(F32) * over_heads([parts[j][k] for j in range(hm)]) for k in range(n))
    att_low = att.astype(BF16)
    part = nn(att_low, wo[...]) + jnp.where(m == 0, mine, 0.0)
    cols = [piece for item in top_all for piece in split_low(item, 3)]
    cols += [piece for item in inv_all for piece in split_low(item, 2)]
    out_buf[me] = with_cols(part.astype(BF16), cols)
    send_all("out", lambda pd, pm: out_buf.at[me], out_buf.at[me], out_buf)

    def slabs_of(buf):
        return [sum(buf[k * nm + g, :, 0:width].astype(F32) for g in range(nm)) for k in range(nd)]

    def own(slabs):
        out = slabs[0]
        for k in range(1, nd):
            out = jnp.where(d == k, slabs[k], out)
        return out

    def norm_rows(i):
        row = norms_ref[i]
        return [row[:, k * width : (k + 1) * width] for k in range(nd)]

    drain("z", z_buf, recv_sem, n - 1)
    z_mine = sum(z_buf[k].astype(F32) * to_rows([parts[j][k] for j in range(hm)]) for k in range(n)).astype(BF16)

    drain("out", out_buf, recv_sem, n - 1)
    hats1, r1 = slab_norm(slabs_of(out_buf), size)
    gains1, shifts1 = norm_rows(2), norm_rows(3)
    normed = [h * g + s for h, g, s in zip(hats1, gains1, shifts1)]
    normed_mine = own(normed)
    normed_low = normed_mine.astype(BF16)

    inner_buf[d] = nn(normed_low, wi[...]).astype(BF16)
    send_dp("inner", inner_buf.at[d], inner_buf.at[d], inner_buf)
    for g in range(nm):
        stat = out_buf[g, :, hw:].astype(F32)
        best = to_rows([joined(stat, 3 * j, 3) for j in range(hm)])
        inv = to_rows([joined(stat, 3 * hm + 2 * j, 2) for j in range(hm)])
        at = slice(g * group, (g + 1) * group)
        col[at, 1:2] = jnp.exp(col[at, 0:1] - best) * inv
    drain("inner", inner_buf, recv_sem, nd - 1)
    inner = sum(inner_buf[k].astype(F32) for k in range(nd))
    cdf = 0.5 * (1.0 + lax.erf(inner * (0.5 ** 0.5)))
    act = (inner * cdf).astype(BF16)
    slope = cdf + inner * jnp.exp(-0.5 * inner * inner) * ((0.5 / math.pi) ** 0.5)
    outer_buf[me] = (nt(act, wt[...]) + jnp.where(m == 0, normed_mine, 0.0)).astype(outer_buf.dtype)
    send_all("outer", lambda pd, pm: outer_buf.at[me], outer_buf.at[me], outer_buf)
    drain("outer", outer_buf, recv_sem, n - 1)
    hats2, r2 = slab_norm(slabs_of(outer_buf), size)
    gains2, shifts2 = norm_rows(4), norm_rows(5)
    for k in range(nd):
        final_buf[e, k] = hats2[k] * gains2[k] + shifts2[k]
    final_at = PHASES.index("final")
    final_copy = pltpu.make_async_remote_copy(
        src_ref=final_buf.at[e], dst_ref=final_buf.at[e], send_sem=send_sem.at[final_at], recv_sem=recv_sem.at[final_at],
        device_id=(1 - e, d, m), device_id_type=MESH,
    )
    final_copy.start()
    final_copy.wait_recv()
    started.append(final_copy.wait_send)

    qs = [final_buf[0, k] for k in range(nd)]
    ps = [final_buf[1, k][0:nb] for k in range(nd)]
    q_r = lax.rsqrt(sum(jnp.sum(x * x, -1, keepdims=True) for x in qs) + eps_norm)
    p_r = lax.rsqrt(sum(jnp.sum(x * x, -1, keepdims=True) for x in ps) + eps_norm)
    q_hat, p_hat = [x * q_r for x in qs], [x * p_r for x in ps]

    def d_sims(left, right, axis, negative, positive, used):
        sims = sum(exact_nt(a, b) for a, b in zip(left, right)) / logit_divisor
        is_positive = lax.broadcasted_iota(jnp.int32, sims.shape, axis) == positive
        sims = jnp.where(jnp.logical_and(negative == 1.0, jnp.logical_not(is_positive)), -1e30, sims)
        best = jnp.max(sims, axis, keepdims=True)
        log_total = best + jnp.log(jnp.sum(jnp.exp(sims - best), axis, keepdims=True))
        target = jnp.sum(jnp.where(is_positive, sims, 0.0), axis, keepdims=True)
        weight = used.astype(F32)
        count = jnp.maximum(jnp.sum(weight, 1 - axis, keepdims=True), 1.0)
        loss = jnp.sum(weight * (log_total - target), 1 - axis, keepdims=True) / count
        grad = (jnp.exp(sims - log_total) - is_positive.astype(F32)) * (weight / count / logit_divisor)
        return loss, grad

    at_row = lax.broadcasted_iota(jnp.int32, (c, c), 0)
    from_query = lax.broadcasted_iota(jnp.int32, (c, c), 1)
    order = (from_query == 2 * (at_row % nb) + at_row // nb).astype(BF16)
    negative = negative_ref[...].astype(F32).astype(BF16)
    column, line = lax.broadcasted_iota(jnp.int32, (c, 1), 0), lax.broadcasted_iota(jnp.int32, (1, c), 1)
    positive = [jnp.zeros((c, 1), jnp.int32), jnp.zeros((1, c), jnp.int32)]
    used = [jnp.zeros((c, 1), jnp.int32), jnp.zeros((1, c), jnp.int32)]
    for k in range(c):
        query = 2 * (k % nb) + k // nb
        for i, place in enumerate((column, line)):
            positive[i] = jnp.where(place == k, positive_ref[query], positive[i])
            used[i] = jnp.where(place == k, used_ref[query], used[i])
    loss, grad_q = d_sims(q_hat, p_hat, 1, nt(order, negative), positive[0], used[0])
    _, grad_p = d_sims(p_hat, q_hat, 0, nt(negative, order), positive[1], used[1])

    def unit_back(hats, r, grads):
        along = sum(jnp.sum(g * h, -1, keepdims=True) for g, h in zip(grads, hats))
        return [r * (g - h * along) for g, h in zip(grads, hats)]

    d_q = unit_back(q_hat, q_r, [exact_nn(grad_q, x) for x in p_hat])
    d_p = unit_back(p_hat, p_r, [exact_nn(grad_p, x) for x in q_hat])
    d_final = [
        jnp.where(is_query, a, jnp.concatenate([b, jnp.zeros_like(b)], axis=0)) for a, b in zip(d_q, d_p)
    ]

    d_second, d_gain2, d_shift2 = slab_norm_back(hats2, r2, d_final, gains2, size)
    d_outer = own(d_second).astype(BF16)
    d_act_buf[d] = nn(d_outer, wt[...]).astype(BF16)
    send_dp("d_act", d_act_buf.at[d], d_act_buf.at[d], d_act_buf)
    g_outer = tn(d_outer, act)
    g_outer_ref[...] = g_outer
    drain("d_act", d_act_buf, recv_sem, nd - 1)
    d_inner = (sum(d_act_buf[k].astype(F32) for k in range(nd)) * slope).astype(BF16)
    d_in_buf[me] = nt(d_inner, wi[...]).astype(d_in_buf.dtype)
    send_all("d_in", lambda pd, pm: d_in_buf.at[me], d_in_buf.at[me], d_in_buf)
    g_inner = tn(normed_low, d_inner)
    g_inner_ref[...] = g_inner
    drain("d_in", d_in_buf, recv_sem, n - 1)
    d_normed = [a + b for a, b in zip(d_second, slabs_of(d_in_buf))]
    d_first, d_gain1, d_shift1 = slab_norm_back(hats1, r1, d_normed, gains1, size)
    d_first_mine = own(d_first)
    d_attn = d_first_mine.astype(BF16)

    part = nt(d_attn, wo[...])
    along = att * part
    lane = lax.broadcasted_iota(jnp.int32, (c, hw), 1) // HEAD
    cols = []
    for j in range(hm):
        cols += split_low(jnp.sum(jnp.where(lane == j, along, 0.0), -1, keepdims=True), 2)
    d_att_buf[me] = with_cols(part.astype(BF16), cols)
    send_all("d_att", lambda pd, pm: d_att_buf.at[me], d_att_buf.at[me], d_att_buf)
    g_out = tn(att_low, d_attn)
    g_out_ref[...] = g_out
    squares = sum(jnp.sum(g * g, 0, keepdims=True) for g in (g_outer, g_inner))
    squares = jnp.sum(squares, -1, keepdims=True) + jnp.sum(jnp.sum(g_out * g_out, 0, keepdims=True), -1, keepdims=True)

    drain("d_att", d_att_buf, recv_sem, n - 1)
    d_atts = []
    for g in range(nm):
        slab = sum(d_att_buf[k * nm + g].astype(F32) for k in range(nd))
        d_att = slab[:, 0:hw].astype(BF16)
        d_atts.append(d_att)
        col[pl.ds(g * group, group), 2:3] = to_rows(
            [joined(slab, hw + 2 * j, 2) for j in range(hm)]
        )
        wide = expand(d_att)
        for k in range(nd):
            basis[pl.ds(heads + g * group, group), k * width : (k + 1) * width] = nt(wide, projection(1, g, k)).astype(BF16)
    d_att_mine = d_atts[0]
    for g in range(1, nm):
        d_att_mine = jnp.where(m == g, d_atts[g], d_att_mine)
    acc[...] = jnp.zeros_like(acc)

    def backward(t, carry):
        at = pl.ds(pl.multiple_of(t * vt, vt), vt)
        d_probs = nt(basis[pl.ds(heads, heads), :], hid[at, :])
        probs = weights[:, at] * col[:, 1:2]
        d_scores = (probs * (d_probs - col[:, 2:3]) * scale).astype(BF16)
        lows[pl.ds(0, heads), at] = d_scores
        lows[pl.ds(heads, heads), at] = probs.astype(BF16)
        acc[...] += nn(d_scores, hid[at, :])
        return carry
    lax.fori_loop(0, tiles, backward, 0)

    for g in range(nm):
        y = acc[pl.ds(g * group, group), :].astype(BF16)
        dq = jnp.zeros((group, hw), F32)
        for k in range(nd):
            dq = dq + nn(y[:, k * width : (k + 1) * width], projection(0, g, k))
            y_src[g, k] = y[:, k * width : (k + 1) * width]
        dq_src[g] = collapse(dq).astype(BF16)
        send_group("dq", g, dq_src.at[g], dq_buf.at[me], dq_buf)
    dq_buf[me] = dq_src[m]
    y_buf[me] = y_src[m, d]
    send_all("y", lambda pd, pm: y_src.at[pm, pd], y_buf.at[me], y_buf)

    lane_t = 128

    def spread(t, carry):
        at = pl.ds(pl.multiple_of(t * lane_t, lane_t), lane_t)
        stage[at, :] = tn(lows[pl.ds(0, 2 * heads), at], basis[pl.ds(0, 2 * heads), :])
        return carry
    lax.fori_loop(0, rows // lane_t, spread, 0)

    drain("dq", dq_buf, recv_sem, n - 1)
    dq_mine = sum(dq_buf[k].astype(F32) for k in range(n)).astype(BF16)
    d_rows_buf[me] = (nt(dq_mine, wq[...]) + jnp.where(m == 0, d_first_mine, 0.0)).astype(d_rows_buf.dtype)
    send_all("d_rows", lambda pd, pm: d_rows_buf.at[me], d_rows_buf.at[me], d_rows_buf)
    g_q = tn(mine_low, dq_mine)
    g_v = tn(z_mine, expand(d_att_mine))
    drain("y", y_buf, recv_sem, n - 1)
    y_mine = sum(y_buf[k].astype(F32) for k in range(n)).astype(BF16)
    g_k = tn(y_mine, expand(q_mine))
    for i, g in enumerate((g_q, g_k, g_v)):
        g_mixed_ref[i] = g
    parts3 = sum(jnp.sum(g * g, 0, keepdims=True) for g in (g_q, g_k, g_v))
    squares = squares + jnp.sum(parts3, -1, keepdims=True)

    drain("d_rows", d_rows_buf, recv_sem, n - 1)
    d_rows = jnp.concatenate([s.astype(BF16) for s in slabs_of(d_rows_buf)], axis=1)
    basis[pl.ds(2 * heads, c), :] = d_rows

    def table_back(t, carry):
        d_gain, d_shift, square = carry
        at = pl.ds(pl.multiple_of(t * lane_t, lane_t), lane_t)
        dy = stage[at, :] + tn(lows[pl.ds(hot_at, c), at], basis[pl.ds(2 * heads, c), :])
        x = emb[at, :].astype(F32)
        x = x - jnp.mean(x, -1, keepdims=True)
        r = lax.rsqrt(jnp.mean(x * x, -1, keepdims=True) + eps_norm)
        hat = x * r
        scaled = dy * gain0
        mean = jnp.mean(scaled, -1, keepdims=True)
        along = jnp.mean(scaled * hat, -1, keepdims=True)
        dx = r * (scaled - mean - hat * along)
        stage[at, :] = dx
        fold = lambda v: jnp.sum(v.reshape(lane_t // 8, 8, size), 0)
        return d_gain + fold(dy * hat), d_shift + fold(dy), square + fold(dx * dx)
    zero = jnp.zeros((8, size), F32)
    d_gain, d_shift, square = lax.fori_loop(0, rows // lane_t, table_back, (zero, zero, zero))
    store = pltpu.make_async_copy(stage, g_table_hbm, store_sem)
    store.start()
    started.append(store.wait)
    d_gain, d_shift = jnp.sum(d_gain, 0, keepdims=True), jnp.sum(d_shift, 0, keepdims=True)
    squares = squares + jnp.sum(jnp.sum(square, 0, keepdims=True), -1, keepdims=True)
    chunks = size // 128
    lines = [v[:, k * 128 : (k + 1) * 128] for v in (d_gain, d_shift) for k in range(chunks)]
    lines.append(jnp.broadcast_to(squares, (1, 128)))
    lines.append(jnp.zeros((16 - len(lines), 128), F32))
    sums_buf[me] = jnp.concatenate(lines, axis=0)

    def send_sums(i, carry):
        pd, pm = peer(i)
        remote("sums", sums_buf.at[me], sums_buf.at[me], (e, pd, pm))
        return carry
    lax.fori_loop(1, n, send_sums, 0)
    sent.append(("sums", sums_buf, n - 1, True))
    drain("sums", sums_buf, recv_sem, n - 1, both=True)
    totals = sum(sums_buf[k] for k in range(n))
    firsts = [jnp.concatenate([totals[v * chunks + k : v * chunks + k + 1] for k in range(chunks)], axis=1) for v in range(2)]
    squares = totals[2 * chunks : 2 * chunks + 1, 0:1]
    for i in range(2):
        g_norms_ref[i : i + 1, :] = firsts[i]
        squares = squares + jnp.sum(firsts[i] * firsts[i], -1, keepdims=True)
    for i, slabs in enumerate((d_gain1, d_shift1, d_gain2, d_shift2)):
        for k in range(nd):
            g_norms_ref[2 + i : 3 + i, k * width : (k + 1) * width] = slabs[k]
            squares = squares + jnp.sum(slabs[k] * slabs[k], -1, keepdims=True)
    norm_buf[e] = jnp.broadcast_to(squares, (8, 128))
    norm_at = PHASES.index("norm")
    norm_copy = pltpu.make_async_remote_copy(
        src_ref=norm_buf.at[e], dst_ref=norm_buf.at[e], send_sem=send_sem.at[norm_at], recv_sem=recv_sem.at[norm_at],
        device_id=(1 - e, d, m), device_id_type=MESH,
    )
    norm_copy.start()
    norm_copy.wait_recv()
    started.append(norm_copy.wait_send)
    grad_norm = jnp.sqrt(norm_buf[0] + norm_buf[1])
    small_ref[...] = jnp.where(
        lax.broadcasted_iota(jnp.int32, (8, 128), 0) == 0, jnp.broadcast_to(loss, (8, 128)), grad_norm
    )

    finish()


def kernel_gradients(
    token_ids, query_lengths, negative_mask, positive_index, used_rows, table, w_mixed, w_out, w_inner, w_outer, norm_params
):
    nd, nm = lax.axis_size("dp"), lax.axis_size("mp")
    n = nd * nm
    blk = token_ids.shape[1]
    _, rows, size = table.shape
    width, hw, ff = w_mixed.shape[1], w_mixed.shape[3], w_inner.shape[2]
    hm = hw // HEAD
    nb = nd * blk
    c = 2 * nb
    group, heads = hm * c, nm * hm * c
    S = jax.ShapeDtypeStruct
    outs = (
        S((8, 128), F32), S((rows, size), F32), S((3, width, hw), F32),
        S((hw, width), F32), S((width, ff), F32), S((width, ff), F32), S((8, size), F32),
    )
    vm, hb = pl.BlockSpec(memory_space=pltpu.VMEM), pl.BlockSpec(memory_space=pl.ANY)
    sm = pl.BlockSpec(memory_space=pltpu.SMEM)
    V = pltpu.VMEM
    wide = hw + HEAD
    scratch = [
        V((rows, size), F32), V((rows, size), BF16), V((rows, size), BF16), V((heads, rows), F32),
        V((2 * heads + c, rows), BF16), V((2 * heads + c, size), BF16), V((c, rows), F32), V((nb, 32, 128), F32),
        V((heads, size), F32), V((heads, 128), F32),
        V((3, width, hw), F32), V((hw, width), F32), V((width, ff), F32), V((width, ff), F32),
        V((width, hw), BF16), V((hw, width), BF16), V((width, ff), BF16), V((width, ff), BF16), V((2, nm, nd, width // 2, 2 * hw), BF16),
        V((nd, blk, 2 * QSLOT), jnp.int32),
        V((nd, c, width), BF16), V((n, c, width), BF16), V((n, c, hw), BF16),
        V((nm, c, wide), BF16), V((n, c, wide), BF16),
        V((nm, nd, group, width), BF16), V((n, group, width), BF16),
        V((n, c, wide), BF16), V((nd, c, ff), BF16), V((n, c, width), BF16), V((2, nd, c, width), F32),
        V((nd, c, ff), BF16), V((n, c, width), BF16), V((n, c, wide), BF16), V((nm, c, hw), BF16), V((n, c, hw), BF16),
        V((nm, nd, group, width), BF16), V((n, group, width), BF16), V((n, c, width), BF16),
        V((n, 16, 128), F32), V((2, 8, 128), F32),
        pltpu.SemaphoreType.DMA((len(PHASES),)), pltpu.SemaphoreType.DMA((len(PHASES),)),
        pltpu.SemaphoreType.DMA((2,)), pltpu.SemaphoreType.DMA((2, nd)), pltpu.SemaphoreType.DMA((2,)),
        pltpu.SemaphoreType.DMA((4,)), pltpu.SemaphoreType.DMA((rows // 384,)), pltpu.SemaphoreType.DMA,
    ]
    small, g_table, g_mixed, g_out, g_inner, g_outer, g_norms = pl.pallas_call(
        partial(grad_kernel, (nd, nm, blk, rows, width, size, hm, ff)),
        out_shape=outs,
        in_specs=[vm, sm, sm, sm, vm, vm, hb, hb, hb, hb, hb],
        out_specs=(vm, hb, vm, vm, vm, vm, vm),
        scratch_shapes=scratch,
        compiler_params=pltpu.CompilerParams(collective_id=ENTRY_ID, has_side_effects=True, vmem_limit_bytes=56 << 20),
        name="gradients",
    )(
        token_ids, query_lengths, positive_index, used_rows, negative_mask.T, norm_params.swapaxes(0, 1), table[0], w_mixed[0].swapaxes(0, 1), w_out[0], w_inner[0],
        w_outer[0].T,
    )
    return small[0, 0], small[1, 0], (g_table, g_mixed.swapaxes(0, 1), g_out, g_inner, g_outer.T, g_norms[0:6])


def on_device(
    token_ids,
    query_lengths,
    negative_mask,
    positive_index,
    used_rows,
    step_count,
    table,
    w_mixed,
    w_out,
    w_inner,
    w_outer,
    norm_params,
    table_m,
    table_v,
    mixed_m,
    mixed_v,
    out_m,
    out_v,
    inner_m,
    inner_v,
    outer_m,
    outer_v,
    norms_m,
    norms_v,
):
    operands = (
        token_ids, query_lengths, negative_mask, positive_index, used_rows, table, w_mixed, w_out, w_inner, w_outer, norm_params
    )
    if table.shape[1] % 384 == 0 and w_mixed.shape[1] % 64 == 0 and table.shape[1] <= 2048:
        loss, grad_norm, grads = kernel_gradients(*operands)
    else:
        loss, grads = gradients(*operands)
        owner = (lax.axis_index("dp") == 0) & (lax.axis_index("mp") == 0)
        squares = jnp.where(owner, jnp.sum(grads[5] * grads[5]), 0.0)
        for grad in grads[:5]:
            squares = squares + jnp.sum(grad * grad)
        grad_norm = jnp.sqrt(lax.psum(squares, ("enc", "dp", "mp")))
    clip = jnp.minimum(1.0, clip_limit / (grad_norm + 1e-06))
    count = step_count[0].astype(F32)
    masters = (table, w_mixed, w_out, w_inner, w_outer, norm_params)
    firsts = (table_m, mixed_m, out_m, inner_m, outer_m, norms_m)
    seconds = (table_v, mixed_v, out_v, inner_v, outer_v, norms_v)
    results = [loss, grad_norm]
    for index in range(6):
        rate, decay = (0.5, 0.0) if index == 5 else (0.06, 0.01)
        results.extend(
            adam_step(
                masters[index], grads[index][None] * clip, firsts[index], seconds[index], rate, decay, count
            )
        )
    return tuple(results)


def solution(mesh):
    table = P("enc", ("dp", "mp"), None)
    mixed = P("enc", "dp", None, "mp")
    columns = P("enc", "mp", "dp")
    units = P("enc", "dp", "mp")
    norms = P("enc", None, None)
    matrices = (table, mixed, columns, units, columns, norms)
    moments = tuple(spec for spec in matrices for _ in range(2))
    updated = tuple(spec for spec in matrices for _ in range(3))
    return jax.shard_map(
        on_device,
        mesh=mesh,
        in_specs=(P("enc", "dp", None), P("dp"), P(), P(), P(), P()) + matrices + moments,
        out_specs=(P(), P()) + updated,
        check_vma=False,
    )
```

```python
import math
from functools import partial

import jax
import jax.numpy as jnp
from jax import lax
from jax.experimental import pallas as pl
from jax.experimental.pallas import tpu as pltpu
from jax.sharding import PartitionSpec as P

HEAD = 64
QSLOT = 128
F32 = jnp.float32
BF16 = jnp.bfloat16

exact_arithmetic_level = lax.Precision.HIGHEST
eps_norm = 1e-06
logit_divisor = 0.05
clip_limit = 0.02
beta_one = 0.9
beta_two = 0.999
adam_eps = 1e-08


def layer_norm(x, gain, shift):
    centred = x - jnp.mean(x, -1, keepdims=True)
    spread = jnp.mean(centred * centred, -1, keepdims=True)
    return centred * lax.rsqrt(spread + eps_norm) * gain + shift


def mul(spec, a, b):
    return jnp.einsum(spec, a, b, preferred_element_type=F32)


def token_counts(ids, lens, is_query, base, rows):
    pos = jnp.arange(ids.shape[1])
    slot = pos // QSLOT
    limit = jnp.where(slot[None, :] == 0, lens[:, 0:1], lens[:, 1:2])
    within = (pos % QSLOT)[None, :] < limit
    same = slot[None, :] == jnp.arange(2)[:, None]
    allowed = jnp.where(is_query, same[:, None, :] & within[None], True)
    local = ids - base
    n_hi = -(-rows // 128)
    high = (local[..., None] >> 7) == jnp.arange(n_hi)
    low = (local[..., None] & 127) == jnp.arange(128)
    left = (allowed[..., None] & high[None]).astype(BF16)
    counts = mul("sbth,btl->sbhl", left, low.astype(BF16))
    return counts.reshape(2 * ids.shape[0], n_hi * 128)[:, :rows]


def contrast(queries, passages, negative_mask, positive_index, used_rows):
    question_direction_rows = queries * lax.rsqrt(
        jnp.sum(queries * queries, -1, keepdims=True) + eps_norm
    )
    document_direction_rows = passages * lax.rsqrt(
        jnp.sum(passages * passages, -1, keepdims=True) + eps_norm
    )
    pairwise_cosine_table = (
        jnp.dot(
            question_direction_rows, document_direction_rows.T, precision=exact_arithmetic_level
        )
        / logit_divisor
    )
    is_positive = jnp.arange(passages.shape[0])[None, :] == positive_index[:, None]
    excluded = (negative_mask == 1) & ~is_positive
    pairwise_cosine_table = jnp.where(excluded, -1e30, pairwise_cosine_table)
    top = jnp.max(pairwise_cosine_table, -1, keepdims=True)
    log_total = top[:, 0] + jnp.log(jnp.sum(jnp.exp(pairwise_cosine_table - top), -1))
    target = jnp.sum(jnp.where(is_positive, pairwise_cosine_table, 0.0), -1)
    weight = used_rows.astype(F32)
    return jnp.sum(weight * (log_total - target)) / jnp.maximum(jnp.sum(weight), 1.0)


def adam_step(weight, grad, first, second, rate, decay, count):
    first_new = beta_one * first + (1.0 - beta_one) * grad
    second_new = beta_two * second + (1.0 - beta_two) * grad * grad
    fix_one = 1.0 - jnp.power(beta_one, count)
    correction_second = 1.0 - jnp.power(beta_two, count)
    update = (
        first_new / fix_one / (jnp.sqrt(second_new / correction_second) + adam_eps) + decay * weight
    )
    return (weight - rate * update, first_new, second_new)


def slot_major(x):
    return x.reshape((x.shape[0] // 2, 2) + x.shape[1:]).swapaxes(0, 1).reshape(x.shape)


def gradients(
    token_ids, query_lengths, negative_mask, positive_index, used_rows, table, w_mixed, w_out, w_inner, w_outer, norm_params
):
    is_query = lax.axis_index("enc") == 0
    d, m = lax.axis_index("dp"), lax.axis_index("mp")
    n_mp = lax.axis_size("mp")
    rows, width = table.shape[1], w_mixed.shape[1]
    hm = w_out.shape[1] // HEAD
    scale = HEAD ** (-0.5)
    norms = norm_params[0]
    base = (d * n_mp + m) * rows

    ids = lax.all_gather(token_ids[0], "dp", axis=0, tiled=True)
    lens = lax.all_gather(query_lengths, "dp", axis=0, tiled=True).reshape(-1, 2)
    blocks = ids.shape[0]
    counts = token_counts(ids, lens, is_query, base, rows)
    cls_ids = jnp.concatenate([ids[:, 0], ids[:, QSLOT]]) - base
    cls_hot = cls_ids[:, None] == jnp.arange(rows)[None, :]

    def mine(x):
        return lax.dynamic_slice_in_dim(x, d * width, width, 1)

    wq, wk, wv = (w_mixed[0, :, i].astype(BF16).reshape(width, hm, HEAD) for i in range(3))
    wo = w_out[0].astype(BF16).reshape(hm, HEAD, width)
    wi, wt = w_inner[0].astype(BF16), w_outer[0].astype(BF16)

    embedded = lax.reduce_precision(table[0], 8, 7)
    hidden, hidden_back = jax.vjp(layer_norm, embedded, norms[0], norms[1])
    hid = hidden.astype(BF16)
    first_rows = lax.psum(
        jnp.dot(cls_hot.astype(F32), hidden, precision=exact_arithmetic_level), ("dp", "mp")
    )
    first_mine = mine(first_rows).astype(BF16)
    q = lax.psum(mul("ci,ihk->hck", first_mine, wq), "dp").astype(BF16)
    u = mul("hck,ihk->hci", q, wk).astype(BF16)
    u = lax.all_gather(lax.all_gather(u, "dp", axis=2, tiled=True), "mp", axis=0, tiled=True)
    scores = jnp.where(counts[None] > 0, mul("hci,vi->hcv", u, hid) * scale, -1e30)
    top = lax.pmax(jnp.max(scores, -1, keepdims=True), ("dp", "mp"))
    weight = counts[None] * jnp.exp(scores - top)
    probs = weight / lax.psum(jnp.sum(weight, -1, keepdims=True), ("dp", "mp"))
    probs_low = probs.astype(BF16)
    z = mul("hcv,vi->hci", probs_low, hid)
    z = lax.psum_scatter(z, "mp", scatter_dimension=0, tiled=True)
    z = lax.psum_scatter(z, "dp", scatter_dimension=2, tiled=True).astype(BF16)
    att = lax.psum(mul("hci,ihk->hck", z, wv), "dp")
    att_low = att.astype(BF16)
    out = lax.psum(mul("hck,hke->ce", att_low, wo), "mp")
    first_sum = first_rows + lax.all_gather(out, "dp", axis=1, tiled=True)
    normed, normed_back = jax.vjp(layer_norm, first_sum, norms[2], norms[3])
    normed_mine = mine(normed).astype(BF16)
    inner = lax.psum(mul("ci,if->cf", normed_mine, wi), "dp")
    act, act_back = jax.vjp(partial(jax.nn.gelu, approximate=False), inner)
    act = act.astype(BF16)
    outer = lax.psum(mul("cf,fe->ce", act, wt), "mp")
    second_sum = normed + lax.all_gather(outer, "dp", axis=1, tiled=True)
    final, final_back = jax.vjp(layer_norm, second_sum, norms[4], norms[5])
    both = lax.all_gather(final, "enc", axis=0)
    loss, loss_back = jax.vjp(
        partial(
            contrast,
            negative_mask=slot_major(negative_mask),
            positive_index=slot_major(positive_index),
            used_rows=slot_major(used_rows),
        ),
        both[0],
        both[1, :blocks],
    )
    d_queries, d_passages = loss_back(jnp.ones((), F32))
    d_passages = jnp.concatenate([d_passages, jnp.zeros_like(d_passages)])
    d_final = jnp.where(is_query, d_queries, d_passages)

    d_second, d_gain2, d_shift2 = final_back(d_final)
    d_outer = mine(d_second).astype(BF16)
    g_outer = mul("cf,ce->fe", act, d_outer)
    d_act = lax.psum(mul("ce,fe->cf", d_outer, wt), "dp")
    d_inner = act_back(d_act)[0].astype(BF16)
    g_inner = mul("ci,cf->if", normed_mine, d_inner)
    d_in = lax.psum(mul("cf,if->ci", d_inner, wi), "mp")
    d_normed = d_second + lax.all_gather(d_in, "dp", axis=1, tiled=True)
    d_first, d_gain1, d_shift1 = normed_back(d_normed)
    d_attn = mine(d_first).astype(BF16)
    g_out = mul("hck,ce->hke", att_low, d_attn).reshape(w_out.shape[1:])
    d_att = lax.psum(mul("ce,hke->hck", d_attn, wo), "dp").astype(BF16)
    w = mul("hck,ihk->hci", d_att, wv).astype(BF16)
    mean_d = jnp.sum(att * d_att.astype(F32), -1, keepdims=True)
    w = lax.all_gather(lax.all_gather(w, "dp", axis=2, tiled=True), "mp", axis=0, tiled=True)
    mean_d = lax.all_gather(mean_d, "mp", axis=0, tiled=True)
    d_probs = mul("hci,vi->hcv", w, hid)
    d_scores = (probs * (d_probs - mean_d)).astype(BF16)
    y = mul("hcv,vi->hci", d_scores, hid)
    y = lax.psum_scatter(y, "mp", scatter_dimension=0, tiled=True)
    y = lax.psum_scatter(y, "dp", scatter_dimension=2, tiled=True).astype(BF16)
    dq = (lax.psum(mul("hci,ihk->hck", y, wk), "dp") * scale).astype(BF16)
    g_q = mul("ci,hck->ihk", first_mine, dq)
    g_k = mul("hci,hck->ihk", y, q) * scale
    g_v = mul("hci,hck->ihk", z, d_att)
    g_mixed = jnp.stack([g_q, g_k, g_v], 1).reshape(w_mixed.shape[1:])
    d_rows = lax.psum(mul("hck,ihk->ci", dq, wq), "mp")
    d_rows = (d_first + lax.all_gather(d_rows, "dp", axis=1, tiled=True)).astype(BF16)
    d_hidden = (
        mul("hcv,hci->vi", d_scores, u) * scale
        + mul("hcv,hci->vi", probs_low, w)
        + mul("cv,ci->vi", cls_hot.astype(BF16), d_rows)
    )
    g_table, d_gain0, d_shift0 = hidden_back(d_hidden)
    sums = lax.psum(jnp.stack([d_gain0, d_shift0]), ("dp", "mp"))
    g_norms = jnp.concatenate([sums, jnp.stack([d_gain1, d_shift1, d_gain2, d_shift2])])
    return loss, (g_table, g_mixed, g_out, g_inner, g_outer, g_norms)


MESH = pl.DeviceIdType.MESH
ENTRY_ID = 3
PHASES = (
    "ids", "rows", "q", "att", "z", "z_dp", "out", "inner", "outer", "final",
    "d_act", "d_in", "d_att", "dq", "y", "y_dp", "d_rows", "sums", "norm",
)
BLOCK = 64


def nt(a, b):
    return lax.dot_general(a, b, (((1,), (1,)), ((), ())), preferred_element_type=F32)


def tn(a, b):
    return lax.dot_general(a, b, (((0,), (0,)), ((), ())), preferred_element_type=F32)


def nn(a, b):
    return jnp.dot(a, b, preferred_element_type=F32)


def exact_nt(a, b):
    return lax.dot_general(
        a, b, (((1,), (1,)), ((), ())), precision=exact_arithmetic_level, preferred_element_type=F32
    )


def exact_nn(a, b):
    return jnp.dot(a, b, precision=exact_arithmetic_level, preferred_element_type=F32)


def slab_norm(slabs, size):
    mean = sum(jnp.sum(s, -1, keepdims=True) for s in slabs) * (1.0 / size)
    slabs = [s - mean for s in slabs]
    spread = sum(jnp.sum(s * s, -1, keepdims=True) for s in slabs) * (1.0 / size)
    r = lax.rsqrt(spread + eps_norm)
    return [s * r for s in slabs], r


def slab_norm_back(hats, r, grads, gains, size):
    scaled = [dy * g for dy, g in zip(grads, gains)]
    mean = sum(jnp.sum(s, -1, keepdims=True) for s in scaled) * (1.0 / size)
    along = sum(jnp.sum(s * h, -1, keepdims=True) for s, h in zip(scaled, hats)) * (1.0 / size)
    d_in = [r * (s - mean - h * along) for s, h in zip(scaled, hats)]
    d_gain = [jnp.sum(dy * h, 0, keepdims=True) for dy, h in zip(grads, hats)]
    d_shift = [jnp.sum(dy, 0, keepdims=True) for dy in grads]
    return d_in, d_gain, d_shift


def joined(x, at, parts):
    return sum(x[:, at + i : at + i + 1] for i in range(parts))


def split_low(x, parts):
    out = []
    for _ in range(parts):
        piece = x.astype(BF16)
        out.append(piece)
        x = x - piece.astype(F32)
    return out


def grad_kernel(cfg, *refs):
    nd, nm, blk, rows, width, size, hm, ff = cfg
    n = nd * nm
    nb = nd * blk
    c = 2 * nb
    hw = hm * HEAD
    group = hm * c
    half = hm * nb
    heads = nm * group
    vt = 384
    tiles = rows // vt
    scale = HEAD ** (-0.5)
    (
        ids_ref, lens_ref, positive_ref, used_ref, negative_ref, norms_ref,
        mixed_f, out_f, inner_f, outer_f, table_hbm, first_hbm, second_hbm,
        small_ref, stage, g_mixed_ref, g_out_ref, g_inner_ref, g_outer_ref, g_norms_ref, table_keep, first_keep, second_keep,
        emb, hid, lows, basis, counts, xs, acc, col, tops, factors,
        wq, wo, wi, wt, kv,
        ids_buf, rows_src, rows_buf, q_buf, att_src, att_buf, z_src, z_mp, z_slab, z_buf, out_buf, inner_buf, outer_buf,
        final_buf, d_act_buf, d_in_buf, d_att_buf, dq_src, dq_buf, y_src, y_mp, y_slab, y_buf, d_rows_buf, sums_buf, norm_buf,
        send_sem, recv_sem, kv_send, kv_recv, kv_spread, table_sem, keep_sem,
    ) = refs
    e, d, m = lax.axis_index("enc"), lax.axis_index("dp"), lax.axis_index("mp")
    me = d * nm + m
    is_query = e == 0
    base = me * rows

    sent, received = [], []

    def halves(go, full):
        pl.when(is_query)(lambda: go(full))
        pl.when(jnp.logical_not(is_query))(lambda: go(full // 2))

    def peer(i):
        p = lax.rem(me + i, n)
        return p // nm, lax.rem(p, nm)

    def remote(name, src, dst, where):
        k = PHASES.index(name)
        pltpu.make_async_remote_copy(
            src_ref=src, dst_ref=dst, send_sem=send_sem.at[k], recv_sem=recv_sem.at[k],
            device_id=where, device_id_type=MESH,
        ).start()

    def send_all(name, src_of, dst, buf):
        sent.append((name, buf, n - 1, False))

        def go(r):
            def one(i, carry):
                pd, pm = peer(i)
                remote(name, src_of(pd, pm).at[pl.ds(0, r)], dst.at[pl.ds(0, r)], (e, pd, pm))
                return carry
            lax.fori_loop(1, n, one, 0)
        halves(go, dst.shape[0])

    def send_group(name, group_of, src, dst, buf):
        if group_of == 0:
            sent.append((name, buf, n - 1, False))

        def go(r):
            for pd in range(nd):
                @pl.when(jnp.logical_or(pd != d, group_of != m))
                def _():
                    remote(name, src.at[pl.ds(0, r)], dst.at[pl.ds(0, r)], (e, pd, group_of))
        halves(go, dst.shape[0])

    def send_dp(name, src, dst, buf, both=False):
        sent.append((name, buf, nd - 1, both))

        def go(r):
            for i in range(1, nd):
                remote(name, src.at[pl.ds(0, r)], dst.at[pl.ds(0, r)], (e, lax.rem(d + i, nd), m))
        if both:
            go(dst.shape[0])
        else:
            halves(go, dst.shape[0])

    def send_mp(name, source, dst, buf):
        sent.append((name, buf, nm - 1, False))

        def go(r):
            for i in range(1, nm):
                g = lax.rem(m + i, nm)
                remote(name, source.at[g, pl.ds(0, r)], dst.at[pl.ds(0, r)], (e, d, g))
        halves(go, dst.shape[0])

    def send_dp_each(name, source, dst, buf):
        sent.append((name, buf, nd - 1, False))

        def go(r):
            for i in range(1, nd):
                k = lax.rem(d + i, nd)
                remote(name, source.at[k, pl.ds(0, r)], dst.at[pl.ds(0, r)], (e, k, m))
        halves(go, dst.shape[0])

    def drain(name, buf, sem, count, both=False):
        k = PHASES.index(name)
        if sem is recv_sem:
            received.append(name)

        def go(r):
            view = buf.at[pl.ds(0, count), pl.ds(0, r)]
            pltpu.make_async_copy(view, view, sem.at[k]).wait()
        if both:
            go(buf.shape[1])
        else:
            halves(go, buf.shape[1])

    def finish():
        for name, buf, count, both in sent:
            drain(name, buf, send_sem, count, both)
            if name not in received:
                drain(name, buf, recv_sem, count, both)
        for item in started:
            item()

    started = []

    table_loads = [
        pltpu.make_async_copy(table_hbm.at[pl.ds(i * vt, vt)], stage.at[pl.ds(i * vt, vt)], table_sem.at[i])
        for i in range(tiles)
    ]
    for item in table_loads:
        item.start()

    @pl.when(jnp.logical_not(is_query))
    def _():
        for buf in (
            rows_buf, q_buf, att_buf, z_mp, z_buf, out_buf, inner_buf, outer_buf, d_act_buf, d_in_buf, d_att_buf, dq_buf,
            y_mp, y_buf, d_rows_buf,
        ):
            r = buf.shape[1] // 2
            for k in range(buf.shape[0]):
                buf[k, r:, :] = jnp.zeros((r, buf.shape[2]), buf.dtype)

    barrier = pltpu.get_barrier_semaphore()

    def greet(i, carry):
        pd, pm = peer(i)
        pl.semaphore_signal(barrier, inc=1, device_id=(e, pd, pm), device_id_type=MESH)
        return carry
    lax.fori_loop(1, n, greet, 0)
    pl.semaphore_signal(barrier, inc=1, device_id=(1 - e, d, m), device_id_type=MESH)
    pl.semaphore_wait(barrier, n)

    row_i = lax.broadcasted_iota(jnp.int32, (blk, 2 * QSLOT), 0)
    lane_i = lax.broadcasted_iota(jnp.int32, (blk, 2 * QSLOT), 1)
    limit = jnp.zeros((blk, 2 * QSLOT), jnp.int32)
    for b in range(blk):
        here = jnp.where(lane_i < QSLOT, lens_ref[2 * b], lens_ref[2 * b + 1])
        limit = jnp.where(row_i == b, here, limit)
    limit = jnp.where(is_query, limit, QSLOT)
    ids_buf[d] = jnp.where((lane_i & (QSLOT - 1)) >= limit, -1, ids_ref[0])
    send_dp("ids", ids_buf.at[d], ids_buf.at[d], ids_buf, both=True)

    fold = width // 2
    for i in range(2):
        kv[i, m, d, :, 0:hw] = mixed_f[1 + i, 0:fold].astype(BF16)
        kv[i, m, d, :, hw:] = mixed_f[1 + i, fold:].astype(BF16)

    def kv_copy(i, src, sem, where):
        piece = kv.at[i, m, src]
        return pltpu.make_async_remote_copy(
            src_ref=piece, dst_ref=piece, send_sem=kv_send.at[i], recv_sem=sem, device_id=where, device_id_type=MESH
        )

    def kv_start(i):
        for k in range(1, nd):
            kv_copy(i, d, kv_recv.at[i, d], (e, lax.rem(d + k, nd), m)).start()
        for k in range(1, nm):
            kv_copy(i, d, kv_spread.at[i], (e, d, lax.rem(m + k, nm))).start()

    def kv_forward(i):
        for k in range(1, nd):
            src = lax.rem(d + k, nd)
            pltpu.make_async_copy(kv.at[i, m, src], kv.at[i, m, src], kv_recv.at[i, src]).wait()
            for j in range(1, nm):
                kv_copy(i, src, kv_spread.at[i], (e, d, lax.rem(m + j, nm))).start()

    def kv_wait(i):
        view = kv.at[i, pl.ds(0, nm - 1)]
        pltpu.make_async_copy(view, view, kv_spread.at[i]).wait()

    def kv_left():
        for i in range(2):
            view = kv.at[i, pl.ds(0, nm - 1)]
            pltpu.make_async_copy(view, view, kv_send.at[i]).wait()
            view = kv.at[i, 0, pl.ds(0, nd - 1)]
            pltpu.make_async_copy(view, view, kv_send.at[i]).wait()
    started.append(kv_left)

    def projection(i, g, k):
        both = kv[i, g, k]
        return jnp.concatenate([both[:, 0:hw], both[:, hw:]], axis=0)

    kv_start(0)
    wq[...] = mixed_f[0].astype(BF16)

    gain0, shift0 = norms_ref[0], norms_ref[1]
    for t in range(tiles):
        table_loads[t].wait()

        def to_low(i, carry):
            at = pl.ds(pl.multiple_of(t * vt + i * BLOCK, BLOCK), BLOCK)
            emb[at, :] = stage[at, :].astype(BF16)
            return carry
        lax.fori_loop(0, vt // BLOCK, to_low, 0)

    drain("ids", ids_buf, recv_sem, nd - 1, both=True)
    ids_all = jnp.concatenate([ids_buf[k] for k in range(nd)], axis=0) - base
    cls = jnp.concatenate([ids_all[:, 0:1], ids_all[:, QSLOT : QSLOT + 1]], axis=0)
    hot_at = 2 * heads
    lows[pl.ds(hot_at, c), :] = (cls == lax.broadcasted_iota(jnp.int32, (c, rows), 1)).astype(BF16)

    def pick(t, total):
        at = pl.ds(pl.multiple_of(t * vt, vt), vt)
        return total + nn(lows[pl.ds(hot_at, c), at], emb[at, :])
    found = lax.fori_loop(0, tiles, pick, jnp.zeros((c, size), F32))
    found_hat, _ = slab_norm([found], size)
    owned = jnp.logical_and(cls >= 0, cls < rows)
    found = jnp.where(owned, found_hat[0] * gain0 + shift0, 0.0).astype(BF16)
    for k in range(nd):
        rows_src[k] = found[:, k * width : (k + 1) * width]
    rows_buf[me] = rows_src[d]
    send_all("rows", lambda pd, pm: rows_src.at[pd], rows_buf.at[me], rows_buf)

    flag = jnp.where(is_query, 1, 0)
    for b in range(nb):
        row = ids_all[b : b + 1, :]
        high, low = row >> 7, row & 127
        lane_b = lax.broadcasted_iota(jnp.int32, (16, 2 * QSLOT), 1)
        is_high = lax.broadcasted_iota(jnp.int32, (16, 2 * QSLOT), 0) == high
        left = [jnp.logical_and(is_high, (lane_b >> 7) * flag == s * flag) for s in range(2)]
        left = jnp.concatenate([item.astype(BF16) for item in left], axis=0)
        right = (lax.broadcasted_iota(jnp.int32, (128, 2 * QSLOT), 0) == low).astype(BF16)
        xs[b] = nt(left, right)
    for t in range(rows // 128):
        for s in range(2):
            counts[s * nb : (s + 1) * nb, t * 128 : (t + 1) * 128] = xs[:, s * 16 + t, :]

    kv_forward(0)
    kv_start(1)

    def normalize(i, carry):
        at = pl.ds(pl.multiple_of(i * BLOCK, BLOCK), BLOCK)
        x = emb[at, :].astype(F32)
        x = x - jnp.mean(x, -1, keepdims=True)
        r = lax.rsqrt(jnp.mean(x * x, -1, keepdims=True) + eps_norm)
        hid[at, :] = (x * r * gain0 + shift0).astype(BF16)
        return carry
    lax.fori_loop(0, rows // BLOCK, normalize, 0)
    for i, (src, dst) in enumerate(((table_hbm, table_keep), (first_hbm, first_keep), (second_hbm, second_keep))):
        keep = pltpu.make_async_copy(src, dst, keep_sem.at[i])
        keep.start()
        started.append(keep.wait)
    wo[...] = out_f[...].astype(BF16)
    wi[...] = inner_f[...].astype(BF16)
    wt[...] = outer_f[...].astype(BF16)

    kv_forward(1)
    drain("rows", rows_buf, recv_sem, n - 1)
    mine = sum(rows_buf[k].astype(F32) for k in range(n))
    mine_low = mine.astype(BF16)
    q_buf[me] = nn(mine_low, wq[...]).astype(BF16)
    send_all("q", lambda pd, pm: q_buf.at[me], q_buf.at[me], q_buf)

    lane_h = lax.broadcasted_iota(jnp.int32, (nb, hw), 1) // HEAD

    def expand(x):
        return jnp.concatenate(
            [
                jnp.where(lane_h == j, x[s * nb : (s + 1) * nb], jnp.zeros((), x.dtype))
                for s in range(2)
                for j in range(hm)
            ],
            axis=0,
        )

    def collapse(x):
        out = []
        for s in range(2):
            parts = [x[s * half + j * nb : s * half + (j + 1) * nb] for j in range(hm)]
            total = parts[0]
            for j in range(1, hm):
                total = jnp.where(lane_h == j, parts[j], total)
            out.append(total)
        return jnp.concatenate(out, axis=0)

    def to_rows(cols):
        return jnp.concatenate([cols[j][s * nb : (s + 1) * nb] for s in range(2) for j in range(hm)], axis=0)

    def to_cols(x):
        return [
            jnp.concatenate([x[s * half + j * nb : s * half + (j + 1) * nb] for s in range(2)], axis=0)
            for j in range(hm)
        ]

    def over_heads(cols):
        lane = lax.broadcasted_iota(jnp.int32, (c, hw), 1) // HEAD
        out = jnp.broadcast_to(cols[0], (c, hw))
        for j in range(1, hm):
            out = jnp.where(lane == j, cols[j], out)
        return out

    def with_cols(x, cols):
        tail = lax.broadcasted_iota(jnp.int32, (c, HEAD), 1)
        extra = jnp.zeros((c, HEAD), F32)
        for k, item in enumerate(cols):
            extra = jnp.where(tail == k, item.astype(F32), extra)
        return jnp.concatenate([x, extra.astype(x.dtype)], axis=1)

    blank = jnp.zeros((c, hw), BF16)
    drain("q", q_buf, recv_sem, n - 1)
    kv_wait(0)
    queries = []
    for g in range(nm):
        q = sum(q_buf[k * nm + g].astype(F32) for k in range(nd)).astype(BF16)
        queries.append(q)
        wide = expand(q)
        for k in range(nd):
            basis[pl.ds(g * group, group), k * width : (k + 1) * width] = nt(wide, projection(0, g, k)).astype(BF16)
    q_mine = queries[0]
    for g in range(1, nm):
        q_mine = jnp.where(m == g, queries[g], q_mine)

    acc[...] = jnp.zeros_like(acc)
    tops[...] = jnp.zeros_like(tops)
    lane_of_tile = lax.broadcasted_iota(jnp.int32, (heads, 8), 1)

    def weigh(t, carry):
        top, total = carry
        at = pl.ds(pl.multiple_of(t * vt, vt), vt)
        s = nt(basis[pl.ds(0, heads), :], hid[at, :]) * scale
        places = [
            (g * group + sl * half + j * nb, pl.ds(sl * nb, nb)) for g in range(nm) for sl in range(2) for j in range(hm)
        ]
        s = [jnp.where(counts[of, at] > 0, s[lo : lo + nb], -1e30) for lo, of in places]
        best = [jnp.maximum(top[lo : lo + nb], jnp.max(x, -1, keepdims=True)) for x, (lo, of) in zip(s, places)]
        sums = []
        for x, high, (lo, of) in zip(s, best, places):
            x = counts[of, at] * jnp.exp(x - high)
            lows[lo : lo + nb, at] = x.astype(BF16)
            sums.append(jnp.sum(x, -1, keepdims=True))
        best = jnp.concatenate(best, axis=0)
        keep = jnp.exp(top - best)
        acc[...] = acc[...] * keep + nn(lows[pl.ds(0, heads), at], hid[at, :])
        tops[...] = jnp.where(lane_of_tile == t, best, tops[...])
        return best, total * keep + jnp.concatenate(sums, axis=0)
    top, total = lax.fori_loop(
        0, tiles, weigh, (jnp.full((heads, 1), -1e30, F32), jnp.zeros((heads, 1), F32))
    )

    kv_wait(1)
    for g in range(nm):
        z = acc[pl.ds(g * group, group), :].astype(BF16)
        att = jnp.zeros((group, hw), F32)
        for k in range(nd):
            att = att + nn(z[:, k * width : (k + 1) * width], projection(1, g, k))
        att = collapse(att).astype(BF16)
        cols = []
        for item in to_cols(top[g * group : (g + 1) * group]):
            cols += split_low(item, 3)
        for item in to_cols(total[g * group : (g + 1) * group]):
            cols += split_low(item, 2)
        att_src[g] = with_cols(att, cols)
        send_group("att", g, att_src.at[g], att_buf.at[me], att_buf)
        z_src[g] = z
    att_buf[me] = att_src[m]
    z_mp[m] = z_src[m]
    send_mp("z", z_src, z_mp.at[m], z_mp)

    drain("att", att_buf, recv_sem, n - 1)
    peaks, sums = [], []
    for k in range(n):
        slab = att_buf[k, :, hw:].astype(F32)
        peaks.append([joined(slab, 3 * j, 3) for j in range(hm)])
        sums.append([joined(slab, 3 * hm + 2 * j, 2) for j in range(hm)])
    top_all, inv_all, parts = [], [], []
    for j in range(hm):
        best = peaks[0][j]
        for k in range(1, n):
            best = jnp.maximum(best, peaks[k][j])
        factor = [jnp.exp(peaks[k][j] - best) for k in range(n)]
        whole = sum(factor[k] * sums[k][j] for k in range(n))
        inv = jnp.where(whole > 0, 1.0 / jnp.where(whole > 0, whole, 1.0), 0.0)
        top_all.append(best)
        inv_all.append(inv)
        parts.append([f * inv for f in factor])
    att = sum(att_buf[k, :, 0:hw].astype(F32) * over_heads([parts[j][k] for j in range(hm)]) for k in range(n))
    att_low = att.astype(BF16)
    part = nn(att_low, wo[...]) + jnp.where(m == 0, mine, 0.0)
    cols = [piece for item in top_all for piece in split_low(item, 3)]
    cols += [piece for item in inv_all for piece in split_low(item, 2)]
    out_buf[me] = with_cols(part.astype(BF16), cols)
    send_all("out", lambda pd, pm: out_buf.at[me], out_buf.at[me], out_buf)

    def slabs_of(buf):
        return [sum(buf[k * nm + g, :, 0:width].astype(F32) for g in range(nm)) for k in range(nd)]

    def own(slabs):
        out = slabs[0]
        for k in range(1, nd):
            out = jnp.where(d == k, slabs[k], out)
        return out

    def norm_rows(i):
        row = norms_ref[i]
        return [row[:, k * width : (k + 1) * width] for k in range(nd)]

    drain("out", out_buf, recv_sem, n - 1)
    hats1, r1 = slab_norm(slabs_of(out_buf), size)
    gains1, shifts1 = norm_rows(2), norm_rows(3)
    normed = [h * g + s for h, g, s in zip(hats1, gains1, shifts1)]
    normed_mine = own(normed)
    normed_low = normed_mine.astype(BF16)

    inner_buf[d] = nn(normed_low, wi[...]).astype(BF16)
    send_dp("inner", inner_buf.at[d], inner_buf.at[d], inner_buf)
    for g in range(nm):
        stat = out_buf[g, :, hw:].astype(F32)
        best = to_rows([joined(stat, 3 * j, 3) for j in range(hm)])
        inv = to_rows([joined(stat, 3 * hm + 2 * j, 2) for j in range(hm)])
        at = pl.ds(g * group, group)
        factors[at, :] = jnp.exp(tops[at, :] - best) * inv
    drain("z", z_mp, recv_sem, nm - 1)
    z = 0.0
    for g in range(nm):
        mine_of = [[parts[j][k * nm + g] for j in range(hm)] for k in range(nd)]
        factor = mine_of[0]
        for k in range(1, nd):
            factor = [jnp.where(d == k, a, b) for a, b in zip(mine_of[k], factor)]
        z = z + z_mp[g].astype(F32) * to_rows(factor)
    for k in range(nd):
        z_slab[k] = z[:, k * width : (k + 1) * width].astype(BF16)
    z_buf[d] = z_slab[d]
    drain("inner", inner_buf, recv_sem, nd - 1)
    inner = sum(inner_buf[k].astype(F32) for k in range(nd))
    cdf = 0.5 * (1.0 + lax.erf(inner * (0.5 ** 0.5)))
    act = (inner * cdf).astype(BF16)
    slope = cdf + inner * jnp.exp(-0.5 * inner * inner) * ((0.5 / math.pi) ** 0.5)
    outer_buf[me] = (nt(act, wt[...]) + jnp.where(m == 0, normed_mine, 0.0)).astype(outer_buf.dtype)
    send_all("outer", lambda pd, pm: outer_buf.at[me], outer_buf.at[me], outer_buf)
    drain("outer", outer_buf, recv_sem, n - 1)
    send_dp_each("z_dp", z_slab, z_buf.at[d], z_buf)
    hats2, r2 = slab_norm(slabs_of(outer_buf), size)
    gains2, shifts2 = norm_rows(4), norm_rows(5)
    for k in range(nd):
        final_buf[e, k] = hats2[k] * gains2[k] + shifts2[k]
    final_at = PHASES.index("final")
    final_copy = pltpu.make_async_remote_copy(
        src_ref=final_buf.at[e], dst_ref=final_buf.at[e], send_sem=send_sem.at[final_at], recv_sem=recv_sem.at[final_at],
        device_id=(1 - e, d, m), device_id_type=MESH,
    )
    final_copy.start()
    final_copy.wait_recv()
    started.append(final_copy.wait_send)

    qs = [final_buf[0, k] for k in range(nd)]
    ps = [final_buf[1, k][0:nb] for k in range(nd)]
    q_r = lax.rsqrt(sum(jnp.sum(x * x, -1, keepdims=True) for x in qs) + eps_norm)
    p_r = lax.rsqrt(sum(jnp.sum(x * x, -1, keepdims=True) for x in ps) + eps_norm)
    q_hat, p_hat = [x * q_r for x in qs], [x * p_r for x in ps]

    def d_sims(left, right, axis, negative, positive, used):
        sims = sum(exact_nt(a, b) for a, b in zip(left, right)) / logit_divisor
        is_positive = lax.broadcasted_iota(jnp.int32, sims.shape, axis) == positive
        sims = jnp.where(jnp.logical_and(negative == 1.0, jnp.logical_not(is_positive)), -1e30, sims)
        best = jnp.max(sims, axis, keepdims=True)
        log_total = best + jnp.log(jnp.sum(jnp.exp(sims - best), axis, keepdims=True))
        target = jnp.sum(jnp.where(is_positive, sims, 0.0), axis, keepdims=True)
        weight = used.astype(F32)
        count = jnp.maximum(jnp.sum(weight, 1 - axis, keepdims=True), 1.0)
        loss = jnp.sum(weight * (log_total - target), 1 - axis, keepdims=True) / count
        grad = (jnp.exp(sims - log_total) - is_positive.astype(F32)) * (weight / count / logit_divisor)
        return loss, grad

    at_row = lax.broadcasted_iota(jnp.int32, (c, c), 0)
    from_query = lax.broadcasted_iota(jnp.int32, (c, c), 1)
    order = (from_query == 2 * (at_row % nb) + at_row // nb).astype(BF16)
    negative = negative_ref[...].astype(F32).astype(BF16)
    column, line = lax.broadcasted_iota(jnp.int32, (c, 1), 0), lax.broadcasted_iota(jnp.int32, (1, c), 1)
    positive = [jnp.zeros((c, 1), jnp.int32), jnp.zeros((1, c), jnp.int32)]
    used = [jnp.zeros((c, 1), jnp.int32), jnp.zeros((1, c), jnp.int32)]
    for k in range(c):
        query = 2 * (k % nb) + k // nb
        for i, place in enumerate((column, line)):
            positive[i] = jnp.where(place == k, positive_ref[query], positive[i])
            used[i] = jnp.where(place == k, used_ref[query], used[i])
    loss, grad_q = d_sims(q_hat, p_hat, 1, nt(order, negative), positive[0], used[0])
    _, grad_p = d_sims(p_hat, q_hat, 0, nt(negative, order), positive[1], used[1])

    def unit_back(hats, r, grads):
        along = sum(jnp.sum(g * h, -1, keepdims=True) for g, h in zip(grads, hats))
        return [r * (g - h * along) for g, h in zip(grads, hats)]

    d_q = unit_back(q_hat, q_r, [exact_nn(grad_q, x) for x in p_hat])
    d_p = unit_back(p_hat, p_r, [exact_nn(grad_p, x) for x in q_hat])
    d_final = [
        jnp.where(is_query, a, jnp.concatenate([b, jnp.zeros_like(b)], axis=0)) for a, b in zip(d_q, d_p)
    ]

    d_second, d_gain2, d_shift2 = slab_norm_back(hats2, r2, d_final, gains2, size)
    d_outer = own(d_second).astype(BF16)
    d_act_buf[d] = nn(d_outer, wt[...]).astype(BF16)
    send_dp("d_act", d_act_buf.at[d], d_act_buf.at[d], d_act_buf)
    g_outer = tn(d_outer, act)
    g_outer_ref[...] = g_outer
    drain("d_act", d_act_buf, recv_sem, nd - 1)
    d_inner = (sum(d_act_buf[k].astype(F32) for k in range(nd)) * slope).astype(BF16)
    d_in_buf[me] = nt(d_inner, wi[...]).astype(d_in_buf.dtype)
    send_all("d_in", lambda pd, pm: d_in_buf.at[me], d_in_buf.at[me], d_in_buf)
    g_inner = tn(normed_low, d_inner)
    g_inner_ref[...] = g_inner
    drain("d_in", d_in_buf, recv_sem, n - 1)
    d_normed = [a + b for a, b in zip(d_second, slabs_of(d_in_buf))]
    d_first, d_gain1, d_shift1 = slab_norm_back(hats1, r1, d_normed, gains1, size)
    d_first_mine = own(d_first)
    d_attn = d_first_mine.astype(BF16)

    part = nt(d_attn, wo[...])
    along = att * part
    lane = lax.broadcasted_iota(jnp.int32, (c, hw), 1) // HEAD
    cols = []
    for j in range(hm):
        cols += split_low(jnp.sum(jnp.where(lane == j, along, 0.0), -1, keepdims=True), 2)
    d_att_buf[me] = with_cols(part.astype(BF16), cols)
    send_all("d_att", lambda pd, pm: d_att_buf.at[me], d_att_buf.at[me], d_att_buf)
    g_out = tn(att_low, d_attn)
    g_out_ref[...] = g_out
    squares = sum(jnp.sum(g * g, 0, keepdims=True) for g in (g_outer, g_inner))
    squares = jnp.sum(squares, -1, keepdims=True) + jnp.sum(jnp.sum(g_out * g_out, 0, keepdims=True), -1, keepdims=True)

    drain("d_att", d_att_buf, recv_sem, n - 1)
    d_atts = []
    for g in range(nm):
        slab = sum(d_att_buf[k * nm + g].astype(F32) for k in range(nd))
        d_att = slab[:, 0:hw].astype(BF16)
        d_atts.append(d_att)
        col[pl.ds(g * group, group), :] = to_rows(
            [joined(slab, hw + 2 * j, 2) for j in range(hm)]
        )
        wide = expand(d_att)
        for k in range(nd):
            basis[pl.ds(heads + g * group, group), k * width : (k + 1) * width] = nt(wide, projection(1, g, k)).astype(BF16)
    d_att_mine = d_atts[0]
    for g in range(1, nm):
        d_att_mine = jnp.where(m == g, d_atts[g], d_att_mine)
    acc[...] = jnp.zeros_like(acc)

    def backward(t, carry):
        at = pl.ds(pl.multiple_of(t * vt, vt), vt)
        d_probs = nt(basis[pl.ds(heads, heads), :], hid[at, :])
        probs = lows[pl.ds(0, heads), at].astype(F32) * jnp.sum(
            jnp.where(lane_of_tile == t, factors[...], 0.0), -1, keepdims=True
        )
        d_scores = (probs * (d_probs - col[...]) * scale).astype(BF16)
        lows[pl.ds(0, heads), at] = d_scores
        lows[pl.ds(heads, heads), at] = probs.astype(BF16)
        acc[...] += nn(d_scores, hid[at, :])
        return carry
    lax.fori_loop(0, tiles, backward, 0)

    for g in range(nm):
        y = acc[pl.ds(g * group, group), :].astype(BF16)
        dq = jnp.zeros((group, hw), F32)
        for k in range(nd):
            dq = dq + nn(y[:, k * width : (k + 1) * width], projection(0, g, k))
        y_src[g] = y
        dq_src[g] = collapse(dq).astype(BF16)
        send_group("dq", g, dq_src.at[g], dq_buf.at[me], dq_buf)
    dq_buf[me] = dq_src[m]
    y_mp[m] = y_src[m]
    send_mp("y", y_src, y_mp.at[m], y_mp)

    lane_t = 128

    def spread(t, carry):
        at = pl.ds(pl.multiple_of(t * lane_t, lane_t), lane_t)
        stage[at, :] = tn(lows[pl.ds(0, 2 * heads), at], basis[pl.ds(0, 2 * heads), :])
        return carry
    lax.fori_loop(0, rows // lane_t, spread, 0)

    drain("dq", dq_buf, recv_sem, n - 1)
    dq_mine = sum(dq_buf[k].astype(F32) for k in range(n)).astype(BF16)
    d_rows_buf[me] = (nt(dq_mine, wq[...]) + jnp.where(m == 0, d_first_mine, 0.0)).astype(d_rows_buf.dtype)
    send_all("d_rows", lambda pd, pm: d_rows_buf.at[me], d_rows_buf.at[me], d_rows_buf)
    g_q = tn(mine_low, dq_mine)
    drain("z_dp", z_buf, recv_sem, nd - 1)
    z_mine = sum(z_buf[k].astype(F32) for k in range(nd)).astype(BF16)
    g_v = tn(z_mine, expand(d_att_mine))
    drain("y", y_mp, recv_sem, nm - 1)
    y = sum(y_mp[g].astype(F32) for g in range(nm))
    for k in range(nd):
        y_slab[k] = y[:, k * width : (k + 1) * width].astype(BF16)
    y_buf[d] = y_slab[d]
    send_dp_each("y_dp", y_slab, y_buf.at[d], y_buf)
    drain("d_rows", d_rows_buf, recv_sem, n - 1)
    d_rows = jnp.concatenate([s.astype(BF16) for s in slabs_of(d_rows_buf)], axis=1)
    basis[pl.ds(2 * heads, c), :] = d_rows

    def table_back(t, carry):
        d_gain, d_shift, square = carry
        at = pl.ds(pl.multiple_of(t * lane_t, lane_t), lane_t)
        dy = stage[at, :] + tn(lows[pl.ds(hot_at, c), at], basis[pl.ds(2 * heads, c), :])
        x = emb[at, :].astype(F32)
        x = x - jnp.mean(x, -1, keepdims=True)
        r = lax.rsqrt(jnp.mean(x * x, -1, keepdims=True) + eps_norm)
        hat = x * r
        scaled = dy * gain0
        mean = jnp.mean(scaled, -1, keepdims=True)
        along = jnp.mean(scaled * hat, -1, keepdims=True)
        dx = r * (scaled - mean - hat * along)
        stage[at, :] = dx
        fold = lambda v: jnp.sum(v.reshape(lane_t // 8, 8, size), 0)
        return d_gain + fold(dy * hat), d_shift + fold(dy), square + fold(dx * dx)
    zero = jnp.zeros((8, size), F32)
    d_gain, d_shift, square = lax.fori_loop(0, rows // lane_t, table_back, (zero, zero, zero))
    drain("y_dp", y_buf, recv_sem, nd - 1)
    y_mine = sum(y_buf[k].astype(F32) for k in range(nd)).astype(BF16)
    g_k = tn(y_mine, expand(q_mine))
    for i, g in enumerate((g_q, g_k, g_v)):
        g_mixed_ref[i] = g
    total = sum(jnp.sum(g * g, 0, keepdims=True) for g in (g_q, g_k, g_v))
    squares = squares + jnp.sum(total, -1, keepdims=True)
    d_gain, d_shift = jnp.sum(d_gain, 0, keepdims=True), jnp.sum(d_shift, 0, keepdims=True)
    squares = squares + jnp.sum(jnp.sum(square, 0, keepdims=True), -1, keepdims=True)
    chunks = size // 128
    lines = [v[:, k * 128 : (k + 1) * 128] for v in (d_gain, d_shift) for k in range(chunks)]
    lines.append(jnp.broadcast_to(squares, (1, 128)))
    lines.append(jnp.zeros((16 - len(lines), 128), F32))
    sums_buf[me] = jnp.concatenate(lines, axis=0)

    def send_sums(i, carry):
        pd, pm = peer(i)
        remote("sums", sums_buf.at[me], sums_buf.at[me], (e, pd, pm))
        return carry
    lax.fori_loop(1, n, send_sums, 0)
    sent.append(("sums", sums_buf, n - 1, True))
    drain("sums", sums_buf, recv_sem, n - 1, both=True)
    totals = sum(sums_buf[k] for k in range(n))
    firsts = [jnp.concatenate([totals[v * chunks + k : v * chunks + k + 1] for k in range(chunks)], axis=1) for v in range(2)]
    squares = totals[2 * chunks : 2 * chunks + 1, 0:1]
    for i in range(2):
        g_norms_ref[i : i + 1, :] = firsts[i]
        squares = squares + jnp.sum(firsts[i] * firsts[i], -1, keepdims=True)
    for i, slabs in enumerate((d_gain1, d_shift1, d_gain2, d_shift2)):
        for k in range(nd):
            g_norms_ref[2 + i : 3 + i, k * width : (k + 1) * width] = slabs[k]
            squares = squares + jnp.sum(slabs[k] * slabs[k], -1, keepdims=True)
    norm_buf[e] = jnp.broadcast_to(squares, (8, 128))
    norm_at = PHASES.index("norm")
    norm_copy = pltpu.make_async_remote_copy(
        src_ref=norm_buf.at[e], dst_ref=norm_buf.at[e], send_sem=send_sem.at[norm_at], recv_sem=recv_sem.at[norm_at],
        device_id=(1 - e, d, m), device_id_type=MESH,
    )
    norm_copy.start()
    norm_copy.wait_recv()
    started.append(norm_copy.wait_send)
    grad_norm = jnp.sqrt(norm_buf[0] + norm_buf[1])
    small_ref[...] = jnp.where(
        lax.broadcasted_iota(jnp.int32, (8, 128), 0) == 0, jnp.broadcast_to(loss, (8, 128)), grad_norm
    )

    finish()


def kernel_gradients(
    token_ids, query_lengths, negative_mask, positive_index, used_rows, table, w_mixed, w_out, w_inner, w_outer, norm_params, table_m, table_v
):
    nd, nm = lax.axis_size("dp"), lax.axis_size("mp")
    n = nd * nm
    blk = token_ids.shape[1]
    _, rows, size = table.shape
    width, hw, ff = w_mixed.shape[1], w_mixed.shape[3], w_inner.shape[2]
    hm = hw // HEAD
    nb = nd * blk
    c = 2 * nb
    group, heads = hm * c, nm * hm * c
    S = jax.ShapeDtypeStruct
    outs = (
        S((8, 128), F32), S((rows, size), F32), S((3, width, hw), F32),
        S((hw, width), F32), S((width, ff), F32), S((width, ff), F32), S((8, size), F32),
    ) + (S((rows, size), F32),) * 3
    vm, hb = pl.BlockSpec(memory_space=pltpu.VMEM), pl.BlockSpec(memory_space=pltpu.HBM)
    sm = pl.BlockSpec(memory_space=pltpu.SMEM)
    V = pltpu.VMEM
    wide = hw + HEAD
    scratch = [
        V((rows, size), BF16), V((rows, size), BF16),
        V((2 * heads + c, rows), BF16), V((2 * heads + c, size), BF16), V((c, rows), F32), V((nb, 32, 128), F32),
        V((heads, size), F32), V((heads, 1), F32), V((heads, 8), F32), V((heads, 8), F32),
        V((width, hw), BF16), V((hw, width), BF16), V((width, ff), BF16), V((width, ff), BF16), V((2, nm, nd, width // 2, 2 * hw), BF16),
        V((nd, blk, 2 * QSLOT), jnp.int32),
        V((nd, c, width), BF16), V((n, c, width), BF16), V((n, c, hw), BF16),
        V((nm, c, wide), BF16), V((n, c, wide), BF16),
        V((nm, group, size), BF16), V((nm, group, size), BF16), V((nd, group, width), BF16), V((nd, group, width), BF16),
        V((n, c, wide), BF16), V((nd, c, ff), BF16), V((n, c, width), BF16), V((2, nd, c, width), F32),
        V((nd, c, ff), BF16), V((n, c, width), BF16), V((n, c, wide), BF16), V((nm, c, hw), BF16), V((n, c, hw), BF16),
        V((nm, group, size), BF16), V((nm, group, size), BF16), V((nd, group, width), BF16), V((nd, group, width), BF16),
        V((n, c, width), BF16),
        V((n, 16, 128), F32), V((2, 8, 128), F32),
        pltpu.SemaphoreType.DMA((len(PHASES),)), pltpu.SemaphoreType.DMA((len(PHASES),)),
        pltpu.SemaphoreType.DMA((2,)), pltpu.SemaphoreType.DMA((2, nd)), pltpu.SemaphoreType.DMA((2,)),
        pltpu.SemaphoreType.DMA((rows // 384,)), pltpu.SemaphoreType.DMA((3,)),
    ]
    small, g_table, g_mixed, g_out, g_inner, g_outer, g_norms, *kept = pl.pallas_call(
        partial(grad_kernel, (nd, nm, blk, rows, width, size, hm, ff)),
        out_shape=outs,
        in_specs=[vm, sm, sm, sm] + [vm] * 6 + [hb] * 3,
        out_specs=(vm,) * 10,
        scratch_shapes=scratch,
        compiler_params=pltpu.CompilerParams(collective_id=ENTRY_ID, has_side_effects=True, vmem_limit_bytes=24 << 20),
        name="gradients",
    )(
        token_ids, query_lengths, positive_index, used_rows, negative_mask.T, norm_params.swapaxes(0, 1),
        w_mixed[0].swapaxes(0, 1), w_out[0], w_inner[0], w_outer[0].T,
        *(pltpu.with_memory_space_constraint(item[0], pltpu.HBM) for item in (table, table_m, table_v)),
    )
    return small, (g_table, g_mixed, g_out, g_inner, g_outer, g_norms), kept


RING = 3
PIECE = 192


def adam_kernel(rates, count_ref, small_ref, *refs):
    k = len(rates)
    operands = [refs[4 * i : 4 * i + 4] for i in range(k)]
    results = [refs[4 * k + 3 * i : 4 * k + 3 * i + 3] for i in range(k)]
    refs = refs[7 * k :]
    ring, ring_sem, own_sem, buffers = refs[:3], refs[3], refs[4], refs[5:]
    norm = small_ref[1:2, 0:1]
    clip = jnp.minimum(1.0, clip_limit / (norm + 1e-06))
    count = jnp.full((1, 1), count_ref[0], jnp.int32).astype(F32)
    fix_one = 1.0 - jnp.exp(count * math.log(beta_one))
    fix_two = 1.0 - jnp.exp(count * math.log(beta_two))
    inv_one, inv_two = 1.0 / fix_one, 1.0 / fix_two
    copies, in_slot, used, turn = [], [None] * RING, 0, 0

    def update(i, at, targets, to):
        grad, weight, first, second = (ref[at] for ref in operands[i])
        rate, decay = rates[i]
        grad = grad * clip
        first = beta_one * first + (1.0 - beta_one) * grad
        second = beta_two * second + ((1.0 - beta_two) * grad) * grad
        step = first * inv_one / (jnp.sqrt(second * inv_two) + adam_eps)
        if decay:
            step = step + decay * weight
        for ref, value in zip(targets, (weight - rate * step, first, second)):
            ref[to] = value

    def send(src, dst, sem):
        copy = pltpu.make_async_copy(src, dst, sem)
        copy.start()
        return copy

    for i in range(k):
        shape = operands[i][1].shape
        if len(shape) == 2 and shape[1] == ring[0].shape[2]:
            for start in range(0, shape[0], PIECE):
                slot = turn % RING
                turn += 1
                if in_slot[slot]:
                    for copy in in_slot[slot]:
                        copy.wait()

                def block(b, carry):
                    at = pl.ds(pl.multiple_of(b * 32, 32), 32)
                    update(i, pl.ds(pl.multiple_of(start + b * 32, 32), 32), [ref.at[slot] for ref in ring], at)
                    return carry
                lax.fori_loop(0, PIECE // 32, block, 0)
                in_slot[slot] = [
                    send(ring[j].at[slot], results[i][j].at[pl.ds(start, PIECE)], ring_sem.at[slot, j]) for j in range(3)
                ]
            continue
        mine = buffers[3 * used : 3 * used + 3]
        if len(shape) == 3:
            for j in range(shape[0]):
                update(i, j, mine, j)
        else:
            update(i, slice(None), mine, slice(None))
        copies += [send(mine[j], results[i][j], own_sem.at[used, j]) for j in range(3)]
        used += 1
    for group in in_slot + [copies]:
        for copy in group or ():
            copy.wait()


def kernel_adam(step_count, small, grads, weights, firsts, seconds):
    k = len(weights)
    rates = tuple((0.5, 0.0) if i == k - 1 else (0.06, 0.01) for i in range(k))
    vm, sm = pl.BlockSpec(memory_space=pltpu.VMEM), pl.BlockSpec(memory_space=pltpu.SMEM)
    shapes = [jax.ShapeDtypeStruct(w.shape, F32) for w in weights for _ in range(3)]
    operands = [item for group in zip(grads, weights, firsts, seconds) for item in group]
    size = weights[0].shape[1]
    alone = [item for item in shapes if len(item.shape) == 3 or item.shape[1] != size]
    return pl.pallas_call(
        partial(adam_kernel, rates),
        out_shape=shapes,
        in_specs=[sm, vm] + [vm] * (4 * k),
        out_specs=[pl.BlockSpec(memory_space=pltpu.HBM)] * (3 * k),
        scratch_shapes=[pltpu.VMEM((RING, PIECE, size), F32)] * 3
        + [pltpu.SemaphoreType.DMA((RING, 3)), pltpu.SemaphoreType.DMA((len(alone) // 3, 3))]
        + [pltpu.VMEM(item.shape, F32) for item in alone],
        compiler_params=pltpu.CompilerParams(vmem_limit_bytes=12 << 20),
        name="adam",
    )(step_count, small, *operands)


def on_device(
    token_ids,
    query_lengths,
    negative_mask,
    positive_index,
    used_rows,
    step_count,
    table,
    w_mixed,
    w_out,
    w_inner,
    w_outer,
    norm_params,
    table_m,
    table_v,
    mixed_m,
    mixed_v,
    out_m,
    out_v,
    inner_m,
    inner_v,
    outer_m,
    outer_v,
    norms_m,
    norms_v,
):
    operands = (
        token_ids, query_lengths, negative_mask, positive_index, used_rows, table, w_mixed, w_out, w_inner, w_outer, norm_params
    )
    masters = (table, w_mixed, w_out, w_inner, w_outer, norm_params)
    firsts = (table_m, mixed_m, out_m, inner_m, outer_m, norms_m)
    seconds = (table_v, mixed_v, out_v, inner_v, outer_v, norms_v)
    if table.shape[1] % 384 == 0 and w_mixed.shape[1] % 64 == 0 and table.shape[1] <= 2048:
        small, grads, kept = kernel_gradients(*operands, table_m, table_v)

        def stored(tab, items):
            _, mixed, out, inner, outer, norm = items
            return tab, mixed[0].swapaxes(0, 1), out[0], inner[0], outer[0].T, norm.swapaxes(0, 1)

        grads = grads[:5] + (grads[5][0:6, None, :],)
        updated = kernel_adam(step_count, small, grads, *map(stored, kept, (masters, firsts, seconds)))
        back = (
            lambda x: x[None],
            lambda x: x.swapaxes(0, 1)[None],
            lambda x: x[None],
            lambda x: x[None],
            lambda x: x.T[None],
            lambda x: x.swapaxes(0, 1),
        )
        return (small[0, 0], small[1, 0]) + tuple(back[i // 3](item) for i, item in enumerate(updated))
    loss, grads = gradients(*operands)
    owner = (lax.axis_index("dp") == 0) & (lax.axis_index("mp") == 0)
    squares = jnp.where(owner, jnp.sum(grads[5] * grads[5]), 0.0)
    for grad in grads[:5]:
        squares = squares + jnp.sum(grad * grad)
    grad_norm = jnp.sqrt(lax.psum(squares, ("enc", "dp", "mp")))
    clip = jnp.minimum(1.0, clip_limit / (grad_norm + 1e-06))
    count = step_count[0].astype(F32)
    results = [loss, grad_norm]
    for index in range(6):
        rate, decay = (0.5, 0.0) if index == 5 else (0.06, 0.01)
        results.extend(
            adam_step(
                masters[index], grads[index][None] * clip, firsts[index], seconds[index], rate, decay, count
            )
        )
    return tuple(results)


def solution(mesh):
    table = P("enc", ("dp", "mp"), None)
    mixed = P("enc", "dp", None, "mp")
    columns = P("enc", "mp", "dp")
    units = P("enc", "dp", "mp")
    norms = P("enc", None, None)
    matrices = (table, mixed, columns, units, columns, norms)
    moments = tuple(spec for spec in matrices for _ in range(2))
    updated = tuple(spec for spec in matrices for _ in range(3))
    return jax.shard_map(
        on_device,
        mesh=mesh,
        in_specs=(P("enc", "dp", None), P("dp"), P(), P(), P(), P()) + matrices + moments,
        out_specs=(P(), P()) + updated,
        check_vma=False,
    )
```

```python
import math
from functools import partial

import jax
import jax.numpy as jnp
from jax import lax
from jax.experimental import pallas as pl
from jax.experimental.pallas import tpu as pltpu
from jax.sharding import PartitionSpec as P

HEAD = 64
QSLOT = 128
F32 = jnp.float32
BF16 = jnp.bfloat16

exact_arithmetic_level = lax.Precision.HIGHEST
eps_norm = 1e-06
logit_divisor = 0.05
clip_limit = 0.02
beta_one = 0.9
beta_two = 0.999
adam_eps = 1e-08


def layer_norm(x, gain, shift):
    centred = x - jnp.mean(x, -1, keepdims=True)
    spread = jnp.mean(centred * centred, -1, keepdims=True)
    return centred * lax.rsqrt(spread + eps_norm) * gain + shift


def mul(spec, a, b):
    return jnp.einsum(spec, a, b, preferred_element_type=F32)


def token_counts(ids, lens, is_query, base, rows):
    pos = jnp.arange(ids.shape[1])
    slot = pos // QSLOT
    limit = jnp.where(slot[None, :] == 0, lens[:, 0:1], lens[:, 1:2])
    within = (pos % QSLOT)[None, :] < limit
    same = slot[None, :] == jnp.arange(2)[:, None]
    allowed = jnp.where(is_query, same[:, None, :] & within[None], True)
    local = ids - base
    n_hi = -(-rows // 128)
    high = (local[..., None] >> 7) == jnp.arange(n_hi)
    low = (local[..., None] & 127) == jnp.arange(128)
    left = (allowed[..., None] & high[None]).astype(BF16)
    counts = mul("sbth,btl->sbhl", left, low.astype(BF16))
    return counts.reshape(2 * ids.shape[0], n_hi * 128)[:, :rows]


def contrast(queries, passages, negative_mask, positive_index, used_rows):
    question_direction_rows = queries * lax.rsqrt(
        jnp.sum(queries * queries, -1, keepdims=True) + eps_norm
    )
    document_direction_rows = passages * lax.rsqrt(
        jnp.sum(passages * passages, -1, keepdims=True) + eps_norm
    )
    pairwise_cosine_table = (
        jnp.dot(
            question_direction_rows, document_direction_rows.T, precision=exact_arithmetic_level
        )
        / logit_divisor
    )
    is_positive = jnp.arange(passages.shape[0])[None, :] == positive_index[:, None]
    excluded = (negative_mask == 1) & ~is_positive
    pairwise_cosine_table = jnp.where(excluded, -1e30, pairwise_cosine_table)
    top = jnp.max(pairwise_cosine_table, -1, keepdims=True)
    log_total = top[:, 0] + jnp.log(jnp.sum(jnp.exp(pairwise_cosine_table - top), -1))
    target = jnp.sum(jnp.where(is_positive, pairwise_cosine_table, 0.0), -1)
    weight = used_rows.astype(F32)
    return jnp.sum(weight * (log_total - target)) / jnp.maximum(jnp.sum(weight), 1.0)


def adam_step(weight, grad, first, second, rate, decay, count):
    first_new = beta_one * first + (1.0 - beta_one) * grad
    second_new = beta_two * second + (1.0 - beta_two) * grad * grad
    fix_one = 1.0 - jnp.power(beta_one, count)
    correction_second = 1.0 - jnp.power(beta_two, count)
    update = (
        first_new / fix_one / (jnp.sqrt(second_new / correction_second) + adam_eps) + decay * weight
    )
    return (weight - rate * update, first_new, second_new)


def slot_major(x):
    return x.reshape((x.shape[0] // 2, 2) + x.shape[1:]).swapaxes(0, 1).reshape(x.shape)


def gradients(
    token_ids, query_lengths, negative_mask, positive_index, used_rows, table, w_mixed, w_out, w_inner, w_outer, norm_params
):
    is_query = lax.axis_index("enc") == 0
    d, m = lax.axis_index("dp"), lax.axis_index("mp")
    n_mp = lax.axis_size("mp")
    rows, width = table.shape[1], w_mixed.shape[1]
    hm = w_out.shape[1] // HEAD
    scale = HEAD ** (-0.5)
    norms = norm_params[0]
    base = (d * n_mp + m) * rows

    ids = lax.all_gather(token_ids[0], "dp", axis=0, tiled=True)
    lens = lax.all_gather(query_lengths, "dp", axis=0, tiled=True).reshape(-1, 2)
    blocks = ids.shape[0]
    counts = token_counts(ids, lens, is_query, base, rows)
    cls_ids = jnp.concatenate([ids[:, 0], ids[:, QSLOT]]) - base
    cls_hot = cls_ids[:, None] == jnp.arange(rows)[None, :]

    def mine(x):
        return lax.dynamic_slice_in_dim(x, d * width, width, 1)

    wq, wk, wv = (w_mixed[0, :, i].astype(BF16).reshape(width, hm, HEAD) for i in range(3))
    wo = w_out[0].astype(BF16).reshape(hm, HEAD, width)
    wi, wt = w_inner[0].astype(BF16), w_outer[0].astype(BF16)

    embedded = lax.reduce_precision(table[0], 8, 7)
    hidden, hidden_back = jax.vjp(layer_norm, embedded, norms[0], norms[1])
    hid = hidden.astype(BF16)
    first_rows = lax.psum(
        jnp.dot(cls_hot.astype(F32), hidden, precision=exact_arithmetic_level), ("dp", "mp")
    )
    first_mine = mine(first_rows).astype(BF16)
    q = lax.psum(mul("ci,ihk->hck", first_mine, wq), "dp").astype(BF16)
    u = mul("hck,ihk->hci", q, wk).astype(BF16)
    u = lax.all_gather(lax.all_gather(u, "dp", axis=2, tiled=True), "mp", axis=0, tiled=True)
    scores = jnp.where(counts[None] > 0, mul("hci,vi->hcv", u, hid) * scale, -1e30)
    top = lax.pmax(jnp.max(scores, -1, keepdims=True), ("dp", "mp"))
    weight = counts[None] * jnp.exp(scores - top)
    probs = weight / lax.psum(jnp.sum(weight, -1, keepdims=True), ("dp", "mp"))
    probs_low = probs.astype(BF16)
    z = mul("hcv,vi->hci", probs_low, hid)
    z = lax.psum_scatter(z, "mp", scatter_dimension=0, tiled=True)
    z = lax.psum_scatter(z, "dp", scatter_dimension=2, tiled=True).astype(BF16)
    att = lax.psum(mul("hci,ihk->hck", z, wv), "dp")
    att_low = att.astype(BF16)
    out = lax.psum(mul("hck,hke->ce", att_low, wo), "mp")
    first_sum = first_rows + lax.all_gather(out, "dp", axis=1, tiled=True)
    normed, normed_back = jax.vjp(layer_norm, first_sum, norms[2], norms[3])
    normed_mine = mine(normed).astype(BF16)
    inner = lax.psum(mul("ci,if->cf", normed_mine, wi), "dp")
    act, act_back = jax.vjp(partial(jax.nn.gelu, approximate=False), inner)
    act = act.astype(BF16)
    outer = lax.psum(mul("cf,fe->ce", act, wt), "mp")
    second_sum = normed + lax.all_gather(outer, "dp", axis=1, tiled=True)
    final, final_back = jax.vjp(layer_norm, second_sum, norms[4], norms[5])
    both = lax.all_gather(final, "enc", axis=0)
    loss, loss_back = jax.vjp(
        partial(
            contrast,
            negative_mask=slot_major(negative_mask),
            positive_index=slot_major(positive_index),
            used_rows=slot_major(used_rows),
        ),
        both[0],
        both[1, :blocks],
    )
    d_queries, d_passages = loss_back(jnp.ones((), F32))
    d_passages = jnp.concatenate([d_passages, jnp.zeros_like(d_passages)])
    d_final = jnp.where(is_query, d_queries, d_passages)

    d_second, d_gain2, d_shift2 = final_back(d_final)
    d_outer = mine(d_second).astype(BF16)
    g_outer = mul("cf,ce->fe", act, d_outer)
    d_act = lax.psum(mul("ce,fe->cf", d_outer, wt), "dp")
    d_inner = act_back(d_act)[0].astype(BF16)
    g_inner = mul("ci,cf->if", normed_mine, d_inner)
    d_in = lax.psum(mul("cf,if->ci", d_inner, wi), "mp")
    d_normed = d_second + lax.all_gather(d_in, "dp", axis=1, tiled=True)
    d_first, d_gain1, d_shift1 = normed_back(d_normed)
    d_attn = mine(d_first).astype(BF16)
    g_out = mul("hck,ce->hke", att_low, d_attn).reshape(w_out.shape[1:])
    d_att = lax.psum(mul("ce,hke->hck", d_attn, wo), "dp").astype(BF16)
    w = mul("hck,ihk->hci", d_att, wv).astype(BF16)
    mean_d = jnp.sum(att * d_att.astype(F32), -1, keepdims=True)
    w = lax.all_gather(lax.all_gather(w, "dp", axis=2, tiled=True), "mp", axis=0, tiled=True)
    mean_d = lax.all_gather(mean_d, "mp", axis=0, tiled=True)
    d_probs = mul("hci,vi->hcv", w, hid)
    d_scores = (probs * (d_probs - mean_d)).astype(BF16)
    y = mul("hcv,vi->hci", d_scores, hid)
    y = lax.psum_scatter(y, "mp", scatter_dimension=0, tiled=True)
    y = lax.psum_scatter(y, "dp", scatter_dimension=2, tiled=True).astype(BF16)
    dq = (lax.psum(mul("hci,ihk->hck", y, wk), "dp") * scale).astype(BF16)
    g_q = mul("ci,hck->ihk", first_mine, dq)
    g_k = mul("hci,hck->ihk", y, q) * scale
    g_v = mul("hci,hck->ihk", z, d_att)
    g_mixed = jnp.stack([g_q, g_k, g_v], 1).reshape(w_mixed.shape[1:])
    d_rows = lax.psum(mul("hck,ihk->ci", dq, wq), "mp")
    d_rows = (d_first + lax.all_gather(d_rows, "dp", axis=1, tiled=True)).astype(BF16)
    d_hidden = (
        mul("hcv,hci->vi", d_scores, u) * scale
        + mul("hcv,hci->vi", probs_low, w)
        + mul("cv,ci->vi", cls_hot.astype(BF16), d_rows)
    )
    g_table, d_gain0, d_shift0 = hidden_back(d_hidden)
    sums = lax.psum(jnp.stack([d_gain0, d_shift0]), ("dp", "mp"))
    g_norms = jnp.concatenate([sums, jnp.stack([d_gain1, d_shift1, d_gain2, d_shift2])])
    return loss, (g_table, g_mixed, g_out, g_inner, g_outer, g_norms)


MESH = pl.DeviceIdType.MESH
ENTRY_ID = 3
PHASES = (
    "ids", "rows", "q", "stat", "att", "z", "z_dp", "out", "inner", "outer", "final",
    "d_act", "d_in", "d_att", "dq", "y", "y_dp", "d_rows", "sums", "norm",
)
BLOCK = 64


def nt(a, b):
    return lax.dot_general(a, b, (((1,), (1,)), ((), ())), preferred_element_type=F32)


def tn(a, b):
    return lax.dot_general(a, b, (((0,), (0,)), ((), ())), preferred_element_type=F32)


def nn(a, b):
    return jnp.dot(a, b, preferred_element_type=F32)


def exact_nt(a, b):
    return lax.dot_general(
        a, b, (((1,), (1,)), ((), ())), precision=exact_arithmetic_level, preferred_element_type=F32
    )


def exact_nn(a, b):
    return jnp.dot(a, b, precision=exact_arithmetic_level, preferred_element_type=F32)


def slab_norm(slabs, size):
    mean = sum(jnp.sum(s, -1, keepdims=True) for s in slabs) * (1.0 / size)
    slabs = [s - mean for s in slabs]
    spread = sum(jnp.sum(s * s, -1, keepdims=True) for s in slabs) * (1.0 / size)
    r = lax.rsqrt(spread + eps_norm)
    return [s * r for s in slabs], r


def slab_norm_back(hats, r, grads, gains, size):
    scaled = [dy * g for dy, g in zip(grads, gains)]
    mean = sum(jnp.sum(s, -1, keepdims=True) for s in scaled) * (1.0 / size)
    along = sum(jnp.sum(s * h, -1, keepdims=True) for s, h in zip(scaled, hats)) * (1.0 / size)
    d_in = [r * (s - mean - h * along) for s, h in zip(scaled, hats)]
    d_gain = [jnp.sum(dy * h, 0, keepdims=True) for dy, h in zip(grads, hats)]
    d_shift = [jnp.sum(dy, 0, keepdims=True) for dy in grads]
    return d_in, d_gain, d_shift


def joined(x, at, parts):
    return sum(x[:, at + i : at + i + 1] for i in range(parts))


def split_low(x, parts):
    out = []
    for _ in range(parts):
        piece = x.astype(BF16)
        out.append(piece)
        x = x - piece.astype(F32)
    return out


def grad_kernel(cfg, *refs):
    nd, nm, blk, rows, width, size, hm, ff = cfg
    n = nd * nm
    nb = nd * blk
    c = 2 * nb
    hw = hm * HEAD
    group = hm * c
    half = hm * nb
    heads = nm * group
    vt = 384
    tiles = rows // vt
    scale = HEAD ** (-0.5)
    (
        *early_hbm, table_hbm, first_hbm, second_hbm,
        small_ref, stage, g_mixed_ref, g_out_ref, g_inner_ref, g_outer_ref, g_norms_ref, table_keep, first_keep, second_keep,
        mixed_f, ids_ref, lens_ref, norms_ref, out_f, inner_f, outer_f, positive_ref, used_ref, negative_ref,
        emb, hid, lows, basis, counts, xs, acc, col, tops, factors,
        wq, wo, wi, wt, kv,
        ids_buf, rows_src, rows_buf, q_buf, stat_src, stat_buf, att_buf, z_src, z_mp, z_slab, z_buf, out_buf, inner_buf, outer_buf,
        final_buf, d_act_buf, d_in_buf, d_att_buf, dq_src, dq_buf, y_src, y_mp, y_slab, y_buf, d_rows_buf, sums_buf, norm_buf,
        send_sem, recv_sem, kv_send, kv_recv, kv_spread, table_sem, keep_sem, early_sem,
    ) = refs
    e, d, m = lax.axis_index("enc"), lax.axis_index("dp"), lax.axis_index("mp")
    me = d * nm + m
    is_query = e == 0
    base = me * rows

    sent, received = [], []

    def halves(go, full):
        pl.when(is_query)(lambda: go(full))
        pl.when(jnp.logical_not(is_query))(lambda: go(full // 2))

    def peer(i):
        p = lax.rem(me + i, n)
        return p // nm, lax.rem(p, nm)

    def remote(name, src, dst, where):
        k = PHASES.index(name)
        pltpu.make_async_remote_copy(
            src_ref=src, dst_ref=dst, send_sem=send_sem.at[k], recv_sem=recv_sem.at[k],
            device_id=where, device_id_type=MESH,
        ).start()

    def send_all(name, src_of, dst, buf):
        sent.append((name, buf, n - 1, False))

        def go(r):
            def one(i, carry):
                pd, pm = peer(i)
                remote(name, src_of(pd, pm).at[pl.ds(0, r)], dst.at[pl.ds(0, r)], (e, pd, pm))
                return carry
            lax.fori_loop(1, n, one, 0)
        halves(go, dst.shape[0])

    def send_group(name, group_of, src, dst, buf):
        if group_of == 0:
            sent.append((name, buf, n - 1, False))

        def go(r):
            for pd in range(nd):
                @pl.when(jnp.logical_or(pd != d, group_of != m))
                def _():
                    remote(name, src.at[pl.ds(0, r)], dst.at[pl.ds(0, r)], (e, pd, group_of))
        halves(go, dst.shape[0])

    def send_dp(name, src, dst, buf, both=False):
        sent.append((name, buf, nd - 1, both))

        def go(r):
            for i in range(1, nd):
                remote(name, src.at[pl.ds(0, r)], dst.at[pl.ds(0, r)], (e, lax.rem(d + i, nd), m))
        if both:
            go(dst.shape[0])
        else:
            halves(go, dst.shape[0])

    def send_mp(name, source, dst, buf):
        sent.append((name, buf, nm - 1, False))

        def go(r):
            for i in range(1, nm):
                g = lax.rem(m + i, nm)
                remote(name, source.at[g, pl.ds(0, r)], dst.at[pl.ds(0, r)], (e, d, g))
        halves(go, dst.shape[0])

    def send_dp_each(name, source, dst, buf):
        sent.append((name, buf, nd - 1, False))

        def go(r):
            for i in range(1, nd):
                k = lax.rem(d + i, nd)
                remote(name, source.at[k, pl.ds(0, r)], dst.at[pl.ds(0, r)], (e, k, m))
        halves(go, dst.shape[0])

    def drain(name, buf, sem, count, both=False):
        k = PHASES.index(name)
        if sem is recv_sem:
            received.append(name)

        def go(r):
            view = buf.at[pl.ds(0, count), pl.ds(0, r)]
            pltpu.make_async_copy(view, view, sem.at[k]).wait()
        if both:
            go(buf.shape[1])
        else:
            halves(go, buf.shape[1])

    def finish():
        for name, buf, count, both in sent:
            drain(name, buf, send_sem, count, both)
            if name not in received:
                drain(name, buf, recv_sem, count, both)
        for item in started:
            item()

    started = []

    early = (mixed_f, ids_ref, lens_ref, norms_ref, out_f, inner_f, outer_f, positive_ref, used_ref, negative_ref)
    early = [pltpu.make_async_copy(src, dst, early_sem.at[i]) for i, (src, dst) in enumerate(zip(early_hbm, early))]
    table_loads = [
        pltpu.make_async_copy(table_hbm.at[pl.ds(i * vt, vt)], stage.at[pl.ds(i * vt, vt)], table_sem.at[i])
        for i in range(tiles)
    ]
    for item in early[:4]:
        item.start()
    for item in table_loads:
        item.start()
    for item in early[4:]:
        item.start()

    @pl.when(jnp.logical_not(is_query))
    def _():
        for buf in (
            rows_buf, q_buf, stat_buf, att_buf, z_mp, z_buf, out_buf, inner_buf, outer_buf, d_act_buf, d_in_buf, d_att_buf, dq_buf,
            y_mp, y_buf, d_rows_buf,
        ):
            r = buf.shape[1] // 2
            for k in range(buf.shape[0]):
                buf[k, r:, :] = jnp.zeros((r, buf.shape[2]), buf.dtype)

    barrier = pltpu.get_barrier_semaphore()

    def greet(i, carry):
        pd, pm = peer(i)
        pl.semaphore_signal(barrier, inc=1, device_id=(e, pd, pm), device_id_type=MESH)
        return carry
    lax.fori_loop(1, n, greet, 0)
    pl.semaphore_signal(barrier, inc=1, device_id=(1 - e, d, m), device_id_type=MESH)
    pl.semaphore_wait(barrier, n)

    early[1].wait()
    early[2].wait()
    row_i = lax.broadcasted_iota(jnp.int32, (blk, 2 * QSLOT), 0)
    lane_i = lax.broadcasted_iota(jnp.int32, (blk, 2 * QSLOT), 1)
    limit = jnp.zeros((blk, 2 * QSLOT), jnp.int32)
    for b in range(blk):
        here = jnp.where(lane_i < QSLOT, lens_ref[2 * b], lens_ref[2 * b + 1])
        limit = jnp.where(row_i == b, here, limit)
    limit = jnp.where(is_query, limit, QSLOT)
    ids_buf[d] = jnp.where((lane_i & (QSLOT - 1)) >= limit, -1, ids_ref[0])
    send_dp("ids", ids_buf.at[d], ids_buf.at[d], ids_buf, both=True)

    early[0].wait()
    fold = width // 2
    for i in range(2):
        kv[i, m, d, :, 0:hw] = mixed_f[1 + i, 0:fold].astype(BF16)
        kv[i, m, d, :, hw:] = mixed_f[1 + i, fold:].astype(BF16)

    def kv_copy(i, src, sem, where):
        piece = kv.at[i, m, src]
        return pltpu.make_async_remote_copy(
            src_ref=piece, dst_ref=piece, send_sem=kv_send.at[i], recv_sem=sem, device_id=where, device_id_type=MESH
        )

    def kv_to_dp(i):
        for k in range(1, nd):
            kv_copy(i, d, kv_recv.at[i, d], (e, lax.rem(d + k, nd), m)).start()

    def kv_to_mp(i, src):
        for k in range(1, nm):
            kv_copy(i, src, kv_spread.at[i], (e, d, lax.rem(m + k, nm))).start()

    def kv_from_dp(i, k):
        src = lax.rem(d + k, nd)
        pltpu.make_async_copy(kv.at[i, m, src], kv.at[i, m, src], kv_recv.at[i, src]).wait()
        return src

    def kv_wait(i):
        view = kv.at[i, pl.ds(0, nm - 1)]
        pltpu.make_async_copy(view, view, kv_spread.at[i]).wait()

    def kv_left():
        for i in range(2):
            view = kv.at[i, pl.ds(0, nm - 1)]
            pltpu.make_async_copy(view, view, kv_send.at[i]).wait()
            view = kv.at[i, 0, pl.ds(0, nd - 1)]
            pltpu.make_async_copy(view, view, kv_send.at[i]).wait()
    started.append(kv_left)

    def projection(i, g, k):
        both = kv[i, g, k]
        return jnp.concatenate([both[:, 0:hw], both[:, hw:]], axis=0)

    kv_to_dp(0)
    kv_to_mp(0, d)
    wq[...] = mixed_f[0].astype(BF16)

    early[3].wait()
    gain0, shift0 = norms_ref[0], norms_ref[1]
    for t in range(tiles):
        table_loads[t].wait()

        def to_low(i, carry):
            at = pl.ds(pl.multiple_of(t * vt + i * BLOCK, BLOCK), BLOCK)
            emb[at, :] = stage[at, :].astype(BF16)
            return carry
        lax.fori_loop(0, vt // BLOCK, to_low, 0)

    for k in range(1, nd):
        kv_to_mp(0, kv_from_dp(0, k))
    drain("ids", ids_buf, recv_sem, nd - 1, both=True)
    ids_all = jnp.concatenate([ids_buf[k] for k in range(nd)], axis=0) - base
    cls = jnp.concatenate([ids_all[:, 0:1], ids_all[:, QSLOT : QSLOT + 1]], axis=0)
    hot_at = 2 * heads
    lows[pl.ds(hot_at, c), :] = (cls == lax.broadcasted_iota(jnp.int32, (c, rows), 1)).astype(BF16)

    def pick(t, total):
        at = pl.ds(pl.multiple_of(t * vt, vt), vt)
        return total + nn(lows[pl.ds(hot_at, c), at], emb[at, :])
    found = lax.fori_loop(0, tiles, pick, jnp.zeros((c, size), F32))
    found_hat, _ = slab_norm([found], size)
    owned = jnp.logical_and(cls >= 0, cls < rows)
    found = jnp.where(owned, found_hat[0] * gain0 + shift0, 0.0).astype(BF16)
    for k in range(nd):
        rows_src[k] = found[:, k * width : (k + 1) * width]
    rows_buf[me] = rows_src[d]
    send_all("rows", lambda pd, pm: rows_src.at[pd], rows_buf.at[me], rows_buf)

    flag = jnp.where(is_query, 1, 0)
    for b in range(nb):
        row = ids_all[b : b + 1, :]
        high, low = row >> 7, row & 127
        lane_b = lax.broadcasted_iota(jnp.int32, (16, 2 * QSLOT), 1)
        is_high = lax.broadcasted_iota(jnp.int32, (16, 2 * QSLOT), 0) == high
        left = [jnp.logical_and(is_high, (lane_b >> 7) * flag == s * flag) for s in range(2)]
        left = jnp.concatenate([item.astype(BF16) for item in left], axis=0)
        right = (lax.broadcasted_iota(jnp.int32, (128, 2 * QSLOT), 0) == low).astype(BF16)
        xs[b] = nt(left, right)
    for t in range(rows // 128):
        for s in range(2):
            counts[s * nb : (s + 1) * nb, t * 128 : (t + 1) * 128] = xs[:, s * 16 + t, :]

    kv_to_dp(1)

    def normalize(i, carry):
        at = pl.ds(pl.multiple_of(i * BLOCK, BLOCK), BLOCK)
        x = emb[at, :].astype(F32)
        x = x - jnp.mean(x, -1, keepdims=True)
        r = lax.rsqrt(jnp.mean(x * x, -1, keepdims=True) + eps_norm)
        hid[at, :] = (x * r * gain0 + shift0).astype(BF16)
        return carry
    lax.fori_loop(0, rows // BLOCK, normalize, 0)
    for i, (src, dst) in enumerate(((table_hbm, table_keep), (first_hbm, first_keep), (second_hbm, second_keep))):
        keep = pltpu.make_async_copy(src, dst, keep_sem.at[i])
        keep.start()
        started.append(keep.wait)
    for item in early[4:]:
        item.wait()
    wo[...] = out_f[...].astype(BF16)
    wi[...] = inner_f[...].astype(BF16)
    wt[...] = outer_f[...].astype(BF16)

    drain("rows", rows_buf, recv_sem, n - 1)
    mine = sum(rows_buf[k].astype(F32) for k in range(n))
    mine_low = mine.astype(BF16)
    q_buf[me] = nn(mine_low, wq[...]).astype(BF16)
    send_all("q", lambda pd, pm: q_buf.at[me], q_buf.at[me], q_buf)

    lane_h = lax.broadcasted_iota(jnp.int32, (nb, hw), 1) // HEAD

    def expand(x):
        return jnp.concatenate(
            [
                jnp.where(lane_h == j, x[s * nb : (s + 1) * nb], jnp.zeros((), x.dtype))
                for s in range(2)
                for j in range(hm)
            ],
            axis=0,
        )

    def collapse(x):
        out = []
        for s in range(2):
            parts = [x[s * half + j * nb : s * half + (j + 1) * nb] for j in range(hm)]
            total = parts[0]
            for j in range(1, hm):
                total = jnp.where(lane_h == j, parts[j], total)
            out.append(total)
        return jnp.concatenate(out, axis=0)

    def to_rows(cols):
        return jnp.concatenate([cols[j][s * nb : (s + 1) * nb] for s in range(2) for j in range(hm)], axis=0)

    def to_cols(x):
        return [
            jnp.concatenate([x[s * half + j * nb : s * half + (j + 1) * nb] for s in range(2)], axis=0)
            for j in range(hm)
        ]

    def over_heads(cols):
        lane = lax.broadcasted_iota(jnp.int32, (c, hw), 1) // HEAD
        out = jnp.broadcast_to(cols[0], (c, hw))
        for j in range(1, hm):
            out = jnp.where(lane == j, cols[j], out)
        return out

    def with_cols(x, cols):
        tail = lax.broadcasted_iota(jnp.int32, (c, HEAD), 1)
        extra = jnp.zeros((c, HEAD), F32)
        for k, item in enumerate(cols):
            extra = jnp.where(tail == k, item.astype(F32), extra)
        return jnp.concatenate([x, extra.astype(x.dtype)], axis=1)

    blank = jnp.zeros((c, hw), BF16)
    drain("q", q_buf, recv_sem, n - 1)
    kv_wait(0)
    queries = []
    for g in range(nm):
        q = sum(q_buf[k * nm + g].astype(F32) for k in range(nd)).astype(BF16)
        queries.append(q)
        wide = expand(q)
        for k in range(nd):
            basis[pl.ds(g * group, group), k * width : (k + 1) * width] = nt(wide, projection(0, g, k)).astype(BF16)
    q_mine = queries[0]
    for g in range(1, nm):
        q_mine = jnp.where(m == g, queries[g], q_mine)

    acc[...] = jnp.zeros_like(acc)
    tops[...] = jnp.zeros_like(tops)
    lane_of_tile = lax.broadcasted_iota(jnp.int32, (heads, 8), 1)

    def weigh(t, carry):
        top, total = carry
        at = pl.ds(pl.multiple_of(t * vt, vt), vt)
        s = nt(basis[pl.ds(0, heads), :], hid[at, :]) * scale
        places = [
            (g * group + sl * half + j * nb, pl.ds(sl * nb, nb)) for g in range(nm) for sl in range(2) for j in range(hm)
        ]
        s = [jnp.where(counts[of, at] > 0, s[lo : lo + nb], -1e30) for lo, of in places]
        best = [jnp.maximum(top[lo : lo + nb], jnp.max(x, -1, keepdims=True)) for x, (lo, of) in zip(s, places)]
        sums = []
        for x, high, (lo, of) in zip(s, best, places):
            x = counts[of, at] * jnp.exp(x - high)
            lows[lo : lo + nb, at] = x.astype(BF16)
            sums.append(jnp.sum(x, -1, keepdims=True))
        best = jnp.concatenate(best, axis=0)
        keep = jnp.exp(top - best)
        acc[...] = acc[...] * keep + nn(lows[pl.ds(0, heads), at], hid[at, :])
        tops[...] = jnp.where(lane_of_tile == t, best, tops[...])
        return best, total * keep + jnp.concatenate(sums, axis=0)
    top, total = lax.fori_loop(
        0, tiles, weigh, (jnp.full((heads, 1), -1e30, F32), jnp.zeros((heads, 1), F32))
    )

    def stat_slab(cols):
        lane = lax.broadcasted_iota(jnp.int32, (c, 128), 1)
        out = jnp.zeros((c, 128), F32)
        for k, item in enumerate(cols):
            out = jnp.where(lane == k, item, out)
        return out

    for g in range(nm):
        at = slice(g * group, (g + 1) * group)
        z_src[g] = acc[at, :].astype(BF16)
        stat_src[g] = stat_slab(to_cols(top[at]) + to_cols(total[at]))
    stat_buf[m] = stat_src[m]
    z_mp[m] = z_src[m]
    send_mp("stat", stat_src, stat_buf.at[m], stat_buf)
    send_mp("z", z_src, z_mp.at[m], z_mp)

    def combine(peaks, sums):
        best = peaks[0]
        for item in peaks[1:]:
            best = jnp.maximum(best, item)
        factor = [jnp.exp(item - best) for item in peaks]
        return best, factor, sum(f * item for f, item in zip(factor, sums))

    drain("stat", stat_buf, recv_sem, nm - 1)
    stats = [stat_buf[g] for g in range(nm)]
    near = [combine([x[:, j : j + 1] for x in stats], [x[:, hm + j : hm + j + 1] for x in stats]) for j in range(hm)]
    scales = [to_rows([near[j][1][g] for j in range(hm)]) for g in range(nm)]
    for k in range(1, nd):
        kv_from_dp(1, k)
    drain("z", z_mp, recv_sem, nm - 1)
    z_near = sum(z_mp[g].astype(F32) * scales[g] for g in range(nm))
    att = 0.0
    for k in range(nd):
        att = att + nn(z_near[:, k * width : (k + 1) * width].astype(BF16), projection(1, m, k))
    cols = [piece for j in range(hm) for piece in split_low(near[j][0], 3)]
    cols += [piece for j in range(hm) for piece in split_low(near[j][2], 2)]
    att_buf[d] = with_cols(collapse(att).astype(BF16), cols)
    send_dp("att", att_buf.at[d], att_buf.at[d], att_buf)

    drain("att", att_buf, recv_sem, nd - 1)
    far = []
    slabs = [att_buf[k, :, hw:].astype(F32) for k in range(nd)]
    for j in range(hm):
        far.append(combine([joined(x, 3 * j, 3) for x in slabs], [joined(x, 3 * hm + 2 * j, 2) for x in slabs]))
    top_all = [item[0] for item in far]
    inv_all = [jnp.where(x > 0, 1.0 / jnp.where(x > 0, x, 1.0), 0.0) for _, _, x in far]
    parts = [[f * inv for f in item[1]] for item, inv in zip(far, inv_all)]
    att = sum(att_buf[k, :, 0:hw].astype(F32) * over_heads([parts[j][k] for j in range(hm)]) for k in range(nd))
    att_low = att.astype(BF16)
    part = nn(att_low, wo[...]) + jnp.where(m == 0, mine, 0.0)
    cols = [piece for item in top_all for piece in split_low(item, 3)]
    cols += [piece for item in inv_all for piece in split_low(item, 2)]
    out_buf[me] = with_cols(part.astype(BF16), cols)
    send_all("out", lambda pd, pm: out_buf.at[me], out_buf.at[me], out_buf)

    def slabs_of(buf):
        return [sum(buf[k * nm + g, :, 0:width].astype(F32) for g in range(nm)) for k in range(nd)]

    def own(slabs):
        out = slabs[0]
        for k in range(1, nd):
            out = jnp.where(d == k, slabs[k], out)
        return out

    def norm_rows(i):
        row = norms_ref[i]
        return [row[:, k * width : (k + 1) * width] for k in range(nd)]

    drain("out", out_buf, recv_sem, n - 1)
    hats1, r1 = slab_norm(slabs_of(out_buf), size)
    gains1, shifts1 = norm_rows(2), norm_rows(3)
    normed = [h * g + s for h, g, s in zip(hats1, gains1, shifts1)]
    normed_mine = own(normed)
    normed_low = normed_mine.astype(BF16)

    inner_buf[d] = nn(normed_low, wi[...]).astype(BF16)
    send_dp("inner", inner_buf.at[d], inner_buf.at[d], inner_buf)
    kv_to_mp(1, d)
    for k in range(1, nd):
        kv_to_mp(1, lax.rem(d + k, nd))
    for g in range(nm):
        stat = out_buf[g, :, hw:].astype(F32)
        best = to_rows([joined(stat, 3 * j, 3) for j in range(hm)])
        inv = to_rows([joined(stat, 3 * hm + 2 * j, 2) for j in range(hm)])
        at = pl.ds(g * group, group)
        factors[at, :] = jnp.exp(tops[at, :] - best) * inv
    z = z_near * to_rows([own(parts[j]) for j in range(hm)])
    for k in range(nd):
        z_slab[k] = z[:, k * width : (k + 1) * width].astype(BF16)
    z_buf[d] = z_slab[d]
    drain("inner", inner_buf, recv_sem, nd - 1)
    inner = sum(inner_buf[k].astype(F32) for k in range(nd))
    cdf = 0.5 * (1.0 + lax.erf(inner * (0.5 ** 0.5)))
    act = (inner * cdf).astype(BF16)
    slope = cdf + inner * jnp.exp(-0.5 * inner * inner) * ((0.5 / math.pi) ** 0.5)
    outer_buf[me] = (nt(act, wt[...]) + jnp.where(m == 0, normed_mine, 0.0)).astype(outer_buf.dtype)
    send_all("outer", lambda pd, pm: outer_buf.at[me], outer_buf.at[me], outer_buf)
    drain("outer", outer_buf, recv_sem, n - 1)
    send_dp_each("z_dp", z_slab, z_buf.at[d], z_buf)
    hats2, r2 = slab_norm(slabs_of(outer_buf), size)
    gains2, shifts2 = norm_rows(4), norm_rows(5)
    for k in range(nd):
        final_buf[e, k] = hats2[k] * gains2[k] + shifts2[k]
    final_at = PHASES.index("final")
    final_copy = pltpu.make_async_remote_copy(
        src_ref=final_buf.at[e], dst_ref=final_buf.at[e], send_sem=send_sem.at[final_at], recv_sem=recv_sem.at[final_at],
        device_id=(1 - e, d, m), device_id_type=MESH,
    )
    final_copy.start()
    final_copy.wait_recv()
    started.append(final_copy.wait_send)

    qs = [final_buf[0, k] for k in range(nd)]
    ps = [final_buf[1, k][0:nb] for k in range(nd)]
    q_r = lax.rsqrt(sum(jnp.sum(x * x, -1, keepdims=True) for x in qs) + eps_norm)
    p_r = lax.rsqrt(sum(jnp.sum(x * x, -1, keepdims=True) for x in ps) + eps_norm)
    q_hat, p_hat = [x * q_r for x in qs], [x * p_r for x in ps]

    def d_sims(left, right, axis, negative, positive, used):
        sims = sum(exact_nt(a, b) for a, b in zip(left, right)) / logit_divisor
        is_positive = lax.broadcasted_iota(jnp.int32, sims.shape, axis) == positive
        sims = jnp.where(jnp.logical_and(negative == 1.0, jnp.logical_not(is_positive)), -1e30, sims)
        best = jnp.max(sims, axis, keepdims=True)
        log_total = best + jnp.log(jnp.sum(jnp.exp(sims - best), axis, keepdims=True))
        target = jnp.sum(jnp.where(is_positive, sims, 0.0), axis, keepdims=True)
        weight = used.astype(F32)
        count = jnp.maximum(jnp.sum(weight, 1 - axis, keepdims=True), 1.0)
        loss = jnp.sum(weight * (log_total - target), 1 - axis, keepdims=True) / count
        grad = (jnp.exp(sims - log_total) - is_positive.astype(F32)) * (weight / count / logit_divisor)
        return loss, grad

    at_row = lax.broadcasted_iota(jnp.int32, (c, c), 0)
    from_query = lax.broadcasted_iota(jnp.int32, (c, c), 1)
    order = (from_query == 2 * (at_row % nb) + at_row // nb).astype(BF16)
    negative = negative_ref[...].astype(F32).astype(BF16)
    column, line = lax.broadcasted_iota(jnp.int32, (c, 1), 0), lax.broadcasted_iota(jnp.int32, (1, c), 1)
    positive = [jnp.zeros((c, 1), jnp.int32), jnp.zeros((1, c), jnp.int32)]
    used = [jnp.zeros((c, 1), jnp.int32), jnp.zeros((1, c), jnp.int32)]
    for k in range(c):
        query = 2 * (k % nb) + k // nb
        for i, place in enumerate((column, line)):
            positive[i] = jnp.where(place == k, positive_ref[query], positive[i])
            used[i] = jnp.where(place == k, used_ref[query], used[i])
    loss, grad_q = d_sims(q_hat, p_hat, 1, nt(order, negative), positive[0], used[0])
    _, grad_p = d_sims(p_hat, q_hat, 0, nt(negative, order), positive[1], used[1])

    def unit_back(hats, r, grads):
        along = sum(jnp.sum(g * h, -1, keepdims=True) for g, h in zip(grads, hats))
        return [r * (g - h * along) for g, h in zip(grads, hats)]

    d_q = unit_back(q_hat, q_r, [exact_nn(grad_q, x) for x in p_hat])
    d_p = unit_back(p_hat, p_r, [exact_nn(grad_p, x) for x in q_hat])
    d_final = [
        jnp.where(is_query, a, jnp.concatenate([b, jnp.zeros_like(b)], axis=0)) for a, b in zip(d_q, d_p)
    ]

    d_second, d_gain2, d_shift2 = slab_norm_back(hats2, r2, d_final, gains2, size)
    d_outer = own(d_second).astype(BF16)
    d_act_buf[d] = nn(d_outer, wt[...]).astype(BF16)
    send_dp("d_act", d_act_buf.at[d], d_act_buf.at[d], d_act_buf)
    g_outer = tn(d_outer, act)
    g_outer_ref[...] = g_outer
    drain("d_act", d_act_buf, recv_sem, nd - 1)
    d_inner = (sum(d_act_buf[k].astype(F32) for k in range(nd)) * slope).astype(BF16)
    d_in_buf[me] = nt(d_inner, wi[...]).astype(d_in_buf.dtype)
    send_all("d_in", lambda pd, pm: d_in_buf.at[me], d_in_buf.at[me], d_in_buf)
    g_inner = tn(normed_low, d_inner)
    g_inner_ref[...] = g_inner
    drain("d_in", d_in_buf, recv_sem, n - 1)
    d_normed = [a + b for a, b in zip(d_second, slabs_of(d_in_buf))]
    d_first, d_gain1, d_shift1 = slab_norm_back(hats1, r1, d_normed, gains1, size)
    d_first_mine = own(d_first)
    d_attn = d_first_mine.astype(BF16)

    part = nt(d_attn, wo[...])
    along = att * part
    lane = lax.broadcasted_iota(jnp.int32, (c, hw), 1) // HEAD
    cols = []
    for j in range(hm):
        cols += split_low(jnp.sum(jnp.where(lane == j, along, 0.0), -1, keepdims=True), 2)
    d_att_buf[me] = with_cols(part.astype(BF16), cols)
    send_all("d_att", lambda pd, pm: d_att_buf.at[me], d_att_buf.at[me], d_att_buf)
    g_out = tn(att_low, d_attn)
    g_out_ref[...] = g_out
    squares = sum(jnp.sum(g * g, 0, keepdims=True) for g in (g_outer, g_inner))
    squares = jnp.sum(squares, -1, keepdims=True) + jnp.sum(jnp.sum(g_out * g_out, 0, keepdims=True), -1, keepdims=True)

    kv_wait(1)
    drain("d_att", d_att_buf, recv_sem, n - 1)
    d_atts = []
    for g in range(nm):
        slab = sum(d_att_buf[k * nm + g].astype(F32) for k in range(nd))
        d_att = slab[:, 0:hw].astype(BF16)
        d_atts.append(d_att)
        col[pl.ds(g * group, group), :] = to_rows(
            [joined(slab, hw + 2 * j, 2) for j in range(hm)]
        )
        wide = expand(d_att)
        for k in range(nd):
            basis[pl.ds(heads + g * group, group), k * width : (k + 1) * width] = nt(wide, projection(1, g, k)).astype(BF16)
    d_att_mine = d_atts[0]
    for g in range(1, nm):
        d_att_mine = jnp.where(m == g, d_atts[g], d_att_mine)
    acc[...] = jnp.zeros_like(acc)

    def backward(t, carry):
        at = pl.ds(pl.multiple_of(t * vt, vt), vt)
        d_probs = nt(basis[pl.ds(heads, heads), :], hid[at, :])
        probs = lows[pl.ds(0, heads), at].astype(F32) * jnp.sum(
            jnp.where(lane_of_tile == t, factors[...], 0.0), -1, keepdims=True
        )
        d_scores = (probs * (d_probs - col[...]) * scale).astype(BF16)
        lows[pl.ds(0, heads), at] = d_scores
        lows[pl.ds(heads, heads), at] = probs.astype(BF16)
        acc[...] += nn(d_scores, hid[at, :])
        return carry
    lax.fori_loop(0, tiles, backward, 0)

    for g in range(nm):
        y = acc[pl.ds(g * group, group), :].astype(BF16)
        dq = jnp.zeros((group, hw), F32)
        for k in range(nd):
            dq = dq + nn(y[:, k * width : (k + 1) * width], projection(0, g, k))
        y_src[g] = y
        dq_src[g] = collapse(dq).astype(BF16)
        send_group("dq", g, dq_src.at[g], dq_buf.at[me], dq_buf)
    dq_buf[me] = dq_src[m]
    y_mp[m] = y_src[m]
    send_mp("y", y_src, y_mp.at[m], y_mp)

    lane_t = 128

    def spread(t, carry):
        at = pl.ds(pl.multiple_of(t * lane_t, lane_t), lane_t)
        stage[at, :] = tn(lows[pl.ds(0, 2 * heads), at], basis[pl.ds(0, 2 * heads), :])
        return carry
    lax.fori_loop(0, rows // lane_t, spread, 0)

    drain("dq", dq_buf, recv_sem, n - 1)
    dq_mine = sum(dq_buf[k].astype(F32) for k in range(n)).astype(BF16)
    d_rows_buf[me] = (nt(dq_mine, wq[...]) + jnp.where(m == 0, d_first_mine, 0.0)).astype(d_rows_buf.dtype)
    send_all("d_rows", lambda pd, pm: d_rows_buf.at[me], d_rows_buf.at[me], d_rows_buf)
    g_q = tn(mine_low, dq_mine)
    drain("z_dp", z_buf, recv_sem, nd - 1)
    z_mine = sum(z_buf[k].astype(F32) for k in range(nd)).astype(BF16)
    g_v = tn(z_mine, expand(d_att_mine))
    drain("y", y_mp, recv_sem, nm - 1)
    y = sum(y_mp[g].astype(F32) for g in range(nm))
    for k in range(nd):
        y_slab[k] = y[:, k * width : (k + 1) * width].astype(BF16)
    y_buf[d] = y_slab[d]
    send_dp_each("y_dp", y_slab, y_buf.at[d], y_buf)
    drain("d_rows", d_rows_buf, recv_sem, n - 1)
    d_rows = jnp.concatenate([s.astype(BF16) for s in slabs_of(d_rows_buf)], axis=1)
    basis[pl.ds(2 * heads, c), :] = d_rows

    def table_back(t, carry):
        d_gain, d_shift, square = carry
        at = pl.ds(pl.multiple_of(t * lane_t, lane_t), lane_t)
        dy = stage[at, :] + tn(lows[pl.ds(hot_at, c), at], basis[pl.ds(2 * heads, c), :])
        x = emb[at, :].astype(F32)
        x = x - jnp.mean(x, -1, keepdims=True)
        r = lax.rsqrt(jnp.mean(x * x, -1, keepdims=True) + eps_norm)
        hat = x * r
        scaled = dy * gain0
        mean = jnp.mean(scaled, -1, keepdims=True)
        along = jnp.mean(scaled * hat, -1, keepdims=True)
        dx = r * (scaled - mean - hat * along)
        stage[at, :] = dx
        fold = lambda v: jnp.sum(v.reshape(lane_t // 8, 8, size), 0)
        return d_gain + fold(dy * hat), d_shift + fold(dy), square + fold(dx * dx)
    zero = jnp.zeros((8, size), F32)
    d_gain, d_shift, square = lax.fori_loop(0, rows // lane_t, table_back, (zero, zero, zero))
    drain("y_dp", y_buf, recv_sem, nd - 1)
    y_mine = sum(y_buf[k].astype(F32) for k in range(nd)).astype(BF16)
    g_k = tn(y_mine, expand(q_mine))
    for i, g in enumerate((g_q, g_k, g_v)):
        g_mixed_ref[i] = g
    total = sum(jnp.sum(g * g, 0, keepdims=True) for g in (g_q, g_k, g_v))
    squares = squares + jnp.sum(total, -1, keepdims=True)
    d_gain, d_shift = jnp.sum(d_gain, 0, keepdims=True), jnp.sum(d_shift, 0, keepdims=True)
    squares = squares + jnp.sum(jnp.sum(square, 0, keepdims=True), -1, keepdims=True)
    chunks = size // 128
    lines = [v[:, k * 128 : (k + 1) * 128] for v in (d_gain, d_shift) for k in range(chunks)]
    lines.append(jnp.broadcast_to(squares, (1, 128)))
    lines.append(jnp.zeros((16 - len(lines), 128), F32))
    sums_buf[me] = jnp.concatenate(lines, axis=0)

    def send_sums(i, carry):
        pd, pm = peer(i)
        remote("sums", sums_buf.at[me], sums_buf.at[me], (e, pd, pm))
        return carry
    lax.fori_loop(1, n, send_sums, 0)
    sent.append(("sums", sums_buf, n - 1, True))
    drain("sums", sums_buf, recv_sem, n - 1, both=True)
    totals = sum(sums_buf[k] for k in range(n))
    firsts = [jnp.concatenate([totals[v * chunks + k : v * chunks + k + 1] for k in range(chunks)], axis=1) for v in range(2)]
    squares = totals[2 * chunks : 2 * chunks + 1, 0:1]
    for i in range(2):
        g_norms_ref[i : i + 1, :] = firsts[i]
        squares = squares + jnp.sum(firsts[i] * firsts[i], -1, keepdims=True)
    for i, slabs in enumerate((d_gain1, d_shift1, d_gain2, d_shift2)):
        for k in range(nd):
            g_norms_ref[2 + i : 3 + i, k * width : (k + 1) * width] = slabs[k]
            squares = squares + jnp.sum(slabs[k] * slabs[k], -1, keepdims=True)
    norm_buf[e] = jnp.broadcast_to(squares, (8, 128))
    norm_at = PHASES.index("norm")
    norm_copy = pltpu.make_async_remote_copy(
        src_ref=norm_buf.at[e], dst_ref=norm_buf.at[e], send_sem=send_sem.at[norm_at], recv_sem=recv_sem.at[norm_at],
        device_id=(1 - e, d, m), device_id_type=MESH,
    )
    norm_copy.start()
    norm_copy.wait_recv()
    started.append(norm_copy.wait_send)
    grad_norm = jnp.sqrt(norm_buf[0] + norm_buf[1])
    small_ref[...] = jnp.where(
        lax.broadcasted_iota(jnp.int32, (8, 128), 0) == 0, jnp.broadcast_to(loss, (8, 128)), grad_norm
    )

    finish()


def kernel_gradients(
    token_ids, query_lengths, negative_mask, positive_index, used_rows, table, w_mixed, w_out, w_inner, w_outer, norm_params, table_m, table_v
):
    nd, nm = lax.axis_size("dp"), lax.axis_size("mp")
    n = nd * nm
    blk = token_ids.shape[1]
    _, rows, size = table.shape
    width, hw, ff = w_mixed.shape[1], w_mixed.shape[3], w_inner.shape[2]
    hm = hw // HEAD
    nb = nd * blk
    c = 2 * nb
    group, heads = hm * c, nm * hm * c
    S = jax.ShapeDtypeStruct
    outs = (
        S((8, 128), F32), S((rows, size), F32), S((3, width, hw), F32),
        S((hw, width), F32), S((width, ff), F32), S((width, ff), F32), S((8, size), F32),
    ) + (S((rows, size), F32),) * 3
    vm, hb = pl.BlockSpec(memory_space=pltpu.VMEM), pl.BlockSpec(memory_space=pltpu.HBM)
    V = pltpu.VMEM
    wide = hw + HEAD
    operands = (
        w_mixed[0].swapaxes(0, 1), token_ids, query_lengths, norm_params.swapaxes(0, 1), w_out[0], w_inner[0], w_outer[0].T,
        positive_index, used_rows, negative_mask.T, table[0], table_m[0], table_v[0],
    )
    local = [V] * 2 + [pltpu.SMEM] + [V] * 4 + [pltpu.SMEM] * 2 + [V]
    scratch = [space(item.shape, item.dtype) for space, item in zip(local, operands)] + [
        V((rows, size), BF16), V((rows, size), BF16),
        V((2 * heads + c, rows), BF16), V((2 * heads + c, size), BF16), V((c, rows), F32), V((nb, 32, 128), F32),
        V((heads, size), F32), V((heads, 1), F32), V((heads, 8), F32), V((heads, 8), F32),
        V((width, hw), BF16), V((hw, width), BF16), V((width, ff), BF16), V((width, ff), BF16), V((2, nm, nd, width // 2, 2 * hw), BF16),
        V((nd, blk, 2 * QSLOT), jnp.int32),
        V((nd, c, width), BF16), V((n, c, width), BF16), V((n, c, hw), BF16),
        V((nm, c, 128), F32), V((nm, c, 128), F32), V((nd, c, wide), BF16),
        V((nm, group, size), BF16), V((nm, group, size), BF16), V((nd, group, width), BF16), V((nd, group, width), BF16),
        V((n, c, wide), BF16), V((nd, c, ff), BF16), V((n, c, width), BF16), V((2, nd, c, width), F32),
        V((nd, c, ff), BF16), V((n, c, width), BF16), V((n, c, wide), BF16), V((nm, c, hw), BF16), V((n, c, hw), BF16),
        V((nm, group, size), BF16), V((nm, group, size), BF16), V((nd, group, width), BF16), V((nd, group, width), BF16),
        V((n, c, width), BF16),
        V((n, 16, 128), F32), V((2, 8, 128), F32),
        pltpu.SemaphoreType.DMA((len(PHASES),)), pltpu.SemaphoreType.DMA((len(PHASES),)),
        pltpu.SemaphoreType.DMA((2,)), pltpu.SemaphoreType.DMA((2, nd)), pltpu.SemaphoreType.DMA((2,)),
        pltpu.SemaphoreType.DMA((rows // 384,)), pltpu.SemaphoreType.DMA((3,)), pltpu.SemaphoreType.DMA((10,)),
    ]
    small, g_table, g_mixed, g_out, g_inner, g_outer, g_norms, *kept = pl.pallas_call(
        partial(grad_kernel, (nd, nm, blk, rows, width, size, hm, ff)),
        out_shape=outs,
        in_specs=[hb] * len(operands),
        out_specs=(vm,) * 10,
        scratch_shapes=scratch,
        compiler_params=pltpu.CompilerParams(collective_id=ENTRY_ID, has_side_effects=True, vmem_limit_bytes=26 << 20),
        name="gradients",
    )(*(pltpu.with_memory_space_constraint(item, pltpu.HBM) for item in operands))
    return small, (g_table, g_mixed, g_out, g_inner, g_outer, g_norms), kept


RING = 3
PIECE = 192


def adam_kernel(rates, count_ref, small_ref, *refs):
    k = len(rates)
    operands = [refs[4 * i : 4 * i + 4] for i in range(k)]
    results = [refs[4 * k + 3 * i : 4 * k + 3 * i + 3] for i in range(k)]
    refs = refs[7 * k :]
    ring, ring_sem, own_sem, buffers = refs[:3], refs[3], refs[4], refs[5:]
    norm = small_ref[1:2, 0:1]
    clip = jnp.minimum(1.0, clip_limit / (norm + 1e-06))
    count = jnp.full((1, 1), count_ref[0], jnp.int32).astype(F32)
    fix_one = 1.0 - jnp.exp(count * math.log(beta_one))
    fix_two = 1.0 - jnp.exp(count * math.log(beta_two))
    inv_one, inv_two = 1.0 / fix_one, 1.0 / fix_two
    copies, in_slot, used, turn = [], [None] * RING, 0, 0

    def update(i, at, targets, to):
        grad, weight, first, second = (ref[at] for ref in operands[i])
        rate, decay = rates[i]
        grad = grad * clip
        first = beta_one * first + (1.0 - beta_one) * grad
        second = beta_two * second + ((1.0 - beta_two) * grad) * grad
        step = first * inv_one / (jnp.sqrt(second * inv_two) + adam_eps)
        if decay:
            step = step + decay * weight
        for ref, value in zip(targets, (weight - rate * step, first, second)):
            ref[to] = value

    def send(src, dst, sem):
        copy = pltpu.make_async_copy(src, dst, sem)
        copy.start()
        return copy

    for i in range(k):
        shape = operands[i][1].shape
        if len(shape) == 2 and shape[1] == ring[0].shape[2]:
            for start in range(0, shape[0], PIECE):
                slot = turn % RING
                turn += 1
                if in_slot[slot]:
                    for copy in in_slot[slot]:
                        copy.wait()

                def block(b, carry):
                    at = pl.ds(pl.multiple_of(b * 32, 32), 32)
                    update(i, pl.ds(pl.multiple_of(start + b * 32, 32), 32), [ref.at[slot] for ref in ring], at)
                    return carry
                lax.fori_loop(0, PIECE // 32, block, 0)
                in_slot[slot] = [
                    send(ring[j].at[slot], results[i][j].at[pl.ds(start, PIECE)], ring_sem.at[slot, j]) for j in range(3)
                ]
            continue
        mine = buffers[3 * used : 3 * used + 3]
        if len(shape) == 3:
            for j in range(shape[0]):
                update(i, j, mine, j)
        else:
            update(i, slice(None), mine, slice(None))
        copies += [send(mine[j], results[i][j], own_sem.at[used, j]) for j in range(3)]
        used += 1
    for group in in_slot + [copies]:
        for copy in group or ():
            copy.wait()


def kernel_adam(step_count, small, grads, weights, firsts, seconds):
    k = len(weights)
    rates = tuple((0.5, 0.0) if i == k - 1 else (0.06, 0.01) for i in range(k))
    vm, sm = pl.BlockSpec(memory_space=pltpu.VMEM), pl.BlockSpec(memory_space=pltpu.SMEM)
    shapes = [jax.ShapeDtypeStruct(w.shape, F32) for w in weights for _ in range(3)]
    operands = [item for group in zip(grads, weights, firsts, seconds) for item in group]
    size = weights[0].shape[1]
    alone = [item for item in shapes if len(item.shape) == 3 or item.shape[1] != size]
    return pl.pallas_call(
        partial(adam_kernel, rates),
        out_shape=shapes,
        in_specs=[sm, vm] + [vm] * (4 * k),
        out_specs=[pl.BlockSpec(memory_space=pltpu.HBM)] * (3 * k),
        scratch_shapes=[pltpu.VMEM((RING, PIECE, size), F32)] * 3
        + [pltpu.SemaphoreType.DMA((RING, 3)), pltpu.SemaphoreType.DMA((len(alone) // 3, 3))]
        + [pltpu.VMEM(item.shape, F32) for item in alone],
        compiler_params=pltpu.CompilerParams(vmem_limit_bytes=12 << 20),
        name="adam",
    )(step_count, small, *operands)


def on_device(
    token_ids,
    query_lengths,
    negative_mask,
    positive_index,
    used_rows,
    step_count,
    table,
    w_mixed,
    w_out,
    w_inner,
    w_outer,
    norm_params,
    table_m,
    table_v,
    mixed_m,
    mixed_v,
    out_m,
    out_v,
    inner_m,
    inner_v,
    outer_m,
    outer_v,
    norms_m,
    norms_v,
):
    operands = (
        token_ids, query_lengths, negative_mask, positive_index, used_rows, table, w_mixed, w_out, w_inner, w_outer, norm_params
    )
    masters = (table, w_mixed, w_out, w_inner, w_outer, norm_params)
    firsts = (table_m, mixed_m, out_m, inner_m, outer_m, norms_m)
    seconds = (table_v, mixed_v, out_v, inner_v, outer_v, norms_v)
    if table.shape[1] % 384 == 0 and w_mixed.shape[1] % 64 == 0 and table.shape[1] <= 2048:
        small, grads, kept = kernel_gradients(*operands, table_m, table_v)

        def stored(tab, items):
            _, mixed, out, inner, outer, norm = items
            return tab, mixed[0].swapaxes(0, 1), out[0], inner[0], outer[0].T, norm.swapaxes(0, 1)

        grads = grads[:5] + (grads[5][0:6, None, :],)
        updated = kernel_adam(step_count, small, grads, *map(stored, kept, (masters, firsts, seconds)))
        back = (
            lambda x: x[None],
            lambda x: x.swapaxes(0, 1)[None],
            lambda x: x[None],
            lambda x: x[None],
            lambda x: x.T[None],
            lambda x: x.swapaxes(0, 1),
        )
        return (small[0, 0], small[1, 0]) + tuple(back[i // 3](item) for i, item in enumerate(updated))
    loss, grads = gradients(*operands)
    owner = (lax.axis_index("dp") == 0) & (lax.axis_index("mp") == 0)
    squares = jnp.where(owner, jnp.sum(grads[5] * grads[5]), 0.0)
    for grad in grads[:5]:
        squares = squares + jnp.sum(grad * grad)
    grad_norm = jnp.sqrt(lax.psum(squares, ("enc", "dp", "mp")))
    clip = jnp.minimum(1.0, clip_limit / (grad_norm + 1e-06))
    count = step_count[0].astype(F32)
    results = [loss, grad_norm]
    for index in range(6):
        rate, decay = (0.5, 0.0) if index == 5 else (0.06, 0.01)
        results.extend(
            adam_step(
                masters[index], grads[index][None] * clip, firsts[index], seconds[index], rate, decay, count
            )
        )
    return tuple(results)


def solution(mesh):
    table = P("enc", ("dp", "mp"), None)
    mixed = P("enc", "dp", None, "mp")
    columns = P("enc", "mp", "dp")
    units = P("enc", "dp", "mp")
    norms = P("enc", None, None)
    matrices = (table, mixed, columns, units, columns, norms)
    moments = tuple(spec for spec in matrices for _ in range(2))
    updated = tuple(spec for spec in matrices for _ in range(3))
    return jax.shard_map(
        on_device,
        mesh=mesh,
        in_specs=(P("enc", "dp", None), P("dp"), P(), P(), P(), P()) + matrices + moments,
        out_specs=(P(), P()) + updated,
        check_vma=False,
    )
```

```python
import math
from functools import partial

import jax
import jax.numpy as jnp
from jax import lax
from jax.experimental import pallas as pl
from jax.experimental.pallas import tpu as pltpu
from jax.sharding import PartitionSpec as P

HEAD = 64
QSLOT = 128
F32 = jnp.float32
BF16 = jnp.bfloat16

exact_arithmetic_level = lax.Precision.HIGHEST
eps_norm = 1e-06
logit_divisor = 0.05
clip_limit = 0.02
beta_one = 0.9
beta_two = 0.999
adam_eps = 1e-08


def layer_norm(x, gain, shift):
    centred = x - jnp.mean(x, -1, keepdims=True)
    spread = jnp.mean(centred * centred, -1, keepdims=True)
    return centred * lax.rsqrt(spread + eps_norm) * gain + shift


def mul(spec, a, b):
    return jnp.einsum(spec, a, b, preferred_element_type=F32)


def token_counts(ids, lens, is_query, base, rows):
    pos = jnp.arange(ids.shape[1])
    slot = pos // QSLOT
    limit = jnp.where(slot[None, :] == 0, lens[:, 0:1], lens[:, 1:2])
    within = (pos % QSLOT)[None, :] < limit
    same = slot[None, :] == jnp.arange(2)[:, None]
    allowed = jnp.where(is_query, same[:, None, :] & within[None], True)
    local = ids - base
    n_hi = -(-rows // 128)
    high = (local[..., None] >> 7) == jnp.arange(n_hi)
    low = (local[..., None] & 127) == jnp.arange(128)
    left = (allowed[..., None] & high[None]).astype(BF16)
    counts = mul("sbth,btl->sbhl", left, low.astype(BF16))
    return counts.reshape(2 * ids.shape[0], n_hi * 128)[:, :rows]


def contrast(queries, passages, negative_mask, positive_index, used_rows):
    question_direction_rows = queries * lax.rsqrt(
        jnp.sum(queries * queries, -1, keepdims=True) + eps_norm
    )
    document_direction_rows = passages * lax.rsqrt(
        jnp.sum(passages * passages, -1, keepdims=True) + eps_norm
    )
    pairwise_cosine_table = (
        jnp.dot(
            question_direction_rows, document_direction_rows.T, precision=exact_arithmetic_level
        )
        / logit_divisor
    )
    is_positive = jnp.arange(passages.shape[0])[None, :] == positive_index[:, None]
    excluded = (negative_mask == 1) & ~is_positive
    pairwise_cosine_table = jnp.where(excluded, -1e30, pairwise_cosine_table)
    top = jnp.max(pairwise_cosine_table, -1, keepdims=True)
    log_total = top[:, 0] + jnp.log(jnp.sum(jnp.exp(pairwise_cosine_table - top), -1))
    target = jnp.sum(jnp.where(is_positive, pairwise_cosine_table, 0.0), -1)
    weight = used_rows.astype(F32)
    return jnp.sum(weight * (log_total - target)) / jnp.maximum(jnp.sum(weight), 1.0)


def adam_step(weight, grad, first, second, rate, decay, count):
    first_new = beta_one * first + (1.0 - beta_one) * grad
    second_new = beta_two * second + (1.0 - beta_two) * grad * grad
    fix_one = 1.0 - jnp.power(beta_one, count)
    correction_second = 1.0 - jnp.power(beta_two, count)
    update = (
        first_new / fix_one / (jnp.sqrt(second_new / correction_second) + adam_eps) + decay * weight
    )
    return (weight - rate * update, first_new, second_new)


def slot_major(x):
    return x.reshape((x.shape[0] // 2, 2) + x.shape[1:]).swapaxes(0, 1).reshape(x.shape)


def gradients(
    token_ids, query_lengths, negative_mask, positive_index, used_rows, table, w_mixed, w_out, w_inner, w_outer, norm_params
):
    is_query = lax.axis_index("enc") == 0
    d, m = lax.axis_index("dp"), lax.axis_index("mp")
    n_mp = lax.axis_size("mp")
    rows, width = table.shape[1], w_mixed.shape[1]
    hm = w_out.shape[1] // HEAD
    scale = HEAD ** (-0.5)
    norms = norm_params[0]
    base = (d * n_mp + m) * rows

    ids = lax.all_gather(token_ids[0], "dp", axis=0, tiled=True)
    lens = lax.all_gather(query_lengths, "dp", axis=0, tiled=True).reshape(-1, 2)
    blocks = ids.shape[0]
    counts = token_counts(ids, lens, is_query, base, rows)
    cls_ids = jnp.concatenate([ids[:, 0], ids[:, QSLOT]]) - base
    cls_hot = cls_ids[:, None] == jnp.arange(rows)[None, :]

    def mine(x):
        return lax.dynamic_slice_in_dim(x, d * width, width, 1)

    wq, wk, wv = (w_mixed[0, :, i].astype(BF16).reshape(width, hm, HEAD) for i in range(3))
    wo = w_out[0].astype(BF16).reshape(hm, HEAD, width)
    wi, wt = w_inner[0].astype(BF16), w_outer[0].astype(BF16)

    embedded = lax.reduce_precision(table[0], 8, 7)
    hidden, hidden_back = jax.vjp(layer_norm, embedded, norms[0], norms[1])
    hid = hidden.astype(BF16)
    first_rows = lax.psum(
        jnp.dot(cls_hot.astype(F32), hidden, precision=exact_arithmetic_level), ("dp", "mp")
    )
    first_mine = mine(first_rows).astype(BF16)
    q = lax.psum(mul("ci,ihk->hck", first_mine, wq), "dp").astype(BF16)
    u = mul("hck,ihk->hci", q, wk).astype(BF16)
    u = lax.all_gather(lax.all_gather(u, "dp", axis=2, tiled=True), "mp", axis=0, tiled=True)
    scores = jnp.where(counts[None] > 0, mul("hci,vi->hcv", u, hid) * scale, -1e30)
    top = lax.pmax(jnp.max(scores, -1, keepdims=True), ("dp", "mp"))
    weight = counts[None] * jnp.exp(scores - top)
    probs = weight / lax.psum(jnp.sum(weight, -1, keepdims=True), ("dp", "mp"))
    probs_low = probs.astype(BF16)
    z = mul("hcv,vi->hci", probs_low, hid)
    z = lax.psum_scatter(z, "mp", scatter_dimension=0, tiled=True)
    z = lax.psum_scatter(z, "dp", scatter_dimension=2, tiled=True).astype(BF16)
    att = lax.psum(mul("hci,ihk->hck", z, wv), "dp")
    att_low = att.astype(BF16)
    out = lax.psum(mul("hck,hke->ce", att_low, wo), "mp")
    first_sum = first_rows + lax.all_gather(out, "dp", axis=1, tiled=True)
    normed, normed_back = jax.vjp(layer_norm, first_sum, norms[2], norms[3])
    normed_mine = mine(normed).astype(BF16)
    inner = lax.psum(mul("ci,if->cf", normed_mine, wi), "dp")
    act, act_back = jax.vjp(partial(jax.nn.gelu, approximate=False), inner)
    act = act.astype(BF16)
    outer = lax.psum(mul("cf,fe->ce", act, wt), "mp")
    second_sum = normed + lax.all_gather(outer, "dp", axis=1, tiled=True)
    final, final_back = jax.vjp(layer_norm, second_sum, norms[4], norms[5])
    both = lax.all_gather(final, "enc", axis=0)
    loss, loss_back = jax.vjp(
        partial(
            contrast,
            negative_mask=slot_major(negative_mask),
            positive_index=slot_major(positive_index),
            used_rows=slot_major(used_rows),
        ),
        both[0],
        both[1, :blocks],
    )
    d_queries, d_passages = loss_back(jnp.ones((), F32))
    d_passages = jnp.concatenate([d_passages, jnp.zeros_like(d_passages)])
    d_final = jnp.where(is_query, d_queries, d_passages)

    d_second, d_gain2, d_shift2 = final_back(d_final)
    d_outer = mine(d_second).astype(BF16)
    g_outer = mul("cf,ce->fe", act, d_outer)
    d_act = lax.psum(mul("ce,fe->cf", d_outer, wt), "dp")
    d_inner = act_back(d_act)[0].astype(BF16)
    g_inner = mul("ci,cf->if", normed_mine, d_inner)
    d_in = lax.psum(mul("cf,if->ci", d_inner, wi), "mp")
    d_normed = d_second + lax.all_gather(d_in, "dp", axis=1, tiled=True)
    d_first, d_gain1, d_shift1 = normed_back(d_normed)
    d_attn = mine(d_first).astype(BF16)
    g_out = mul("hck,ce->hke", att_low, d_attn).reshape(w_out.shape[1:])
    d_att = lax.psum(mul("ce,hke->hck", d_attn, wo), "dp").astype(BF16)
    w = mul("hck,ihk->hci", d_att, wv).astype(BF16)
    mean_d = jnp.sum(att * d_att.astype(F32), -1, keepdims=True)
    w = lax.all_gather(lax.all_gather(w, "dp", axis=2, tiled=True), "mp", axis=0, tiled=True)
    mean_d = lax.all_gather(mean_d, "mp", axis=0, tiled=True)
    d_probs = mul("hci,vi->hcv", w, hid)
    d_scores = (probs * (d_probs - mean_d)).astype(BF16)
    y = mul("hcv,vi->hci", d_scores, hid)
    y = lax.psum_scatter(y, "mp", scatter_dimension=0, tiled=True)
    y = lax.psum_scatter(y, "dp", scatter_dimension=2, tiled=True).astype(BF16)
    dq = (lax.psum(mul("hci,ihk->hck", y, wk), "dp") * scale).astype(BF16)
    g_q = mul("ci,hck->ihk", first_mine, dq)
    g_k = mul("hci,hck->ihk", y, q) * scale
    g_v = mul("hci,hck->ihk", z, d_att)
    g_mixed = jnp.stack([g_q, g_k, g_v], 1).reshape(w_mixed.shape[1:])
    d_rows = lax.psum(mul("hck,ihk->ci", dq, wq), "mp")
    d_rows = (d_first + lax.all_gather(d_rows, "dp", axis=1, tiled=True)).astype(BF16)
    d_hidden = (
        mul("hcv,hci->vi", d_scores, u) * scale
        + mul("hcv,hci->vi", probs_low, w)
        + mul("cv,ci->vi", cls_hot.astype(BF16), d_rows)
    )
    g_table, d_gain0, d_shift0 = hidden_back(d_hidden)
    sums = lax.psum(jnp.stack([d_gain0, d_shift0]), ("dp", "mp"))
    g_norms = jnp.concatenate([sums, jnp.stack([d_gain1, d_shift1, d_gain2, d_shift2])])
    return loss, (g_table, g_mixed, g_out, g_inner, g_outer, g_norms)


MESH = pl.DeviceIdType.MESH
ENTRY_ID = 3
PHASES = (
    "ids", "rows", "q", "stat", "att", "z", "z_dp", "out", "inner", "outer", "final",
    "d_act", "d_in", "d_att", "dq", "y", "y_dp", "d_rows", "sums", "norm",
)
BLOCK = 64
UNROLL = True


def nt(a, b):
    return lax.dot_general(a, b, (((1,), (1,)), ((), ())), preferred_element_type=F32)


def tn(a, b):
    return lax.dot_general(a, b, (((0,), (0,)), ((), ())), preferred_element_type=F32)


def nn(a, b):
    return jnp.dot(a, b, preferred_element_type=F32)


def exact_nt(a, b):
    return lax.dot_general(
        a, b, (((1,), (1,)), ((), ())), precision=exact_arithmetic_level, preferred_element_type=F32
    )


def exact_nn(a, b):
    return jnp.dot(a, b, precision=exact_arithmetic_level, preferred_element_type=F32)


def slab_norm(slabs, size):
    mean = sum(jnp.sum(s, -1, keepdims=True) for s in slabs) * (1.0 / size)
    slabs = [s - mean for s in slabs]
    spread = sum(jnp.sum(s * s, -1, keepdims=True) for s in slabs) * (1.0 / size)
    r = lax.rsqrt(spread + eps_norm)
    return [s * r for s in slabs], r


def slab_norm_back(hats, r, grads, gains, size):
    scaled = [dy * g for dy, g in zip(grads, gains)]
    mean = sum(jnp.sum(s, -1, keepdims=True) for s in scaled) * (1.0 / size)
    along = sum(jnp.sum(s * h, -1, keepdims=True) for s, h in zip(scaled, hats)) * (1.0 / size)
    d_in = [r * (s - mean - h * along) for s, h in zip(scaled, hats)]
    d_gain = [jnp.sum(dy * h, 0, keepdims=True) for dy, h in zip(grads, hats)]
    d_shift = [jnp.sum(dy, 0, keepdims=True) for dy in grads]
    return d_in, d_gain, d_shift


def joined(x, at, parts):
    return sum(x[:, at + i : at + i + 1] for i in range(parts))


def split_low(x, parts):
    out = []
    for _ in range(parts):
        piece = x.astype(BF16)
        out.append(piece)
        x = x - piece.astype(F32)
    return out


def grad_kernel(cfg, *refs):
    nd, nm, blk, rows, width, size, hm, ff = cfg
    n = nd * nm
    nb = nd * blk
    c = 2 * nb
    hw = hm * HEAD
    group = hm * c
    half = hm * nb
    heads = nm * group
    vt = 384
    tiles = rows // vt
    scale = HEAD ** (-0.5)
    (
        *early_hbm, table_hbm, first_hbm, second_hbm,
        small_ref, stage, g_mixed_ref, g_out_ref, g_inner_ref, g_outer_ref, g_norms_ref, table_keep, first_keep, second_keep,
        mixed_f, ids_ref, lens_ref, norms_ref, out_f, inner_f, outer_f, positive_ref, used_ref, negative_ref,
        emb, hid, lows, basis, counts, xs, acc, col, tops, factors, found_at,
        wq, wo, wi, wt, kv,
        ids_buf, rows_src, rows_buf, q_buf, stat_src, stat_buf, att_buf, z_src, z_mp, z_slab, z_buf, out_buf, inner_buf, outer_buf,
        final_buf, d_act_buf, d_in_buf, d_att_buf, dq_src, dq_buf, y_src, y_mp, y_slab, y_buf, d_rows_buf, sums_buf, norm_buf,
        send_sem, recv_sem, kv_send, kv_recv, kv_spread, table_sem, keep_sem, early_sem,
    ) = refs
    e, d, m = lax.axis_index("enc"), lax.axis_index("dp"), lax.axis_index("mp")
    me = d * nm + m
    is_query = e == 0
    base = me * rows

    sent, received = [], []

    def halves(go, full):
        pl.when(is_query)(lambda: go(full))
        pl.when(jnp.logical_not(is_query))(lambda: go(full // 2))

    def peer(i):
        p = lax.rem(me + i, n)
        return p // nm, lax.rem(p, nm)

    def remote(name, src, dst, where):
        k = PHASES.index(name)
        pltpu.make_async_remote_copy(
            src_ref=src, dst_ref=dst, send_sem=send_sem.at[k], recv_sem=recv_sem.at[k],
            device_id=where, device_id_type=MESH,
        ).start()

    def send_all(name, src_of, dst, buf):
        sent.append((name, buf, n - 1, False))

        def go(r):
            def one(i, carry):
                pd, pm = peer(i)
                remote(name, src_of(pd, pm).at[pl.ds(0, r)], dst.at[pl.ds(0, r)], (e, pd, pm))
                return carry
            lax.fori_loop(1, n, one, 0)
        halves(go, dst.shape[0])

    def send_group(name, group_of, src, dst, buf):
        if group_of == 0:
            sent.append((name, buf, n - 1, False))

        def go(r):
            for pd in range(nd):
                @pl.when(jnp.logical_or(pd != d, group_of != m))
                def _():
                    remote(name, src.at[pl.ds(0, r)], dst.at[pl.ds(0, r)], (e, pd, group_of))
        halves(go, dst.shape[0])

    def send_dp(name, src, dst, buf, both=False):
        sent.append((name, buf, nd - 1, both))

        def go(r):
            for i in range(1, nd):
                remote(name, src.at[pl.ds(0, r)], dst.at[pl.ds(0, r)], (e, lax.rem(d + i, nd), m))
        if both:
            go(dst.shape[0])
        else:
            halves(go, dst.shape[0])

    def send_mp(name, source, dst, buf):
        sent.append((name, buf, nm - 1, False))

        def go(r):
            for i in range(1, nm):
                g = lax.rem(m + i, nm)
                remote(name, source.at[g, pl.ds(0, r)], dst.at[pl.ds(0, r)], (e, d, g))
        halves(go, dst.shape[0])

    def send_dp_each(name, source, dst, buf):
        sent.append((name, buf, nd - 1, False))

        def go(r):
            for i in range(1, nd):
                k = lax.rem(d + i, nd)
                remote(name, source.at[k, pl.ds(0, r)], dst.at[pl.ds(0, r)], (e, k, m))
        halves(go, dst.shape[0])

    def drain(name, buf, sem, count, both=False):
        k = PHASES.index(name)
        if sem is recv_sem:
            received.append(name)

        def go(r):
            view = buf.at[pl.ds(0, count), pl.ds(0, r)]
            pltpu.make_async_copy(view, view, sem.at[k]).wait()
        if both:
            go(buf.shape[1])
        else:
            halves(go, buf.shape[1])

    def finish():
        for name, buf, count, both in sent:
            drain(name, buf, send_sem, count, both)
            if name not in received:
                drain(name, buf, recv_sem, count, both)
        for item in started:
            item()

    started = []

    early = (mixed_f, ids_ref, lens_ref, norms_ref, out_f, inner_f, outer_f, positive_ref, used_ref, negative_ref)
    early = [pltpu.make_async_copy(src, dst, early_sem.at[i]) for i, (src, dst) in enumerate(zip(early_hbm, early))]
    table_loads = [
        pltpu.make_async_copy(table_hbm.at[pl.ds(i * vt, vt)], stage.at[pl.ds(i * vt, vt)], table_sem.at[i])
        for i in range(tiles)
    ]
    for item in early[:4]:
        item.start()
    for item in table_loads:
        item.start()
    for item in early[4:]:
        item.start()

    @pl.when(jnp.logical_not(is_query))
    def _():
        for buf in (
            rows_buf, q_buf, stat_buf, att_buf, z_mp, z_buf, out_buf, inner_buf, outer_buf, d_act_buf, d_in_buf, d_att_buf, dq_buf,
            y_mp, y_buf, d_rows_buf,
        ):
            r = buf.shape[1] // 2
            for k in range(buf.shape[0]):
                buf[k, r:, :] = jnp.zeros((r, buf.shape[2]), buf.dtype)

    barrier = pltpu.get_barrier_semaphore()

    def greet(i, carry):
        pd, pm = peer(i)
        pl.semaphore_signal(barrier, inc=1, device_id=(e, pd, pm), device_id_type=MESH)
        return carry
    lax.fori_loop(1, n, greet, 0)
    pl.semaphore_signal(barrier, inc=1, device_id=(1 - e, d, m), device_id_type=MESH)
    pl.semaphore_wait(barrier, n)

    early[1].wait()
    early[2].wait()
    row_i = lax.broadcasted_iota(jnp.int32, (blk, 2 * QSLOT), 0)
    lane_i = lax.broadcasted_iota(jnp.int32, (blk, 2 * QSLOT), 1)
    limit = jnp.zeros((blk, 2 * QSLOT), jnp.int32)
    for b in range(blk):
        here = jnp.where(lane_i < QSLOT, lens_ref[2 * b], lens_ref[2 * b + 1])
        limit = jnp.where(row_i == b, here, limit)
    limit = jnp.where(is_query, limit, QSLOT)
    ids_buf[d] = jnp.where((lane_i & (QSLOT - 1)) >= limit, -1, ids_ref[0])
    send_dp("ids", ids_buf.at[d], ids_buf.at[d], ids_buf, both=True)

    early[0].wait()
    fold = width // 2
    for i in range(2):
        kv[i, m, d, :, 0:hw] = mixed_f[1 + i, 0:fold].astype(BF16)
        kv[i, m, d, :, hw:] = mixed_f[1 + i, fold:].astype(BF16)

    def kv_copy(i, src, sem, where):
        piece = kv.at[i, m, src]
        return pltpu.make_async_remote_copy(
            src_ref=piece, dst_ref=piece, send_sem=kv_send.at[i], recv_sem=sem, device_id=where, device_id_type=MESH
        )

    def partner(k):
        if nd != 4:
            return lax.rem(d + k, nd)
        return (d + 1 - 2 * lax.rem(d, 2), d + 2 - 4 * (d // 2), 3 - d)[k - 1]

    def kv_to_dp(i):
        for k in range(1, nd):
            kv_copy(i, d, kv_recv.at[i, d], (e, lax.rem(d + k, nd), m)).start()

    def kv_to_mp(i, src):
        for k in range(1, nm):
            kv_copy(i, src, kv_spread.at[i], (e, d, lax.rem(m + k, nm))).start()

    def kv_from_dp(i, k):
        src = partner(k)
        pltpu.make_async_copy(kv.at[i, m, src], kv.at[i, m, src], kv_recv.at[i, src]).wait()
        return src

    def kv_wait(i):
        view = kv.at[i, pl.ds(0, nm - 1)]
        pltpu.make_async_copy(view, view, kv_spread.at[i]).wait()

    def kv_left():
        for i in range(2):
            view = kv.at[i, pl.ds(0, nm - 1)]
            pltpu.make_async_copy(view, view, kv_send.at[i]).wait()
            view = kv.at[i, 0, pl.ds(0, nd - 1)]
            pltpu.make_async_copy(view, view, kv_send.at[i]).wait()
    started.append(kv_left)

    def projection(i, g, k):
        both = kv[i, g, k]
        return jnp.concatenate([both[:, 0:hw], both[:, hw:]], axis=0)

    kv_to_dp(0)
    kv_to_mp(0, d)
    wq[...] = mixed_f[0].astype(BF16)

    early[3].wait()
    gain0, shift0 = norms_ref[0], norms_ref[1]
    for t in range(tiles):
        table_loads[t].wait()

        def to_low(i, carry):
            at = pl.ds(pl.multiple_of(t * vt + i * BLOCK, BLOCK), BLOCK)
            emb[at, :] = stage[at, :].astype(BF16)
            return carry
        lax.fori_loop(0, vt // BLOCK, to_low, 0)

    drain("ids", ids_buf, recv_sem, nd - 1, both=True)
    ids_all = jnp.concatenate([ids_buf[k] for k in range(nd)], axis=0) - base
    cls = jnp.concatenate([ids_all[:, 0:1], ids_all[:, QSLOT : QSLOT + 1]], axis=0)
    hot_at = 2 * heads
    lows[pl.ds(hot_at, c), :] = (cls == lax.broadcasted_iota(jnp.int32, (c, rows), 1)).astype(BF16)

    def pick(t, total):
        at = pl.ds(pl.multiple_of(t * vt, vt), vt)
        return total + nn(lows[pl.ds(hot_at, c), at], emb[at, :])
    found = lax.fori_loop(0, tiles, pick, jnp.zeros((c, size), F32))
    found_hat, found_r = slab_norm([found], size)
    found_at[...] = found_hat[0]
    owned = jnp.logical_and(cls >= 0, cls < rows)
    found = jnp.where(owned, found_hat[0] * gain0 + shift0, 0.0).astype(BF16)
    for k in range(nd):
        rows_src[k] = found[:, k * width : (k + 1) * width]
    rows_buf[me] = rows_src[d]
    send_all("rows", lambda pd, pm: rows_src.at[pd], rows_buf.at[me], rows_buf)

    for k in range(1, nd):
        kv_to_mp(0, kv_from_dp(0, k))
    flag = jnp.where(is_query, 1, 0)
    for b in range(nb):
        row = ids_all[b : b + 1, :]
        high, low = row >> 7, row & 127
        lane_b = lax.broadcasted_iota(jnp.int32, (16, 2 * QSLOT), 1)
        is_high = lax.broadcasted_iota(jnp.int32, (16, 2 * QSLOT), 0) == high
        left = [jnp.logical_and(is_high, (lane_b >> 7) * flag == s * flag) for s in range(2)]
        left = jnp.concatenate([item.astype(BF16) for item in left], axis=0)
        right = (lax.broadcasted_iota(jnp.int32, (128, 2 * QSLOT), 0) == low).astype(BF16)
        xs[b] = nt(left, right)
    for t in range(rows // 128):
        for s in range(2):
            counts[s * nb : (s + 1) * nb, t * 128 : (t + 1) * 128] = xs[:, s * 16 + t, :]

    kv_to_dp(1)

    def normalize(i, carry):
        at = pl.ds(pl.multiple_of(i * BLOCK, BLOCK), BLOCK)
        x = emb[at, :].astype(F32)
        x = x - jnp.mean(x, -1, keepdims=True)
        r = lax.rsqrt(jnp.mean(x * x, -1, keepdims=True) + eps_norm)
        hid[at, :] = (x * r * gain0 + shift0).astype(BF16)
        return carry
    lax.fori_loop(0, rows // BLOCK, normalize, 0)
    for i, (src, dst) in enumerate(((table_hbm, table_keep), (first_hbm, first_keep), (second_hbm, second_keep))):
        keep = pltpu.make_async_copy(src, dst, keep_sem.at[i])
        keep.start()
        started.append(keep.wait)
    for item in early[4:]:
        item.wait()
    wo[...] = out_f[...].astype(BF16)
    wi[...] = inner_f[...].astype(BF16)
    wt[...] = outer_f[...].astype(BF16)

    drain("rows", rows_buf, recv_sem, n - 1)
    mine = sum(rows_buf[k].astype(F32) for k in range(n))
    mine_low = mine.astype(BF16)
    q_buf[me] = nn(mine_low, wq[...]).astype(BF16)
    send_all("q", lambda pd, pm: q_buf.at[me], q_buf.at[me], q_buf)

    lane_h = lax.broadcasted_iota(jnp.int32, (nb, hw), 1) // HEAD

    def expand(x):
        return jnp.concatenate(
            [
                jnp.where(lane_h == j, x[s * nb : (s + 1) * nb], jnp.zeros((), x.dtype))
                for s in range(2)
                for j in range(hm)
            ],
            axis=0,
        )

    def collapse(x):
        out = []
        for s in range(2):
            parts = [x[s * half + j * nb : s * half + (j + 1) * nb] for j in range(hm)]
            total = parts[0]
            for j in range(1, hm):
                total = jnp.where(lane_h == j, parts[j], total)
            out.append(total)
        return jnp.concatenate(out, axis=0)

    def to_rows(cols):
        return jnp.concatenate([cols[j][s * nb : (s + 1) * nb] for s in range(2) for j in range(hm)], axis=0)

    def to_cols(x):
        return [
            jnp.concatenate([x[s * half + j * nb : s * half + (j + 1) * nb] for s in range(2)], axis=0)
            for j in range(hm)
        ]

    def over_heads(cols):
        lane = lax.broadcasted_iota(jnp.int32, (c, hw), 1) // HEAD
        out = jnp.broadcast_to(cols[0], (c, hw))
        for j in range(1, hm):
            out = jnp.where(lane == j, cols[j], out)
        return out

    def with_cols(x, cols):
        tail = lax.broadcasted_iota(jnp.int32, (c, HEAD), 1)
        extra = jnp.zeros((c, HEAD), F32)
        for k, item in enumerate(cols):
            extra = jnp.where(tail == k, item.astype(F32), extra)
        return jnp.concatenate([x, extra.astype(x.dtype)], axis=1)

    blank = jnp.zeros((c, hw), BF16)
    drain("q", q_buf, recv_sem, n - 1)
    kv_wait(0)
    queries = []
    for g in range(nm):
        q = sum(q_buf[k * nm + g].astype(F32) for k in range(nd)).astype(BF16)
        queries.append(q)
        wide = expand(q)
        for k in range(nd):
            basis[pl.ds(g * group, group), k * width : (k + 1) * width] = nt(wide, projection(0, g, k)).astype(BF16)
    q_mine = queries[0]
    for g in range(1, nm):
        q_mine = jnp.where(m == g, queries[g], q_mine)

    acc[...] = jnp.zeros_like(acc)
    tops[...] = jnp.zeros_like(tops)
    lane_of_tile = lax.broadcasted_iota(jnp.int32, (heads, 8), 1)

    def weigh(t, carry):
        top, total = carry
        at = pl.ds(pl.multiple_of(t * vt, vt), vt)
        s = nt(basis[pl.ds(0, heads), :], hid[at, :]) * scale
        places = [
            (g * group + sl * half + j * nb, pl.ds(sl * nb, nb)) for g in range(nm) for sl in range(2) for j in range(hm)
        ]
        s = [jnp.where(counts[of, at] > 0, s[lo : lo + nb], -1e30) for lo, of in places]
        best = [jnp.maximum(top[lo : lo + nb], jnp.max(x, -1, keepdims=True)) for x, (lo, of) in zip(s, places)]
        sums = []
        for x, high, (lo, of) in zip(s, best, places):
            x = counts[of, at] * jnp.exp(x - high)
            lows[lo : lo + nb, at] = x.astype(BF16)
            sums.append(jnp.sum(x, -1, keepdims=True))
        best = jnp.concatenate(best, axis=0)
        keep = jnp.exp(top - best)
        acc[...] = acc[...] * keep + nn(lows[pl.ds(0, heads), at], hid[at, :])
        tops[...] = jnp.where(lane_of_tile == t, best, tops[...])
        return best, total * keep + jnp.concatenate(sums, axis=0)
    top, total = lax.fori_loop(
        0, tiles, weigh, (jnp.full((heads, 1), -1e30, F32), jnp.zeros((heads, 1), F32)), unroll=UNROLL
    )

    def stat_slab(cols):
        lane = lax.broadcasted_iota(jnp.int32, (c, 128), 1)
        out = jnp.zeros((c, 128), F32)
        for k, item in enumerate(cols):
            out = jnp.where(lane == k, item, out)
        return out

    for g in range(nm):
        at = slice(g * group, (g + 1) * group)
        z_src[g] = acc[at, :].astype(BF16)
        stat_src[g] = stat_slab(to_cols(top[at]) + to_cols(total[at]))
    stat_buf[m] = stat_src[m]
    z_mp[m] = z_src[m]
    send_mp("stat", stat_src, stat_buf.at[m], stat_buf)
    send_mp("z", z_src, z_mp.at[m], z_mp)

    def combine(peaks, sums):
        best = peaks[0]
        for item in peaks[1:]:
            best = jnp.maximum(best, item)
        factor = [jnp.exp(item - best) for item in peaks]
        return best, factor, sum(f * item for f, item in zip(factor, sums))

    drain("stat", stat_buf, recv_sem, nm - 1)
    stats = [stat_buf[g] for g in range(nm)]
    near = [combine([x[:, j : j + 1] for x in stats], [x[:, hm + j : hm + j + 1] for x in stats]) for j in range(hm)]
    scales = [to_rows([near[j][1][g] for j in range(hm)]) for g in range(nm)]
    for k in range(1, nd):
        kv_from_dp(1, k)
    drain("z", z_mp, recv_sem, nm - 1)
    z_near = sum(z_mp[g].astype(F32) * scales[g] for g in range(nm))
    att = 0.0
    for k in range(nd):
        att = att + nn(z_near[:, k * width : (k + 1) * width].astype(BF16), projection(1, m, k))
    cols = [piece for j in range(hm) for piece in split_low(near[j][0], 3)]
    cols += [piece for j in range(hm) for piece in split_low(near[j][2], 2)]
    att_buf[d] = with_cols(collapse(att).astype(BF16), cols)
    send_dp("att", att_buf.at[d], att_buf.at[d], att_buf)

    drain("att", att_buf, recv_sem, nd - 1)
    far = []
    slabs = [att_buf[k, :, hw:].astype(F32) for k in range(nd)]
    for j in range(hm):
        far.append(combine([joined(x, 3 * j, 3) for x in slabs], [joined(x, 3 * hm + 2 * j, 2) for x in slabs]))
    top_all = [item[0] for item in far]
    inv_all = [jnp.where(x > 0, 1.0 / jnp.where(x > 0, x, 1.0), 0.0) for _, _, x in far]
    parts = [[f * inv for f in item[1]] for item, inv in zip(far, inv_all)]
    att = sum(att_buf[k, :, 0:hw].astype(F32) * over_heads([parts[j][k] for j in range(hm)]) for k in range(nd))
    att_low = att.astype(BF16)
    part = nn(att_low, wo[...]) + jnp.where(m == 0, mine, 0.0)
    cols = [piece for item in top_all for piece in split_low(item, 3)]
    cols += [piece for item in inv_all for piece in split_low(item, 2)]
    out_buf[me] = with_cols(part.astype(BF16), cols)
    send_all("out", lambda pd, pm: out_buf.at[me], out_buf.at[me], out_buf)

    def slabs_of(buf):
        return [sum(buf[k * nm + g, :, 0:width].astype(F32) for g in range(nm)) for k in range(nd)]

    def own(slabs):
        out = slabs[0]
        for k in range(1, nd):
            out = jnp.where(d == k, slabs[k], out)
        return out

    def norm_rows(i):
        row = norms_ref[i]
        return [row[:, k * width : (k + 1) * width] for k in range(nd)]

    drain("out", out_buf, recv_sem, n - 1)
    hats1, r1 = slab_norm(slabs_of(out_buf), size)
    gains1, shifts1 = norm_rows(2), norm_rows(3)
    normed = [h * g + s for h, g, s in zip(hats1, gains1, shifts1)]
    normed_mine = own(normed)
    normed_low = normed_mine.astype(BF16)

    inner_buf[d] = nn(normed_low, wi[...]).astype(BF16)
    send_dp("inner", inner_buf.at[d], inner_buf.at[d], inner_buf)
    kv_to_mp(1, d)
    for k in range(1, nd):
        kv_to_mp(1, lax.rem(d + k, nd))
    for g in range(nm):
        stat = out_buf[g, :, hw:].astype(F32)
        best = to_rows([joined(stat, 3 * j, 3) for j in range(hm)])
        inv = to_rows([joined(stat, 3 * hm + 2 * j, 2) for j in range(hm)])
        at = pl.ds(g * group, group)
        factors[at, :] = jnp.exp(tops[at, :] - best) * inv
    z = z_near * to_rows([own(parts[j]) for j in range(hm)])
    for k in range(nd):
        z_slab[k] = z[:, k * width : (k + 1) * width].astype(BF16)
    z_buf[d] = z_slab[d]
    drain("inner", inner_buf, recv_sem, nd - 1)
    inner = sum(inner_buf[k].astype(F32) for k in range(nd))
    cdf = 0.5 * (1.0 + lax.erf(inner * (0.5 ** 0.5)))
    act = (inner * cdf).astype(BF16)
    slope = cdf + inner * jnp.exp(-0.5 * inner * inner) * ((0.5 / math.pi) ** 0.5)
    outer_buf[me] = (nt(act, wt[...]) + jnp.where(m == 0, normed_mine, 0.0)).astype(outer_buf.dtype)
    send_all("outer", lambda pd, pm: outer_buf.at[me], outer_buf.at[me], outer_buf)
    drain("outer", outer_buf, recv_sem, n - 1)
    send_dp_each("z_dp", z_slab, z_buf.at[d], z_buf)
    hats2, r2 = slab_norm(slabs_of(outer_buf), size)
    gains2, shifts2 = norm_rows(4), norm_rows(5)
    for k in range(nd):
        final_buf[e, k] = hats2[k] * gains2[k] + shifts2[k]
    final_at = PHASES.index("final")
    final_copy = pltpu.make_async_remote_copy(
        src_ref=final_buf.at[e], dst_ref=final_buf.at[e], send_sem=send_sem.at[final_at], recv_sem=recv_sem.at[final_at],
        device_id=(1 - e, d, m), device_id_type=MESH,
    )
    final_copy.start()
    final_copy.wait_recv()
    started.append(final_copy.wait_send)

    qs = [final_buf[0, k] for k in range(nd)]
    ps = [final_buf[1, k][0:nb] for k in range(nd)]
    q_r = lax.rsqrt(sum(jnp.sum(x * x, -1, keepdims=True) for x in qs) + eps_norm)
    p_r = lax.rsqrt(sum(jnp.sum(x * x, -1, keepdims=True) for x in ps) + eps_norm)
    q_hat, p_hat = [x * q_r for x in qs], [x * p_r for x in ps]

    def d_sims(left, right, axis, negative, positive, used):
        sims = sum(exact_nt(a, b) for a, b in zip(left, right)) / logit_divisor
        is_positive = lax.broadcasted_iota(jnp.int32, sims.shape, axis) == positive
        sims = jnp.where(jnp.logical_and(negative == 1.0, jnp.logical_not(is_positive)), -1e30, sims)
        best = jnp.max(sims, axis, keepdims=True)
        log_total = best + jnp.log(jnp.sum(jnp.exp(sims - best), axis, keepdims=True))
        target = jnp.sum(jnp.where(is_positive, sims, 0.0), axis, keepdims=True)
        weight = used.astype(F32)
        count = jnp.maximum(jnp.sum(weight, 1 - axis, keepdims=True), 1.0)
        loss = jnp.sum(weight * (log_total - target), 1 - axis, keepdims=True) / count
        grad = (jnp.exp(sims - log_total) - is_positive.astype(F32)) * (weight / count / logit_divisor)
        return loss, grad

    at_row = lax.broadcasted_iota(jnp.int32, (c, c), 0)
    from_query = lax.broadcasted_iota(jnp.int32, (c, c), 1)
    order = (from_query == 2 * (at_row % nb) + at_row // nb).astype(BF16)
    negative = negative_ref[...].astype(F32).astype(BF16)
    column, line = lax.broadcasted_iota(jnp.int32, (c, 1), 0), lax.broadcasted_iota(jnp.int32, (1, c), 1)
    positive = [jnp.zeros((c, 1), jnp.int32), jnp.zeros((1, c), jnp.int32)]
    used = [jnp.zeros((c, 1), jnp.int32), jnp.zeros((1, c), jnp.int32)]
    for k in range(c):
        query = 2 * (k % nb) + k // nb
        for i, place in enumerate((column, line)):
            positive[i] = jnp.where(place == k, positive_ref[query], positive[i])
            used[i] = jnp.where(place == k, used_ref[query], used[i])
    loss, grad_q = d_sims(q_hat, p_hat, 1, nt(order, negative), positive[0], used[0])
    _, grad_p = d_sims(p_hat, q_hat, 0, nt(negative, order), positive[1], used[1])

    def unit_back(hats, r, grads):
        along = sum(jnp.sum(g * h, -1, keepdims=True) for g, h in zip(grads, hats))
        return [r * (g - h * along) for g, h in zip(grads, hats)]

    d_q = unit_back(q_hat, q_r, [exact_nn(grad_q, x) for x in p_hat])
    d_p = unit_back(p_hat, p_r, [exact_nn(grad_p, x) for x in q_hat])
    d_final = [
        jnp.where(is_query, a, jnp.concatenate([b, jnp.zeros_like(b)], axis=0)) for a, b in zip(d_q, d_p)
    ]

    d_second, d_gain2, d_shift2 = slab_norm_back(hats2, r2, d_final, gains2, size)
    d_outer = own(d_second).astype(BF16)
    d_act_buf[d] = nn(d_outer, wt[...]).astype(BF16)
    send_dp("d_act", d_act_buf.at[d], d_act_buf.at[d], d_act_buf)
    g_outer = tn(d_outer, act)
    g_outer_ref[...] = g_outer
    drain("d_act", d_act_buf, recv_sem, nd - 1)
    d_inner = (sum(d_act_buf[k].astype(F32) for k in range(nd)) * slope).astype(BF16)
    d_in_buf[me] = nt(d_inner, wi[...]).astype(d_in_buf.dtype)
    send_all("d_in", lambda pd, pm: d_in_buf.at[me], d_in_buf.at[me], d_in_buf)
    g_inner = tn(normed_low, d_inner)
    g_inner_ref[...] = g_inner
    drain("d_in", d_in_buf, recv_sem, n - 1)
    d_normed = [a + b for a, b in zip(d_second, slabs_of(d_in_buf))]
    d_first, d_gain1, d_shift1 = slab_norm_back(hats1, r1, d_normed, gains1, size)
    d_first_mine = own(d_first)
    d_attn = d_first_mine.astype(BF16)

    part = nt(d_attn, wo[...])
    along = att * part
    lane = lax.broadcasted_iota(jnp.int32, (c, hw), 1) // HEAD
    cols = []
    for j in range(hm):
        cols += split_low(jnp.sum(jnp.where(lane == j, along, 0.0), -1, keepdims=True), 2)
    d_att_buf[me] = with_cols(part.astype(BF16), cols)
    send_all("d_att", lambda pd, pm: d_att_buf.at[me], d_att_buf.at[me], d_att_buf)
    g_out = tn(att_low, d_attn)
    g_out_ref[...] = g_out
    squares = sum(jnp.sum(g * g, 0, keepdims=True) for g in (g_outer, g_inner))
    squares = jnp.sum(squares, -1, keepdims=True) + jnp.sum(jnp.sum(g_out * g_out, 0, keepdims=True), -1, keepdims=True)

    kv_wait(1)
    drain("d_att", d_att_buf, recv_sem, n - 1)
    d_atts = []
    for g in range(nm):
        slab = sum(d_att_buf[k * nm + g].astype(F32) for k in range(nd))
        d_att = slab[:, 0:hw].astype(BF16)
        d_atts.append(d_att)
        col[pl.ds(g * group, group), :] = to_rows(
            [joined(slab, hw + 2 * j, 2) for j in range(hm)]
        )
        wide = expand(d_att)
        for k in range(nd):
            basis[pl.ds(heads + g * group, group), k * width : (k + 1) * width] = nt(wide, projection(1, g, k)).astype(BF16)
    d_att_mine = d_atts[0]
    for g in range(1, nm):
        d_att_mine = jnp.where(m == g, d_atts[g], d_att_mine)
    acc[...] = jnp.zeros_like(acc)

    def backward(t, carry):
        at = pl.ds(pl.multiple_of(t * vt, vt), vt)
        d_probs = nt(basis[pl.ds(heads, heads), :], hid[at, :])
        probs = lows[pl.ds(0, heads), at].astype(F32) * jnp.sum(
            jnp.where(lane_of_tile == t, factors[...], 0.0), -1, keepdims=True
        )
        d_scores = (probs * (d_probs - col[...]) * scale).astype(BF16)
        lows[pl.ds(0, heads), at] = d_scores
        lows[pl.ds(heads, heads), at] = probs.astype(BF16)
        acc[...] += nn(d_scores, hid[at, :])
        return carry
    lax.fori_loop(0, tiles, backward, 0, unroll=UNROLL)

    for g in range(nm):
        y = acc[pl.ds(g * group, group), :].astype(BF16)
        dq = jnp.zeros((group, hw), F32)
        for k in range(nd):
            dq = dq + nn(y[:, k * width : (k + 1) * width], projection(0, g, k))
        y_src[g] = y
        dq_src[g] = collapse(dq).astype(BF16)
        send_group("dq", g, dq_src.at[g], dq_buf.at[me], dq_buf)
    dq_buf[me] = dq_src[m]
    y_mp[m] = y_src[m]
    send_mp("y", y_src, y_mp.at[m], y_mp)

    lane_t = 128

    def spread(t, carry):
        at = pl.ds(pl.multiple_of(t * lane_t, lane_t), lane_t)
        stage[at, :] = tn(lows[pl.ds(0, 2 * heads), at], basis[pl.ds(0, 2 * heads), :])
        return carry
    lax.fori_loop(0, rows // lane_t, spread, 0)

    drain("dq", dq_buf, recv_sem, n - 1)
    dq_mine = sum(dq_buf[k].astype(F32) for k in range(n)).astype(BF16)
    d_rows_buf[me] = (nt(dq_mine, wq[...]) + jnp.where(m == 0, d_first_mine, 0.0)).astype(d_rows_buf.dtype)
    send_all("d_rows", lambda pd, pm: d_rows_buf.at[me], d_rows_buf.at[me], d_rows_buf)
    g_q = tn(mine_low, dq_mine)
    drain("z_dp", z_buf, recv_sem, nd - 1)
    z_mine = sum(z_buf[k].astype(F32) for k in range(nd)).astype(BF16)
    g_v = tn(z_mine, expand(d_att_mine))
    drain("y", y_mp, recv_sem, nm - 1)
    y = sum(y_mp[g].astype(F32) for g in range(nm))
    for k in range(nd):
        y_slab[k] = y[:, k * width : (k + 1) * width].astype(BF16)
    y_buf[d] = y_slab[d]
    send_dp_each("y_dp", y_slab, y_buf.at[d], y_buf)
    fold8 = lambda v: jnp.sum(v.reshape(v.shape[0] // 8, 8, size), 0)

    def table_back(t, carry):
        d_gain, d_shift = carry
        at = pl.ds(pl.multiple_of(t * BLOCK, BLOCK), BLOCK)
        dy = stage[at, :]
        x = emb[at, :].astype(F32)
        x = x - jnp.mean(x, -1, keepdims=True)
        r = lax.rsqrt(jnp.mean(x * x, -1, keepdims=True) + eps_norm)
        hat = x * r
        scaled = dy * gain0
        mean = jnp.mean(scaled, -1, keepdims=True)
        along = jnp.mean(scaled * hat, -1, keepdims=True)
        stage[at, :] = r * (scaled - mean - hat * along)
        return d_gain + fold8(dy * hat), d_shift + fold8(dy)
    zero = jnp.zeros((8, size), F32)
    d_gain, d_shift = lax.fori_loop(0, rows // BLOCK, table_back, (zero, zero))

    drain("d_rows", d_rows_buf, recv_sem, n - 1)
    d_rows = jnp.concatenate(slabs_of(d_rows_buf), axis=1)
    d_rows = jnp.where(owned, d_rows, 0.0)
    hat = found_at[...]
    d_found, extra_gain, extra_shift = slab_norm_back([hat], found_r, [d_rows], [gain0], size)
    d_found = jnp.where(owned, d_found[0], 0.0).astype(BF16)

    def table_add(t, square):
        at = pl.ds(pl.multiple_of(t * lane_t, lane_t), lane_t)
        grad = stage[at, :] + tn(lows[pl.ds(hot_at, c), at], d_found)
        stage[at, :] = grad
        return square + fold8(grad * grad)
    square = lax.fori_loop(0, rows // lane_t, table_add, zero)
    d_gain = jnp.sum(d_gain, 0, keepdims=True) + extra_gain[0]
    d_shift = jnp.sum(d_shift, 0, keepdims=True) + extra_shift[0]
    drain("y_dp", y_buf, recv_sem, nd - 1)
    y_mine = sum(y_buf[k].astype(F32) for k in range(nd)).astype(BF16)
    g_k = tn(y_mine, expand(q_mine))
    for i, g in enumerate((g_q, g_k, g_v)):
        g_mixed_ref[i] = g
    total = sum(jnp.sum(g * g, 0, keepdims=True) for g in (g_q, g_k, g_v))
    squares = squares + jnp.sum(total, -1, keepdims=True)
    squares = squares + jnp.sum(jnp.sum(square, 0, keepdims=True), -1, keepdims=True)
    chunks = size // 128
    lines = [v[:, k * 128 : (k + 1) * 128] for v in (d_gain, d_shift) for k in range(chunks)]
    lines.append(jnp.broadcast_to(squares, (1, 128)))
    lines.append(jnp.zeros((16 - len(lines), 128), F32))
    sums_buf[me] = jnp.concatenate(lines, axis=0)

    def send_sums(i, carry):
        pd, pm = peer(i)
        remote("sums", sums_buf.at[me], sums_buf.at[me], (e, pd, pm))
        return carry
    lax.fori_loop(1, n, send_sums, 0)
    sent.append(("sums", sums_buf, n - 1, True))
    drain("sums", sums_buf, recv_sem, n - 1, both=True)
    totals = sum(sums_buf[k] for k in range(n))
    firsts = [jnp.concatenate([totals[v * chunks + k : v * chunks + k + 1] for k in range(chunks)], axis=1) for v in range(2)]
    squares = totals[2 * chunks : 2 * chunks + 1, 0:1]
    for i in range(2):
        g_norms_ref[i : i + 1, :] = firsts[i]
        squares = squares + jnp.sum(firsts[i] * firsts[i], -1, keepdims=True)
    for i, slabs in enumerate((d_gain1, d_shift1, d_gain2, d_shift2)):
        for k in range(nd):
            g_norms_ref[2 + i : 3 + i, k * width : (k + 1) * width] = slabs[k]
            squares = squares + jnp.sum(slabs[k] * slabs[k], -1, keepdims=True)
    norm_buf[e] = jnp.broadcast_to(squares, (8, 128))
    norm_at = PHASES.index("norm")
    norm_copy = pltpu.make_async_remote_copy(
        src_ref=norm_buf.at[e], dst_ref=norm_buf.at[e], send_sem=send_sem.at[norm_at], recv_sem=recv_sem.at[norm_at],
        device_id=(1 - e, d, m), device_id_type=MESH,
    )
    norm_copy.start()
    norm_copy.wait_recv()
    started.append(norm_copy.wait_send)
    grad_norm = jnp.sqrt(norm_buf[0] + norm_buf[1])
    small_ref[...] = jnp.where(
        lax.broadcasted_iota(jnp.int32, (8, 128), 0) == 0, jnp.broadcast_to(loss, (8, 128)), grad_norm
    )

    finish()


def kernel_gradients(
    token_ids, query_lengths, negative_mask, positive_index, used_rows, table, w_mixed, w_out, w_inner, w_outer, norm_params, table_m, table_v
):
    nd, nm = lax.axis_size("dp"), lax.axis_size("mp")
    n = nd * nm
    blk = token_ids.shape[1]
    _, rows, size = table.shape
    width, hw, ff = w_mixed.shape[1], w_mixed.shape[3], w_inner.shape[2]
    hm = hw // HEAD
    nb = nd * blk
    c = 2 * nb
    group, heads = hm * c, nm * hm * c
    S = jax.ShapeDtypeStruct
    outs = (
        S((8, 128), F32), S((rows, size), F32), S((3, width, hw), F32),
        S((hw, width), F32), S((width, ff), F32), S((width, ff), F32), S((8, size), F32),
    ) + (S((rows, size), F32),) * 3
    vm, hb = pl.BlockSpec(memory_space=pltpu.VMEM), pl.BlockSpec(memory_space=pltpu.HBM)
    V = pltpu.VMEM
    wide = hw + HEAD
    operands = (
        w_mixed[0].swapaxes(0, 1), token_ids, query_lengths, norm_params.swapaxes(0, 1), w_out[0], w_inner[0], w_outer[0].T,
        positive_index, used_rows, negative_mask.T, table[0], table_m[0], table_v[0],
    )
    local = [V] * 2 + [pltpu.SMEM] + [V] * 4 + [pltpu.SMEM] * 2 + [V]
    scratch = [space(item.shape, item.dtype) for space, item in zip(local, operands)] + [
        V((rows, size), BF16), V((rows, size), BF16),
        V((2 * heads + c, rows), BF16), V((2 * heads, size), BF16), V((c, rows), F32), V((nb, 32, 128), F32),
        V((heads, size), F32), V((heads, 1), F32), V((heads, 8), F32), V((heads, 8), F32), V((c, size), F32),
        V((width, hw), BF16), V((hw, width), BF16), V((width, ff), BF16), V((width, ff), BF16), V((2, nm, nd, width // 2, 2 * hw), BF16),
        V((nd, blk, 2 * QSLOT), jnp.int32),
        V((nd, c, width), BF16), V((n, c, width), BF16), V((n, c, hw), BF16),
        V((nm, c, 128), F32), V((nm, c, 128), F32), V((nd, c, wide), BF16),
        V((nm, group, size), BF16), V((nm, group, size), BF16), V((nd, group, width), BF16), V((nd, group, width), BF16),
        V((n, c, wide), BF16), V((nd, c, ff), BF16), V((n, c, width), BF16), V((2, nd, c, width), F32),
        V((nd, c, ff), BF16), V((n, c, width), BF16), V((n, c, wide), BF16), V((nm, c, hw), BF16), V((n, c, hw), BF16),
        V((nm, group, size), BF16), V((nm, group, size), BF16), V((nd, group, width), BF16), V((nd, group, width), BF16),
        V((n, c, width), BF16),
        V((n, 16, 128), F32), V((2, 8, 128), F32),
        pltpu.SemaphoreType.DMA((len(PHASES),)), pltpu.SemaphoreType.DMA((len(PHASES),)),
        pltpu.SemaphoreType.DMA((2,)), pltpu.SemaphoreType.DMA((2, nd)), pltpu.SemaphoreType.DMA((2,)),
        pltpu.SemaphoreType.DMA((rows // 384,)), pltpu.SemaphoreType.DMA((3,)), pltpu.SemaphoreType.DMA((10,)),
    ]
    small, g_table, g_mixed, g_out, g_inner, g_outer, g_norms, *kept = pl.pallas_call(
        partial(grad_kernel, (nd, nm, blk, rows, width, size, hm, ff)),
        out_shape=outs,
        in_specs=[hb] * len(operands),
        out_specs=(vm,) * 10,
        scratch_shapes=scratch,
        compiler_params=pltpu.CompilerParams(collective_id=ENTRY_ID, has_side_effects=True, vmem_limit_bytes=27 << 20),
        name="gradients",
    )(*(pltpu.with_memory_space_constraint(item, pltpu.HBM) for item in operands))
    return small, (g_table, g_mixed, g_out, g_inner, g_outer, g_norms), kept


RING = 3
PIECE = 192


def adam_kernel(rates, count_ref, small_ref, *refs):
    k = len(rates)
    operands = [refs[4 * i : 4 * i + 4] for i in range(k)]
    results = [refs[4 * k + 3 * i : 4 * k + 3 * i + 3] for i in range(k)]
    refs = refs[7 * k :]
    ring, ring_sem, own_sem, buffers = refs[:3], refs[3], refs[4], refs[5:]
    norm = small_ref[1:2, 0:1]
    clip = jnp.minimum(1.0, clip_limit / (norm + 1e-06))
    count = jnp.full((1, 1), count_ref[0], jnp.int32).astype(F32)
    fix_one = 1.0 - jnp.exp(count * math.log(beta_one))
    fix_two = 1.0 - jnp.exp(count * math.log(beta_two))
    inv_one, inv_two = 1.0 / fix_one, 1.0 / fix_two
    copies, in_slot, used, turn = [], [None] * RING, 0, 0

    def update(i, at, targets, to):
        grad, weight, first, second = (ref[at] for ref in operands[i])
        rate, decay = rates[i]
        grad = grad * clip
        first = beta_one * first + (1.0 - beta_one) * grad
        second = beta_two * second + ((1.0 - beta_two) * grad) * grad
        step = first * inv_one / (jnp.sqrt(second * inv_two) + adam_eps)
        if decay:
            step = step + decay * weight
        for ref, value in zip(targets, (weight - rate * step, first, second)):
            ref[to] = value

    def send(src, dst, sem):
        copy = pltpu.make_async_copy(src, dst, sem)
        copy.start()
        return copy

    for i in range(k):
        shape = operands[i][1].shape
        if len(shape) == 2 and shape[1] == ring[0].shape[2]:
            for start in range(0, shape[0], PIECE):
                slot = turn % RING
                turn += 1
                if in_slot[slot]:
                    for copy in in_slot[slot]:
                        copy.wait()

                def block(b, carry):
                    at = pl.ds(pl.multiple_of(b * 32, 32), 32)
                    update(i, pl.ds(pl.multiple_of(start + b * 32, 32), 32), [ref.at[slot] for ref in ring], at)
                    return carry
                lax.fori_loop(0, PIECE // 32, block, 0)
                in_slot[slot] = [
                    send(ring[j].at[slot], results[i][j].at[pl.ds(start, PIECE)], ring_sem.at[slot, j]) for j in range(3)
                ]
            continue
        mine = buffers[3 * used : 3 * used + 3]
        if len(shape) == 3:
            for j in range(shape[0]):
                update(i, j, mine, j)
        else:
            update(i, slice(None), mine, slice(None))
        copies += [send(mine[j], results[i][j], own_sem.at[used, j]) for j in range(3)]
        used += 1
    for group in in_slot + [copies]:
        for copy in group or ():
            copy.wait()


def kernel_adam(step_count, small, grads, weights, firsts, seconds):
    k = len(weights)
    rates = tuple((0.5, 0.0) if i == k - 1 else (0.06, 0.01) for i in range(k))
    vm, sm = pl.BlockSpec(memory_space=pltpu.VMEM), pl.BlockSpec(memory_space=pltpu.SMEM)
    shapes = [jax.ShapeDtypeStruct(w.shape, F32) for w in weights for _ in range(3)]
    operands = [item for group in zip(grads, weights, firsts, seconds) for item in group]
    size = weights[0].shape[1]
    alone = [item for item in shapes if len(item.shape) == 3 or item.shape[1] != size]
    return pl.pallas_call(
        partial(adam_kernel, rates),
        out_shape=shapes,
        in_specs=[sm, vm] + [vm] * (4 * k),
        out_specs=[pl.BlockSpec(memory_space=pltpu.HBM)] * (3 * k),
        scratch_shapes=[pltpu.VMEM((RING, PIECE, size), F32)] * 3
        + [pltpu.SemaphoreType.DMA((RING, 3)), pltpu.SemaphoreType.DMA((len(alone) // 3, 3))]
        + [pltpu.VMEM(item.shape, F32) for item in alone],
        compiler_params=pltpu.CompilerParams(vmem_limit_bytes=12 << 20),
        name="adam",
    )(step_count, small, *operands)


def on_device(
    token_ids,
    query_lengths,
    negative_mask,
    positive_index,
    used_rows,
    step_count,
    table,
    w_mixed,
    w_out,
    w_inner,
    w_outer,
    norm_params,
    table_m,
    table_v,
    mixed_m,
    mixed_v,
    out_m,
    out_v,
    inner_m,
    inner_v,
    outer_m,
    outer_v,
    norms_m,
    norms_v,
):
    operands = (
        token_ids, query_lengths, negative_mask, positive_index, used_rows, table, w_mixed, w_out, w_inner, w_outer, norm_params
    )
    masters = (table, w_mixed, w_out, w_inner, w_outer, norm_params)
    firsts = (table_m, mixed_m, out_m, inner_m, outer_m, norms_m)
    seconds = (table_v, mixed_v, out_v, inner_v, outer_v, norms_v)
    if table.shape[1] % 384 == 0 and w_mixed.shape[1] % 64 == 0 and table.shape[1] <= 2048:
        small, grads, kept = kernel_gradients(*operands, table_m, table_v)

        def stored(tab, items):
            _, mixed, out, inner, outer, norm = items
            return tab, mixed[0].swapaxes(0, 1), out[0], inner[0], outer[0].T, norm.swapaxes(0, 1)

        grads = grads[:5] + (grads[5][0:6, None, :],)
        updated = kernel_adam(step_count, small, grads, *map(stored, kept, (masters, firsts, seconds)))
        back = (
            lambda x: x[None],
            lambda x: x.swapaxes(0, 1)[None],
            lambda x: x[None],
            lambda x: x[None],
            lambda x: x.T[None],
            lambda x: x.swapaxes(0, 1),
        )
        return (small[0, 0], small[1, 0]) + tuple(back[i // 3](item) for i, item in enumerate(updated))
    loss, grads = gradients(*operands)
    owner = (lax.axis_index("dp") == 0) & (lax.axis_index("mp") == 0)
    squares = jnp.where(owner, jnp.sum(grads[5] * grads[5]), 0.0)
    for grad in grads[:5]:
        squares = squares + jnp.sum(grad * grad)
    grad_norm = jnp.sqrt(lax.psum(squares, ("enc", "dp", "mp")))
    clip = jnp.minimum(1.0, clip_limit / (grad_norm + 1e-06))
    count = step_count[0].astype(F32)
    results = [loss, grad_norm]
    for index in range(6):
        rate, decay = (0.5, 0.0) if index == 5 else (0.06, 0.01)
        results.extend(
            adam_step(
                masters[index], grads[index][None] * clip, firsts[index], seconds[index], rate, decay, count
            )
        )
    return tuple(results)


def solution(mesh):
    table = P("enc", ("dp", "mp"), None)
    mixed = P("enc", "dp", None, "mp")
    columns = P("enc", "mp", "dp")
    units = P("enc", "dp", "mp")
    norms = P("enc", None, None)
    matrices = (table, mixed, columns, units, columns, norms)
    moments = tuple(spec for spec in matrices for _ in range(2))
    updated = tuple(spec for spec in matrices for _ in range(3))
    return jax.shard_map(
        on_device,
        mesh=mesh,
        in_specs=(P("enc", "dp", None), P("dp"), P(), P(), P(), P()) + matrices + moments,
        out_specs=(P(), P()) + updated,
        check_vma=False,
    )
```

```python
import math
from functools import partial

import jax
import jax.numpy as jnp
from jax import lax
from jax.experimental import pallas as pl
from jax.experimental.pallas import tpu as pltpu
from jax.sharding import PartitionSpec as P

HEAD = 64
QSLOT = 128
F32 = jnp.float32
BF16 = jnp.bfloat16

exact_arithmetic_level = lax.Precision.HIGHEST
eps_norm = 1e-06
logit_divisor = 0.05
clip_limit = 0.02
beta_one = 0.9
beta_two = 0.999
adam_eps = 1e-08


def layer_norm(x, gain, shift):
    centred = x - jnp.mean(x, -1, keepdims=True)
    spread = jnp.mean(centred * centred, -1, keepdims=True)
    return centred * lax.rsqrt(spread + eps_norm) * gain + shift


def mul(spec, a, b):
    return jnp.einsum(spec, a, b, preferred_element_type=F32)


def token_counts(ids, lens, is_query, base, rows):
    pos = jnp.arange(ids.shape[1])
    slot = pos // QSLOT
    limit = jnp.where(slot[None, :] == 0, lens[:, 0:1], lens[:, 1:2])
    within = (pos % QSLOT)[None, :] < limit
    same = slot[None, :] == jnp.arange(2)[:, None]
    allowed = jnp.where(is_query, same[:, None, :] & within[None], True)
    local = ids - base
    n_hi = -(-rows // 128)
    high = (local[..., None] >> 7) == jnp.arange(n_hi)
    low = (local[..., None] & 127) == jnp.arange(128)
    left = (allowed[..., None] & high[None]).astype(BF16)
    counts = mul("sbth,btl->sbhl", left, low.astype(BF16))
    return counts.reshape(2 * ids.shape[0], n_hi * 128)[:, :rows]


def contrast(queries, passages, negative_mask, positive_index, used_rows):
    question_direction_rows = queries * lax.rsqrt(
        jnp.sum(queries * queries, -1, keepdims=True) + eps_norm
    )
    document_direction_rows = passages * lax.rsqrt(
        jnp.sum(passages * passages, -1, keepdims=True) + eps_norm
    )
    pairwise_cosine_table = (
        jnp.dot(
            question_direction_rows, document_direction_rows.T, precision=exact_arithmetic_level
        )
        / logit_divisor
    )
    is_positive = jnp.arange(passages.shape[0])[None, :] == positive_index[:, None]
    excluded = (negative_mask == 1) & ~is_positive
    pairwise_cosine_table = jnp.where(excluded, -1e30, pairwise_cosine_table)
    top = jnp.max(pairwise_cosine_table, -1, keepdims=True)
    log_total = top[:, 0] + jnp.log(jnp.sum(jnp.exp(pairwise_cosine_table - top), -1))
    target = jnp.sum(jnp.where(is_positive, pairwise_cosine_table, 0.0), -1)
    weight = used_rows.astype(F32)
    return jnp.sum(weight * (log_total - target)) / jnp.maximum(jnp.sum(weight), 1.0)


def adam_step(weight, grad, first, second, rate, decay, count):
    first_new = beta_one * first + (1.0 - beta_one) * grad
    second_new = beta_two * second + (1.0 - beta_two) * grad * grad
    fix_one = 1.0 - jnp.power(beta_one, count)
    correction_second = 1.0 - jnp.power(beta_two, count)
    update = (
        first_new / fix_one / (jnp.sqrt(second_new / correction_second) + adam_eps) + decay * weight
    )
    return (weight - rate * update, first_new, second_new)


def slot_major(x):
    return x.reshape((x.shape[0] // 2, 2) + x.shape[1:]).swapaxes(0, 1).reshape(x.shape)


def gradients(
    token_ids, query_lengths, negative_mask, positive_index, used_rows, table, w_mixed, w_out, w_inner, w_outer, norm_params
):
    is_query = lax.axis_index("enc") == 0
    d, m = lax.axis_index("dp"), lax.axis_index("mp")
    n_mp = lax.axis_size("mp")
    rows, width = table.shape[1], w_mixed.shape[1]
    hm = w_out.shape[1] // HEAD
    scale = HEAD ** (-0.5)
    norms = norm_params[0]
    base = (d * n_mp + m) * rows

    ids = lax.all_gather(token_ids[0], "dp", axis=0, tiled=True)
    lens = lax.all_gather(query_lengths, "dp", axis=0, tiled=True).reshape(-1, 2)
    blocks = ids.shape[0]
    counts = token_counts(ids, lens, is_query, base, rows)
    cls_ids = jnp.concatenate([ids[:, 0], ids[:, QSLOT]]) - base
    cls_hot = cls_ids[:, None] == jnp.arange(rows)[None, :]

    def mine(x):
        return lax.dynamic_slice_in_dim(x, d * width, width, 1)

    wq, wk, wv = (w_mixed[0, :, i].astype(BF16).reshape(width, hm, HEAD) for i in range(3))
    wo = w_out[0].astype(BF16).reshape(hm, HEAD, width)
    wi, wt = w_inner[0].astype(BF16), w_outer[0].astype(BF16)

    embedded = lax.reduce_precision(table[0], 8, 7)
    hidden, hidden_back = jax.vjp(layer_norm, embedded, norms[0], norms[1])
    hid = hidden.astype(BF16)
    first_rows = lax.psum(
        jnp.dot(cls_hot.astype(F32), hidden, precision=exact_arithmetic_level), ("dp", "mp")
    )
    first_mine = mine(first_rows).astype(BF16)
    q = lax.psum(mul("ci,ihk->hck", first_mine, wq), "dp").astype(BF16)
    u = mul("hck,ihk->hci", q, wk).astype(BF16)
    u = lax.all_gather(lax.all_gather(u, "dp", axis=2, tiled=True), "mp", axis=0, tiled=True)
    scores = jnp.where(counts[None] > 0, mul("hci,vi->hcv", u, hid) * scale, -1e30)
    top = lax.pmax(jnp.max(scores, -1, keepdims=True), ("dp", "mp"))
    weight = counts[None] * jnp.exp(scores - top)
    probs = weight / lax.psum(jnp.sum(weight, -1, keepdims=True), ("dp", "mp"))
    probs_low = probs.astype(BF16)
    z = mul("hcv,vi->hci", probs_low, hid)
    z = lax.psum_scatter(z, "mp", scatter_dimension=0, tiled=True)
    z = lax.psum_scatter(z, "dp", scatter_dimension=2, tiled=True).astype(BF16)
    att = lax.psum(mul("hci,ihk->hck", z, wv), "dp")
    att_low = att.astype(BF16)
    out = lax.psum(mul("hck,hke->ce", att_low, wo), "mp")
    first_sum = first_rows + lax.all_gather(out, "dp", axis=1, tiled=True)
    normed, normed_back = jax.vjp(layer_norm, first_sum, norms[2], norms[3])
    normed_mine = mine(normed).astype(BF16)
    inner = lax.psum(mul("ci,if->cf", normed_mine, wi), "dp")
    act, act_back = jax.vjp(partial(jax.nn.gelu, approximate=False), inner)
    act = act.astype(BF16)
    outer = lax.psum(mul("cf,fe->ce", act, wt), "mp")
    second_sum = normed + lax.all_gather(outer, "dp", axis=1, tiled=True)
    final, final_back = jax.vjp(layer_norm, second_sum, norms[4], norms[5])
    both = lax.all_gather(final, "enc", axis=0)
    loss, loss_back = jax.vjp(
        partial(
            contrast,
            negative_mask=slot_major(negative_mask),
            positive_index=slot_major(positive_index),
            used_rows=slot_major(used_rows),
        ),
        both[0],
        both[1, :blocks],
    )
    d_queries, d_passages = loss_back(jnp.ones((), F32))
    d_passages = jnp.concatenate([d_passages, jnp.zeros_like(d_passages)])
    d_final = jnp.where(is_query, d_queries, d_passages)

    d_second, d_gain2, d_shift2 = final_back(d_final)
    d_outer = mine(d_second).astype(BF16)
    g_outer = mul("cf,ce->fe", act, d_outer)
    d_act = lax.psum(mul("ce,fe->cf", d_outer, wt), "dp")
    d_inner = act_back(d_act)[0].astype(BF16)
    g_inner = mul("ci,cf->if", normed_mine, d_inner)
    d_in = lax.psum(mul("cf,if->ci", d_inner, wi), "mp")
    d_normed = d_second + lax.all_gather(d_in, "dp", axis=1, tiled=True)
    d_first, d_gain1, d_shift1 = normed_back(d_normed)
    d_attn = mine(d_first).astype(BF16)
    g_out = mul("hck,ce->hke", att_low, d_attn).reshape(w_out.shape[1:])
    d_att = lax.psum(mul("ce,hke->hck", d_attn, wo), "dp").astype(BF16)
    w = mul("hck,ihk->hci", d_att, wv).astype(BF16)
    mean_d = jnp.sum(att * d_att.astype(F32), -1, keepdims=True)
    w = lax.all_gather(lax.all_gather(w, "dp", axis=2, tiled=True), "mp", axis=0, tiled=True)
    mean_d = lax.all_gather(mean_d, "mp", axis=0, tiled=True)
    d_probs = mul("hci,vi->hcv", w, hid)
    d_scores = (probs * (d_probs - mean_d)).astype(BF16)
    y = mul("hcv,vi->hci", d_scores, hid)
    y = lax.psum_scatter(y, "mp", scatter_dimension=0, tiled=True)
    y = lax.psum_scatter(y, "dp", scatter_dimension=2, tiled=True).astype(BF16)
    dq = (lax.psum(mul("hci,ihk->hck", y, wk), "dp") * scale).astype(BF16)
    g_q = mul("ci,hck->ihk", first_mine, dq)
    g_k = mul("hci,hck->ihk", y, q) * scale
    g_v = mul("hci,hck->ihk", z, d_att)
    g_mixed = jnp.stack([g_q, g_k, g_v], 1).reshape(w_mixed.shape[1:])
    d_rows = lax.psum(mul("hck,ihk->ci", dq, wq), "mp")
    d_rows = (d_first + lax.all_gather(d_rows, "dp", axis=1, tiled=True)).astype(BF16)
    d_hidden = (
        mul("hcv,hci->vi", d_scores, u) * scale
        + mul("hcv,hci->vi", probs_low, w)
        + mul("cv,ci->vi", cls_hot.astype(BF16), d_rows)
    )
    g_table, d_gain0, d_shift0 = hidden_back(d_hidden)
    sums = lax.psum(jnp.stack([d_gain0, d_shift0]), ("dp", "mp"))
    g_norms = jnp.concatenate([sums, jnp.stack([d_gain1, d_shift1, d_gain2, d_shift2])])
    return loss, (g_table, g_mixed, g_out, g_inner, g_outer, g_norms)


MESH = pl.DeviceIdType.MESH
ENTRY_ID = 3
PHASES = (
    "ids", "rows", "q", "stat", "att", "z", "z_dp", "out", "inner", "outer", "final",
    "d_act", "d_in", "d_att", "dq", "y", "y_dp", "d_rows", "sums", "norm",
)
BLOCK = 64
UNROLL = True


def nt(a, b):
    return lax.dot_general(a, b, (((1,), (1,)), ((), ())), preferred_element_type=F32)


def tn(a, b):
    return lax.dot_general(a, b, (((0,), (0,)), ((), ())), preferred_element_type=F32)


def nn(a, b):
    return jnp.dot(a, b, preferred_element_type=F32)


def exact_nt(a, b):
    return lax.dot_general(
        a, b, (((1,), (1,)), ((), ())), precision=exact_arithmetic_level, preferred_element_type=F32
    )


def exact_nn(a, b):
    return jnp.dot(a, b, precision=exact_arithmetic_level, preferred_element_type=F32)


def slab_norm(slabs, size):
    mean = sum(jnp.sum(s, -1, keepdims=True) for s in slabs) * (1.0 / size)
    slabs = [s - mean for s in slabs]
    spread = sum(jnp.sum(s * s, -1, keepdims=True) for s in slabs) * (1.0 / size)
    r = lax.rsqrt(spread + eps_norm)
    return [s * r for s in slabs], r


def slab_norm_back(hats, r, grads, gains, size):
    scaled = [dy * g for dy, g in zip(grads, gains)]
    mean = sum(jnp.sum(s, -1, keepdims=True) for s in scaled) * (1.0 / size)
    along = sum(jnp.sum(s * h, -1, keepdims=True) for s, h in zip(scaled, hats)) * (1.0 / size)
    d_in = [r * (s - mean - h * along) for s, h in zip(scaled, hats)]
    d_gain = [jnp.sum(dy * h, 0, keepdims=True) for dy, h in zip(grads, hats)]
    d_shift = [jnp.sum(dy, 0, keepdims=True) for dy in grads]
    return d_in, d_gain, d_shift


def joined(x, at, parts):
    return sum(x[:, at + i : at + i + 1] for i in range(parts))


def split_low(x, parts):
    out = []
    for _ in range(parts):
        piece = x.astype(BF16)
        out.append(piece)
        x = x - piece.astype(F32)
    return out


def grad_kernel(cfg, *refs):
    nd, nm, blk, rows, width, size, hm, ff = cfg
    n = nd * nm
    nb = nd * blk
    c = 2 * nb
    hw = hm * HEAD
    group = hm * c
    half = hm * nb
    heads = nm * group
    vt = 384
    tiles = rows // vt
    scale = HEAD ** (-0.5)
    (
        *early_hbm, table_hbm, first_hbm, second_hbm,
        small_ref, stage, g_mixed_ref, g_out_ref, g_inner_ref, g_outer_ref, g_norms_ref, table_keep, first_keep, second_keep,
        mixed_f, ids_ref, lens_ref, norms_ref, out_f, inner_f, outer_f, positive_ref, used_ref, negative_ref,
        emb, hid, lows, basis, counts, xs, acc, col, tops, factors, found_at,
        wq, wo, wi, wt, kv,
        ids_buf, rows_src, rows_buf, q_buf, stat_src, stat_buf, att_buf, z_src, z_mp, z_slab, z_buf, out_buf, inner_buf, outer_buf,
        final_buf, d_act_buf, d_in_buf, d_att_buf, dq_src, dq_buf, y_src, y_mp, y_slab, y_buf, d_rows_buf, sums_buf, norm_buf,
        send_sem, recv_sem, kv_send, kv_recv, kv_spread, table_sem, keep_sem, early_sem,
    ) = refs
    e, d, m = lax.axis_index("enc"), lax.axis_index("dp"), lax.axis_index("mp")
    me = d * nm + m
    is_query = e == 0
    base = me * rows

    sent, received = [], []

    def halves(go, full):
        pl.when(is_query)(lambda: go(full))
        pl.when(jnp.logical_not(is_query))(lambda: go(full // 2))

    def peer(i):
        p = lax.rem(me + i, n)
        return p // nm, lax.rem(p, nm)

    def remote(name, src, dst, where):
        k = PHASES.index(name)
        pltpu.make_async_remote_copy(
            src_ref=src, dst_ref=dst, send_sem=send_sem.at[k], recv_sem=recv_sem.at[k],
            device_id=where, device_id_type=MESH,
        ).start()

    def send_all(name, src_of, dst, buf):
        sent.append((name, buf, n - 1, False))

        def go(r):
            def one(i, carry):
                pd, pm = peer(i)
                remote(name, src_of(pd, pm).at[pl.ds(0, r)], dst.at[pl.ds(0, r)], (e, pd, pm))
                return carry
            lax.fori_loop(1, n, one, 0)
        halves(go, dst.shape[0])

    def send_group(name, group_of, src, dst, buf):
        if group_of == 0:
            sent.append((name, buf, n - 1, False))

        def go(r):
            for pd in range(nd):
                @pl.when(jnp.logical_or(pd != d, group_of != m))
                def _():
                    remote(name, src.at[pl.ds(0, r)], dst.at[pl.ds(0, r)], (e, pd, group_of))
        halves(go, dst.shape[0])

    def send_dp(name, src, dst, buf, both=False):
        sent.append((name, buf, nd - 1, both))

        def go(r):
            for i in range(1, nd):
                remote(name, src.at[pl.ds(0, r)], dst.at[pl.ds(0, r)], (e, lax.rem(d + i, nd), m))
        if both:
            go(dst.shape[0])
        else:
            halves(go, dst.shape[0])

    def send_mp(name, source, dst, buf):
        sent.append((name, buf, nm - 1, False))

        def go(r):
            for i in range(1, nm):
                g = lax.rem(m + i, nm)
                remote(name, source.at[g, pl.ds(0, r)], dst.at[pl.ds(0, r)], (e, d, g))
        halves(go, dst.shape[0])

    def send_dp_each(name, source, dst, buf):
        sent.append((name, buf, nd - 1, False))

        def go(r):
            for i in range(1, nd):
                k = lax.rem(d + i, nd)
                remote(name, source.at[k, pl.ds(0, r)], dst.at[pl.ds(0, r)], (e, k, m))
        halves(go, dst.shape[0])

    def drain(name, buf, sem, count, both=False):
        k = PHASES.index(name)
        if sem is recv_sem:
            received.append(name)

        def go(r):
            view = buf.at[pl.ds(0, count), pl.ds(0, r)]
            pltpu.make_async_copy(view, view, sem.at[k]).wait()
        if both:
            go(buf.shape[1])
        else:
            halves(go, buf.shape[1])

    def finish():
        for name, buf, count, both in sent:
            drain(name, buf, send_sem, count, both)
            if name not in received:
                drain(name, buf, recv_sem, count, both)
        for item in started:
            item()

    started = []

    early = (mixed_f, ids_ref, lens_ref, norms_ref, out_f, inner_f, outer_f, positive_ref, used_ref, negative_ref)
    early = [pltpu.make_async_copy(src, dst, early_sem.at[i]) for i, (src, dst) in enumerate(zip(early_hbm, early))]
    table_loads = [
        pltpu.make_async_copy(table_hbm.at[pl.ds(i * vt, vt)], stage.at[pl.ds(i * vt, vt)], table_sem.at[i])
        for i in range(tiles)
    ]
    for item in early[:4]:
        item.start()
    for item in table_loads:
        item.start()
    for item in early[4:]:
        item.start()

    @pl.when(jnp.logical_not(is_query))
    def _():
        for buf in (
            rows_buf, q_buf, stat_buf, att_buf, z_mp, z_buf, out_buf, inner_buf, outer_buf, d_act_buf, d_in_buf, d_att_buf, dq_buf,
            y_mp, y_buf, d_rows_buf,
        ):
            r = buf.shape[1] // 2
            for k in range(buf.shape[0]):
                buf[k, r:, :] = jnp.zeros((r, buf.shape[2]), buf.dtype)

    barrier = pltpu.get_barrier_semaphore()

    def greet(i, carry):
        pd, pm = peer(i)
        pl.semaphore_signal(barrier, inc=1, device_id=(e, pd, pm), device_id_type=MESH)
        return carry
    lax.fori_loop(1, n, greet, 0)
    pl.semaphore_signal(barrier, inc=1, device_id=(1 - e, d, m), device_id_type=MESH)
    pl.semaphore_wait(barrier, n)

    early[1].wait()
    early[2].wait()
    row_i = lax.broadcasted_iota(jnp.int32, (blk, 2 * QSLOT), 0)
    lane_i = lax.broadcasted_iota(jnp.int32, (blk, 2 * QSLOT), 1)
    limit = jnp.zeros((blk, 2 * QSLOT), jnp.int32)
    for b in range(blk):
        here = jnp.where(lane_i < QSLOT, lens_ref[2 * b], lens_ref[2 * b + 1])
        limit = jnp.where(row_i == b, here, limit)
    limit = jnp.where(is_query, limit, QSLOT)
    ids_buf[d] = jnp.where((lane_i & (QSLOT - 1)) >= limit, -1, ids_ref[0])
    send_dp("ids", ids_buf.at[d], ids_buf.at[d], ids_buf, both=True)

    early[0].wait()
    fold = width // 2
    for i in range(2):
        kv[i, m, d, :, 0:hw] = mixed_f[1 + i, 0:fold].astype(BF16)
        kv[i, m, d, :, hw:] = mixed_f[1 + i, fold:].astype(BF16)

    def kv_copy(i, src, sem, where):
        piece = kv.at[i, m, src]
        return pltpu.make_async_remote_copy(
            src_ref=piece, dst_ref=piece, send_sem=kv_send.at[i], recv_sem=sem, device_id=where, device_id_type=MESH
        )

    def partner(k):
        if nd != 4:
            return lax.rem(d + k, nd)
        return (d + 1 - 2 * lax.rem(d, 2), d + 2 - 4 * (d // 2), 3 - d)[k - 1]

    def kv_to_dp(i):
        for k in range(1, nd):
            kv_copy(i, d, kv_recv.at[i, d], (e, lax.rem(d + k, nd), m)).start()

    def kv_to_mp(i, src):
        for k in range(1, nm):
            kv_copy(i, src, kv_spread.at[i], (e, d, lax.rem(m + k, nm))).start()

    def kv_from_dp(i, k):
        src = partner(k)
        pltpu.make_async_copy(kv.at[i, m, src], kv.at[i, m, src], kv_recv.at[i, src]).wait()
        return src

    def kv_wait(i):
        view = kv.at[i, pl.ds(0, nm - 1)]
        pltpu.make_async_copy(view, view, kv_spread.at[i]).wait()

    def kv_left():
        for i in range(2):
            view = kv.at[i, pl.ds(0, nm - 1)]
            pltpu.make_async_copy(view, view, kv_send.at[i]).wait()
            view = kv.at[i, 0, pl.ds(0, nd - 1)]
            pltpu.make_async_copy(view, view, kv_send.at[i]).wait()
    started.append(kv_left)

    def projection(i, g, k):
        both = kv[i, g, k]
        return jnp.concatenate([both[:, 0:hw], both[:, hw:]], axis=0)

    kv_to_dp(0)
    kv_to_mp(0, d)
    wq[...] = mixed_f[0].astype(BF16)

    early[3].wait()
    gain0, shift0 = norms_ref[0], norms_ref[1]
    for t in range(tiles):
        table_loads[t].wait()

        def to_low(i, carry):
            at = pl.ds(pl.multiple_of(t * vt + i * BLOCK, BLOCK), BLOCK)
            emb[at, :] = stage[at, :].astype(BF16)
            return carry
        lax.fori_loop(0, vt // BLOCK, to_low, 0)

    drain("ids", ids_buf, recv_sem, nd - 1, both=True)
    ids_all = jnp.concatenate([ids_buf[k] for k in range(nd)], axis=0) - base
    cls = jnp.concatenate([ids_all[:, 0:1], ids_all[:, QSLOT : QSLOT + 1]], axis=0)
    hot_at = 2 * heads
    lows[pl.ds(hot_at, c), :] = (cls == lax.broadcasted_iota(jnp.int32, (c, rows), 1)).astype(BF16)

    def pick(t, total):
        at = pl.ds(pl.multiple_of(t * vt, vt), vt)
        return total + nn(lows[pl.ds(hot_at, c), at], emb[at, :])
    found = lax.fori_loop(0, tiles, pick, jnp.zeros((c, size), F32))
    found_hat, found_r = slab_norm([found], size)
    found_at[...] = found_hat[0]
    owned = jnp.logical_and(cls >= 0, cls < rows)
    found = jnp.where(owned, found_hat[0] * gain0 + shift0, 0.0).astype(BF16)
    for k in range(nd):
        rows_src[k] = found[:, k * width : (k + 1) * width]
    rows_buf[me] = rows_src[d]
    send_all("rows", lambda pd, pm: rows_src.at[pd], rows_buf.at[me], rows_buf)

    for k in range(1, nd):
        kv_to_mp(0, kv_from_dp(0, k))
    flag = jnp.where(is_query, 1, 0)
    for b in range(nb):
        row = ids_all[b : b + 1, :]
        high, low = row >> 7, row & 127
        lane_b = lax.broadcasted_iota(jnp.int32, (16, 2 * QSLOT), 1)
        is_high = lax.broadcasted_iota(jnp.int32, (16, 2 * QSLOT), 0) == high
        left = [jnp.logical_and(is_high, (lane_b >> 7) * flag == s * flag) for s in range(2)]
        left = jnp.concatenate([item.astype(BF16) for item in left], axis=0)
        right = (lax.broadcasted_iota(jnp.int32, (128, 2 * QSLOT), 0) == low).astype(BF16)
        xs[b] = nt(left, right)
    for t in range(rows // 128):
        for s in range(2):
            counts[s * nb : (s + 1) * nb, t * 128 : (t + 1) * 128] = xs[:, s * 16 + t, :]

    kv_to_dp(1)

    def normalize(i, carry):
        at = pl.ds(pl.multiple_of(i * BLOCK, BLOCK), BLOCK)
        x = emb[at, :].astype(F32)
        x = x - jnp.mean(x, -1, keepdims=True)
        r = lax.rsqrt(jnp.mean(x * x, -1, keepdims=True) + eps_norm)
        hid[at, :] = (x * r * gain0 + shift0).astype(BF16)
        return carry
    lax.fori_loop(0, rows // BLOCK, normalize, 0)
    for i, (src, dst) in enumerate(((table_hbm, table_keep), (first_hbm, first_keep), (second_hbm, second_keep))):
        keep = pltpu.make_async_copy(src, dst, keep_sem.at[i])
        keep.start()
        started.append(keep.wait)
    for item in early[4:]:
        item.wait()
    wo[...] = out_f[...].astype(BF16)
    wi[...] = inner_f[...].astype(BF16)
    wt[...] = outer_f[...].astype(BF16)

    drain("rows", rows_buf, recv_sem, n - 1)
    mine = sum(rows_buf[k].astype(F32) for k in range(n))
    mine_low = mine.astype(BF16)
    q_buf[me] = nn(mine_low, wq[...]).astype(BF16)
    send_all("q", lambda pd, pm: q_buf.at[me], q_buf.at[me], q_buf)

    lane_h = lax.broadcasted_iota(jnp.int32, (nb, hw), 1) // HEAD

    def expand(x):
        return jnp.concatenate(
            [
                jnp.where(lane_h == j, x[s * nb : (s + 1) * nb], jnp.zeros((), x.dtype))
                for s in range(2)
                for j in range(hm)
            ],
            axis=0,
        )

    def collapse(x):
        out = []
        for s in range(2):
            parts = [x[s * half + j * nb : s * half + (j + 1) * nb] for j in range(hm)]
            total = parts[0]
            for j in range(1, hm):
                total = jnp.where(lane_h == j, parts[j], total)
            out.append(total)
        return jnp.concatenate(out, axis=0)

    def to_rows(cols):
        return jnp.concatenate([cols[j][s * nb : (s + 1) * nb] for s in range(2) for j in range(hm)], axis=0)

    def to_cols(x):
        return [
            jnp.concatenate([x[s * half + j * nb : s * half + (j + 1) * nb] for s in range(2)], axis=0)
            for j in range(hm)
        ]

    def over_heads(cols):
        lane = lax.broadcasted_iota(jnp.int32, (c, hw), 1) // HEAD
        out = jnp.broadcast_to(cols[0], (c, hw))
        for j in range(1, hm):
            out = jnp.where(lane == j, cols[j], out)
        return out

    def with_cols(x, cols):
        tail = lax.broadcasted_iota(jnp.int32, (c, HEAD), 1)
        extra = jnp.zeros((c, HEAD), F32)
        for k, item in enumerate(cols):
            extra = jnp.where(tail == k, item.astype(F32), extra)
        return jnp.concatenate([x, extra.astype(x.dtype)], axis=1)

    blank = jnp.zeros((c, hw), BF16)
    drain("q", q_buf, recv_sem, n - 1)
    kv_wait(0)
    queries = []
    for g in range(nm):
        q = sum(q_buf[k * nm + g].astype(F32) for k in range(nd)).astype(BF16)
        queries.append(q)
        wide = expand(q)
        for k in range(nd):
            basis[pl.ds(g * group, group), k * width : (k + 1) * width] = nt(wide, projection(0, g, k)).astype(BF16)
    q_mine = queries[0]
    for g in range(1, nm):
        q_mine = jnp.where(m == g, queries[g], q_mine)

    acc[...] = jnp.zeros_like(acc)
    tops[...] = jnp.zeros_like(tops)
    lane_of_tile = lax.broadcasted_iota(jnp.int32, (heads, 8), 1)

    def weigh(t, carry):
        top, total = carry
        at = pl.ds(pl.multiple_of(t * vt, vt), vt)
        s = nt(basis[pl.ds(0, heads), :], hid[at, :]) * scale
        places = [
            (g * group + sl * half + j * nb, pl.ds(sl * nb, nb)) for g in range(nm) for sl in range(2) for j in range(hm)
        ]
        s = [jnp.where(counts[of, at] > 0, s[lo : lo + nb], -1e30) for lo, of in places]
        best = [jnp.maximum(top[lo : lo + nb], jnp.max(x, -1, keepdims=True)) for x, (lo, of) in zip(s, places)]
        sums = []
        for x, high, (lo, of) in zip(s, best, places):
            x = counts[of, at] * jnp.exp(x - high)
            lows[lo : lo + nb, at] = x.astype(BF16)
            sums.append(jnp.sum(x, -1, keepdims=True))
        best = jnp.concatenate(best, axis=0)
        keep = jnp.exp(top - best)
        acc[...] = acc[...] * keep + nn(lows[pl.ds(0, heads), at], hid[at, :])
        tops[...] = jnp.where(lane_of_tile == t, best, tops[...])
        return best, total * keep + jnp.concatenate(sums, axis=0)
    top, total = lax.fori_loop(
        0, tiles, weigh, (jnp.full((heads, 1), -1e30, F32), jnp.zeros((heads, 1), F32)), unroll=UNROLL
    )

    def stat_slab(cols):
        lane = lax.broadcasted_iota(jnp.int32, (c, 128), 1)
        out = jnp.zeros((c, 128), F32)
        for k, item in enumerate(cols):
            out = jnp.where(lane == k, item, out)
        return out

    for g in range(nm):
        at = slice(g * group, (g + 1) * group)
        z_src[g] = acc[at, :].astype(BF16)
        stat_src[g] = stat_slab(to_cols(top[at]) + to_cols(total[at]))
    stat_buf[m] = stat_src[m]
    z_mp[m] = z_src[m]
    send_mp("stat", stat_src, stat_buf.at[m], stat_buf)
    send_mp("z", z_src, z_mp.at[m], z_mp)

    def combine(peaks, sums):
        best = peaks[0]
        for item in peaks[1:]:
            best = jnp.maximum(best, item)
        factor = [jnp.exp(item - best) for item in peaks]
        return best, factor, sum(f * item for f, item in zip(factor, sums))

    drain("stat", stat_buf, recv_sem, nm - 1)
    stats = [stat_buf[g] for g in range(nm)]
    near = [combine([x[:, j : j + 1] for x in stats], [x[:, hm + j : hm + j + 1] for x in stats]) for j in range(hm)]
    scales = [to_rows([near[j][1][g] for j in range(hm)]) for g in range(nm)]
    for k in range(1, nd):
        kv_from_dp(1, k)
    drain("z", z_mp, recv_sem, nm - 1)
    z_near = sum(z_mp[g].astype(F32) * scales[g] for g in range(nm))
    att = 0.0
    for k in range(nd):
        att = att + nn(z_near[:, k * width : (k + 1) * width].astype(BF16), projection(1, m, k))
    cols = [piece for j in range(hm) for piece in split_low(near[j][0], 3)]
    cols += [piece for j in range(hm) for piece in split_low(near[j][2], 2)]
    att_buf[d] = with_cols(collapse(att).astype(BF16), cols)
    send_dp("att", att_buf.at[d], att_buf.at[d], att_buf)

    drain("att", att_buf, recv_sem, nd - 1)
    far = []
    slabs = [att_buf[k, :, hw:].astype(F32) for k in range(nd)]
    for j in range(hm):
        far.append(combine([joined(x, 3 * j, 3) for x in slabs], [joined(x, 3 * hm + 2 * j, 2) for x in slabs]))
    top_all = [item[0] for item in far]
    inv_all = [jnp.where(x > 0, 1.0 / jnp.where(x > 0, x, 1.0), 0.0) for _, _, x in far]
    parts = [[f * inv for f in item[1]] for item, inv in zip(far, inv_all)]
    att = sum(att_buf[k, :, 0:hw].astype(F32) * over_heads([parts[j][k] for j in range(hm)]) for k in range(nd))
    att_low = att.astype(BF16)
    part = nn(att_low, wo[...]) + jnp.where(m == 0, mine, 0.0)
    cols = [piece for item in top_all for piece in split_low(item, 3)]
    cols += [piece for item in inv_all for piece in split_low(item, 2)]
    out_buf[me] = with_cols(part.astype(BF16), cols)
    send_all("out", lambda pd, pm: out_buf.at[me], out_buf.at[me], out_buf)

    def slabs_of(buf):
        return [sum(buf[k * nm + g, :, 0:width].astype(F32) for g in range(nm)) for k in range(nd)]

    def own(slabs):
        out = slabs[0]
        for k in range(1, nd):
            out = jnp.where(d == k, slabs[k], out)
        return out

    def norm_rows(i):
        row = norms_ref[i]
        return [row[:, k * width : (k + 1) * width] for k in range(nd)]

    drain("out", out_buf, recv_sem, n - 1)
    hats1, r1 = slab_norm(slabs_of(out_buf), size)
    gains1, shifts1 = norm_rows(2), norm_rows(3)
    normed = [h * g + s for h, g, s in zip(hats1, gains1, shifts1)]
    normed_mine = own(normed)
    normed_low = normed_mine.astype(BF16)

    inner_buf[d] = nn(normed_low, wi[...]).astype(BF16)
    send_dp("inner", inner_buf.at[d], inner_buf.at[d], inner_buf)
    kv_to_mp(1, d)
    for k in range(1, nd):
        kv_to_mp(1, lax.rem(d + k, nd))
    for g in range(nm):
        stat = out_buf[g, :, hw:].astype(F32)
        best = to_rows([joined(stat, 3 * j, 3) for j in range(hm)])
        inv = to_rows([joined(stat, 3 * hm + 2 * j, 2) for j in range(hm)])
        at = pl.ds(g * group, group)
        factors[at, :] = jnp.exp(tops[at, :] - best) * inv
    z = z_near * to_rows([own(parts[j]) for j in range(hm)])
    for k in range(nd):
        z_slab[k] = z[:, k * width : (k + 1) * width].astype(BF16)
    z_buf[d] = z_slab[d]
    drain("inner", inner_buf, recv_sem, nd - 1)
    inner = sum(inner_buf[k].astype(F32) for k in range(nd))
    cdf = 0.5 * (1.0 + lax.erf(inner * (0.5 ** 0.5)))
    act = (inner * cdf).astype(BF16)
    slope = cdf + inner * jnp.exp(-0.5 * inner * inner) * ((0.5 / math.pi) ** 0.5)
    outer_buf[me] = (nt(act, wt[...]) + jnp.where(m == 0, normed_mine, 0.0)).astype(outer_buf.dtype)
    send_all("outer", lambda pd, pm: outer_buf.at[me], outer_buf.at[me], outer_buf)
    drain("outer", outer_buf, recv_sem, n - 1)
    send_dp_each("z_dp", z_slab, z_buf.at[d], z_buf)
    hats2, r2 = slab_norm(slabs_of(outer_buf), size)
    gains2, shifts2 = norm_rows(4), norm_rows(5)
    for k in range(nd):
        final_buf[e, k] = hats2[k] * gains2[k] + shifts2[k]
    final_at = PHASES.index("final")
    final_copy = pltpu.make_async_remote_copy(
        src_ref=final_buf.at[e], dst_ref=final_buf.at[e], send_sem=send_sem.at[final_at], recv_sem=recv_sem.at[final_at],
        device_id=(1 - e, d, m), device_id_type=MESH,
    )
    final_copy.start()
    final_copy.wait_recv()
    started.append(final_copy.wait_send)

    qs = [final_buf[0, k] for k in range(nd)]
    ps = [final_buf[1, k][0:nb] for k in range(nd)]
    q_r = lax.rsqrt(sum(jnp.sum(x * x, -1, keepdims=True) for x in qs) + eps_norm)
    p_r = lax.rsqrt(sum(jnp.sum(x * x, -1, keepdims=True) for x in ps) + eps_norm)
    q_hat, p_hat = [x * q_r for x in qs], [x * p_r for x in ps]

    def d_sims(left, right, axis, negative, positive, used):
        sims = sum(exact_nt(a, b) for a, b in zip(left, right)) / logit_divisor
        is_positive = lax.broadcasted_iota(jnp.int32, sims.shape, axis) == positive
        sims = jnp.where(jnp.logical_and(negative == 1.0, jnp.logical_not(is_positive)), -1e30, sims)
        best = jnp.max(sims, axis, keepdims=True)
        log_total = best + jnp.log(jnp.sum(jnp.exp(sims - best), axis, keepdims=True))
        target = jnp.sum(jnp.where(is_positive, sims, 0.0), axis, keepdims=True)
        weight = used.astype(F32)
        count = jnp.maximum(jnp.sum(weight, 1 - axis, keepdims=True), 1.0)
        loss = jnp.sum(weight * (log_total - target), 1 - axis, keepdims=True) / count
        grad = (jnp.exp(sims - log_total) - is_positive.astype(F32)) * (weight / count / logit_divisor)
        return loss, grad

    at_row = lax.broadcasted_iota(jnp.int32, (c, c), 0)
    from_query = lax.broadcasted_iota(jnp.int32, (c, c), 1)
    order = (from_query == 2 * (at_row % nb) + at_row // nb).astype(BF16)
    negative = negative_ref[...].astype(F32).astype(BF16)
    column, line = lax.broadcasted_iota(jnp.int32, (c, 1), 0), lax.broadcasted_iota(jnp.int32, (1, c), 1)
    positive = [jnp.zeros((c, 1), jnp.int32), jnp.zeros((1, c), jnp.int32)]
    used = [jnp.zeros((c, 1), jnp.int32), jnp.zeros((1, c), jnp.int32)]
    for k in range(c):
        query = 2 * (k % nb) + k // nb
        for i, place in enumerate((column, line)):
            positive[i] = jnp.where(place == k, positive_ref[query], positive[i])
            used[i] = jnp.where(place == k, used_ref[query], used[i])
    loss, grad_q = d_sims(q_hat, p_hat, 1, nt(order, negative), positive[0], used[0])
    _, grad_p = d_sims(p_hat, q_hat, 0, nt(negative, order), positive[1], used[1])

    def unit_back(hats, r, grads):
        along = sum(jnp.sum(g * h, -1, keepdims=True) for g, h in zip(grads, hats))
        return [r * (g - h * along) for g, h in zip(grads, hats)]

    d_q = unit_back(q_hat, q_r, [exact_nn(grad_q, x) for x in p_hat])
    d_p = unit_back(p_hat, p_r, [exact_nn(grad_p, x) for x in q_hat])
    d_final = [
        jnp.where(is_query, a, jnp.concatenate([b, jnp.zeros_like(b)], axis=0)) for a, b in zip(d_q, d_p)
    ]

    d_second, d_gain2, d_shift2 = slab_norm_back(hats2, r2, d_final, gains2, size)
    d_outer = own(d_second).astype(BF16)
    d_act_buf[d] = nn(d_outer, wt[...]).astype(BF16)
    send_dp("d_act", d_act_buf.at[d], d_act_buf.at[d], d_act_buf)
    g_outer = tn(d_outer, act)
    g_outer_ref[...] = g_outer
    drain("d_act", d_act_buf, recv_sem, nd - 1)
    d_inner = (sum(d_act_buf[k].astype(F32) for k in range(nd)) * slope).astype(BF16)
    d_in_buf[me] = nt(d_inner, wi[...]).astype(d_in_buf.dtype)
    send_all("d_in", lambda pd, pm: d_in_buf.at[me], d_in_buf.at[me], d_in_buf)
    g_inner = tn(normed_low, d_inner)
    g_inner_ref[...] = g_inner
    drain("d_in", d_in_buf, recv_sem, n - 1)
    d_normed = [a + b for a, b in zip(d_second, slabs_of(d_in_buf))]
    d_first, d_gain1, d_shift1 = slab_norm_back(hats1, r1, d_normed, gains1, size)
    d_first_mine = own(d_first)
    d_attn = d_first_mine.astype(BF16)

    part = nt(d_attn, wo[...])
    along = att * part
    lane = lax.broadcasted_iota(jnp.int32, (c, hw), 1) // HEAD
    cols = []
    for j in range(hm):
        cols += split_low(jnp.sum(jnp.where(lane == j, along, 0.0), -1, keepdims=True), 2)
    d_att_buf[me] = with_cols(part.astype(BF16), cols)
    send_all("d_att", lambda pd, pm: d_att_buf.at[me], d_att_buf.at[me], d_att_buf)
    g_out = tn(att_low, d_attn)
    g_out_ref[...] = g_out
    squares = sum(jnp.sum(g * g, 0, keepdims=True) for g in (g_outer, g_inner))
    squares = jnp.sum(squares, -1, keepdims=True) + jnp.sum(jnp.sum(g_out * g_out, 0, keepdims=True), -1, keepdims=True)

    kv_wait(1)
    drain("d_att", d_att_buf, recv_sem, n - 1)
    d_atts = []
    for g in range(nm):
        slab = sum(d_att_buf[k * nm + g].astype(F32) for k in range(nd))
        d_att = slab[:, 0:hw].astype(BF16)
        d_atts.append(d_att)
        col[pl.ds(g * group, group), :] = to_rows(
            [joined(slab, hw + 2 * j, 2) for j in range(hm)]
        )
        wide = expand(d_att)
        for k in range(nd):
            basis[pl.ds(heads + g * group, group), k * width : (k + 1) * width] = nt(wide, projection(1, g, k)).astype(BF16)
    d_att_mine = d_atts[0]
    for g in range(1, nm):
        d_att_mine = jnp.where(m == g, d_atts[g], d_att_mine)
    acc[...] = jnp.zeros_like(acc)

    def backward(t, carry):
        at = pl.ds(pl.multiple_of(t * vt, vt), vt)
        d_probs = nt(basis[pl.ds(heads, heads), :], hid[at, :])
        probs = lows[pl.ds(0, heads), at].astype(F32) * jnp.sum(
            jnp.where(lane_of_tile == t, factors[...], 0.0), -1, keepdims=True
        )
        d_scores = (probs * (d_probs - col[...]) * scale).astype(BF16)
        lows[pl.ds(0, heads), at] = d_scores
        lows[pl.ds(heads, heads), at] = probs.astype(BF16)
        acc[...] += nn(d_scores, hid[at, :])
        return carry
    lax.fori_loop(0, tiles, backward, 0, unroll=UNROLL)

    for g in range(nm):
        y = acc[pl.ds(g * group, group), :].astype(BF16)
        dq = jnp.zeros((group, hw), F32)
        for k in range(nd):
            dq = dq + nn(y[:, k * width : (k + 1) * width], projection(0, g, k))
        y_src[g] = y
        dq_src[g] = collapse(dq).astype(BF16)
        send_group("dq", g, dq_src.at[g], dq_buf.at[me], dq_buf)
    dq_buf[me] = dq_src[m]
    y_mp[m] = y_src[m]
    send_mp("y", y_src, y_mp.at[m], y_mp)

    lane_t = 128

    def spread(t, carry):
        at = pl.ds(pl.multiple_of(t * lane_t, lane_t), lane_t)
        stage[at, :] = tn(lows[pl.ds(0, 2 * heads), at], basis[pl.ds(0, 2 * heads), :])
        return carry
    lax.fori_loop(0, rows // lane_t, spread, 0, unroll=3)

    drain("dq", dq_buf, recv_sem, n - 1)
    dq_mine = sum(dq_buf[k].astype(F32) for k in range(n)).astype(BF16)
    d_rows_buf[me] = (nt(dq_mine, wq[...]) + jnp.where(m == 0, d_first_mine, 0.0)).astype(d_rows_buf.dtype)
    send_all("d_rows", lambda pd, pm: d_rows_buf.at[me], d_rows_buf.at[me], d_rows_buf)
    g_q = tn(mine_low, dq_mine)
    drain("z_dp", z_buf, recv_sem, nd - 1)
    z_mine = sum(z_buf[k].astype(F32) for k in range(nd)).astype(BF16)
    g_v = tn(z_mine, expand(d_att_mine))
    drain("y", y_mp, recv_sem, nm - 1)
    y = sum(y_mp[g].astype(F32) for g in range(nm))
    for k in range(nd):
        y_slab[k] = y[:, k * width : (k + 1) * width].astype(BF16)
    y_buf[d] = y_slab[d]
    send_dp_each("y_dp", y_slab, y_buf.at[d], y_buf)
    fold8 = lambda v: jnp.sum(v.reshape(v.shape[0] // 8, 8, size), 0)

    def table_back(t, carry):
        d_gain, d_shift = carry
        at = pl.ds(pl.multiple_of(t * BLOCK, BLOCK), BLOCK)
        dy = stage[at, :]
        x = emb[at, :].astype(F32)
        x = x - jnp.mean(x, -1, keepdims=True)
        r = lax.rsqrt(jnp.mean(x * x, -1, keepdims=True) + eps_norm)
        hat = x * r
        scaled = dy * gain0
        mean = jnp.mean(scaled, -1, keepdims=True)
        along = jnp.mean(scaled * hat, -1, keepdims=True)
        stage[at, :] = r * (scaled - mean - hat * along)
        return d_gain + fold8(dy * hat), d_shift + fold8(dy)
    zero = jnp.zeros((8, size), F32)
    d_gain, d_shift = lax.fori_loop(0, rows // BLOCK, table_back, (zero, zero))

    drain("d_rows", d_rows_buf, recv_sem, n - 1)
    d_rows = jnp.concatenate(slabs_of(d_rows_buf), axis=1)
    d_rows = jnp.where(owned, d_rows, 0.0)
    hat = found_at[...]
    d_found, extra_gain, extra_shift = slab_norm_back([hat], found_r, [d_rows], [gain0], size)
    d_found = jnp.where(owned, d_found[0], 0.0).astype(BF16)

    def table_add(t, square):
        at = pl.ds(pl.multiple_of(t * lane_t, lane_t), lane_t)
        grad = stage[at, :] + tn(lows[pl.ds(hot_at, c), at], d_found)
        stage[at, :] = grad
        return square + fold8(grad * grad)
    square = lax.fori_loop(0, rows // lane_t, table_add, zero, unroll=3)
    d_gain = jnp.sum(d_gain, 0, keepdims=True) + extra_gain[0]
    d_shift = jnp.sum(d_shift, 0, keepdims=True) + extra_shift[0]
    drain("y_dp", y_buf, recv_sem, nd - 1)
    y_mine = sum(y_buf[k].astype(F32) for k in range(nd)).astype(BF16)
    g_k = tn(y_mine, expand(q_mine))
    for i, g in enumerate((g_q, g_k, g_v)):
        g_mixed_ref[i] = g
    total = sum(jnp.sum(g * g, 0, keepdims=True) for g in (g_q, g_k, g_v))
    squares = squares + jnp.sum(total, -1, keepdims=True)
    squares = squares + jnp.sum(jnp.sum(square, 0, keepdims=True), -1, keepdims=True)
    chunks = size // 128
    lines = [v[:, k * 128 : (k + 1) * 128] for v in (d_gain, d_shift) for k in range(chunks)]
    lines.append(jnp.broadcast_to(squares, (1, 128)))
    lines.append(jnp.zeros((16 - len(lines), 128), F32))
    sums_buf[me] = jnp.concatenate(lines, axis=0)

    def send_sums(i, carry):
        pd, pm = peer(i)
        remote("sums", sums_buf.at[me], sums_buf.at[me], (e, pd, pm))
        return carry
    lax.fori_loop(1, n, send_sums, 0)
    sent.append(("sums", sums_buf, n - 1, True))
    drain("sums", sums_buf, recv_sem, n - 1, both=True)
    totals = sum(sums_buf[k] for k in range(n))
    firsts = [jnp.concatenate([totals[v * chunks + k : v * chunks + k + 1] for k in range(chunks)], axis=1) for v in range(2)]
    squares = totals[2 * chunks : 2 * chunks + 1, 0:1]
    for i in range(2):
        g_norms_ref[i : i + 1, :] = firsts[i]
        squares = squares + jnp.sum(firsts[i] * firsts[i], -1, keepdims=True)
    for i, slabs in enumerate((d_gain1, d_shift1, d_gain2, d_shift2)):
        for k in range(nd):
            g_norms_ref[2 + i : 3 + i, k * width : (k + 1) * width] = slabs[k]
            squares = squares + jnp.sum(slabs[k] * slabs[k], -1, keepdims=True)
    norm_buf[e] = jnp.broadcast_to(squares, (8, 128))
    norm_at = PHASES.index("norm")
    norm_copy = pltpu.make_async_remote_copy(
        src_ref=norm_buf.at[e], dst_ref=norm_buf.at[e], send_sem=send_sem.at[norm_at], recv_sem=recv_sem.at[norm_at],
        device_id=(1 - e, d, m), device_id_type=MESH,
    )
    norm_copy.start()
    norm_copy.wait_recv()
    started.append(norm_copy.wait_send)
    grad_norm = jnp.sqrt(norm_buf[0] + norm_buf[1])
    small_ref[...] = jnp.where(
        lax.broadcasted_iota(jnp.int32, (8, 128), 0) == 0, jnp.broadcast_to(loss, (8, 128)), grad_norm
    )

    finish()


def kernel_gradients(
    token_ids, query_lengths, negative_mask, positive_index, used_rows, table, w_mixed, w_out, w_inner, w_outer, norm_params, table_m, table_v
):
    nd, nm = lax.axis_size("dp"), lax.axis_size("mp")
    n = nd * nm
    blk = token_ids.shape[1]
    _, rows, size = table.shape
    width, hw, ff = w_mixed.shape[1], w_mixed.shape[3], w_inner.shape[2]
    hm = hw // HEAD
    nb = nd * blk
    c = 2 * nb
    group, heads = hm * c, nm * hm * c
    S = jax.ShapeDtypeStruct
    outs = (
        S((8, 128), F32), S((rows, size), F32), S((3, width, hw), F32),
        S((hw, width), F32), S((width, ff), F32), S((width, ff), F32), S((8, size), F32),
    ) + (S((rows, size), F32),) * 3
    vm, hb = pl.BlockSpec(memory_space=pltpu.VMEM), pl.BlockSpec(memory_space=pltpu.HBM)
    V = pltpu.VMEM
    wide = hw + HEAD
    operands = (
        w_mixed[0].swapaxes(0, 1), token_ids, query_lengths, norm_params.swapaxes(0, 1), w_out[0], w_inner[0], w_outer[0].T,
        positive_index, used_rows, negative_mask.T, table[0], table_m[0], table_v[0],
    )
    local = [V] * 2 + [pltpu.SMEM] + [V] * 4 + [pltpu.SMEM] * 2 + [V]
    scratch = [space(item.shape, item.dtype) for space, item in zip(local, operands)] + [
        V((rows, size), BF16), V((rows, size), BF16),
        V((2 * heads + c, rows), BF16), V((2 * heads, size), BF16), V((c, rows), F32), V((nb, 32, 128), F32),
        V((heads, size), F32), V((heads, 1), F32), V((heads, 8), F32), V((heads, 8), F32), V((c, size), F32),
        V((width, hw), BF16), V((hw, width), BF16), V((width, ff), BF16), V((width, ff), BF16), V((2, nm, nd, width // 2, 2 * hw), BF16),
        V((nd, blk, 2 * QSLOT), jnp.int32),
        V((nd, c, width), BF16), V((n, c, width), BF16), V((n, c, hw), BF16),
        V((nm, c, 128), F32), V((nm, c, 128), F32), V((nd, c, wide), BF16),
        V((nm, group, size), BF16), V((nm, group, size), BF16), V((nd, group, width), BF16), V((nd, group, width), BF16),
        V((n, c, wide), BF16), V((nd, c, ff), BF16), V((n, c, width), BF16), V((2, nd, c, width), F32),
        V((nd, c, ff), BF16), V((n, c, width), BF16), V((n, c, wide), BF16), V((nm, c, hw), BF16), V((n, c, hw), BF16),
        V((nm, group, size), BF16), V((nm, group, size), BF16), V((nd, group, width), BF16), V((nd, group, width), BF16),
        V((n, c, width), BF16),
        V((n, 16, 128), F32), V((2, 8, 128), F32),
        pltpu.SemaphoreType.DMA((len(PHASES),)), pltpu.SemaphoreType.DMA((len(PHASES),)),
        pltpu.SemaphoreType.DMA((2,)), pltpu.SemaphoreType.DMA((2, nd)), pltpu.SemaphoreType.DMA((2,)),
        pltpu.SemaphoreType.DMA((rows // 384,)), pltpu.SemaphoreType.DMA((3,)), pltpu.SemaphoreType.DMA((10,)),
    ]
    small, g_table, g_mixed, g_out, g_inner, g_outer, g_norms, *kept = pl.pallas_call(
        partial(grad_kernel, (nd, nm, blk, rows, width, size, hm, ff)),
        out_shape=outs,
        in_specs=[hb] * len(operands),
        out_specs=(vm,) * 10,
        scratch_shapes=scratch,
        compiler_params=pltpu.CompilerParams(collective_id=ENTRY_ID, has_side_effects=True, vmem_limit_bytes=27 << 20),
        name="gradients",
    )(*(pltpu.with_memory_space_constraint(item, pltpu.HBM) for item in operands))
    return small, (g_table, g_mixed, g_out, g_inner, g_outer, g_norms), kept


RING = 3
PIECE = 192


def adam_kernel(rates, count_ref, small_ref, *refs):
    k = len(rates)
    operands = [refs[4 * i : 4 * i + 4] for i in range(k)]
    results = [refs[4 * k + 3 * i : 4 * k + 3 * i + 3] for i in range(k)]
    refs = refs[7 * k :]
    ring, ring_sem, own_sem, buffers = refs[:3], refs[3], refs[4], refs[5:]
    norm = small_ref[1:2, 0:1]
    clip = jnp.minimum(1.0, clip_limit / (norm + 1e-06))
    count = jnp.full((1, 1), count_ref[0], jnp.int32).astype(F32)
    fix_one = 1.0 - jnp.exp(count * math.log(beta_one))
    fix_two = 1.0 - jnp.exp(count * math.log(beta_two))
    inv_one, inv_two = 1.0 / fix_one, 1.0 / fix_two
    copies, in_slot, used, turn = [], [None] * RING, 0, 0

    def update(i, at, targets, to):
        grad, weight, first, second = (ref[at] for ref in operands[i])
        rate, decay = rates[i]
        grad = grad * clip
        first = beta_one * first + (1.0 - beta_one) * grad
        second = beta_two * second + ((1.0 - beta_two) * grad) * grad
        step = first * inv_one / (jnp.sqrt(second * inv_two) + adam_eps)
        if decay:
            step = step + decay * weight
        for ref, value in zip(targets, (weight - rate * step, first, second)):
            ref[to] = value

    def send(src, dst, sem):
        copy = pltpu.make_async_copy(src, dst, sem)
        copy.start()
        return copy

    for i in range(k):
        shape = operands[i][1].shape
        if len(shape) == 2 and shape[1] == ring[0].shape[2]:
            for start in range(0, shape[0], PIECE):
                slot = turn % RING
                turn += 1
                if in_slot[slot]:
                    for copy in in_slot[slot]:
                        copy.wait()

                def block(b, carry):
                    at = pl.ds(pl.multiple_of(b * 32, 32), 32)
                    update(i, pl.ds(pl.multiple_of(start + b * 32, 32), 32), [ref.at[slot] for ref in ring], at)
                    return carry
                lax.fori_loop(0, PIECE // 32, block, 0, unroll=True)
                in_slot[slot] = [
                    send(ring[j].at[slot], results[i][j].at[pl.ds(start, PIECE)], ring_sem.at[slot, j]) for j in range(3)
                ]
            continue
        mine = buffers[3 * used : 3 * used + 3]
        if len(shape) == 3:
            for j in range(shape[0]):
                update(i, j, mine, j)
        else:
            update(i, slice(None), mine, slice(None))
        copies += [send(mine[j], results[i][j], own_sem.at[used, j]) for j in range(3)]
        used += 1
    for group in in_slot + [copies]:
        for copy in group or ():
            copy.wait()


def kernel_adam(step_count, small, grads, weights, firsts, seconds):
    k = len(weights)
    rates = tuple((0.5, 0.0) if i == k - 1 else (0.06, 0.01) for i in range(k))
    vm, sm = pl.BlockSpec(memory_space=pltpu.VMEM), pl.BlockSpec(memory_space=pltpu.SMEM)
    shapes = [jax.ShapeDtypeStruct(w.shape, F32) for w in weights for _ in range(3)]
    operands = [item for group in zip(grads, weights, firsts, seconds) for item in group]
    size = weights[0].shape[1]
    alone = [item for item in shapes if len(item.shape) == 3 or item.shape[1] != size]
    return pl.pallas_call(
        partial(adam_kernel, rates),
        out_shape=shapes,
        in_specs=[sm, vm] + [vm] * (4 * k),
        out_specs=[pl.BlockSpec(memory_space=pltpu.HBM)] * (3 * k),
        scratch_shapes=[pltpu.VMEM((RING, PIECE, size), F32)] * 3
        + [pltpu.SemaphoreType.DMA((RING, 3)), pltpu.SemaphoreType.DMA((len(alone) // 3, 3))]
        + [pltpu.VMEM(item.shape, F32) for item in alone],
        compiler_params=pltpu.CompilerParams(vmem_limit_bytes=12 << 20),
        name="adam",
    )(step_count, small, *operands)


def on_device(
    token_ids,
    query_lengths,
    negative_mask,
    positive_index,
    used_rows,
    step_count,
    table,
    w_mixed,
    w_out,
    w_inner,
    w_outer,
    norm_params,
    table_m,
    table_v,
    mixed_m,
    mixed_v,
    out_m,
    out_v,
    inner_m,
    inner_v,
    outer_m,
    outer_v,
    norms_m,
    norms_v,
):
    operands = (
        token_ids, query_lengths, negative_mask, positive_index, used_rows, table, w_mixed, w_out, w_inner, w_outer, norm_params
    )
    masters = (table, w_mixed, w_out, w_inner, w_outer, norm_params)
    firsts = (table_m, mixed_m, out_m, inner_m, outer_m, norms_m)
    seconds = (table_v, mixed_v, out_v, inner_v, outer_v, norms_v)
    if table.shape[1] % 384 == 0 and w_mixed.shape[1] % 64 == 0 and table.shape[1] <= 2048:
        small, grads, kept = kernel_gradients(*operands, table_m, table_v)

        def stored(tab, items):
            _, mixed, out, inner, outer, norm = items
            return tab, mixed[0].swapaxes(0, 1), out[0], inner[0], outer[0].T, norm.swapaxes(0, 1)

        grads = grads[:5] + (grads[5][0:6, None, :],)
        updated = kernel_adam(step_count, small, grads, *map(stored, kept, (masters, firsts, seconds)))
        back = (
            lambda x: x[None],
            lambda x: x.swapaxes(0, 1)[None],
            lambda x: x[None],
            lambda x: x[None],
            lambda x: x.T[None],
            lambda x: x.swapaxes(0, 1),
        )
        return (small[0, 0], small[1, 0]) + tuple(back[i // 3](item) for i, item in enumerate(updated))
    loss, grads = gradients(*operands)
    owner = (lax.axis_index("dp") == 0) & (lax.axis_index("mp") == 0)
    squares = jnp.where(owner, jnp.sum(grads[5] * grads[5]), 0.0)
    for grad in grads[:5]:
        squares = squares + jnp.sum(grad * grad)
    grad_norm = jnp.sqrt(lax.psum(squares, ("enc", "dp", "mp")))
    clip = jnp.minimum(1.0, clip_limit / (grad_norm + 1e-06))
    count = step_count[0].astype(F32)
    results = [loss, grad_norm]
    for index in range(6):
        rate, decay = (0.5, 0.0) if index == 5 else (0.06, 0.01)
        results.extend(
            adam_step(
                masters[index], grads[index][None] * clip, firsts[index], seconds[index], rate, decay, count
            )
        )
    return tuple(results)


def solution(mesh):
    table = P("enc", ("dp", "mp"), None)
    mixed = P("enc", "dp", None, "mp")
    columns = P("enc", "mp", "dp")
    units = P("enc", "dp", "mp")
    norms = P("enc", None, None)
    matrices = (table, mixed, columns, units, columns, norms)
    moments = tuple(spec for spec in matrices for _ in range(2))
    updated = tuple(spec for spec in matrices for _ in range(3))
    return jax.shard_map(
        on_device,
        mesh=mesh,
        in_specs=(P("enc", "dp", None), P("dp"), P(), P(), P(), P()) + matrices + moments,
        out_specs=(P(), P()) + updated,
        check_vma=False,
    )
```

```python
import math
from functools import partial

import jax
import jax.numpy as jnp
from jax import lax
from jax.experimental import pallas as pl
from jax.experimental.pallas import tpu as pltpu
from jax.sharding import PartitionSpec as P

HEAD = 64
QSLOT = 128
F32 = jnp.float32
BF16 = jnp.bfloat16

exact_arithmetic_level = lax.Precision.HIGHEST
eps_norm = 1e-06
logit_divisor = 0.05
clip_limit = 0.02
beta_one = 0.9
beta_two = 0.999
adam_eps = 1e-08


def layer_norm(x, gain, shift):
    centred = x - jnp.mean(x, -1, keepdims=True)
    spread = jnp.mean(centred * centred, -1, keepdims=True)
    return centred * lax.rsqrt(spread + eps_norm) * gain + shift


def mul(spec, a, b):
    return jnp.einsum(spec, a, b, preferred_element_type=F32)


def token_counts(ids, lens, is_query, base, rows):
    pos = jnp.arange(ids.shape[1])
    slot = pos // QSLOT
    limit = jnp.where(slot[None, :] == 0, lens[:, 0:1], lens[:, 1:2])
    within = (pos % QSLOT)[None, :] < limit
    same = slot[None, :] == jnp.arange(2)[:, None]
    allowed = jnp.where(is_query, same[:, None, :] & within[None], True)
    local = ids - base
    n_hi = -(-rows // 128)
    high = (local[..., None] >> 7) == jnp.arange(n_hi)
    low = (local[..., None] & 127) == jnp.arange(128)
    left = (allowed[..., None] & high[None]).astype(BF16)
    counts = mul("sbth,btl->sbhl", left, low.astype(BF16))
    return counts.reshape(2 * ids.shape[0], n_hi * 128)[:, :rows]


def contrast(queries, passages, negative_mask, positive_index, used_rows):
    question_direction_rows = queries * lax.rsqrt(
        jnp.sum(queries * queries, -1, keepdims=True) + eps_norm
    )
    document_direction_rows = passages * lax.rsqrt(
        jnp.sum(passages * passages, -1, keepdims=True) + eps_norm
    )
    pairwise_cosine_table = (
        jnp.dot(
            question_direction_rows, document_direction_rows.T, precision=exact_arithmetic_level
        )
        / logit_divisor
    )
    is_positive = jnp.arange(passages.shape[0])[None, :] == positive_index[:, None]
    excluded = (negative_mask == 1) & ~is_positive
    pairwise_cosine_table = jnp.where(excluded, -1e30, pairwise_cosine_table)
    top = jnp.max(pairwise_cosine_table, -1, keepdims=True)
    log_total = top[:, 0] + jnp.log(jnp.sum(jnp.exp(pairwise_cosine_table - top), -1))
    target = jnp.sum(jnp.where(is_positive, pairwise_cosine_table, 0.0), -1)
    weight = used_rows.astype(F32)
    return jnp.sum(weight * (log_total - target)) / jnp.maximum(jnp.sum(weight), 1.0)


def adam_step(weight, grad, first, second, rate, decay, count):
    first_new = beta_one * first + (1.0 - beta_one) * grad
    second_new = beta_two * second + (1.0 - beta_two) * grad * grad
    fix_one = 1.0 - jnp.power(beta_one, count)
    correction_second = 1.0 - jnp.power(beta_two, count)
    update = (
        first_new / fix_one / (jnp.sqrt(second_new / correction_second) + adam_eps) + decay * weight
    )
    return (weight - rate * update, first_new, second_new)


def slot_major(x):
    return x.reshape((x.shape[0] // 2, 2) + x.shape[1:]).swapaxes(0, 1).reshape(x.shape)


def gradients(
    token_ids, query_lengths, negative_mask, positive_index, used_rows, table, w_mixed, w_out, w_inner, w_outer, norm_params
):
    is_query = lax.axis_index("enc") == 0
    d, m = lax.axis_index("dp"), lax.axis_index("mp")
    n_mp = lax.axis_size("mp")
    rows, width = table.shape[1], w_mixed.shape[1]
    hm = w_out.shape[1] // HEAD
    scale = HEAD ** (-0.5)
    norms = norm_params[0]
    base = (d * n_mp + m) * rows

    ids = lax.all_gather(token_ids[0], "dp", axis=0, tiled=True)
    lens = lax.all_gather(query_lengths, "dp", axis=0, tiled=True).reshape(-1, 2)
    blocks = ids.shape[0]
    counts = token_counts(ids, lens, is_query, base, rows)
    cls_ids = jnp.concatenate([ids[:, 0], ids[:, QSLOT]]) - base
    cls_hot = cls_ids[:, None] == jnp.arange(rows)[None, :]

    def mine(x):
        return lax.dynamic_slice_in_dim(x, d * width, width, 1)

    wq, wk, wv = (w_mixed[0, :, i].astype(BF16).reshape(width, hm, HEAD) for i in range(3))
    wo = w_out[0].astype(BF16).reshape(hm, HEAD, width)
    wi, wt = w_inner[0].astype(BF16), w_outer[0].astype(BF16)

    embedded = lax.reduce_precision(table[0], 8, 7)
    hidden, hidden_back = jax.vjp(layer_norm, embedded, norms[0], norms[1])
    hid = hidden.astype(BF16)
    first_rows = lax.psum(
        jnp.dot(cls_hot.astype(F32), hidden, precision=exact_arithmetic_level), ("dp", "mp")
    )
    first_mine = mine(first_rows).astype(BF16)
    q = lax.psum(mul("ci,ihk->hck", first_mine, wq), "dp").astype(BF16)
    u = mul("hck,ihk->hci", q, wk).astype(BF16)
    u = lax.all_gather(lax.all_gather(u, "dp", axis=2, tiled=True), "mp", axis=0, tiled=True)
    scores = jnp.where(counts[None] > 0, mul("hci,vi->hcv", u, hid) * scale, -1e30)
    top = lax.pmax(jnp.max(scores, -1, keepdims=True), ("dp", "mp"))
    weight = counts[None] * jnp.exp(scores - top)
    probs = weight / lax.psum(jnp.sum(weight, -1, keepdims=True), ("dp", "mp"))
    probs_low = probs.astype(BF16)
    z = mul("hcv,vi->hci", probs_low, hid)
    z = lax.psum_scatter(z, "mp", scatter_dimension=0, tiled=True)
    z = lax.psum_scatter(z, "dp", scatter_dimension=2, tiled=True).astype(BF16)
    att = lax.psum(mul("hci,ihk->hck", z, wv), "dp")
    att_low = att.astype(BF16)
    out = lax.psum(mul("hck,hke->ce", att_low, wo), "mp")
    first_sum = first_rows + lax.all_gather(out, "dp", axis=1, tiled=True)
    normed, normed_back = jax.vjp(layer_norm, first_sum, norms[2], norms[3])
    normed_mine = mine(normed).astype(BF16)
    inner = lax.psum(mul("ci,if->cf", normed_mine, wi), "dp")
    act, act_back = jax.vjp(partial(jax.nn.gelu, approximate=False), inner)
    act = act.astype(BF16)
    outer = lax.psum(mul("cf,fe->ce", act, wt), "mp")
    second_sum = normed + lax.all_gather(outer, "dp", axis=1, tiled=True)
    final, final_back = jax.vjp(layer_norm, second_sum, norms[4], norms[5])
    both = lax.all_gather(final, "enc", axis=0)
    loss, loss_back = jax.vjp(
        partial(
            contrast,
            negative_mask=slot_major(negative_mask),
            positive_index=slot_major(positive_index),
            used_rows=slot_major(used_rows),
        ),
        both[0],
        both[1, :blocks],
    )
    d_queries, d_passages = loss_back(jnp.ones((), F32))
    d_passages = jnp.concatenate([d_passages, jnp.zeros_like(d_passages)])
    d_final = jnp.where(is_query, d_queries, d_passages)

    d_second, d_gain2, d_shift2 = final_back(d_final)
    d_outer = mine(d_second).astype(BF16)
    g_outer = mul("cf,ce->fe", act, d_outer)
    d_act = lax.psum(mul("ce,fe->cf", d_outer, wt), "dp")
    d_inner = act_back(d_act)[0].astype(BF16)
    g_inner = mul("ci,cf->if", normed_mine, d_inner)
    d_in = lax.psum(mul("cf,if->ci", d_inner, wi), "mp")
    d_normed = d_second + lax.all_gather(d_in, "dp", axis=1, tiled=True)
    d_first, d_gain1, d_shift1 = normed_back(d_normed)
    d_attn = mine(d_first).astype(BF16)
    g_out = mul("hck,ce->hke", att_low, d_attn).reshape(w_out.shape[1:])
    d_att = lax.psum(mul("ce,hke->hck", d_attn, wo), "dp").astype(BF16)
    w = mul("hck,ihk->hci", d_att, wv).astype(BF16)
    mean_d = jnp.sum(att * d_att.astype(F32), -1, keepdims=True)
    w = lax.all_gather(lax.all_gather(w, "dp", axis=2, tiled=True), "mp", axis=0, tiled=True)
    mean_d = lax.all_gather(mean_d, "mp", axis=0, tiled=True)
    d_probs = mul("hci,vi->hcv", w, hid)
    d_scores = (probs * (d_probs - mean_d)).astype(BF16)
    y = mul("hcv,vi->hci", d_scores, hid)
    y = lax.psum_scatter(y, "mp", scatter_dimension=0, tiled=True)
    y = lax.psum_scatter(y, "dp", scatter_dimension=2, tiled=True).astype(BF16)
    dq = (lax.psum(mul("hci,ihk->hck", y, wk), "dp") * scale).astype(BF16)
    g_q = mul("ci,hck->ihk", first_mine, dq)
    g_k = mul("hci,hck->ihk", y, q) * scale
    g_v = mul("hci,hck->ihk", z, d_att)
    g_mixed = jnp.stack([g_q, g_k, g_v], 1).reshape(w_mixed.shape[1:])
    d_rows = lax.psum(mul("hck,ihk->ci", dq, wq), "mp")
    d_rows = (d_first + lax.all_gather(d_rows, "dp", axis=1, tiled=True)).astype(BF16)
    d_hidden = (
        mul("hcv,hci->vi", d_scores, u) * scale
        + mul("hcv,hci->vi", probs_low, w)
        + mul("cv,ci->vi", cls_hot.astype(BF16), d_rows)
    )
    g_table, d_gain0, d_shift0 = hidden_back(d_hidden)
    sums = lax.psum(jnp.stack([d_gain0, d_shift0]), ("dp", "mp"))
    g_norms = jnp.concatenate([sums, jnp.stack([d_gain1, d_shift1, d_gain2, d_shift2])])
    return loss, (g_table, g_mixed, g_out, g_inner, g_outer, g_norms)


MESH = pl.DeviceIdType.MESH
ENTRY_ID = 3
PHASES = (
    "ids", "rows", "q", "stat", "att", "z", "z_dp", "out", "inner", "outer", "final",
    "d_act", "d_in", "d_att", "dq", "y", "y_dp", "d_rows", "sums", "norm",
)
BLOCK = 64
UNROLL = True


def nt(a, b):
    return lax.dot_general(a, b, (((1,), (1,)), ((), ())), preferred_element_type=F32)


def tn(a, b):
    return lax.dot_general(a, b, (((0,), (0,)), ((), ())), preferred_element_type=F32)


def nn(a, b):
    return jnp.dot(a, b, preferred_element_type=F32)


def exact_nt(a, b):
    return lax.dot_general(
        a, b, (((1,), (1,)), ((), ())), precision=exact_arithmetic_level, preferred_element_type=F32
    )


def exact_nn(a, b):
    return jnp.dot(a, b, precision=exact_arithmetic_level, preferred_element_type=F32)


def slab_norm(slabs, size):
    mean = sum(jnp.sum(s, -1, keepdims=True) for s in slabs) * (1.0 / size)
    slabs = [s - mean for s in slabs]
    spread = sum(jnp.sum(s * s, -1, keepdims=True) for s in slabs) * (1.0 / size)
    r = lax.rsqrt(spread + eps_norm)
    return [s * r for s in slabs], r


def slab_norm_back(hats, r, grads, gains, size):
    scaled = [dy * g for dy, g in zip(grads, gains)]
    mean = sum(jnp.sum(s, -1, keepdims=True) for s in scaled) * (1.0 / size)
    along = sum(jnp.sum(s * h, -1, keepdims=True) for s, h in zip(scaled, hats)) * (1.0 / size)
    d_in = [r * (s - mean - h * along) for s, h in zip(scaled, hats)]
    d_gain = [jnp.sum(dy * h, 0, keepdims=True) for dy, h in zip(grads, hats)]
    d_shift = [jnp.sum(dy, 0, keepdims=True) for dy in grads]
    return d_in, d_gain, d_shift


def joined(x, at, parts):
    return sum(x[:, at + i : at + i + 1] for i in range(parts))


def split_low(x, parts):
    out = []
    for _ in range(parts):
        piece = x.astype(BF16)
        out.append(piece)
        x = x - piece.astype(F32)
    return out


def grad_kernel(cfg, *refs):
    nd, nm, blk, rows, width, size, hm, ff = cfg
    n = nd * nm
    nb = nd * blk
    c = 2 * nb
    hw = hm * HEAD
    group = hm * c
    half = hm * nb
    heads = nm * group
    vt = 384
    tiles = rows // vt
    scale = HEAD ** (-0.5)
    (
        *early_hbm, table_hbm, first_hbm, second_hbm,
        small_ref, stage, g_mixed_ref, g_out_ref, g_inner_ref, g_outer_ref, g_norms_ref, table_keep, first_keep, second_keep,
        mixed_f, ids_ref, lens_ref, norms_ref, out_f, inner_f, outer_f, positive_ref, used_ref, negative_ref,
        emb, hid, lows, basis, counts, xs, acc, col, tops, factors, found_at,
        wq, wo, wi, wt, kv,
        ids_buf, rows_src, rows_buf, q_buf, stat_src, stat_buf, att_buf, z_src, z_mp, z_slab, z_buf, out_buf, inner_buf, outer_buf,
        final_buf, d_act_buf, d_in_buf, d_att_buf, dq_src, dq_buf, y_src, y_mp, y_slab, y_buf, d_rows_buf, sums_buf, norm_buf,
        send_sem, recv_sem, kv_send, kv_recv, kv_spread, table_sem, keep_sem, early_sem,
    ) = refs
    e, d, m = lax.axis_index("enc"), lax.axis_index("dp"), lax.axis_index("mp")
    me = d * nm + m
    is_query = e == 0
    base = me * rows

    sent, received = [], []

    def halves(go, full):
        pl.when(is_query)(lambda: go(full))
        pl.when(jnp.logical_not(is_query))(lambda: go(full // 2))

    def peer(i):
        p = lax.rem(me + i, n)
        return p // nm, lax.rem(p, nm)

    def remote(name, src, dst, where):
        k = PHASES.index(name)
        pltpu.make_async_remote_copy(
            src_ref=src, dst_ref=dst, send_sem=send_sem.at[k], recv_sem=recv_sem.at[k],
            device_id=where, device_id_type=MESH,
        ).start()

    def send_all(name, src_of, dst, buf):
        sent.append((name, buf, n - 1, False))

        def go(r):
            def one(i, carry):
                pd, pm = peer(i)
                remote(name, src_of(pd, pm).at[pl.ds(0, r)], dst.at[pl.ds(0, r)], (e, pd, pm))
                return carry
            lax.fori_loop(1, n, one, 0)
        halves(go, dst.shape[0])

    def send_group(name, group_of, src, dst, buf):
        if group_of == 0:
            sent.append((name, buf, n - 1, False))

        def go(r):
            for pd in range(nd):
                @pl.when(jnp.logical_or(pd != d, group_of != m))
                def _():
                    remote(name, src.at[pl.ds(0, r)], dst.at[pl.ds(0, r)], (e, pd, group_of))
        halves(go, dst.shape[0])

    def send_dp(name, src, dst, buf, both=False):
        sent.append((name, buf, nd - 1, both))

        def go(r):
            for i in range(1, nd):
                remote(name, src.at[pl.ds(0, r)], dst.at[pl.ds(0, r)], (e, lax.rem(d + i, nd), m))
        if both:
            go(dst.shape[0])
        else:
            halves(go, dst.shape[0])

    def send_mp(name, source, dst, buf):
        sent.append((name, buf, nm - 1, False))

        def go(r):
            for i in range(1, nm):
                g = lax.rem(m + i, nm)
                remote(name, source.at[g, pl.ds(0, r)], dst.at[pl.ds(0, r)], (e, d, g))
        halves(go, dst.shape[0])

    def send_dp_each(name, source, dst, buf):
        sent.append((name, buf, nd - 1, False))

        def go(r):
            for i in range(1, nd):
                k = lax.rem(d + i, nd)
                remote(name, source.at[k, pl.ds(0, r)], dst.at[pl.ds(0, r)], (e, k, m))
        halves(go, dst.shape[0])

    def drain(name, buf, sem, count, both=False):
        k = PHASES.index(name)
        if sem is recv_sem:
            received.append(name)

        def go(r):
            view = buf.at[pl.ds(0, count), pl.ds(0, r)]
            pltpu.make_async_copy(view, view, sem.at[k]).wait()
        if both:
            go(buf.shape[1])
        else:
            halves(go, buf.shape[1])

    def finish():
        for name, buf, count, both in sent:
            drain(name, buf, send_sem, count, both)
            if name not in received:
                drain(name, buf, recv_sem, count, both)
        for item in started:
            item()

    started = []

    early = (mixed_f, ids_ref, lens_ref, norms_ref, out_f, inner_f, outer_f, positive_ref, used_ref, negative_ref)
    early = [pltpu.make_async_copy(src, dst, early_sem.at[i]) for i, (src, dst) in enumerate(zip(early_hbm, early))]
    table_loads = [
        pltpu.make_async_copy(table_hbm.at[pl.ds(i * vt, vt)], stage.at[pl.ds(i * vt, vt)], table_sem.at[i])
        for i in range(tiles)
    ]
    for item in early[:4]:
        item.start()
    for item in table_loads:
        item.start()
    for item in early[4:]:
        item.start()

    @pl.when(jnp.logical_not(is_query))
    def _():
        for buf in (
            rows_buf, q_buf, stat_buf, att_buf, z_mp, z_buf, out_buf, inner_buf, outer_buf, d_act_buf, d_in_buf, d_att_buf, dq_buf,
            y_mp, y_buf, d_rows_buf,
        ):
            r = buf.shape[1] // 2
            for k in range(buf.shape[0]):
                buf[k, r:, :] = jnp.zeros((r, buf.shape[2]), buf.dtype)

    barrier = pltpu.get_barrier_semaphore()

    def greet(i, carry):
        pd, pm = peer(i)
        pl.semaphore_signal(barrier, inc=1, device_id=(e, pd, pm), device_id_type=MESH)
        return carry
    lax.fori_loop(1, n, greet, 0)
    pl.semaphore_signal(barrier, inc=1, device_id=(1 - e, d, m), device_id_type=MESH)
    pl.semaphore_wait(barrier, n)

    early[1].wait()
    early[2].wait()
    row_i = lax.broadcasted_iota(jnp.int32, (blk, 2 * QSLOT), 0)
    lane_i = lax.broadcasted_iota(jnp.int32, (blk, 2 * QSLOT), 1)
    limit = jnp.zeros((blk, 2 * QSLOT), jnp.int32)
    for b in range(blk):
        here = jnp.where(lane_i < QSLOT, lens_ref[2 * b], lens_ref[2 * b + 1])
        limit = jnp.where(row_i == b, here, limit)
    limit = jnp.where(is_query, limit, QSLOT)
    ids_buf[d] = jnp.where((lane_i & (QSLOT - 1)) >= limit, -1, ids_ref[0])
    send_dp("ids", ids_buf.at[d], ids_buf.at[d], ids_buf, both=True)

    early[0].wait()
    fold = width // 2
    for i in range(2):
        kv[i, m, d, :, 0:hw] = mixed_f[1 + i, 0:fold].astype(BF16)
        kv[i, m, d, :, hw:] = mixed_f[1 + i, fold:].astype(BF16)

    def kv_copy(i, src, sem, where):
        piece = kv.at[i, m, src]
        return pltpu.make_async_remote_copy(
            src_ref=piece, dst_ref=piece, send_sem=kv_send.at[i], recv_sem=sem, device_id=where, device_id_type=MESH
        )

    def partner(k):
        if nd != 4:
            return lax.rem(d + k, nd)
        return (d + 1 - 2 * lax.rem(d, 2), d + 2 - 4 * (d // 2), 3 - d)[k - 1]

    def kv_to_dp(i):
        for k in range(1, nd):
            kv_copy(i, d, kv_recv.at[i, d], (e, lax.rem(d + k, nd), m)).start()

    def kv_to_mp(i, src):
        for k in range(1, nm):
            kv_copy(i, src, kv_spread.at[i], (e, d, lax.rem(m + k, nm))).start()

    def kv_from_dp(i, k):
        src = partner(k)
        pltpu.make_async_copy(kv.at[i, m, src], kv.at[i, m, src], kv_recv.at[i, src]).wait()
        return src

    def kv_wait(i):
        view = kv.at[i, pl.ds(0, nm - 1)]
        pltpu.make_async_copy(view, view, kv_spread.at[i]).wait()

    def kv_left():
        for i in range(2):
            view = kv.at[i, pl.ds(0, nm - 1)]
            pltpu.make_async_copy(view, view, kv_send.at[i]).wait()
            view = kv.at[i, 0, pl.ds(0, nd - 1)]
            pltpu.make_async_copy(view, view, kv_send.at[i]).wait()
    started.append(kv_left)

    def projection(i, g, k):
        both = kv[i, g, k]
        return jnp.concatenate([both[:, 0:hw], both[:, hw:]], axis=0)

    kv_to_dp(0)
    kv_to_mp(0, d)
    wq[...] = mixed_f[0].astype(BF16)

    early[3].wait()
    gain0, shift0 = norms_ref[0], norms_ref[1]
    for t in range(tiles):
        table_loads[t].wait()

        def to_low(i, carry):
            at = pl.ds(pl.multiple_of(t * vt + i * BLOCK, BLOCK), BLOCK)
            emb[at, :] = stage[at, :].astype(BF16)
            return carry
        lax.fori_loop(0, vt // BLOCK, to_low, 0, unroll=True)

    drain("ids", ids_buf, recv_sem, nd - 1, both=True)
    ids_all = jnp.concatenate([ids_buf[k] for k in range(nd)], axis=0) - base
    cls = jnp.concatenate([ids_all[:, 0:1], ids_all[:, QSLOT : QSLOT + 1]], axis=0)
    hot_at = 2 * heads
    lows[pl.ds(hot_at, c), :] = (cls == lax.broadcasted_iota(jnp.int32, (c, rows), 1)).astype(BF16)

    def pick(t, total):
        at = pl.ds(pl.multiple_of(t * vt, vt), vt)
        return total + nn(lows[pl.ds(hot_at, c), at], emb[at, :])
    found = lax.fori_loop(0, tiles, pick, jnp.zeros((c, size), F32), unroll=True)
    found_hat, found_r = slab_norm([found], size)
    found_at[...] = found_hat[0]
    owned = jnp.logical_and(cls >= 0, cls < rows)
    found = jnp.where(owned, found_hat[0] * gain0 + shift0, 0.0).astype(BF16)
    for k in range(nd):
        rows_src[k] = found[:, k * width : (k + 1) * width]
    rows_buf[me] = rows_src[d]
    send_all("rows", lambda pd, pm: rows_src.at[pd], rows_buf.at[me], rows_buf)

    for k in range(1, nd):
        kv_to_mp(0, kv_from_dp(0, k))
    flag = jnp.where(is_query, 1, 0)
    for b in range(nb):
        row = ids_all[b : b + 1, :]
        high, low = row >> 7, row & 127
        lane_b = lax.broadcasted_iota(jnp.int32, (16, 2 * QSLOT), 1)
        is_high = lax.broadcasted_iota(jnp.int32, (16, 2 * QSLOT), 0) == high
        left = [jnp.logical_and(is_high, (lane_b >> 7) * flag == s * flag) for s in range(2)]
        left = jnp.concatenate([item.astype(BF16) for item in left], axis=0)
        right = (lax.broadcasted_iota(jnp.int32, (128, 2 * QSLOT), 0) == low).astype(BF16)
        xs[b] = nt(left, right)
    for t in range(rows // 128):
        for s in range(2):
            counts[s * nb : (s + 1) * nb, t * 128 : (t + 1) * 128] = xs[:, s * 16 + t, :]

    kv_to_dp(1)

    def normalize(i, carry):
        at = pl.ds(pl.multiple_of(i * BLOCK, BLOCK), BLOCK)
        x = emb[at, :].astype(F32)
        x = x - jnp.mean(x, -1, keepdims=True)
        r = lax.rsqrt(jnp.mean(x * x, -1, keepdims=True) + eps_norm)
        hid[at, :] = (x * r * gain0 + shift0).astype(BF16)
        return carry
    lax.fori_loop(0, rows // BLOCK, normalize, 0, unroll=2)
    for i, (src, dst) in enumerate(((table_hbm, table_keep), (first_hbm, first_keep), (second_hbm, second_keep))):
        keep = pltpu.make_async_copy(src, dst, keep_sem.at[i])
        keep.start()
        started.append(keep.wait)
    for item in early[4:]:
        item.wait()
    wo[...] = out_f[...].astype(BF16)
    wi[...] = inner_f[...].astype(BF16)
    wt[...] = outer_f[...].astype(BF16)

    drain("rows", rows_buf, recv_sem, n - 1)
    mine = sum(rows_buf[k].astype(F32) for k in range(n))
    mine_low = mine.astype(BF16)
    q_buf[me] = nn(mine_low, wq[...]).astype(BF16)
    send_all("q", lambda pd, pm: q_buf.at[me], q_buf.at[me], q_buf)

    lane_h = lax.broadcasted_iota(jnp.int32, (nb, hw), 1) // HEAD

    def expand(x):
        return jnp.concatenate(
            [
                jnp.where(lane_h == j, x[s * nb : (s + 1) * nb], jnp.zeros((), x.dtype))
                for s in range(2)
                for j in range(hm)
            ],
            axis=0,
        )

    def collapse(x):
        out = []
        for s in range(2):
            parts = [x[s * half + j * nb : s * half + (j + 1) * nb] for j in range(hm)]
            total = parts[0]
            for j in range(1, hm):
                total = jnp.where(lane_h == j, parts[j], total)
            out.append(total)
        return jnp.concatenate(out, axis=0)

    def to_rows(cols):
        return jnp.concatenate([cols[j][s * nb : (s + 1) * nb] for s in range(2) for j in range(hm)], axis=0)

    def to_cols(x):
        return [
            jnp.concatenate([x[s * half + j * nb : s * half + (j + 1) * nb] for s in range(2)], axis=0)
            for j in range(hm)
        ]

    def over_heads(cols):
        lane = lax.broadcasted_iota(jnp.int32, (c, hw), 1) // HEAD
        out = jnp.broadcast_to(cols[0], (c, hw))
        for j in range(1, hm):
            out = jnp.where(lane == j, cols[j], out)
        return out

    def with_cols(x, cols):
        tail = lax.broadcasted_iota(jnp.int32, (c, HEAD), 1)
        extra = jnp.zeros((c, HEAD), F32)
        for k, item in enumerate(cols):
            extra = jnp.where(tail == k, item.astype(F32), extra)
        return jnp.concatenate([x, extra.astype(x.dtype)], axis=1)

    blank = jnp.zeros((c, hw), BF16)
    drain("q", q_buf, recv_sem, n - 1)
    kv_wait(0)
    queries = []
    for g in range(nm):
        q = sum(q_buf[k * nm + g].astype(F32) for k in range(nd)).astype(BF16)
        queries.append(q)
        wide = expand(q)
        for k in range(nd):
            basis[pl.ds(g * group, group), k * width : (k + 1) * width] = nt(wide, projection(0, g, k)).astype(BF16)
    q_mine = queries[0]
    for g in range(1, nm):
        q_mine = jnp.where(m == g, queries[g], q_mine)

    acc[...] = jnp.zeros_like(acc)
    tops[...] = jnp.zeros_like(tops)
    lane_of_tile = lax.broadcasted_iota(jnp.int32, (heads, 8), 1)

    def weigh(t, carry):
        top, total = carry
        at = pl.ds(pl.multiple_of(t * vt, vt), vt)
        s = nt(basis[pl.ds(0, heads), :], hid[at, :]) * scale
        places = [
            (g * group + sl * half + j * nb, pl.ds(sl * nb, nb)) for g in range(nm) for sl in range(2) for j in range(hm)
        ]
        s = [jnp.where(counts[of, at] > 0, s[lo : lo + nb], -1e30) for lo, of in places]
        best = [jnp.maximum(top[lo : lo + nb], jnp.max(x, -1, keepdims=True)) for x, (lo, of) in zip(s, places)]
        sums = []
        for x, high, (lo, of) in zip(s, best, places):
            x = counts[of, at] * jnp.exp(x - high)
            lows[lo : lo + nb, at] = x.astype(BF16)
            sums.append(jnp.sum(x, -1, keepdims=True))
        best = jnp.concatenate(best, axis=0)
        keep = jnp.exp(top - best)
        acc[...] = acc[...] * keep + nn(lows[pl.ds(0, heads), at], hid[at, :])
        tops[...] = jnp.where(lane_of_tile == t, best, tops[...])
        return best, total * keep + jnp.concatenate(sums, axis=0)
    top, total = lax.fori_loop(
        0, tiles, weigh, (jnp.full((heads, 1), -1e30, F32), jnp.zeros((heads, 1), F32)), unroll=UNROLL
    )

    def stat_slab(cols):
        lane = lax.broadcasted_iota(jnp.int32, (c, 128), 1)
        out = jnp.zeros((c, 128), F32)
        for k, item in enumerate(cols):
            out = jnp.where(lane == k, item, out)
        return out

    for g in range(nm):
        at = slice(g * group, (g + 1) * group)
        z_src[g] = acc[at, :].astype(BF16)
        stat_src[g] = stat_slab(to_cols(top[at]) + to_cols(total[at]))
    stat_buf[m] = stat_src[m]
    z_mp[m] = z_src[m]
    send_mp("stat", stat_src, stat_buf.at[m], stat_buf)
    send_mp("z", z_src, z_mp.at[m], z_mp)

    def combine(peaks, sums):
        best = peaks[0]
        for item in peaks[1:]:
            best = jnp.maximum(best, item)
        factor = [jnp.exp(item - best) for item in peaks]
        return best, factor, sum(f * item for f, item in zip(factor, sums))

    drain("stat", stat_buf, recv_sem, nm - 1)
    stats = [stat_buf[g] for g in range(nm)]
    near = [combine([x[:, j : j + 1] for x in stats], [x[:, hm + j : hm + j + 1] for x in stats]) for j in range(hm)]
    scales = [to_rows([near[j][1][g] for j in range(hm)]) for g in range(nm)]
    for k in range(1, nd):
        kv_from_dp(1, k)
    drain("z", z_mp, recv_sem, nm - 1)
    z_near = sum(z_mp[g].astype(F32) * scales[g] for g in range(nm))
    att = 0.0
    for k in range(nd):
        att = att + nn(z_near[:, k * width : (k + 1) * width].astype(BF16), projection(1, m, k))
    cols = [piece for j in range(hm) for piece in split_low(near[j][0], 3)]
    cols += [piece for j in range(hm) for piece in split_low(near[j][2], 2)]
    att_buf[d] = with_cols(collapse(att).astype(BF16), cols)
    send_dp("att", att_buf.at[d], att_buf.at[d], att_buf)

    drain("att", att_buf, recv_sem, nd - 1)
    far = []
    slabs = [att_buf[k, :, hw:].astype(F32) for k in range(nd)]
    for j in range(hm):
        far.append(combine([joined(x, 3 * j, 3) for x in slabs], [joined(x, 3 * hm + 2 * j, 2) for x in slabs]))
    top_all = [item[0] for item in far]
    inv_all = [jnp.where(x > 0, 1.0 / jnp.where(x > 0, x, 1.0), 0.0) for _, _, x in far]
    parts = [[f * inv for f in item[1]] for item, inv in zip(far, inv_all)]
    att = sum(att_buf[k, :, 0:hw].astype(F32) * over_heads([parts[j][k] for j in range(hm)]) for k in range(nd))
    att_low = att.astype(BF16)
    part = nn(att_low, wo[...]) + jnp.where(m == 0, mine, 0.0)
    cols = [piece for item in top_all for piece in split_low(item, 3)]
    cols += [piece for item in inv_all for piece in split_low(item, 2)]
    out_buf[me] = with_cols(part.astype(BF16), cols)
    send_all("out", lambda pd, pm: out_buf.at[me], out_buf.at[me], out_buf)

    def slabs_of(buf):
        return [sum(buf[k * nm + g, :, 0:width].astype(F32) for g in range(nm)) for k in range(nd)]

    def own(slabs):
        out = slabs[0]
        for k in range(1, nd):
            out = jnp.where(d == k, slabs[k], out)
        return out

    def norm_rows(i):
        row = norms_ref[i]
        return [row[:, k * width : (k + 1) * width] for k in range(nd)]

    drain("out", out_buf, recv_sem, n - 1)
    hats1, r1 = slab_norm(slabs_of(out_buf), size)
    gains1, shifts1 = norm_rows(2), norm_rows(3)
    normed = [h * g + s for h, g, s in zip(hats1, gains1, shifts1)]
    normed_mine = own(normed)
    normed_low = normed_mine.astype(BF16)

    inner_buf[d] = nn(normed_low, wi[...]).astype(BF16)
    send_dp("inner", inner_buf.at[d], inner_buf.at[d], inner_buf)
    kv_to_mp(1, d)
    for k in range(1, nd):
        kv_to_mp(1, lax.rem(d + k, nd))
    for g in range(nm):
        stat = out_buf[g, :, hw:].astype(F32)
        best = to_rows([joined(stat, 3 * j, 3) for j in range(hm)])
        inv = to_rows([joined(stat, 3 * hm + 2 * j, 2) for j in range(hm)])
        at = pl.ds(g * group, group)
        factors[at, :] = jnp.exp(tops[at, :] - best) * inv
    z = z_near * to_rows([own(parts[j]) for j in range(hm)])
    for k in range(nd):
        z_slab[k] = z[:, k * width : (k + 1) * width].astype(BF16)
    z_buf[d] = z_slab[d]
    drain("inner", inner_buf, recv_sem, nd - 1)
    inner = sum(inner_buf[k].astype(F32) for k in range(nd))
    cdf = 0.5 * (1.0 + lax.erf(inner * (0.5 ** 0.5)))
    act = (inner * cdf).astype(BF16)
    slope = cdf + inner * jnp.exp(-0.5 * inner * inner) * ((0.5 / math.pi) ** 0.5)
    outer_buf[me] = (nt(act, wt[...]) + jnp.where(m == 0, normed_mine, 0.0)).astype(outer_buf.dtype)
    send_all("outer", lambda pd, pm: outer_buf.at[me], outer_buf.at[me], outer_buf)
    drain("outer", outer_buf, recv_sem, n - 1)
    send_dp_each("z_dp", z_slab, z_buf.at[d], z_buf)
    hats2, r2 = slab_norm(slabs_of(outer_buf), size)
    gains2, shifts2 = norm_rows(4), norm_rows(5)
    for k in range(nd):
        final_buf[e, k] = hats2[k] * gains2[k] + shifts2[k]
    final_at = PHASES.index("final")
    final_copy = pltpu.make_async_remote_copy(
        src_ref=final_buf.at[e], dst_ref=final_buf.at[e], send_sem=send_sem.at[final_at], recv_sem=recv_sem.at[final_at],
        device_id=(1 - e, d, m), device_id_type=MESH,
    )
    final_copy.start()
    final_copy.wait_recv()
    started.append(final_copy.wait_send)

    qs = [final_buf[0, k] for k in range(nd)]
    ps = [final_buf[1, k][0:nb] for k in range(nd)]
    q_r = lax.rsqrt(sum(jnp.sum(x * x, -1, keepdims=True) for x in qs) + eps_norm)
    p_r = lax.rsqrt(sum(jnp.sum(x * x, -1, keepdims=True) for x in ps) + eps_norm)
    q_hat, p_hat = [x * q_r for x in qs], [x * p_r for x in ps]

    def d_sims(left, right, axis, negative, positive, used):
        sims = sum(exact_nt(a, b) for a, b in zip(left, right)) / logit_divisor
        is_positive = lax.broadcasted_iota(jnp.int32, sims.shape, axis) == positive
        sims = jnp.where(jnp.logical_and(negative == 1.0, jnp.logical_not(is_positive)), -1e30, sims)
        best = jnp.max(sims, axis, keepdims=True)
        log_total = best + jnp.log(jnp.sum(jnp.exp(sims - best), axis, keepdims=True))
        target = jnp.sum(jnp.where(is_positive, sims, 0.0), axis, keepdims=True)
        weight = used.astype(F32)
        count = jnp.maximum(jnp.sum(weight, 1 - axis, keepdims=True), 1.0)
        loss = jnp.sum(weight * (log_total - target), 1 - axis, keepdims=True) / count
        grad = (jnp.exp(sims - log_total) - is_positive.astype(F32)) * (weight / count / logit_divisor)
        return loss, grad

    at_row = lax.broadcasted_iota(jnp.int32, (c, c), 0)
    from_query = lax.broadcasted_iota(jnp.int32, (c, c), 1)
    order = (from_query == 2 * (at_row % nb) + at_row // nb).astype(BF16)
    negative = negative_ref[...].astype(F32).astype(BF16)
    column, line = lax.broadcasted_iota(jnp.int32, (c, 1), 0), lax.broadcasted_iota(jnp.int32, (1, c), 1)
    positive = [jnp.zeros((c, 1), jnp.int32), jnp.zeros((1, c), jnp.int32)]
    used = [jnp.zeros((c, 1), jnp.int32), jnp.zeros((1, c), jnp.int32)]
    for k in range(c):
        query = 2 * (k % nb) + k // nb
        for i, place in enumerate((column, line)):
            positive[i] = jnp.where(place == k, positive_ref[query], positive[i])
            used[i] = jnp.where(place == k, used_ref[query], used[i])
    loss, grad_q = d_sims(q_hat, p_hat, 1, nt(order, negative), positive[0], used[0])
    _, grad_p = d_sims(p_hat, q_hat, 0, nt(negative, order), positive[1], used[1])

    def unit_back(hats, r, grads):
        along = sum(jnp.sum(g * h, -1, keepdims=True) for g, h in zip(grads, hats))
        return [r * (g - h * along) for g, h in zip(grads, hats)]

    d_q = unit_back(q_hat, q_r, [exact_nn(grad_q, x) for x in p_hat])
    d_p = unit_back(p_hat, p_r, [exact_nn(grad_p, x) for x in q_hat])
    d_final = [
        jnp.where(is_query, a, jnp.concatenate([b, jnp.zeros_like(b)], axis=0)) for a, b in zip(d_q, d_p)
    ]

    d_second, d_gain2, d_shift2 = slab_norm_back(hats2, r2, d_final, gains2, size)
    d_outer = own(d_second).astype(BF16)
    d_act_buf[d] = nn(d_outer, wt[...]).astype(BF16)
    send_dp("d_act", d_act_buf.at[d], d_act_buf.at[d], d_act_buf)
    g_outer = tn(d_outer, act)
    g_outer_ref[...] = g_outer
    drain("d_act", d_act_buf, recv_sem, nd - 1)
    d_inner = (sum(d_act_buf[k].astype(F32) for k in range(nd)) * slope).astype(BF16)
    d_in_buf[me] = nt(d_inner, wi[...]).astype(d_in_buf.dtype)
    send_all("d_in", lambda pd, pm: d_in_buf.at[me], d_in_buf.at[me], d_in_buf)
    g_inner = tn(normed_low, d_inner)
    g_inner_ref[...] = g_inner
    drain("d_in", d_in_buf, recv_sem, n - 1)
    d_normed = [a + b for a, b in zip(d_second, slabs_of(d_in_buf))]
    d_first, d_gain1, d_shift1 = slab_norm_back(hats1, r1, d_normed, gains1, size)
    d_first_mine = own(d_first)
    d_attn = d_first_mine.astype(BF16)

    part = nt(d_attn, wo[...])
    along = att * part
    lane = lax.broadcasted_iota(jnp.int32, (c, hw), 1) // HEAD
    cols = []
    for j in range(hm):
        cols += split_low(jnp.sum(jnp.where(lane == j, along, 0.0), -1, keepdims=True), 2)
    d_att_buf[me] = with_cols(part.astype(BF16), cols)
    send_all("d_att", lambda pd, pm: d_att_buf.at[me], d_att_buf.at[me], d_att_buf)
    g_out = tn(att_low, d_attn)
    g_out_ref[...] = g_out
    squares = sum(jnp.sum(g * g, 0, keepdims=True) for g in (g_outer, g_inner))
    squares = jnp.sum(squares, -1, keepdims=True) + jnp.sum(jnp.sum(g_out * g_out, 0, keepdims=True), -1, keepdims=True)

    kv_wait(1)
    drain("d_att", d_att_buf, recv_sem, n - 1)
    d_atts = []
    for g in range(nm):
        slab = sum(d_att_buf[k * nm + g].astype(F32) for k in range(nd))
        d_att = slab[:, 0:hw].astype(BF16)
        d_atts.append(d_att)
        col[pl.ds(g * group, group), :] = to_rows(
            [joined(slab, hw + 2 * j, 2) for j in range(hm)]
        )
        wide = expand(d_att)
        for k in range(nd):
            basis[pl.ds(heads + g * group, group), k * width : (k + 1) * width] = nt(wide, projection(1, g, k)).astype(BF16)
    d_att_mine = d_atts[0]
    for g in range(1, nm):
        d_att_mine = jnp.where(m == g, d_atts[g], d_att_mine)
    acc[...] = jnp.zeros_like(acc)

    def backward(t, carry):
        at = pl.ds(pl.multiple_of(t * vt, vt), vt)
        d_probs = nt(basis[pl.ds(heads, heads), :], hid[at, :])
        probs = lows[pl.ds(0, heads), at].astype(F32) * jnp.sum(
            jnp.where(lane_of_tile == t, factors[...], 0.0), -1, keepdims=True
        )
        d_scores = (probs * (d_probs - col[...]) * scale).astype(BF16)
        lows[pl.ds(0, heads), at] = d_scores
        lows[pl.ds(heads, heads), at] = probs.astype(BF16)
        acc[...] += nn(d_scores, hid[at, :])
        return carry
    lax.fori_loop(0, tiles, backward, 0, unroll=UNROLL)

    for g in range(nm):
        y = acc[pl.ds(g * group, group), :].astype(BF16)
        dq = jnp.zeros((group, hw), F32)
        for k in range(nd):
            dq = dq + nn(y[:, k * width : (k + 1) * width], projection(0, g, k))
        y_src[g] = y
        dq_src[g] = collapse(dq).astype(BF16)
        send_group("dq", g, dq_src.at[g], dq_buf.at[me], dq_buf)
    dq_buf[me] = dq_src[m]
    y_mp[m] = y_src[m]
    send_mp("y", y_src, y_mp.at[m], y_mp)

    lane_t = 128

    def spread(t, carry):
        at = pl.ds(pl.multiple_of(t * lane_t, lane_t), lane_t)
        stage[at, :] = tn(lows[pl.ds(0, 2 * heads), at], basis[pl.ds(0, 2 * heads), :])
        return carry
    lax.fori_loop(0, rows // lane_t, spread, 0, unroll=3)

    drain("dq", dq_buf, recv_sem, n - 1)
    dq_mine = sum(dq_buf[k].astype(F32) for k in range(n)).astype(BF16)
    d_rows_buf[me] = (nt(dq_mine, wq[...]) + jnp.where(m == 0, d_first_mine, 0.0)).astype(d_rows_buf.dtype)
    send_all("d_rows", lambda pd, pm: d_rows_buf.at[me], d_rows_buf.at[me], d_rows_buf)
    g_q = tn(mine_low, dq_mine)
    drain("z_dp", z_buf, recv_sem, nd - 1)
    z_mine = sum(z_buf[k].astype(F32) for k in range(nd)).astype(BF16)
    g_v = tn(z_mine, expand(d_att_mine))
    drain("y", y_mp, recv_sem, nm - 1)
    y = sum(y_mp[g].astype(F32) for g in range(nm))
    for k in range(nd):
        y_slab[k] = y[:, k * width : (k + 1) * width].astype(BF16)
    y_buf[d] = y_slab[d]
    send_dp_each("y_dp", y_slab, y_buf.at[d], y_buf)
    fold8 = lambda v: jnp.sum(v.reshape(v.shape[0] // 8, 8, size), 0)

    def table_back(t, carry):
        d_gain, d_shift = carry
        at = pl.ds(pl.multiple_of(t * BLOCK, BLOCK), BLOCK)
        dy = stage[at, :]
        x = emb[at, :].astype(F32)
        x = x - jnp.mean(x, -1, keepdims=True)
        r = lax.rsqrt(jnp.mean(x * x, -1, keepdims=True) + eps_norm)
        hat = x * r
        scaled = dy * gain0
        mean = jnp.mean(scaled, -1, keepdims=True)
        along = jnp.mean(scaled * hat, -1, keepdims=True)
        stage[at, :] = r * (scaled - mean - hat * along)
        return d_gain + fold8(dy * hat), d_shift + fold8(dy)
    zero = jnp.zeros((8, size), F32)
    d_gain, d_shift = lax.fori_loop(0, rows // BLOCK, table_back, (zero, zero), unroll=2)

    drain("d_rows", d_rows_buf, recv_sem, n - 1)
    d_rows = jnp.concatenate(slabs_of(d_rows_buf), axis=1)
    d_rows = jnp.where(owned, d_rows, 0.0)
    hat = found_at[...]
    d_found, extra_gain, extra_shift = slab_norm_back([hat], found_r, [d_rows], [gain0], size)
    d_found = jnp.where(owned, d_found[0], 0.0).astype(BF16)

    def table_add(t, square):
        at = pl.ds(pl.multiple_of(t * lane_t, lane_t), lane_t)
        grad = stage[at, :] + tn(lows[pl.ds(hot_at, c), at], d_found)
        stage[at, :] = grad
        return square + fold8(grad * grad)
    square = lax.fori_loop(0, rows // lane_t, table_add, zero, unroll=3)
    d_gain = jnp.sum(d_gain, 0, keepdims=True) + extra_gain[0]
    d_shift = jnp.sum(d_shift, 0, keepdims=True) + extra_shift[0]
    drain("y_dp", y_buf, recv_sem, nd - 1)
    y_mine = sum(y_buf[k].astype(F32) for k in range(nd)).astype(BF16)
    g_k = tn(y_mine, expand(q_mine))
    for i, g in enumerate((g_q, g_k, g_v)):
        g_mixed_ref[i] = g
    total = sum(jnp.sum(g * g, 0, keepdims=True) for g in (g_q, g_k, g_v))
    squares = squares + jnp.sum(total, -1, keepdims=True)
    squares = squares + jnp.sum(jnp.sum(square, 0, keepdims=True), -1, keepdims=True)
    chunks = size // 128
    lines = [v[:, k * 128 : (k + 1) * 128] for v in (d_gain, d_shift) for k in range(chunks)]
    lines.append(jnp.broadcast_to(squares, (1, 128)))
    lines.append(jnp.zeros((16 - len(lines), 128), F32))
    sums_buf[me] = jnp.concatenate(lines, axis=0)

    def send_sums(i, carry):
        pd, pm = peer(i)
        remote("sums", sums_buf.at[me], sums_buf.at[me], (e, pd, pm))
        return carry
    lax.fori_loop(1, n, send_sums, 0)
    sent.append(("sums", sums_buf, n - 1, True))
    drain("sums", sums_buf, recv_sem, n - 1, both=True)
    totals = sum(sums_buf[k] for k in range(n))
    firsts = [jnp.concatenate([totals[v * chunks + k : v * chunks + k + 1] for k in range(chunks)], axis=1) for v in range(2)]
    squares = totals[2 * chunks : 2 * chunks + 1, 0:1]
    for i in range(2):
        g_norms_ref[i : i + 1, :] = firsts[i]
        squares = squares + jnp.sum(firsts[i] * firsts[i], -1, keepdims=True)
    for i, slabs in enumerate((d_gain1, d_shift1, d_gain2, d_shift2)):
        for k in range(nd):
            g_norms_ref[2 + i : 3 + i, k * width : (k + 1) * width] = slabs[k]
            squares = squares + jnp.sum(slabs[k] * slabs[k], -1, keepdims=True)
    norm_buf[e] = jnp.broadcast_to(squares, (8, 128))
    norm_at = PHASES.index("norm")
    norm_copy = pltpu.make_async_remote_copy(
        src_ref=norm_buf.at[e], dst_ref=norm_buf.at[e], send_sem=send_sem.at[norm_at], recv_sem=recv_sem.at[norm_at],
        device_id=(1 - e, d, m), device_id_type=MESH,
    )
    norm_copy.start()
    norm_copy.wait_recv()
    started.append(norm_copy.wait_send)
    grad_norm = jnp.sqrt(norm_buf[0] + norm_buf[1])
    small_ref[...] = jnp.where(
        lax.broadcasted_iota(jnp.int32, (8, 128), 0) == 0, jnp.broadcast_to(loss, (8, 128)), grad_norm
    )

    finish()


def kernel_gradients(
    token_ids, query_lengths, negative_mask, positive_index, used_rows, table, w_mixed, w_out, w_inner, w_outer, norm_params, table_m, table_v
):
    nd, nm = lax.axis_size("dp"), lax.axis_size("mp")
    n = nd * nm
    blk = token_ids.shape[1]
    _, rows, size = table.shape
    width, hw, ff = w_mixed.shape[1], w_mixed.shape[3], w_inner.shape[2]
    hm = hw // HEAD
    nb = nd * blk
    c = 2 * nb
    group, heads = hm * c, nm * hm * c
    S = jax.ShapeDtypeStruct
    outs = (
        S((8, 128), F32), S((rows, size), F32), S((3, width, hw), F32),
        S((hw, width), F32), S((width, ff), F32), S((width, ff), F32), S((8, size), F32),
    ) + (S((rows, size), F32),) * 3
    vm, hb = pl.BlockSpec(memory_space=pltpu.VMEM), pl.BlockSpec(memory_space=pltpu.HBM)
    V = pltpu.VMEM
    wide = hw + HEAD
    operands = (
        w_mixed[0].swapaxes(0, 1), token_ids, query_lengths, norm_params.swapaxes(0, 1), w_out[0], w_inner[0], w_outer[0].T,
        positive_index, used_rows, negative_mask.T, table[0], table_m[0], table_v[0],
    )
    local = [V] * 2 + [pltpu.SMEM] + [V] * 4 + [pltpu.SMEM] * 2 + [V]
    scratch = [space(item.shape, item.dtype) for space, item in zip(local, operands)] + [
        V((rows, size), BF16), V((rows, size), BF16),
        V((2 * heads + c, rows), BF16), V((2 * heads, size), BF16), V((c, rows), F32), V((nb, 32, 128), F32),
        V((heads, size), F32), V((heads, 1), F32), V((heads, 8), F32), V((heads, 8), F32), V((c, size), F32),
        V((width, hw), BF16), V((hw, width), BF16), V((width, ff), BF16), V((width, ff), BF16), V((2, nm, nd, width // 2, 2 * hw), BF16),
        V((nd, blk, 2 * QSLOT), jnp.int32),
        V((nd, c, width), BF16), V((n, c, width), BF16), V((n, c, hw), BF16),
        V((nm, c, 128), F32), V((nm, c, 128), F32), V((nd, c, wide), BF16),
        V((nm, group, size), BF16), V((nm, group, size), BF16), V((nd, group, width), BF16), V((nd, group, width), BF16),
        V((n, c, wide), BF16), V((nd, c, ff), BF16), V((n, c, width), BF16), V((2, nd, c, width), F32),
        V((nd, c, ff), BF16), V((n, c, width), BF16), V((n, c, wide), BF16), V((nm, c, hw), BF16), V((n, c, hw), BF16),
        V((nm, group, size), BF16), V((nm, group, size), BF16), V((nd, group, width), BF16), V((nd, group, width), BF16),
        V((n, c, width), BF16),
        V((n, 16, 128), F32), V((2, 8, 128), F32),
        pltpu.SemaphoreType.DMA((len(PHASES),)), pltpu.SemaphoreType.DMA((len(PHASES),)),
        pltpu.SemaphoreType.DMA((2,)), pltpu.SemaphoreType.DMA((2, nd)), pltpu.SemaphoreType.DMA((2,)),
        pltpu.SemaphoreType.DMA((rows // 384,)), pltpu.SemaphoreType.DMA((3,)), pltpu.SemaphoreType.DMA((10,)),
    ]
    small, g_table, g_mixed, g_out, g_inner, g_outer, g_norms, *kept = pl.pallas_call(
        partial(grad_kernel, (nd, nm, blk, rows, width, size, hm, ff)),
        out_shape=outs,
        in_specs=[hb] * len(operands),
        out_specs=(vm,) * 10,
        scratch_shapes=scratch,
        compiler_params=pltpu.CompilerParams(collective_id=ENTRY_ID, has_side_effects=True, vmem_limit_bytes=27 << 20),
        name="gradients",
    )(*(pltpu.with_memory_space_constraint(item, pltpu.HBM) for item in operands))
    return small, (g_table, g_mixed, g_out, g_inner, g_outer, g_norms), kept


RING = 4
PIECE = 192


def adam_kernel(rates, count_ref, small_ref, *refs):
    k = len(rates)
    operands = [refs[4 * i : 4 * i + 4] for i in range(k)]
    results = [refs[4 * k + 3 * i : 4 * k + 3 * i + 3] for i in range(k)]
    refs = refs[7 * k :]
    ring, ring_sem, own_sem, buffers = refs[:3], refs[3], refs[4], refs[5:]
    norm = small_ref[1:2, 0:1]
    clip = jnp.minimum(1.0, clip_limit / (norm + 1e-06))
    count = jnp.full((1, 1), count_ref[0], jnp.int32).astype(F32)
    fix_one = 1.0 - jnp.exp(count * math.log(beta_one))
    fix_two = 1.0 - jnp.exp(count * math.log(beta_two))
    inv_one, inv_two = 1.0 / fix_one, 1.0 / fix_two
    copies, in_slot, used, turn = [], [None] * RING, 0, 0

    def update(i, at, targets, to):
        grad, weight, first, second = (ref[at] for ref in operands[i])
        rate, decay = rates[i]
        grad = grad * clip
        first = beta_one * first + (1.0 - beta_one) * grad
        second = beta_two * second + ((1.0 - beta_two) * grad) * grad
        step = first * inv_one / (jnp.sqrt(second * inv_two) + adam_eps)
        if decay:
            step = step + decay * weight
        for ref, value in zip(targets, (weight - rate * step, first, second)):
            ref[to] = value

    def send(src, dst, sem):
        copy = pltpu.make_async_copy(src, dst, sem)
        copy.start()
        return copy

    for i in range(k):
        shape = operands[i][1].shape
        if len(shape) == 2 and shape[1] == ring[0].shape[2]:
            for start in range(0, shape[0], PIECE):
                slot = turn % RING
                turn += 1
                if in_slot[slot]:
                    for copy in in_slot[slot]:
                        copy.wait()

                def block(b, carry):
                    at = pl.ds(pl.multiple_of(b * 32, 32), 32)
                    update(i, pl.ds(pl.multiple_of(start + b * 32, 32), 32), [ref.at[slot] for ref in ring], at)
                    return carry
                lax.fori_loop(0, PIECE // 32, block, 0, unroll=True)
                in_slot[slot] = [
                    send(ring[j].at[slot], results[i][j].at[pl.ds(start, PIECE)], ring_sem.at[slot, j]) for j in range(3)
                ]
            continue
        mine = buffers[3 * used : 3 * used + 3]
        if len(shape) == 3:
            for j in range(shape[0]):
                update(i, j, mine, j)
        else:
            update(i, slice(None), mine, slice(None))
        copies += [send(mine[j], results[i][j], own_sem.at[used, j]) for j in range(3)]
        used += 1
    for group in in_slot + [copies]:
        for copy in group or ():
            copy.wait()


def kernel_adam(step_count, small, grads, weights, firsts, seconds):
    k = len(weights)
    rates = tuple((0.5, 0.0) if i == k - 1 else (0.06, 0.01) for i in range(k))
    vm, sm = pl.BlockSpec(memory_space=pltpu.VMEM), pl.BlockSpec(memory_space=pltpu.SMEM)
    shapes = [jax.ShapeDtypeStruct(w.shape, F32) for w in weights for _ in range(3)]
    operands = [item for group in zip(grads, weights, firsts, seconds) for item in group]
    size = weights[0].shape[1]
    alone = [item for item in shapes if len(item.shape) == 3 or item.shape[1] != size]
    return pl.pallas_call(
        partial(adam_kernel, rates),
        out_shape=shapes,
        in_specs=[sm, vm] + [vm] * (4 * k),
        out_specs=[pl.BlockSpec(memory_space=pltpu.HBM)] * (3 * k),
        scratch_shapes=[pltpu.VMEM((RING, PIECE, size), F32)] * 3
        + [pltpu.SemaphoreType.DMA((RING, 3)), pltpu.SemaphoreType.DMA((len(alone) // 3, 3))]
        + [pltpu.VMEM(item.shape, F32) for item in alone],
        compiler_params=pltpu.CompilerParams(vmem_limit_bytes=12 << 20),
        name="adam",
    )(step_count, small, *operands)


def on_device(
    token_ids,
    query_lengths,
    negative_mask,
    positive_index,
    used_rows,
    step_count,
    table,
    w_mixed,
    w_out,
    w_inner,
    w_outer,
    norm_params,
    table_m,
    table_v,
    mixed_m,
    mixed_v,
    out_m,
    out_v,
    inner_m,
    inner_v,
    outer_m,
    outer_v,
    norms_m,
    norms_v,
):
    operands = (
        token_ids, query_lengths, negative_mask, positive_index, used_rows, table, w_mixed, w_out, w_inner, w_outer, norm_params
    )
    masters = (table, w_mixed, w_out, w_inner, w_outer, norm_params)
    firsts = (table_m, mixed_m, out_m, inner_m, outer_m, norms_m)
    seconds = (table_v, mixed_v, out_v, inner_v, outer_v, norms_v)
    if table.shape[1] % 384 == 0 and w_mixed.shape[1] % 64 == 0 and table.shape[1] <= 2048:
        small, grads, kept = kernel_gradients(*operands, table_m, table_v)

        def stored(tab, items):
            _, mixed, out, inner, outer, norm = items
            return tab, mixed[0].swapaxes(0, 1), out[0], inner[0], outer[0].T, norm.swapaxes(0, 1)

        grads = grads[:5] + (grads[5][0:6, None, :],)
        updated = kernel_adam(step_count, small, grads, *map(stored, kept, (masters, firsts, seconds)))
        back = (
            lambda x: x[None],
            lambda x: x.swapaxes(0, 1)[None],
            lambda x: x[None],
            lambda x: x[None],
            lambda x: x.T[None],
            lambda x: x.swapaxes(0, 1),
        )
        return (small[0, 0], small[1, 0]) + tuple(back[i // 3](item) for i, item in enumerate(updated))
    loss, grads = gradients(*operands)
    owner = (lax.axis_index("dp") == 0) & (lax.axis_index("mp") == 0)
    squares = jnp.where(owner, jnp.sum(grads[5] * grads[5]), 0.0)
    for grad in grads[:5]:
        squares = squares + jnp.sum(grad * grad)
    grad_norm = jnp.sqrt(lax.psum(squares, ("enc", "dp", "mp")))
    clip = jnp.minimum(1.0, clip_limit / (grad_norm + 1e-06))
    count = step_count[0].astype(F32)
    results = [loss, grad_norm]
    for index in range(6):
        rate, decay = (0.5, 0.0) if index == 5 else (0.06, 0.01)
        results.extend(
            adam_step(
                masters[index], grads[index][None] * clip, firsts[index], seconds[index], rate, decay, count
            )
        )
    return tuple(results)


def solution(mesh):
    table = P("enc", ("dp", "mp"), None)
    mixed = P("enc", "dp", None, "mp")
    columns = P("enc", "mp", "dp")
    units = P("enc", "dp", "mp")
    norms = P("enc", None, None)
    matrices = (table, mixed, columns, units, columns, norms)
    moments = tuple(spec for spec in matrices for _ in range(2))
    updated = tuple(spec for spec in matrices for _ in range(3))
    return jax.shard_map(
        on_device,
        mesh=mesh,
        in_specs=(P("enc", "dp", None), P("dp"), P(), P(), P(), P()) + matrices + moments,
        out_specs=(P(), P()) + updated,
        check_vma=False,
    )
```
